32 devices in a mesh: fsdp: 4 (over y, x), ctx: 2 (over core), tp: 4 (over z).
Axes of the slice: x: 2, y: 2, z: 4, core: 2. Of those that a mesh axis runs over, the one named last changes fastest.
Arguments:
- hidden_in: bfloat16 [8, 2048, 1536], P('fsdp', 'ctx', 'tp'), may hold values from -6 to 6
- lengths: int32 [8], P('fsdp'), may hold values from 512 to 2048, as said below
- norm_gain: bfloat16 [1536], P('tp'), may hold values from 0.5 to 1.5
- proj_gate_inner: bfloat16 [1536, 2, 3072], P(('fsdp', 'ctx'), None, 'tp'), may hold values from -0.15625 to 0.15625
- proj_write_read: bfloat16 [1536, 256], P(('fsdp', 'ctx')), may hold values from -0.15625 to 0.15625
- proj_step: bfloat16 [1536, 48], P(('fsdp', 'ctx'), 'tp'), may hold values from -0.15625 to 0.15625
- conv_inner: float32 [4, 3072], P(None, 'tp'), may hold values from -3 to 3
- conv_inner_bias: float32 [3072], P('tp'), may hold values from -1.75 to 1.75
- conv_write_read: float32 [4, 256], replicated, may hold values from -3 to 3
- conv_write_read_bias: float32 [256], replicated, may hold values from -1.75 to 1.75
- step_bias: float32 [48], P('tp'), may hold values from -7 to -1
- log_rate: float32 [48], P('tp'), may hold values from -3 to 1
- skip_gain: float32 [48], P('tp'), may hold values from 0.5 to 1.5
- gate_gain: float32 [3072], P('tp'), may hold values from 0.5 to 1.5
- proj_out: bfloat16 [1536, 3072], P(('fsdp', 'ctx'), 'tp'), may hold values from -0.109375 to 0.109375
- out_cotangent: bfloat16 [8, 2048, 1536], P('fsdp', 'ctx', 'tp'), may hold values from -6 to 6
Outputs:
- hidden_out: bfloat16 [8, 2048, 1536], P('fsdp', 'ctx', 'tp')
- grad_hidden_in: float32 [8, 2048, 1536], P('fsdp', 'ctx', 'tp')
- grad_norm_gain: float32 [1536], P('tp')
- grad_proj_gate_inner: float32 [1536, 2, 3072], P(('fsdp', 'ctx'), None, 'tp')
- grad_proj_write_read: float32 [1536, 256], P(('fsdp', 'ctx'))
- grad_proj_step: float32 [1536, 48], P(('fsdp', 'ctx'), 'tp')
- grad_conv_inner: float32 [4, 3072], P(None, 'tp')
- grad_conv_inner_bias: float32 [3072], P('tp')
- grad_conv_write_read: float32 [4, 256], replicated
- grad_conv_write_read_bias: float32 [256], replicated
- grad_step_bias: float32 [48], P('tp')
- grad_log_rate: float32 [48], P('tp')
- grad_skip_gain: float32 [48], P('tp')
- grad_gate_gain: float32 [3072], P('tp')
- grad_proj_out: float32 [1536, 3072], P(('fsdp', 'ctx'), 'tp')
The draws below stay inside these ranges and needn't reach their ends.
Inputs may be any that keep to these rules, and one draw needn't show every extreme that they name: lengths[s] is the number of valid leading positions of slot s; in every draw some slot is full.
All inputs are finite; a program needn't handle non-finite values.
Results may differ from the reference program's by a relative error of at most 0.017.
Values may be sent and summed in bfloat16 or wider, within the bound.
A program may use at most 192 MiB of HBM per device.

```python
from functools import partial
import jax
import jax.numpy as jnp
from jax import lax

D = 1536
HEADS = 48
HEADDIM = 64
STATE = 128
CONV = 4
GROUP = 256
INNER = 3072
SLOTS = 8
SEQ_LEN = 2048


def draw_lengths(key, part):
    first, second = jax.random.split(key)
    picked = jax.random.randint(first, (SLOTS,), SEQ_LEN // 4, SEQ_LEN + 1)
    full_slot = jax.random.randint(second, (), 0, SLOTS)
    return jnp.where(jnp.arange(SLOTS) == full_slot, SEQ_LEN, picked).astype(jnp.int32)


def level_of(rng, dims, shards, low, largest):
    def one(axis_at, blocks):
        heights = jax.random.uniform(jax.random.fold_in(jax.random.fold_in(rng, 6), axis_at), (blocks,), jnp.float32, low / len(shards), largest / len(shards))
        return jnp.repeat(jnp.exp(heights), dims[axis_at] // blocks).reshape((-1,) + (1,) * (len(dims) - axis_at - 1))

    loudness = one(*shards[0])
    for cut in shards[1:]:
        loudness = loudness * one(*cut)
    return loudness


def normal_values(own_key, shape, scale, most, cuts=(), kind=jnp.bfloat16):
    result = jax.random.normal(own_key, shape, jnp.float32) * scale
    if len(cuts) > 0:
        result = level_of(own_key, shape, cuts, -0.22, 0.18) * result
    return jnp.clip(result, min=-most, max=most).astype(kind)


def setup_inputs(seed: int = 0) -> dict:
    streams_of = jax.random.split(jax.random.key(seed), 17)
    return {
        "hidden_in": normal_values(streams_of[0], (SLOTS, SEQ_LEN, D), 1.0, 6.0, ((0, 4), (1, 2), (2, 4))),
        "lengths": draw_lengths(jax.random.fold_in(streams_of[16], 71), 0),
        "norm_gain": jnp.clip(1.0 + 0.1 * jax.random.normal(streams_of[2], (D,), jnp.float32), 0.5, 1.5).astype(jnp.bfloat16),
        "proj_gate_inner": normal_values(streams_of[3], (D, 2, INNER), D ** -0.5, 0.15625, ((0, 8), (2, 4))),
        "proj_write_read": normal_values(streams_of[4], (D, 2 * STATE), D ** -0.5, 0.15625, ((0, 8),)),
        "proj_step": normal_values(streams_of[5], (D, HEADS), D ** -0.5, 0.15625, ((0, 8), (1, 4))),
        "conv_inner": normal_values(streams_of[6], (CONV, INNER), CONV ** -0.5, 3.0, ((1, 4),), jnp.float32),
        "conv_inner_bias": normal_values(streams_of[7], (INNER,), 0.3, 1.75, ((0, 4),), jnp.float32),
        "conv_write_read": normal_values(streams_of[8], (CONV, 2 * STATE), CONV ** -0.5, 3.0, (), jnp.float32),
        "conv_write_read_bias": normal_values(streams_of[9], (2 * STATE,), 0.3, 1.75, (), jnp.float32),
        "step_bias": jnp.clip(-7.0 + 6.0 * jax.random.uniform(streams_of[10], (HEADS,), jnp.float32) ** level_of(streams_of[10], (HEADS,), ((0, 4),), -0.2, 0.2), -7.0, -1.0),
        "log_rate": jnp.clip(-3.0 + 4.0 * jax.random.uniform(streams_of[11], (HEADS,), jnp.float32) ** level_of(streams_of[11], (HEADS,), ((0, 4),), -0.2, 0.2), -3.0, 1.0),
        "skip_gain": jnp.clip(0.5 + 1.0 * jax.random.uniform(streams_of[12], (HEADS,), jnp.float32) ** level_of(streams_of[12], (HEADS,), ((0, 4),), -0.2, 0.2), 0.5, 1.5),
        "gate_gain": jnp.clip(1.0 + 0.1 * jax.random.normal(streams_of[13], (INNER,), jnp.float32), 0.5, 1.5),
        "proj_out": normal_values(streams_of[14], (D, INNER), INNER ** -0.5, 0.109375, ((0, 8), (1, 4))),
        "out_cotangent": normal_values(streams_of[15], (SLOTS, SEQ_LEN, D), 1.0, 6.0, ((0, 4), (1, 2), (2, 4))),
    }


EPSILON = 1e-05
HIGHEST = lax.Precision.HIGHEST

@jax.custom_vjp
def low(v):
    return lax.optimization_barrier(v.astype(jnp.bfloat16)).astype(jnp.float32)

@jax.custom_vjp
def low_back(v):
    return v

def low_keep(v):
    return (low(v), None)

def low_pass(kept, grad):
    return (grad,)

def back_keep(v):
    return (v, None)

def back_low(kept, grad):
    return (low(grad),)
low.defvjp(low_keep, low_pass)
low_back.defvjp(back_keep, back_low)

def conv_silu(padded, conv_taps, conv_bias):
    tap_count = conv_taps.shape[0]
    length = padded.shape[-2] - tap_count + 1
    summed = conv_bias
    for offset in range(tap_count):
        summed = summed + conv_taps[offset] * padded[..., offset:offset + length, :]
    return jax.nn.silu(summed)

def decay_terms(scores, write_piece, read_piece, step_rows, log_rate):
    length = scores.shape[0]
    cumulative = jnp.cumsum(step_rows * (-jnp.exp(log_rate))[:, None], axis=1)
    lower_mask = jnp.arange(length)[:, None] >= jnp.arange(length)[None, :]
    spread = jnp.where(lower_mask[None], cumulative[:, :, None] - cumulative[:, None, :], 0.0)
    weights = scores[None] * jnp.where(lower_mask[None], jnp.exp(spread), 0.0) * step_rows[:, None, :]
    read_scaled = read_piece[None] * jnp.exp(cumulative)[:, :, None]
    write_scaled = write_piece[None] * (jnp.exp(cumulative[:, -1:] - cumulative) * step_rows)[:, :, None]
    return (weights, read_scaled, write_scaled, jnp.exp(cumulative[:, -1]))

def state_group(log_rate, state, pieces):
    inner_piece, write_piece, read_piece, step_rows = pieces
    scores = low_back(jnp.dot(read_piece, write_piece.T, precision=HIGHEST))
    weights, read_scaled, write_scaled, block_decay = decay_terms(scores, write_piece, read_piece, step_rows, log_rate)
    intra_part = jnp.einsum('hts,shp->thp', low(weights), inner_piece, precision=HIGHEST)
    inter_part = jnp.einsum('htn,hpn->thp', low(read_scaled), low(state), precision=HIGHEST)
    diag_part = low_back(intra_part + inter_part)
    local_state = low_back(jnp.einsum('shp,hsn->hpn', inner_piece, low(write_scaled), precision=HIGHEST))
    return (block_decay[:, None, None] * state + local_state, diag_part)

def layer_slot(params, seq_in, valid_rows):
    norm_gain, proj_gate_inner, proj_write_read, proj_step, conv_inner, conv_inner_bias, conv_write_read, conv_write_read_bias, step_bias, log_rate, skip_gain, gate_gain, proj_out = params
    mean_square = lax.optimization_barrier(jnp.mean(seq_in * seq_in, axis=-1, keepdims=True))
    normed = low(seq_in * lax.rsqrt(mean_square + EPSILON) * norm_gain)
    gate_inner = jnp.einsum('ld,dki->lki', normed, proj_gate_inner, precision=HIGHEST)
    gate_pre = low_back(gate_inner[:, 0])
    inner_pre = low_back(low(gate_inner[:, 1]))
    write_read_pre = low_back(low(jnp.dot(normed, proj_write_read, precision=HIGHEST)))
    step_raw = low_back(jnp.dot(normed, proj_step, precision=HIGHEST))
    rim_rows = CONV - 1
    inner_act = low(conv_silu(jnp.pad(inner_pre, ((rim_rows, 0), (0, 0))), conv_inner, conv_inner_bias))
    write_read_act = low(conv_silu(jnp.pad(write_read_pre, ((rim_rows, 0), (0, 0))), conv_write_read, conv_write_read_bias))
    step_size = jax.nn.softplus(step_raw + step_bias)
    groups = SEQ_LEN // GROUP
    inner_blocks = inner_act.reshape(groups, GROUP, HEADS, HEADDIM)
    write_blocks = write_read_act[:, :STATE].reshape(groups, GROUP, STATE)
    read_blocks = write_read_act[:, STATE:].reshape(groups, GROUP, STATE)
    step_blocks = step_size.reshape(groups, GROUP, HEADS).transpose(0, 2, 1)
    start_state = jnp.zeros((HEADS, HEADDIM, STATE), jnp.float32)
    final_state, diag_part = lax.scan(jax.checkpoint(partial(state_group, log_rate)), start_state, (inner_blocks, write_blocks, read_blocks, step_blocks))
    mixed_out = diag_part.reshape(SEQ_LEN, HEADS, HEADDIM) + skip_gain[:, None] * inner_act.reshape(SEQ_LEN, HEADS, HEADDIM)
    mixed_out = mixed_out.reshape(SEQ_LEN, INNER)
    gated_out = mixed_out * jax.nn.silu(gate_pre)
    gate_rms = lax.rsqrt(lax.optimization_barrier(jnp.mean(gated_out * gated_out, axis=-1, keepdims=True)) + EPSILON)
    normed_out = low(gated_out * gate_rms * gate_gain)
    branch = low_back(jnp.dot(normed_out, proj_out.T, precision=HIGHEST))
    return seq_in + valid_rows[:, None] * branch

def forward(lengths, hidden, *params):

    def one_slot(pieces):
        seq_in, count = pieces
        valid_rows = (jnp.arange(SEQ_LEN) < count).astype(jnp.float32)
        return layer_slot(params, seq_in, valid_rows)
    return lax.map(one_slot, (hidden, lengths))

def reference(hidden_in, lengths, norm_gain, proj_gate_inner, proj_write_read, proj_step, conv_inner, conv_inner_bias, conv_write_read, conv_write_read_bias, step_bias, log_rate, skip_gain, gate_gain, proj_out, out_cotangent):
    params = tuple((weight_arg.astype(jnp.float32) for weight_arg in (norm_gain, proj_gate_inner, proj_write_read, proj_step, conv_inner, conv_inner_bias, conv_write_read, conv_write_read_bias, step_bias, log_rate, skip_gain, gate_gain, proj_out)))
    hidden_out, pull_back = jax.vjp(partial(forward, lengths), hidden_in.astype(jnp.float32), *params)
    gradients = pull_back(out_cotangent.astype(jnp.float32))
    return (hidden_out.astype(jnp.bfloat16), gradients[0], gradients[1], gradients[2], gradients[3], gradients[4], gradients[5], gradients[6], gradients[7], gradients[8], gradients[9], gradients[10], gradients[11], gradients[12], gradients[13])
```

```python
import functools

import jax
import jax.numpy as jnp
from jax import lax
from jax.experimental import pallas as pl
from jax.experimental.pallas import tpu as pltpu
from jax.sharding import PartitionSpec as P

HEADDIM = 64
STATE = 128
CONV = 4
GROUP = 256
INNER = 3072
EPSILON = 1e-05
PAIR = 2 * HEADDIM
HEADS_STEP = 6
LANES_STEP = HEADS_STEP * HEADDIM
F32 = jnp.float32
BF16 = jnp.bfloat16
HIGHEST = lax.Precision.HIGHEST
OUTER = (("fsdp", "ctx"))


def swap(x, bit):
    count = lax.axis_size("tp")
    return lax.ppermute(x, "tp", [(i, i ^ bit) for i in range(count)])


def passed_along(x, axis, by):
    count = lax.axis_size(axis)
    pairs = [(i, i + by) for i in range(count) if 0 <= i + by < count]
    return lax.ppermute(x, axis, pairs)


def carried_in(decay, final, combine, reverse):
    count, position = (lax.axis_size("ctx"), lax.axis_index("ctx"))
    if count == 2:
        return passed_along(final.astype(BF16), "ctx", -1 if reverse else 1).astype(F32)
    decays = lax.all_gather(decay.astype(BF16), "ctx").astype(F32)
    finals = lax.all_gather(final.astype(BF16), "ctx")
    start = jnp.zeros_like(final)

    def lap(k, before):
        at = count - 1 - k if reverse else k
        reached = at > position if reverse else at < position
        new = decays[at] * before + finals[at].astype(F32)
        return jnp.where(reached, new, before)

    return lax.fori_loop(0, count, lap, start)


def conv_silu(padded, conv_taps, conv_bias):
    tap_count = conv_taps.shape[0]
    length = padded.shape[-2] - tap_count + 1
    summed = conv_bias
    for offset in range(tap_count):
        summed = summed + conv_taps[offset] * padded[..., offset : offset + length, :]
    return jax.nn.silu(summed)


def dot(a, b, da, db):
    return lax.dot_general(a, b, (((da,), (db,)), ((), ())), preferred_element_type=F32)


def low_lanes(rows):
    return lax.broadcasted_iota(jnp.int32, (rows, PAIR), 1) < HEADDIM


def spread_heads(cols, pair, low_half):
    return jnp.where(low_half, cols[:, 2 * pair : 2 * pair + 1], cols[:, 2 * pair + 1 : 2 * pair + 2])


def state_kernel(a_ref, b_ref, scale_ref, out_ref):
    scale = scale_ref[0]
    low_half = low_lanes(GROUP)
    for pair in range(HEADS_STEP // 2):
        lanes = slice(PAIR * pair, PAIR * (pair + 1))
        scaled = (b_ref[:, lanes].astype(F32) * spread_heads(scale, pair, low_half)).astype(BF16)
        out_ref[0, :, lanes] = dot(a_ref[...], scaled, 0, 0)


def block_outer(rows_a, cols_b, scale):
    tokens, width = cols_b.shape
    blocks, steps = tokens // GROUP, width // LANES_STEP
    return pl.pallas_call(
        state_kernel,
        grid=(blocks, steps),
        in_specs=[
            pl.BlockSpec((GROUP, STATE), lambda b, g: (b, 0)),
            pl.BlockSpec((GROUP, LANES_STEP), lambda b, g: (b, g)),
            pl.BlockSpec((1, GROUP, HEADS_STEP), lambda b, g: (g, b, 0)),
        ],
        out_specs=pl.BlockSpec((1, STATE, LANES_STEP), lambda b, g: (b, 0, g)),
        out_shape=jax.ShapeDtypeStruct((blocks, STATE, width), F32),
        cost_estimate=pl.CostEstimate(
            flops=2 * tokens * STATE * width,
            bytes_accessed=tokens * width * 2 + blocks * STATE * width * 4,
            transcendentals=0,
        ),
        name="block_outer",
    )(rows_a, cols_b, scale)


def mix_kernel(
    x_ref, gate_ref, w_ref, r_ref, step_ref, cum_ref, cumt_ref, state_ref, skip_ref,
    mixed_ref, square_ref, scores_ref,
):
    g = pl.program_id(1)

    @pl.when(g == 0)
    def _():
        scores_ref[...] = dot(r_ref[...], w_ref[...], 1, 1)
        square_ref[...] = jnp.zeros_like(square_ref)

    cum, cumt, step = cum_ref[0], cumt_ref[0, 0], step_ref[0]
    grown = jnp.exp(cum)
    low_half = low_lanes(GROUP)
    lower = lax.broadcasted_iota(jnp.int32, (GROUP, GROUP), 0) >= lax.broadcasted_iota(
        jnp.int32, (GROUP, GROUP), 1
    )
    squares = jnp.zeros((GROUP, 1), F32)
    for pair in range(HEADS_STEP // 2):
        lanes = slice(PAIR * pair, PAIR * (pair + 1))
        x = x_ref[:, lanes].astype(F32)
        stepped = x * spread_heads(step, pair, low_half)
        halves = (
            jnp.where(low_half, stepped, 0.0).astype(BF16),
            jnp.where(low_half, 0.0, stepped).astype(BF16),
        )
        total = dot(r_ref[...], state_ref[0, :, lanes], 1, 0) * spread_heads(grown, pair, low_half)
        for side in range(2):
            head = 2 * pair + side
            spread = jnp.where(lower, cum[:, head : head + 1] - cumt[head : head + 1, :], -1e30)
            weights = (scores_ref[...] * jnp.exp(spread)).astype(BF16)
            total = total + dot(weights, halves[side], 1, 0)
        mixed = total + skip_ref[:, lanes] * x
        mixed_ref[:, lanes] = mixed
        gate = gate_ref[:, lanes].astype(F32)
        gated = mixed * (gate * jax.nn.sigmoid(gate))
        squares = squares + jnp.sum(gated * gated, axis=1, keepdims=True)
    square_ref[...] += squares


def mix_blocks(x, gate, write, read, step, cum, cumt, states, skip):
    tokens, width = x.shape
    blocks, steps = tokens // GROUP, width // LANES_STEP
    wide = pl.BlockSpec((GROUP, LANES_STEP), lambda b, g: (b, g))
    narrow = pl.BlockSpec((GROUP, STATE), lambda b, g: (b, 0))
    cols = pl.BlockSpec((1, GROUP, HEADS_STEP), lambda b, g: (g, b, 0))
    return pl.pallas_call(
        mix_kernel,
        grid=(blocks, steps),
        in_specs=[
            wide, wide, narrow, narrow, cols, cols,
            pl.BlockSpec((1, 1, HEADS_STEP, GROUP), lambda b, g: (g, b, 0, 0)),
            pl.BlockSpec((1, STATE, LANES_STEP), lambda b, g: (b, 0, g)),
            pl.BlockSpec((1, LANES_STEP), lambda b, g: (0, g)),
        ],
        out_specs=[wide, pl.BlockSpec((GROUP, 1), lambda b, g: (b, 0))],
        out_shape=[
            jax.ShapeDtypeStruct((tokens, width), F32),
            jax.ShapeDtypeStruct((tokens, 1), F32),
        ],
        scratch_shapes=[pltpu.VMEM((GROUP, GROUP), F32)],
        cost_estimate=pl.CostEstimate(
            flops=2 * tokens * width * (2 * GROUP + 2 * STATE) * 2,
            bytes_accessed=tokens * width * 10,
            transcendentals=tokens * GROUP * width // HEADDIM,
        ),
        name="mix_blocks",
    )(x, gate, write, read, step, cum, cumt, states, skip)


def segment_sums(values):
    rows = lax.broadcasted_iota(jnp.int32, (LANES_STEP, HEADS_STEP), 0) // HEADDIM
    chosen = (rows == lax.broadcasted_iota(jnp.int32, (LANES_STEP, HEADS_STEP), 1)).astype(BF16)
    high = values.astype(BF16)
    rest = (values - high.astype(F32)).astype(BF16)
    return dot(high, chosen, 1, 0) + dot(rest, chosen, 1, 0)


def back_kernel(
    x_ref, mixed_ref, grad_ref, w_ref, r_ref, step_ref, cum_ref, cumt_ref, state_ref, flow_ref, skip_ref,
    gx_ref, gw_ref, gr_ref, u_ref, v_ref, i_ref,
    scores_ref, gscores_ref, prod_ref,
):
    g = pl.program_id(1)

    @pl.when(g == 0)
    def _():
        scores_ref[...] = dot(r_ref[...], w_ref[...], 1, 1)
        gscores_ref[...] = jnp.zeros_like(gscores_ref)
        gw_ref[...] = jnp.zeros_like(gw_ref)
        gr_ref[...] = jnp.zeros_like(gr_ref)

    cum, cumt, step = cum_ref[0], cumt_ref[0, 0], step_ref[0]
    grown = jnp.exp(cum)
    shrunk = jnp.exp(cum[GROUP - 1 : GROUP, :] - cum)
    low_half = low_lanes(GROUP)
    lower = lax.broadcasted_iota(jnp.int32, (GROUP, GROUP), 0) >= lax.broadcasted_iota(
        jnp.int32, (GROUP, GROUP), 1
    )
    grad_write = jnp.zeros((GROUP, STATE), F32)
    grad_read = jnp.zeros((GROUP, STATE), F32)
    for pair in range(HEADS_STEP // 2):
        lanes = slice(PAIR * pair, PAIR * (pair + 1))
        x = x_ref[:, lanes].astype(F32)
        grad = grad_ref[:, lanes]
        grad_f = grad.astype(F32)
        skip = skip_ref[:, lanes]
        steps = spread_heads(step, pair, low_half)
        tail = spread_heads(shrunk, pair, low_half)
        stepped = x * steps
        x_halves = (
            jnp.where(low_half, stepped, 0.0).astype(BF16),
            jnp.where(low_half, 0.0, stepped).astype(BF16),
        )
        g_halves = (
            jnp.where(low_half, grad_f, 0.0).astype(BF16),
            jnp.where(low_half, 0.0, grad_f).astype(BF16),
        )
        flow = flow_ref[0, :, lanes]
        grad_read = grad_read + dot(
            (grad_f * spread_heads(grown, pair, low_half)).astype(BF16), state_ref[0, :, lanes], 1, 1
        )
        grad_write = grad_write + dot((stepped * tail).astype(BF16), flow, 1, 1)
        stepped_low = stepped.astype(BF16).astype(F32)
        inter = dot(w_ref[...], flow, 1, 0) * tail
        total = jnp.zeros_like(inter)
        for side in range(2):
            head = 2 * pair + side
            decay = jnp.exp(jnp.where(lower, cum[:, head : head + 1] - cumt[head : head + 1, :], -1e30))
            weights = (scores_ref[...] * decay).astype(BF16)
            total = total + dot(weights, g_halves[side], 0, 0)
            gscores_ref[...] += dot(grad, x_halves[side], 1, 1) * decay
        both = total + inter
        gx_ref[:, lanes] = steps * both + skip * grad_f
        prod_ref[0, :, lanes] = x * both
        prod_ref[1, :, lanes] = grad_f * (mixed_ref[:, lanes] - skip * x) - stepped_low * total
        prod_ref[2, :, lanes] = stepped_low * inter
    u_ref[0] = segment_sums(prod_ref[0])
    v_ref[0] = segment_sums(prod_ref[1])
    i_ref[0] = segment_sums(prod_ref[2])
    gw_ref[...] += grad_write
    gr_ref[...] += grad_read

    @pl.when(g == pl.num_programs(1) - 1)
    def _():
        low = gscores_ref[...].astype(BF16)
        gr_ref[...] += dot(low, w_ref[...], 1, 0)
        gw_ref[...] += dot(low, r_ref[...], 0, 0)


def back_blocks(x, mixed, grad, write, read, step, cum, cumt, states, flows, skip):
    tokens, width = x.shape
    blocks, steps = tokens // GROUP, width // LANES_STEP
    wide = pl.BlockSpec((GROUP, LANES_STEP), lambda b, g: (b, g))
    narrow = pl.BlockSpec((GROUP, STATE), lambda b, g: (b, 0))
    cols = pl.BlockSpec((1, GROUP, HEADS_STEP), lambda b, g: (g, b, 0))
    state = pl.BlockSpec((1, STATE, LANES_STEP), lambda b, g: (b, 0, g))
    return pl.pallas_call(
        back_kernel,
        grid=(blocks, steps),
        in_specs=[
            wide, wide, wide, narrow, narrow, cols, cols,
            pl.BlockSpec((1, 1, HEADS_STEP, GROUP), lambda b, g: (g, b, 0, 0)),
            state, state,
            pl.BlockSpec((1, LANES_STEP), lambda b, g: (0, g)),
        ],
        out_specs=[wide, narrow, narrow, cols, cols, cols],
        out_shape=[
            jax.ShapeDtypeStruct((tokens, width), F32),
            jax.ShapeDtypeStruct((tokens, STATE), F32),
            jax.ShapeDtypeStruct((tokens, STATE), F32),
            jax.ShapeDtypeStruct((steps, tokens, HEADS_STEP), F32),
            jax.ShapeDtypeStruct((steps, tokens, HEADS_STEP), F32),
            jax.ShapeDtypeStruct((steps, tokens, HEADS_STEP), F32),
        ],
        scratch_shapes=[
            pltpu.VMEM((GROUP, GROUP), F32),
            pltpu.VMEM((GROUP, GROUP), F32),
            pltpu.VMEM((3, GROUP, LANES_STEP), F32),
        ],
        cost_estimate=pl.CostEstimate(
            flops=2 * tokens * width * (4 * GROUP + 4 * STATE) * 2,
            bytes_accessed=tokens * width * 14,
            transcendentals=tokens * GROUP * width // HEADDIM,
        ),
        name="back_blocks",
    )(x, mixed, grad, write, read, step, cum, cumt, states, flows, skip)


def pack(parts):
    return jnp.concatenate([part.reshape(-1) for part in parts])


def unpack(vector, shapes):
    parts, at = [], 0
    for shape in shapes:
        size = 1
        for dim in shape:
            size *= dim
        parts.append(vector[at : at + size].reshape(shape))
        at += size
    return parts


def on_device(
    hidden_in,
    lengths,
    norm_gain,
    proj_gate_inner,
    proj_write_read,
    proj_step,
    conv_inner,
    conv_inner_bias,
    conv_write_read,
    conv_write_read_bias,
    step_bias,
    log_rate,
    skip_gain,
    gate_gain,
    proj_out,
    out_cotangent,
):
    slot_count, seq_here, width_here = hidden_in.shape
    slots = slot_count // 2
    tokens = slots * seq_here
    heads_own = step_bias.shape[0]
    inner_own = gate_gain.shape[0]
    heads = 2 * heads_own
    inner = 2 * inner_own
    tp_count = lax.axis_size("tp")
    width = tp_count * width_here
    groups = seq_here // GROUP
    blocks = slots * groups
    head_steps = heads // HEADS_STEP
    rim_rows = CONV - 1
    place = lax.axis_index("tp")
    far_half, near_side = place // 2, place % 2

    def half_of(whole, which):
        return lax.dynamic_slice_in_dim(whole, which * slots, slots, 0)

    def ordered(own, near, far, both, axis):
        first = lambda a, b: jnp.where(near_side == 0, a, b)
        a0, a1, b0, b1 = first(own, near), first(near, own), first(far, both), first(both, far)
        lower = lambda a, b: jnp.where(far_half == 0, a, b)
        return jnp.concatenate(
            [lower(a0, b0), lower(a1, b1), lower(b0, a0), lower(b1, a1)], axis=axis
        )

    def all_features(local):
        mine, other = half_of(local, far_half), half_of(local, 1 - far_half)
        far = swap(other, 2)
        near = swap(mine, 1)
        both = swap(far, 1)
        return ordered(mine, near, far, both, 2).reshape(tokens, width)

    def own_features(piece):
        relay = swap(piece(place ^ 3).astype(BF16), 1)
        keep = swap(piece(place ^ 1).astype(BF16), 1)
        sent = swap((piece(place ^ 2) + relay.astype(F32)).astype(BF16), 2)
        kept = (piece(place) + keep.astype(F32)).reshape(slots, seq_here, width_here)
        other = sent.astype(F32).reshape(slots, seq_here, width_here)
        return both_halves(kept, other)

    def both_halves(kept, other):
        return jnp.where(
            far_half == 0,
            jnp.concatenate([kept, other], axis=0),
            jnp.concatenate([other, kept], axis=0),
        )

    full_x = all_features(hidden_in)
    full_gain = ordered(norm_gain, swap(norm_gain, 1), swap(norm_gain, 2), swap(norm_gain, 3), 0)

    small_shapes = [(CONV, inner_own), (inner_own,), (inner_own,), (heads_own,), (heads_own,), (heads_own,)]
    own_small = pack([conv_inner, conv_inner_bias, gate_gain, step_bias, log_rate, skip_gain])
    far_small = unpack(swap(own_small, 2), small_shapes)
    taps = jnp.concatenate([conv_inner, far_small[0]], axis=1)
    taps_bias = jnp.concatenate([conv_inner_bias, far_small[1]])
    gain_gate = jnp.concatenate([gate_gain, far_small[2]])
    bias_step = jnp.concatenate([step_bias, far_small[3]])
    rate_log = jnp.concatenate([log_rate, far_small[4]])
    gain_skip = jnp.concatenate([skip_gain, far_small[5]])
    rate = -jnp.exp(rate_log)
    skip_lanes = jnp.repeat(gain_skip, HEADDIM)[None]

    def gathered(x):
        return lax.all_gather(x, ("fsdp", "ctx"), axis=0, tiled=True)

    narrow_cols = 2 * STATE + heads
    narrow_pad = -narrow_cols % 128
    narrow_shard = jnp.concatenate(
        [proj_write_read, proj_step, swap(proj_step, 2)]
        + [jnp.zeros((proj_step.shape[0], narrow_pad), BF16)],
        axis=1,
    )
    full_narrow = gathered(narrow_shard)
    own_gi, far_gi = gathered(proj_gate_inner), gathered(swap(proj_gate_inner, 2))
    own_out, far_out = gathered(proj_out), gathered(swap(proj_out, 2))
    full_gate = jnp.concatenate([own_gi[:, 0], far_gi[:, 0]], axis=1)
    full_inner = jnp.concatenate([own_gi[:, 1], far_gi[:, 1]], axis=1)
    full_out = jnp.concatenate([own_out, far_out], axis=1)
    full_cot = all_features(out_cotangent)

    in_float = full_x.astype(F32)
    in_scale = lax.rsqrt(jnp.mean(in_float * in_float, axis=-1, keepdims=True) + EPSILON)
    normed = (in_float * in_scale * full_gain.astype(F32)).astype(BF16)
    narrow_pre = dot(normed, full_narrow, 1, 0)
    write_read_pre = narrow_pre[:, : 2 * STATE].astype(BF16)
    step_raw = narrow_pre[:, 2 * STATE : narrow_cols]
    gate_pre = dot(normed, full_gate, 1, 0).astype(BF16)
    inner_pre = dot(normed, full_inner, 1, 0).astype(BF16)

    def padded(pre):
        by_slot = pre.reshape(slots, seq_here, pre.shape[-1])
        rim = passed_along(by_slot[:, seq_here - rim_rows :], "ctx", 1)
        return jnp.concatenate([rim, by_slot], axis=1).astype(F32)

    inner_pad, write_read_pad = padded(inner_pre), padded(write_read_pre)
    write_read_act = (
        conv_silu(write_read_pad, conv_write_read, conv_write_read_bias)
        .astype(BF16)
        .reshape(tokens, 2 * STATE)
    )
    inner_act = conv_silu(inner_pad, taps, taps_bias).astype(BF16).reshape(tokens, inner)
    write, read = write_read_act[:, :STATE], write_read_act[:, STATE:]

    step_size = jax.nn.softplus(step_raw + bias_step)
    step_blocks = step_size.reshape(blocks, GROUP, heads)
    lower = (jnp.arange(GROUP)[:, None] >= jnp.arange(GROUP)[None, :]).astype(F32)
    cum = jnp.einsum("ts,bsh->bth", lower, step_blocks * rate, precision=HIGHEST)

    def by_steps(cols):
        return cols.reshape(tokens, head_steps, HEADS_STEP).transpose(1, 0, 2)

    def from_steps(cols):
        return cols.transpose(1, 0, 2).reshape(blocks, GROUP, heads)

    step_cols, cum_cols = by_steps(step_size), by_steps(cum)
    cum_rows = cum.reshape(blocks, GROUP, head_steps, HEADS_STEP).transpose(2, 0, 3, 1)
    last = cum[:, GROUP - 1]
    write_scale = by_steps(jnp.exp(last[:, None] - cum) * step_blocks)
    decay = jnp.exp(last)
    decay_lanes = jnp.repeat(decay, HEADDIM, axis=1).reshape(slots, groups, 1, inner)

    local_state = block_outer(write, inner_act, write_scale).reshape(slots, groups, STATE, inner)
    carried = local_state[:, 0]
    device_decay = decay_lanes[:, 0]
    for position in range(1, groups):
        carried = decay_lanes[:, position] * carried + local_state[:, position]
        device_decay = device_decay * decay_lanes[:, position]
    current = carried_in(device_decay, carried, None, False)
    state_list = []
    for position in range(groups):
        state_list.append(current)
        current = decay_lanes[:, position] * current + local_state[:, position]
    states = jnp.stack(state_list, axis=1)
    states_low = states.astype(BF16).reshape(blocks, STATE, inner)

    mixed_out, squares = mix_blocks(
        inner_act, gate_pre, write, read, step_cols, cum_cols, cum_rows, states_low, skip_lanes
    )
    square_sum = squares + swap(squares, 1)
    out_scale = lax.rsqrt(square_sum / INNER + EPSILON)
    gate_float = gate_pre.astype(F32)
    gate_sigmoid = jax.nn.sigmoid(gate_float)
    gate_act = gate_float * gate_sigmoid
    gated_out = mixed_out * gate_act
    gate_hat = gated_out * out_scale
    normed_out = (gate_hat * gain_gate).astype(BF16)

    def branch_piece(which):
        rows = lax.dynamic_slice_in_dim(full_out, which * width_here, width_here, 0)
        return dot(normed_out, rows, 1, 1)

    branch = own_features(branch_piece)
    position_ids = lax.axis_index("ctx") * seq_here + jnp.arange(seq_here)
    valid_rows = (position_ids[None, :] < lengths[:, None]).astype(F32)
    hidden_out = (hidden_in.astype(F32) + valid_rows[..., None] * branch).astype(BF16)
    valid_here = half_of(valid_rows, far_half).reshape(tokens, 1)
    masked = (full_cot.astype(F32) * valid_here).astype(BF16)

    grad_proj_out = dot(masked, normed_out, 0, 0).astype(BF16)
    grad_normed_out = dot(masked, full_out, 1, 0)
    grad_gate_gain = jnp.sum(grad_normed_out * gate_hat, axis=0)
    grad_hat = grad_normed_out * gain_gate
    cross_part = jnp.sum(grad_hat * gate_hat, axis=-1, keepdims=True)
    cross_term = cross_part + swap(cross_part, 1)
    grad_gated = out_scale * (grad_hat - gate_hat * (cross_term / INNER))
    grad_mixed = grad_gated * gate_act
    grad_gate_pre = (
        grad_gated * mixed_out * gate_sigmoid * (1.0 + gate_float * (1.0 - gate_sigmoid))
    ).astype(BF16)
    grad_skip_lanes = jnp.sum(grad_mixed * inner_act.astype(F32), axis=0)
    grad_diag = grad_mixed.astype(BF16)
    grad_gate_w = dot(normed, grad_gate_pre, 0, 0).astype(BF16)

    read_scale = by_steps(jnp.exp(cum))
    local_grad = block_outer(read, grad_diag, read_scale).reshape(slots, groups, STATE, inner)
    flowing = local_grad[:, groups - 1]
    for position in reversed(range(groups - 1)):
        flowing = decay_lanes[:, position] * flowing + local_grad[:, position]
    flowing = carried_in(device_decay, flowing, None, True)
    flow_list = []
    for position in reversed(range(groups)):
        flow_list.insert(0, flowing)
        flowing = decay_lanes[:, position] * flowing + local_grad[:, position]
    flows = jnp.stack(flow_list, axis=1)
    last_grad = (
        jnp.sum(flows * states, axis=2).reshape(blocks, heads, HEADDIM).sum(axis=2) * decay
    )
    flows_low = flows.astype(BF16).reshape(blocks, STATE, inner)

    grad_inner_act, grad_write, grad_read, u_cols, v_cols, inter_cols = back_blocks(
        inner_act, mixed_out, grad_diag, write, read, step_cols, cum_cols, cum_rows,
        states_low, flows_low, skip_lanes,
    )
    u_blocks, v_blocks, inter_blocks = from_steps(u_cols), from_steps(v_cols), from_steps(inter_cols)
    reverse_sum = (
        jnp.einsum("ts,bth->bsh", lower, v_blocks, precision=HIGHEST)
        + jnp.einsum("st,bth->bsh", lower - jnp.eye(GROUP, dtype=F32), inter_blocks, precision=HIGHEST)
        + last_grad[:, None]
    )
    grad_step_size = u_blocks + rate * reverse_sum
    grad_log_rate = jnp.sum(reverse_sum * step_blocks, axis=(0, 1)) * rate
    grad_step_raw = grad_step_size.reshape(tokens, heads) * jax.nn.sigmoid(step_raw + bias_step)
    grad_step_bias = jnp.sum(grad_step_raw, axis=0)

    unused_inner, inner_pull = jax.vjp(conv_silu, inner_pad, taps, taps_bias)
    grad_inner_pad, grad_taps, grad_taps_bias = inner_pull(
        grad_inner_act.reshape(slots, seq_here, inner)
    )
    unused_write_read, write_read_pull = jax.vjp(
        conv_silu, write_read_pad, conv_write_read, conv_write_read_bias
    )
    grad_write_read_pad, grad_conv_write_read, grad_conv_write_read_bias = write_read_pull(
        jnp.concatenate([grad_write, grad_read], axis=1).reshape(slots, seq_here, 2 * STATE)
    )

    def unpadded(grad):
        back = passed_along(grad[:, :rim_rows], "ctx", -1)
        full = grad[:, rim_rows:].at[:, seq_here - rim_rows :].add(back)
        return full.astype(BF16).reshape(tokens, grad.shape[-1])

    grad_inner_pre, grad_write_read_pre = unpadded(grad_inner_pad), unpadded(grad_write_read_pad)
    grad_narrow = jnp.concatenate(
        [grad_write_read_pre, grad_step_raw.astype(BF16), jnp.zeros((tokens, narrow_pad), BF16)], axis=1
    )
    grad_inner_w = dot(normed, grad_inner_pre, 0, 0).astype(BF16)
    grad_narrow_w = dot(normed, grad_narrow, 0, 0).astype(BF16)

    def normed_piece(which):
        def rows(full):
            return lax.dynamic_slice_in_dim(full, which * width_here, width_here, 0)

        return (
            dot(grad_gate_pre, rows(full_gate), 1, 1)
            + dot(grad_inner_pre, rows(full_inner), 1, 1)
            + dot(grad_narrow, rows(full_narrow), 1, 1)
        )

    grad_normed = own_features(normed_piece)

    def reduced(x):
        return lax.psum_scatter(x, ("fsdp", "ctx"), scatter_dimension=0, tiled=True)

    def home(x, axis):
        own = lax.slice_in_dim(x, 0, x.shape[axis] // 2, axis=axis).astype(F32)
        away = lax.slice_in_dim(x, x.shape[axis] // 2, x.shape[axis], axis=axis)
        return own + swap(away, 2).astype(F32)

    grad_out_home = home(reduced(grad_proj_out), 1)
    grad_gate_home = home(reduced(grad_gate_w), 1)
    grad_inner_home = home(reduced(grad_inner_w), 1)
    narrow_reduced = reduced(grad_narrow_w)
    write_read_home = narrow_reduced[:, : 2 * STATE].astype(F32)
    write_read_home = write_read_home + swap(write_read_home, 1)
    write_read_home = write_read_home + swap(write_read_home, 2)
    step_home = home(narrow_reduced[:, 2 * STATE : narrow_cols], 1)

    own_gain = norm_gain.astype(F32)
    other_scale = swap(in_scale, 2)
    own_scale = both_halves(
        in_scale.reshape(slots, seq_here, 1), other_scale.reshape(slots, seq_here, 1)
    )
    own_hat = hidden_in.astype(F32) * own_scale
    grad_hat_in = grad_normed * own_gain
    cross_in = jnp.sum(grad_hat_in * own_hat, axis=-1, keepdims=True)
    cross_in = lax.psum(cross_in, "tp") / width
    grad_hidden_in = own_scale * (grad_hat_in - own_hat * cross_in) + out_cotangent.astype(F32)
    grad_norm_gain = jnp.sum(grad_normed * own_hat, axis=(0, 1))

    grad_skip_gain = jnp.sum(grad_skip_lanes.reshape(heads, HEADDIM), axis=1)
    shared_shapes = [(CONV, 2 * STATE), (2 * STATE,), (width_here,)]
    head_shapes = [(CONV, inner), (inner,), (inner,), (heads,), (heads,), (heads,)]
    smalls = lax.psum(
        pack(
            [
                grad_taps, grad_taps_bias, grad_gate_gain, grad_step_bias, grad_log_rate, grad_skip_gain,
                grad_conv_write_read, grad_conv_write_read_bias, grad_norm_gain,
            ]
        ),
        ("fsdp", "ctx"),
    )
    parts = unpack(smalls, head_shapes + shared_shapes)
    shared = pack(parts[6:8])
    shared = shared + swap(shared, 1)
    shared = shared + swap(shared, 2)
    wr_taps, wr_bias = unpack(shared, shared_shapes[:2])
    away = swap(pack([lax.slice_in_dim(p, p.shape[-1] // 2, p.shape[-1], axis=p.ndim - 1) for p in parts[:6]]), 2)
    homes = [
        lax.slice_in_dim(p, 0, p.shape[-1] // 2, axis=p.ndim - 1) + a
        for p, a in zip(parts[:6], unpack(away, small_shapes))
    ]
    return (
        hidden_out,
        grad_hidden_in,
        parts[8],
        jnp.stack([grad_gate_home, grad_inner_home], axis=1),
        write_read_home,
        step_home,
        homes[0],
        homes[1],
        wr_taps,
        wr_bias,
        homes[3],
        homes[4],
        homes[5],
        homes[2],
        grad_out_home,
    )


def solution(mesh):
    rows = ("fsdp", "ctx")
    acts = P("fsdp", "ctx", "tp")
    placed = (
        acts,
        P("fsdp"),
        P("tp"),
        P(rows, None, "tp"),
        P(rows, None),
        P(rows, "tp"),
        P(None, "tp"),
        P("tp"),
        P(),
        P(),
        P("tp"),
        P("tp"),
        P("tp"),
        P("tp"),
        P(rows, "tp"),
        acts,
    )
    return jax.shard_map(
        on_device,
        mesh=mesh,
        in_specs=placed,
        out_specs=(
            acts,
            acts,
            P("tp"),
            P(rows, None, "tp"),
            P(rows, None),
            P(rows, "tp"),
            P(None, "tp"),
            P("tp"),
            P(),
            P(),
            P("tp"),
            P("tp"),
            P("tp"),
            P("tp"),
            P(rows, "tp"),
        ),
        check_vma=False,
    )
```

```python
import functools

import jax
import jax.numpy as jnp
from jax import lax
from jax.experimental import pallas as pl
from jax.experimental.pallas import tpu as pltpu
from jax.sharding import PartitionSpec as P

HEADDIM = 64
STATE = 128
CONV = 4
GROUP = 256
INNER = 3072
EPSILON = 1e-05
PAIR = 2 * HEADDIM
HEADS_STEP = 6
LANES_STEP = HEADS_STEP * HEADDIM
F32 = jnp.float32
BF16 = jnp.bfloat16
HIGHEST = lax.Precision.HIGHEST


def swap(x, bit):
    count = lax.axis_size("tp")
    return lax.ppermute(x, "tp", [(i, i ^ bit) for i in range(count)])


def passed_along(x, axis, by):
    count = lax.axis_size(axis)
    pairs = [(i, i + by) for i in range(count) if 0 <= i + by < count]
    return lax.ppermute(x, axis, pairs)


def carried_in(decay, final, combine, reverse):
    count, position = (lax.axis_size("ctx"), lax.axis_index("ctx"))
    if count == 2:
        return passed_along(final.astype(BF16), "ctx", -1 if reverse else 1).astype(F32)
    decays = lax.all_gather(decay.astype(BF16), "ctx").astype(F32)
    finals = lax.all_gather(final.astype(BF16), "ctx")
    start = jnp.zeros_like(final)

    def lap(k, before):
        at = count - 1 - k if reverse else k
        reached = at > position if reverse else at < position
        new = decays[at] * before + finals[at].astype(F32)
        return jnp.where(reached, new, before)

    return lax.fori_loop(0, count, lap, start)


def conv_silu(padded, conv_taps, conv_bias):
    tap_count = conv_taps.shape[0]
    length = padded.shape[-2] - tap_count + 1
    summed = conv_bias
    for offset in range(tap_count):
        summed = summed + conv_taps[offset] * padded[..., offset : offset + length, :]
    return jax.nn.silu(summed)


def dot(a, b, da, db):
    return lax.dot_general(a, b, (((da,), (db,)), ((), ())), preferred_element_type=F32)


def low_lanes(rows):
    return lax.broadcasted_iota(jnp.int32, (rows, PAIR), 1) < HEADDIM


def spread_heads(cols, pair, low_half):
    return jnp.where(low_half, cols[:, 2 * pair : 2 * pair + 1], cols[:, 2 * pair + 1 : 2 * pair + 2])


def state_kernel(a_ref, b_ref, scale_ref, out_ref, scaled_ref):
    scale = scale_ref[0]
    low_half = low_lanes(GROUP)
    for pair in range(HEADS_STEP // 2):
        lanes = slice(PAIR * pair, PAIR * (pair + 1))
        scaled = b_ref[:, lanes].astype(F32) * spread_heads(scale, pair, low_half)
        scaled_ref[:, lanes] = scaled.astype(BF16)
    out_ref[0] = dot(a_ref[...], scaled_ref[...], 1, 0)


def block_outer(cols_a, cols_b, scale):
    tokens, width = cols_b.shape
    blocks, steps = tokens // GROUP, width // LANES_STEP
    return pl.pallas_call(
        state_kernel,
        grid=(blocks, steps),
        in_specs=[
            pl.BlockSpec((STATE, GROUP), lambda b, g: (0, b)),
            pl.BlockSpec((GROUP, LANES_STEP), lambda b, g: (b, g)),
            pl.BlockSpec((1, GROUP, HEADS_STEP), lambda b, g: (g, b, 0)),
        ],
        out_specs=pl.BlockSpec((1, STATE, LANES_STEP), lambda b, g: (b, 0, g)),
        out_shape=jax.ShapeDtypeStruct((blocks, STATE, width), F32),
        scratch_shapes=[pltpu.VMEM((GROUP, LANES_STEP), BF16)],
        cost_estimate=pl.CostEstimate(
            flops=2 * tokens * STATE * width,
            bytes_accessed=tokens * width * 2 + blocks * STATE * width * 4,
            transcendentals=0,
        ),
        name="block_outer",
    )(cols_a, cols_b, scale)


def mix_kernel(
    x_ref, gate_ref, gno_ref, w_ref, r_ref, step_ref, cum_ref, cumt_ref, state_ref, skip_ref, gain_ref,
    mixed_ref, stats_ref, scores_ref, sums_ref,
):
    g = pl.program_id(1)

    @pl.when(g == 0)
    def _():
        scores_ref[...] = dot(r_ref[...], w_ref[...], 1, 1)
        sums_ref[...] = jnp.zeros_like(sums_ref)

    cum, cumt, step = cum_ref[0], cumt_ref[0, 0], step_ref[0]
    grown = jnp.exp(cum)
    low_half = low_lanes(GROUP)
    lower = lax.broadcasted_iota(jnp.int32, (GROUP, GROUP), 0) >= lax.broadcasted_iota(
        jnp.int32, (GROUP, GROUP), 1
    )
    squares = jnp.zeros((GROUP, 1), F32)
    crosses = jnp.zeros((GROUP, 1), F32)
    for pair in range(HEADS_STEP // 2):
        lanes = slice(PAIR * pair, PAIR * (pair + 1))
        x = x_ref[:, lanes].astype(F32)
        stepped = x * spread_heads(step, pair, low_half)
        halves = (
            jnp.where(low_half, stepped, 0.0).astype(BF16),
            jnp.where(low_half, 0.0, stepped).astype(BF16),
        )
        total = dot(r_ref[...], state_ref[0, :, lanes], 1, 0) * spread_heads(grown, pair, low_half)
        for side in range(2):
            head = 2 * pair + side
            spread = jnp.where(lower, cum[:, head : head + 1] - cumt[head : head + 1, :], -1e30)
            weights = (scores_ref[...] * jnp.exp(spread)).astype(BF16)
            total = total + dot(weights, halves[side], 1, 0)
        mixed = total + skip_ref[:, lanes] * x
        mixed_ref[:, lanes] = mixed
        gate = gate_ref[:, lanes].astype(F32)
        gated = mixed * (gate * jax.nn.sigmoid(gate))
        squares = squares + jnp.sum(gated * gated, axis=1, keepdims=True)
        grad_hat = gno_ref[:, lanes].astype(F32) * gain_ref[:, lanes]
        crosses = crosses + jnp.sum(gated * grad_hat, axis=1, keepdims=True)
    lane = lax.broadcasted_iota(jnp.int32, (GROUP, 128), 1)
    sums_ref[...] += jnp.where(lane == 0, squares, jnp.where(lane == 1, crosses, 0.0))

    @pl.when(g == pl.num_programs(1) - 1)
    def _():
        stats_ref[0] = sums_ref[...].T[:8]


def mix_blocks(x, gate, gno, write, read, step, cum, cumt, states, skip, gain):
    tokens, width = x.shape
    blocks, steps = tokens // GROUP, width // LANES_STEP
    wide = pl.BlockSpec((GROUP, LANES_STEP), lambda b, g: (b, g))
    narrow = pl.BlockSpec((GROUP, STATE), lambda b, g: (b, 0))
    cols = pl.BlockSpec((1, GROUP, HEADS_STEP), lambda b, g: (g, b, 0))
    return pl.pallas_call(
        mix_kernel,
        grid=(blocks, steps),
        in_specs=[
            wide, wide, wide, narrow, narrow, cols, cols,
            pl.BlockSpec((1, 1, HEADS_STEP, GROUP), lambda b, g: (g, b, 0, 0)),
            pl.BlockSpec((1, STATE, LANES_STEP), lambda b, g: (b, 0, g)),
            pl.BlockSpec((1, LANES_STEP), lambda b, g: (0, g)),
            pl.BlockSpec((1, LANES_STEP), lambda b, g: (0, g)),
        ],
        out_specs=[wide, pl.BlockSpec((1, 8, GROUP), lambda b, g: (b, 0, 0))],
        out_shape=[
            jax.ShapeDtypeStruct((tokens, width), F32),
            jax.ShapeDtypeStruct((blocks, 8, GROUP), F32),
        ],
        scratch_shapes=[pltpu.VMEM((GROUP, GROUP), F32), pltpu.VMEM((GROUP, 128), F32)],
        cost_estimate=pl.CostEstimate(
            flops=2 * tokens * width * (2 * GROUP + 2 * STATE) * 2,
            bytes_accessed=tokens * width * 10,
            transcendentals=tokens * GROUP * width // HEADDIM,
        ),
        name="mix_blocks",
    )(x, gate, gno, write, read, step, cum, cumt, states, skip, gain)


def gate_kernel(
    mixed_ref, gate_ref, gno_ref, x_ref, stats_ref, gain_ref, rt_ref, cum_ref,
    normed_ref, ggate_ref, gdiag_ref, gain_sum_ref, skip_sum_ref, flow_ref, scaled_ref,
):
    @pl.when(pl.program_id(1) == 0)
    def _():
        gain_sum_ref[...] = jnp.zeros_like(gain_sum_ref)
        skip_sum_ref[...] = jnp.zeros_like(skip_sum_ref)

    stats = stats_ref[0].T
    scale = lax.rsqrt(stats[:, 0:1] / INNER + EPSILON)
    cross = scale * stats[:, 1:2] / INNER
    grown = jnp.exp(cum_ref[0])
    low_half = low_lanes(GROUP)
    for pair in range(HEADS_STEP // 2):
        lanes = slice(PAIR * pair, PAIR * (pair + 1))
        mixed = mixed_ref[:, lanes]
        gate = gate_ref[:, lanes].astype(F32)
        gno = gno_ref[:, lanes].astype(F32)
        gain = gain_ref[:, lanes]
        sig = jax.nn.sigmoid(gate)
        act = gate * sig
        hat = mixed * act * scale
        normed_ref[:, lanes] = (hat * gain).astype(BF16)
        gain_sum_ref[:, lanes] += jnp.sum(gno * hat, axis=0, keepdims=True)
        grad_gated = scale * (gno * gain - hat * cross)
        grad_mixed = grad_gated * act
        ggate_ref[:, lanes] = (grad_gated * mixed * sig * (1.0 + gate * (1.0 - sig))).astype(BF16)
        skip_sum_ref[:, lanes] += jnp.sum(grad_mixed * x_ref[:, lanes].astype(F32), axis=0, keepdims=True)
        diag = grad_mixed.astype(BF16)
        gdiag_ref[:, lanes] = diag
        scaled_ref[:, lanes] = (diag.astype(F32) * spread_heads(grown, pair, low_half)).astype(BF16)
    flow_ref[0] = dot(rt_ref[...], scaled_ref[...], 1, 0)


def gate_blocks(mixed, gate, gno, x, stats, gain, read_t, cum):
    tokens, width = x.shape
    blocks, steps = tokens // GROUP, width // LANES_STEP
    wide = pl.BlockSpec((GROUP, LANES_STEP), lambda g, b: (b, g))
    line = pl.BlockSpec((1, LANES_STEP), lambda g, b: (0, g))
    return pl.pallas_call(
        gate_kernel,
        grid=(steps, blocks),
        in_specs=[
            wide, wide, wide, wide,
            pl.BlockSpec((1, 8, GROUP), lambda g, b: (b, 0, 0)),
            line,
            pl.BlockSpec((STATE, GROUP), lambda g, b: (0, b)),
            pl.BlockSpec((1, GROUP, HEADS_STEP), lambda g, b: (g, b, 0)),
        ],
        out_specs=[
            wide, wide, wide, line, line,
            pl.BlockSpec((1, STATE, LANES_STEP), lambda g, b: (b, 0, g)),
        ],
        out_shape=[
            jax.ShapeDtypeStruct((tokens, width), BF16),
            jax.ShapeDtypeStruct((tokens, width), BF16),
            jax.ShapeDtypeStruct((tokens, width), BF16),
            jax.ShapeDtypeStruct((1, width), F32),
            jax.ShapeDtypeStruct((1, width), F32),
            jax.ShapeDtypeStruct((blocks, STATE, width), F32),
        ],
        scratch_shapes=[pltpu.VMEM((GROUP, LANES_STEP), BF16)],
        cost_estimate=pl.CostEstimate(
            flops=2 * tokens * STATE * width,
            bytes_accessed=tokens * width * 16 + blocks * STATE * width * 4,
            transcendentals=tokens * width,
        ),
        name="gate_blocks",
    )(mixed, gate, gno, x, stats, gain, read_t, cum)


def segment_sums(values):
    rows = lax.broadcasted_iota(jnp.int32, (LANES_STEP, HEADS_STEP), 0) // HEADDIM
    chosen = (rows == lax.broadcasted_iota(jnp.int32, (LANES_STEP, HEADS_STEP), 1)).astype(BF16)
    high = values.astype(BF16)
    rest = (values - high.astype(F32)).astype(BF16)
    return dot(high, chosen, 1, 0) + dot(rest, chosen, 1, 0)


def back_kernel(
    x_ref, mixed_ref, grad_ref, w_ref, r_ref, step_ref, cum_ref, cumt_ref, state_ref, flow_ref, skip_ref,
    gx_ref, gw_ref, gr_ref, u_ref, v_ref, i_ref,
    scores_ref, gscores_ref, prod_ref,
):
    g = pl.program_id(1)

    @pl.when(g == 0)
    def _():
        scores_ref[...] = dot(r_ref[...], w_ref[...], 1, 1)
        gscores_ref[...] = jnp.zeros_like(gscores_ref)
        gw_ref[...] = jnp.zeros_like(gw_ref)
        gr_ref[...] = jnp.zeros_like(gr_ref)

    cum, cumt, step = cum_ref[0], cumt_ref[0, 0], step_ref[0]
    grown = jnp.exp(cum)
    shrunk = jnp.exp(cum[GROUP - 1 : GROUP, :] - cum)
    low_half = low_lanes(GROUP)
    lower = lax.broadcasted_iota(jnp.int32, (GROUP, GROUP), 0) >= lax.broadcasted_iota(
        jnp.int32, (GROUP, GROUP), 1
    )
    grad_write = jnp.zeros((GROUP, STATE), F32)
    grad_read = jnp.zeros((GROUP, STATE), F32)
    for pair in range(HEADS_STEP // 2):
        lanes = slice(PAIR * pair, PAIR * (pair + 1))
        x = x_ref[:, lanes].astype(F32)
        grad = grad_ref[:, lanes]
        grad_f = grad.astype(F32)
        skip = skip_ref[:, lanes]
        steps = spread_heads(step, pair, low_half)
        tail = spread_heads(shrunk, pair, low_half)
        stepped = x * steps
        x_halves = (
            jnp.where(low_half, stepped, 0.0).astype(BF16),
            jnp.where(low_half, 0.0, stepped).astype(BF16),
        )
        g_halves = (
            jnp.where(low_half, grad_f, 0.0).astype(BF16),
            jnp.where(low_half, 0.0, grad_f).astype(BF16),
        )
        flow = flow_ref[0, :, lanes]
        grad_read = grad_read + dot(
            (grad_f * spread_heads(grown, pair, low_half)).astype(BF16), state_ref[0, :, lanes], 1, 1
        )
        grad_write = grad_write + dot((stepped * tail).astype(BF16), flow, 1, 1)
        stepped_low = stepped.astype(BF16).astype(F32)
        inter = dot(w_ref[...], flow, 1, 0) * tail
        total = jnp.zeros_like(inter)
        for side in range(2):
            head = 2 * pair + side
            decay = jnp.exp(jnp.where(lower, cum[:, head : head + 1] - cumt[head : head + 1, :], -1e30))
            weights = (scores_ref[...] * decay).astype(BF16)
            total = total + dot(weights, g_halves[side], 0, 0)
            gscores_ref[...] += dot(grad, x_halves[side], 1, 1) * decay
        both = total + inter
        gx_ref[:, lanes] = steps * both + skip * grad_f
        prod_ref[0, :, lanes] = x * both
        prod_ref[1, :, lanes] = grad_f * (mixed_ref[:, lanes] - skip * x) - stepped_low * total
        prod_ref[2, :, lanes] = stepped_low * inter
    u_ref[0] = segment_sums(prod_ref[0])
    v_ref[0] = segment_sums(prod_ref[1])
    i_ref[0] = segment_sums(prod_ref[2])
    gw_ref[...] += grad_write
    gr_ref[...] += grad_read

    @pl.when(g == pl.num_programs(1) - 1)
    def _():
        low = gscores_ref[...].astype(BF16)
        gr_ref[...] += dot(low, w_ref[...], 1, 0)
        gw_ref[...] += dot(low, r_ref[...], 0, 0)


def back_blocks(x, mixed, grad, write, read, step, cum, cumt, states, flows, skip):
    tokens, width = x.shape
    blocks, steps = tokens // GROUP, width // LANES_STEP
    wide = pl.BlockSpec((GROUP, LANES_STEP), lambda b, g: (b, g))
    narrow = pl.BlockSpec((GROUP, STATE), lambda b, g: (b, 0))
    cols = pl.BlockSpec((1, GROUP, HEADS_STEP), lambda b, g: (g, b, 0))
    state = pl.BlockSpec((1, STATE, LANES_STEP), lambda b, g: (b, 0, g))
    return pl.pallas_call(
        back_kernel,
        grid=(blocks, steps),
        in_specs=[
            wide, wide, wide, narrow, narrow, cols, cols,
            pl.BlockSpec((1, 1, HEADS_STEP, GROUP), lambda b, g: (g, b, 0, 0)),
            state, state,
            pl.BlockSpec((1, LANES_STEP), lambda b, g: (0, g)),
        ],
        out_specs=[wide, narrow, narrow, cols, cols, cols],
        out_shape=[
            jax.ShapeDtypeStruct((tokens, width), F32),
            jax.ShapeDtypeStruct((tokens, STATE), F32),
            jax.ShapeDtypeStruct((tokens, STATE), F32),
            jax.ShapeDtypeStruct((steps, tokens, HEADS_STEP), F32),
            jax.ShapeDtypeStruct((steps, tokens, HEADS_STEP), F32),
            jax.ShapeDtypeStruct((steps, tokens, HEADS_STEP), F32),
        ],
        scratch_shapes=[
            pltpu.VMEM((GROUP, GROUP), F32),
            pltpu.VMEM((GROUP, GROUP), F32),
            pltpu.VMEM((3, GROUP, LANES_STEP), F32),
        ],
        cost_estimate=pl.CostEstimate(
            flops=2 * tokens * width * (4 * GROUP + 4 * STATE) * 2,
            bytes_accessed=tokens * width * 14,
            transcendentals=tokens * GROUP * width // HEADDIM,
        ),
        name="back_blocks",
    )(x, mixed, grad, write, read, step, cum, cumt, states, flows, skip)


def after(x, other):
    return lax.optimization_barrier((x, other))[0]


def everywhere(x):
    for axis in ("ctx", "fsdp"):
        count, bit = lax.axis_size(axis), 1
        if count & (count - 1):
            x = lax.psum(x, axis)
            continue
        while bit < count:
            x = x + lax.ppermute(x, axis, [(i, i ^ bit) for i in range(count)])
            bit *= 2
    return x


def pack(parts):
    return jnp.concatenate([part.reshape(-1) for part in parts])


def unpack(vector, shapes):
    parts, at = [], 0
    for shape in shapes:
        size = 1
        for dim in shape:
            size *= dim
        parts.append(vector[at : at + size].reshape(shape))
        at += size
    return parts


def on_device(
    hidden_in,
    lengths,
    norm_gain,
    proj_gate_inner,
    proj_write_read,
    proj_step,
    conv_inner,
    conv_inner_bias,
    conv_write_read,
    conv_write_read_bias,
    step_bias,
    log_rate,
    skip_gain,
    gate_gain,
    proj_out,
    out_cotangent,
):
    slot_count, seq_here, width_here = hidden_in.shape
    slots = slot_count // 2
    tokens = slots * seq_here
    heads_own = step_bias.shape[0]
    inner_own = gate_gain.shape[0]
    heads = 2 * heads_own
    inner = 2 * inner_own
    tp_count = lax.axis_size("tp")
    width = tp_count * width_here
    groups = seq_here // GROUP
    blocks = slots * groups
    head_steps = heads // HEADS_STEP
    rim_rows = CONV - 1
    place = lax.axis_index("tp")
    far_half, near_side = place // 2, place % 2

    def half_of(whole, which):
        return lax.dynamic_slice_in_dim(whole, which * slots, slots, 0)

    def ordered(own, near, far, both, axis):
        first = lambda a, b: jnp.where(near_side == 0, a, b)
        a0, a1, b0, b1 = first(own, near), first(near, own), first(far, both), first(both, far)
        lower = lambda a, b: jnp.where(far_half == 0, a, b)
        return jnp.concatenate(
            [lower(a0, b0), lower(a1, b1), lower(b0, a0), lower(b1, a1)], axis=axis
        )

    def own_features(piece):
        relay = swap(piece(place ^ 3).astype(BF16), 1)
        keep = swap(piece(place ^ 1).astype(BF16), 1)
        sent = swap((piece(place ^ 2) + relay.astype(F32)).astype(BF16), 2)
        kept = (piece(place) + keep.astype(F32)).reshape(slots, seq_here, width_here)
        other = sent.astype(F32).reshape(slots, seq_here, width_here)
        return both_halves(kept, other)

    def both_halves(kept, other):
        return jnp.where(
            far_half == 0,
            jnp.concatenate([kept, other], axis=0),
            jnp.concatenate([other, kept], axis=0),
        )

    small_shapes = [(CONV, inner_own), (inner_own,), (inner_own,), (heads_own,), (heads_own,), (heads_own,)]
    own_small = pack([conv_inner, conv_inner_bias, gate_gain, step_bias, log_rate, skip_gain])
    far_small = unpack(swap(own_small, 2), small_shapes)
    taps = jnp.concatenate([conv_inner, far_small[0]], axis=1)
    taps_bias = jnp.concatenate([conv_inner_bias, far_small[1]])
    gain_gate = jnp.concatenate([gate_gain, far_small[2]])
    bias_step = jnp.concatenate([step_bias, far_small[3]])
    rate_log = jnp.concatenate([log_rate, far_small[4]])
    gain_skip = jnp.concatenate([skip_gain, far_small[5]])
    rate = -jnp.exp(rate_log)
    skip_lanes = jnp.repeat(gain_skip, HEADDIM)[None]

    def gathered(x):
        return lax.all_gather(x, ("fsdp", "ctx"), axis=0, tiled=True)

    x_mine, x_other = half_of(hidden_in, far_half), half_of(hidden_in, 1 - far_half)
    cot_mine, cot_other = half_of(out_cotangent, far_half), half_of(out_cotangent, 1 - far_half)
    narrow_cols = 2 * STATE + heads
    narrow_pad = -narrow_cols % 128
    narrow_shard = jnp.concatenate(
        [proj_write_read, proj_step, swap(proj_step, 2)]
        + [jnp.zeros((proj_step.shape[0], narrow_pad), BF16)],
        axis=1,
    )
    inner_shard, gate_shard = proj_gate_inner[:, 1], proj_gate_inner[:, 0]
    inner_far = swap(inner_shard, 2)
    x_near = swap(x_mine, 1)
    x_far = swap(after(x_other, inner_far), 2)
    gate_far = swap(after(gate_shard, x_far), 2)
    x_both = swap(x_far, 1)
    cot_dep = after(x_both, gate_far)
    cot_near = swap(after(cot_mine, cot_dep), 1)
    cot_far = swap(after(cot_other, cot_dep), 2)
    out_far = swap(after(proj_out, cot_far), 2)
    cot_both = swap(cot_far, 1)
    full_narrow = gathered(narrow_shard)
    full_inner = gathered(jnp.concatenate([inner_shard, inner_far], axis=1))
    full_gate = gathered(jnp.concatenate([after(gate_shard, full_inner), gate_far], axis=1))
    full_out = gathered(jnp.concatenate([after(proj_out, full_gate), out_far], axis=1))
    full_x = ordered(x_mine, x_near, x_far, x_both, 2).reshape(tokens, width)
    full_gain = ordered(norm_gain, swap(norm_gain, 1), swap(norm_gain, 2), swap(norm_gain, 3), 0)
    full_cot = ordered(cot_mine, cot_near, cot_far, cot_both, 2).reshape(tokens, width)

    in_float = full_x.astype(F32)
    in_scale = lax.rsqrt(jnp.mean(in_float * in_float, axis=-1, keepdims=True) + EPSILON)
    normed = (in_float * in_scale * full_gain.astype(F32)).astype(BF16)
    narrow_pre = dot(normed, full_narrow, 1, 0)
    write_read_pre = narrow_pre[:, : 2 * STATE].astype(BF16)
    step_raw = narrow_pre[:, 2 * STATE : narrow_cols]
    gate_pre = dot(normed, full_gate, 1, 0).astype(BF16)
    inner_pre = dot(normed, full_inner, 1, 0).astype(BF16)

    def padded(pre):
        by_slot = pre.reshape(slots, seq_here, pre.shape[-1])
        rim = passed_along(by_slot[:, seq_here - rim_rows :], "ctx", 1)
        return jnp.concatenate([rim, by_slot], axis=1).astype(F32)

    inner_pad, write_read_pad = padded(inner_pre), padded(write_read_pre)
    write_read_act = (
        conv_silu(write_read_pad, conv_write_read, conv_write_read_bias)
        .astype(BF16)
        .reshape(tokens, 2 * STATE)
    )
    inner_act = conv_silu(inner_pad, taps, taps_bias).astype(BF16).reshape(tokens, inner)
    write, read = write_read_act[:, :STATE], write_read_act[:, STATE:]

    step_size = jax.nn.softplus(step_raw + bias_step)
    step_blocks = step_size.reshape(blocks, GROUP, heads)
    lower = (jnp.arange(GROUP)[:, None] >= jnp.arange(GROUP)[None, :]).astype(F32)
    cum = jnp.einsum("ts,bsh->bth", lower, step_blocks * rate, precision=HIGHEST)

    def by_steps(cols):
        return cols.reshape(tokens, head_steps, HEADS_STEP).transpose(1, 0, 2)

    def from_steps(cols):
        return cols.transpose(1, 0, 2).reshape(blocks, GROUP, heads)

    step_cols, cum_cols = by_steps(step_size), by_steps(cum)
    cum_rows = cum.reshape(blocks, GROUP, head_steps, HEADS_STEP).transpose(2, 0, 3, 1)
    last = cum[:, GROUP - 1]
    write_scale = by_steps(jnp.exp(last[:, None] - cum) * step_blocks)
    decay = jnp.exp(last)
    decay_lanes = jnp.repeat(decay, HEADDIM, axis=1).reshape(slots, groups, 1, inner)

    local_state = block_outer(write.T, inner_act, write_scale).reshape(slots, groups, STATE, inner)
    carried = local_state[:, 0]
    device_decay = decay_lanes[:, 0]
    for position in range(1, groups):
        carried = decay_lanes[:, position] * carried + local_state[:, position]
        device_decay = device_decay * decay_lanes[:, position]
    current = carried_in(device_decay, carried, None, False)
    state_list = []
    for position in range(groups):
        state_list.append(current)
        current = decay_lanes[:, position] * current + local_state[:, position]
    states = jnp.stack(state_list, axis=1)
    states_low = states.astype(BF16).reshape(blocks, STATE, inner)

    position_ids = lax.axis_index("ctx") * seq_here + jnp.arange(seq_here)
    valid_rows = (position_ids[None, :] < lengths[:, None]).astype(F32)
    valid_here = half_of(valid_rows, far_half).reshape(tokens, 1)
    masked = (full_cot.astype(F32) * valid_here).astype(BF16)
    grad_normed_out = dot(masked, full_out, 1, 0).astype(BF16)
    mixed_out, stats = mix_blocks(
        inner_act, gate_pre, grad_normed_out, write, read, step_cols, cum_cols, cum_rows, states_low,
        skip_lanes, gain_gate[None],
    )
    stats = stats + swap(stats, 1)
    normed_out, grad_gate_pre, grad_diag, grad_gate_gain, grad_skip_lanes, local_grad = gate_blocks(
        mixed_out, gate_pre, grad_normed_out, inner_act, stats, gain_gate[None], read.T, cum_cols
    )
    local_grad = local_grad.reshape(slots, groups, STATE, inner)

    def branch_piece(which):
        rows = lax.dynamic_slice_in_dim(full_out, which * width_here, width_here, 0)
        return dot(normed_out, rows, 1, 1)

    branch = own_features(branch_piece)
    hidden_out = (hidden_in.astype(F32) + valid_rows[..., None] * branch).astype(BF16)
    grad_proj_out = dot(masked, normed_out, 0, 0).astype(BF16)
    grad_gate_w = dot(normed, grad_gate_pre, 0, 0).astype(BF16)

    flowing = local_grad[:, groups - 1]
    for position in reversed(range(groups - 1)):
        flowing = decay_lanes[:, position] * flowing + local_grad[:, position]
    flowing = carried_in(device_decay, flowing, None, True)
    flow_list = []
    for position in reversed(range(groups)):
        flow_list.insert(0, flowing)
        flowing = decay_lanes[:, position] * flowing + local_grad[:, position]
    flows = jnp.stack(flow_list, axis=1)
    last_grad = (
        jnp.sum(flows * states, axis=2).reshape(blocks, heads, HEADDIM).sum(axis=2) * decay
    )
    flows_low = flows.astype(BF16).reshape(blocks, STATE, inner)
    flows_low = after(flows_low, (grad_proj_out, grad_gate_w))

    grad_inner_act, grad_write, grad_read, u_cols, v_cols, inter_cols = back_blocks(
        inner_act, mixed_out, grad_diag, write, read, step_cols, cum_cols, cum_rows,
        states_low, flows_low, skip_lanes,
    )
    u_blocks, v_blocks, inter_blocks = from_steps(u_cols), from_steps(v_cols), from_steps(inter_cols)
    reverse_sum = (
        jnp.einsum("ts,bth->bsh", lower, v_blocks, precision=HIGHEST)
        + jnp.einsum("st,bth->bsh", lower - jnp.eye(GROUP, dtype=F32), inter_blocks, precision=HIGHEST)
        + last_grad[:, None]
    )
    grad_step_size = u_blocks + rate * reverse_sum
    grad_log_rate = jnp.sum(reverse_sum * step_blocks, axis=(0, 1)) * rate
    grad_step_raw = grad_step_size.reshape(tokens, heads) * jax.nn.sigmoid(step_raw + bias_step)
    grad_step_bias = jnp.sum(grad_step_raw, axis=0)

    unused_inner, inner_pull = jax.vjp(conv_silu, inner_pad, taps, taps_bias)
    grad_inner_pad, grad_taps, grad_taps_bias = inner_pull(
        grad_inner_act.reshape(slots, seq_here, inner)
    )
    unused_write_read, write_read_pull = jax.vjp(
        conv_silu, write_read_pad, conv_write_read, conv_write_read_bias
    )
    grad_write_read_pad, grad_conv_write_read, grad_conv_write_read_bias = write_read_pull(
        jnp.concatenate([grad_write, grad_read], axis=1).reshape(slots, seq_here, 2 * STATE)
    )

    def unpadded(grad):
        back = passed_along(grad[:, :rim_rows], "ctx", -1)
        full = grad[:, rim_rows:].at[:, seq_here - rim_rows :].add(back)
        return full.astype(BF16).reshape(tokens, grad.shape[-1])

    grad_inner_pre, grad_write_read_pre = unpadded(grad_inner_pad), unpadded(grad_write_read_pad)
    grad_narrow = jnp.concatenate(
        [grad_write_read_pre, grad_step_raw.astype(BF16), jnp.zeros((tokens, narrow_pad), BF16)], axis=1
    )
    grad_inner_w = dot(normed, grad_inner_pre, 0, 0).astype(BF16)
    grad_narrow_w = dot(normed, grad_narrow, 0, 0).astype(BF16)

    kept_sums = []

    def normed_piece(which):
        def rows(full):
            return lax.dynamic_slice_in_dim(full, which * width_here, width_here, 0)

        piece = (
            dot(grad_gate_pre, rows(full_gate), 1, 1)
            + dot(grad_inner_pre, rows(full_inner), 1, 1)
            + dot(grad_narrow, rows(full_narrow), 1, 1)
        )
        cols = lax.dynamic_slice_in_dim(full_x, which * width_here, width_here, 1).astype(F32)
        gain = lax.dynamic_slice_in_dim(full_gain, which * width_here, width_here, 0).astype(F32)
        by_hat = piece * (cols * in_scale)
        kept_sums.append((which, jnp.sum(by_hat, axis=0), jnp.sum(by_hat * gain, axis=1)))
        return piece

    grad_normed = own_features(normed_piece)
    grad_gain_full = jnp.zeros((width,), F32)
    cross_rows = jnp.zeros((tokens,), F32)
    for which, by_feature, by_row in kept_sums:
        grad_gain_full = lax.dynamic_update_slice_in_dim(grad_gain_full, by_feature, which * width_here, 0)
        cross_rows = cross_rows + by_row
    cross_rows = cross_rows + swap(cross_rows, 1)

    def reduced(x):
        return lax.psum_scatter(x, ("fsdp", "ctx"), scatter_dimension=0, tiled=True)

    def home(x, axis):
        own = lax.slice_in_dim(x, 0, x.shape[axis] // 2, axis=axis).astype(F32)
        away = lax.slice_in_dim(x, x.shape[axis] // 2, x.shape[axis], axis=axis)
        return own + swap(away, 2).astype(F32)

    grad_out_home = home(reduced(grad_proj_out), 1)
    grad_gate_home = home(reduced(grad_gate_w), 1)
    grad_inner_home = home(reduced(grad_inner_w), 1)
    narrow_reduced = reduced(grad_narrow_w)
    write_read_home = narrow_reduced[:, : 2 * STATE].astype(F32)
    write_read_home = write_read_home + swap(write_read_home, 1)
    write_read_home = write_read_home + swap(write_read_home, 2)
    step_home = home(narrow_reduced[:, 2 * STATE : narrow_cols], 1)

    own_gain = norm_gain.astype(F32)
    other_scale = swap(in_scale, 2)
    own_scale = both_halves(
        in_scale.reshape(slots, seq_here, 1), other_scale.reshape(slots, seq_here, 1)
    )
    own_hat = hidden_in.astype(F32) * own_scale
    grad_hat_in = grad_normed * own_gain
    cross_in = both_halves(
        cross_rows.reshape(slots, seq_here, 1), swap(cross_rows, 2).reshape(slots, seq_here, 1)
    ) / width
    grad_hidden_in = own_scale * (grad_hat_in - own_hat * cross_in) + out_cotangent.astype(F32)

    grad_skip_gain = jnp.sum(grad_skip_lanes.reshape(heads, HEADDIM), axis=1)
    shared_shapes = [(CONV, 2 * STATE), (2 * STATE,), (width,)]
    head_shapes = [(CONV, inner), (inner,), (inner,), (heads,), (heads,), (heads,)]
    smalls = everywhere(
        pack(
            [
                grad_taps, grad_taps_bias, grad_gate_gain, grad_step_bias, grad_log_rate, grad_skip_gain,
                grad_conv_write_read, grad_conv_write_read_bias, grad_gain_full,
            ]
        )
    )
    parts = unpack(smalls, head_shapes + shared_shapes)
    shared = pack(parts[6:9])
    shared = shared + swap(shared, 1)
    shared = shared + swap(shared, 2)
    wr_taps, wr_bias, gain_all = unpack(shared, shared_shapes)
    grad_norm_gain = lax.dynamic_slice_in_dim(gain_all, place * width_here, width_here, 0)
    away = swap(pack([lax.slice_in_dim(p, p.shape[-1] // 2, p.shape[-1], axis=p.ndim - 1) for p in parts[:6]]), 2)
    homes = [
        lax.slice_in_dim(p, 0, p.shape[-1] // 2, axis=p.ndim - 1) + a
        for p, a in zip(parts[:6], unpack(away, small_shapes))
    ]
    return (
        hidden_out,
        grad_hidden_in,
        grad_norm_gain,
        jnp.stack([grad_gate_home, grad_inner_home], axis=1),
        write_read_home,
        step_home,
        homes[0],
        homes[1],
        wr_taps,
        wr_bias,
        homes[3],
        homes[4],
        homes[5],
        homes[2],
        grad_out_home,
    )


def solution(mesh):
    rows = ("fsdp", "ctx")
    acts = P("fsdp", "ctx", "tp")
    placed = (
        acts,
        P("fsdp"),
        P("tp"),
        P(rows, None, "tp"),
        P(rows, None),
        P(rows, "tp"),
        P(None, "tp"),
        P("tp"),
        P(),
        P(),
        P("tp"),
        P("tp"),
        P("tp"),
        P("tp"),
        P(rows, "tp"),
        acts,
    )
    return jax.shard_map(
        on_device,
        mesh=mesh,
        in_specs=placed,
        out_specs=(
            acts,
            acts,
            P("tp"),
            P(rows, None, "tp"),
            P(rows, None),
            P(rows, "tp"),
            P(None, "tp"),
            P("tp"),
            P(),
            P(),
            P("tp"),
            P("tp"),
            P("tp"),
            P("tp"),
            P(rows, "tp"),
        ),
        check_vma=False,
    )
```

```python
import functools

import jax
import jax.numpy as jnp
from jax import lax
from jax.experimental import pallas as pl
from jax.experimental.pallas import tpu as pltpu
from jax.sharding import PartitionSpec as P

HEADDIM = 64
STATE = 128
CONV = 4
GROUP = 256
INNER = 3072
EPSILON = 1e-05
PAIR = 2 * HEADDIM
HEADS_STEP = 6
LANES_STEP = HEADS_STEP * HEADDIM
F32 = jnp.float32
BF16 = jnp.bfloat16
HIGHEST = lax.Precision.HIGHEST


def swap(x, bit):
    count = lax.axis_size("tp")
    return lax.ppermute(x, "tp", [(i, i ^ bit) for i in range(count)])


def passed_along(x, axis, by):
    count = lax.axis_size(axis)
    pairs = [(i, i + by) for i in range(count) if 0 <= i + by < count]
    return lax.ppermute(x, axis, pairs)


def carried_in(decay, final, combine, reverse):
    count, position = (lax.axis_size("ctx"), lax.axis_index("ctx"))
    if count == 2:
        return passed_along(final.astype(BF16), "ctx", -1 if reverse else 1).astype(F32)
    decays = lax.all_gather(decay.astype(BF16), "ctx").astype(F32)
    finals = lax.all_gather(final.astype(BF16), "ctx")
    start = jnp.zeros_like(final)

    def lap(k, before):
        at = count - 1 - k if reverse else k
        reached = at > position if reverse else at < position
        new = decays[at] * before + finals[at].astype(F32)
        return jnp.where(reached, new, before)

    return lax.fori_loop(0, count, lap, start)


def dot(a, b, da, db):
    return lax.dot_general(a, b, (((da,), (db,)), ((), ())), preferred_element_type=F32)


def low_lanes(rows):
    return lax.broadcasted_iota(jnp.int32, (rows, PAIR), 1) < HEADDIM


def spread_heads(cols, first, low_half):
    return jnp.where(low_half, cols[:, first : first + 1], cols[:, first + 1 : first + 2])


def lower_mask():
    return lax.broadcasted_iota(jnp.int32, (GROUP, GROUP), 0) >= lax.broadcasted_iota(
        jnp.int32, (GROUP, GROUP), 1
    )


def split_dot(ones, values, terms, contract):
    total, rest = None, values
    for _ in range(terms):
        part = rest.astype(BF16)
        rest = rest - part.astype(F32)
        piece = dot(ones, part, contract, 0)
        total = piece if total is None else total + piece
    return total


def turned(cols, heads_before):
    return pltpu.roll(cols, lax.rem(128 - heads_before, 128), 1)


def start_kernel(
    groups, heads,
    inner_ref, rim_ref, narrow_ref, nrim_ref, taps_ref, bias_ref, ntaps_ref, nbias_ref, sbias_ref, rate_ref,
    x_ref, slope_ref, wr_ref, nslope_ref, cols_ref, rows_ref, local_ref, decay_ref,
    ext_ref, next_ref, scaled_ref,
):
    first = lax.rem(pl.program_id(0), groups) == 0

    @pl.when(first)
    def _():
        ext_ref[5:8, :] = rim_ref[0].astype(F32)
        next_ref[5:8, :] = nrim_ref[0].astype(F32)

    @pl.when(jnp.logical_not(first))
    def _():
        ext_ref[0:8, :] = ext_ref[GROUP : GROUP + 8, :]
        next_ref[0:8, :] = next_ref[GROUP : GROUP + 8, :]

    def conv(source, taps, bias, lanes):
        total = bias[:, lanes]
        for k in range(CONV):
            total = total + taps[k : k + 1, lanes] * source[5 + k : 5 + k + GROUP, lanes]
        sig = jax.nn.sigmoid(total)
        return total * sig, sig * (1.0 + total * (1.0 - sig))

    for part in range(2 * STATE // 128):
        lanes = slice(128 * part, 128 * (part + 1))
        next_ref[8 : GROUP + 8, lanes] = narrow_ref[:, lanes].astype(BF16).astype(F32)
        act, slope = conv(next_ref, ntaps_ref, nbias_ref, lanes)
        wr_ref[:, lanes] = act.astype(BF16)
        nslope_ref[:, lanes] = slope

    raw = narrow_ref[:, 2 * STATE :] + sbias_ref[...]
    lane = lax.broadcasted_iota(jnp.int32, (GROUP, 128), 1)
    step = jnp.maximum(raw, 0.0) + jnp.log1p(jnp.exp(-jnp.abs(raw)))
    step = jnp.where(lane < heads, step, 0.0)
    sig = jnp.where(lane < heads, jax.nn.sigmoid(raw), 0.0)
    cum = split_dot(lower_mask().astype(BF16), step * rate_ref[...], 3, 1)
    cols = step + pltpu.roll(cum, heads, 1) + pltpu.roll(sig, 2 * heads, 1)
    cols_ref[...] = cols
    rows_ref[0] = cum.T[:heads]
    last = cum[GROUP - 1 : GROUP, :]
    scale = jnp.exp(last - cum) * step
    decay = jnp.exp(last)
    low_half, low_row = low_lanes(GROUP), low_lanes(1)
    for pair in range(heads // 2):
        lanes = slice(PAIR * pair, PAIR * (pair + 1))
        ext_ref[8 : GROUP + 8, lanes] = inner_ref[:, lanes].astype(F32)
        act, slope = conv(ext_ref, taps_ref, bias_ref, lanes)
        x = act.astype(BF16)
        x_ref[:, lanes] = x
        slope_ref[:, lanes] = slope.astype(BF16)
        scaled_ref[:, lanes] = (x.astype(F32) * spread_heads(scale, 2 * pair, low_half)).astype(BF16)
        decay_ref[0, :, lanes] = spread_heads(decay, 2 * pair, low_row)
    local_ref[0] = dot(wr_ref[:, :STATE], scaled_ref[...], 0, 0)


def start_blocks(inner_pre, rim, narrow, nrim, taps, bias, ntaps, nbias, sbias, rate, groups, heads):
    tokens, width = inner_pre.shape
    blocks = tokens // GROUP
    rows = lambda w: pl.BlockSpec((GROUP, w), lambda b: (b, 0))
    whole = lambda x: pl.BlockSpec(x.shape, lambda b: (0,) * x.ndim)
    return pl.pallas_call(
        functools.partial(start_kernel, groups, heads),
        grid=(blocks,),
        in_specs=[
            rows(width),
            pl.BlockSpec((1, CONV - 1, width), lambda b: (b // groups, 0, 0)),
            rows(narrow.shape[1]),
            pl.BlockSpec((1, CONV - 1, 2 * STATE), lambda b: (b // groups, 0, 0)),
            whole(taps), whole(bias), whole(ntaps), whole(nbias), whole(sbias), whole(rate),
        ],
        out_specs=[
            rows(width), rows(width), rows(2 * STATE), rows(2 * STATE), rows(128),
            pl.BlockSpec((1, heads, GROUP), lambda b: (b, 0, 0)),
            pl.BlockSpec((1, STATE, width), lambda b: (b, 0, 0)),
            pl.BlockSpec((1, 1, width), lambda b: (b, 0, 0)),
        ],
        out_shape=[
            jax.ShapeDtypeStruct((tokens, width), BF16),
            jax.ShapeDtypeStruct((tokens, width), BF16),
            jax.ShapeDtypeStruct((tokens, 2 * STATE), BF16),
            jax.ShapeDtypeStruct((tokens, 2 * STATE), F32),
            jax.ShapeDtypeStruct((tokens, 128), F32),
            jax.ShapeDtypeStruct((blocks, heads, GROUP), F32),
            jax.ShapeDtypeStruct((blocks, STATE, width), F32),
            jax.ShapeDtypeStruct((blocks, 1, width), F32),
        ],
        scratch_shapes=[
            pltpu.VMEM((GROUP + 8, width), F32),
            pltpu.VMEM((GROUP + 8, 2 * STATE), F32),
            pltpu.VMEM((GROUP, width), BF16),
        ],
        cost_estimate=pl.CostEstimate(
            flops=2 * tokens * STATE * width + 20 * tokens * width,
            bytes_accessed=tokens * width * 6 + blocks * STATE * width * 4,
            transcendentals=tokens * width,
        ),
        name="start_blocks",
    )(inner_pre, rim, narrow, nrim, taps, bias, ntaps, nbias, sbias, rate)


def mix_kernel(
    heads,
    x_ref, gate_ref, gno_ref, wr_ref, cols_ref, rows_ref, state_ref, skip_ref, gain_ref,
    mixed_ref, stats_ref, scores_ref, sums_ref,
):
    g = pl.program_id(1)

    @pl.when(g == 0)
    def _():
        scores_ref[...] = dot(wr_ref[:, STATE:], wr_ref[:, :STATE], 1, 1)
        sums_ref[...] = jnp.zeros_like(sums_ref)

    cols = turned(cols_ref[...], g * HEADS_STEP)
    grown = jnp.exp(cols)
    low_half = low_lanes(GROUP)
    lower = lower_mask()
    squares = jnp.zeros((GROUP, 1), F32)
    crosses = jnp.zeros((GROUP, 1), F32)
    for pair in range(HEADS_STEP // 2):
        lanes = slice(PAIR * pair, PAIR * (pair + 1))
        x = x_ref[:, lanes].astype(F32)
        stepped = x * spread_heads(cols, 2 * pair, low_half)
        halves = (
            jnp.where(low_half, stepped, 0.0).astype(BF16),
            jnp.where(low_half, 0.0, stepped).astype(BF16),
        )
        total = dot(wr_ref[:, STATE:], state_ref[0, :, lanes], 1, 0)
        total = total * spread_heads(grown, heads + 2 * pair, low_half)
        for side in range(2):
            head = 2 * pair + side
            row = rows_ref[0, pl.ds(g * HEADS_STEP + head, 1), :]
            spread = jnp.where(lower, cols[:, heads + head : heads + head + 1] - row, -1e30)
            weights = (scores_ref[...] * jnp.exp(spread)).astype(BF16)
            total = total + dot(weights, halves[side], 1, 0)
        mixed = total + skip_ref[:, lanes] * x
        mixed_ref[:, lanes] = mixed
        gate = gate_ref[:, lanes].astype(F32)
        gated = mixed * (gate * jax.nn.sigmoid(gate))
        squares = squares + jnp.sum(gated * gated, axis=1, keepdims=True)
        grad_hat = gno_ref[:, lanes].astype(F32) * gain_ref[:, lanes]
        crosses = crosses + jnp.sum(gated * grad_hat, axis=1, keepdims=True)
    lane = lax.broadcasted_iota(jnp.int32, (GROUP, 128), 1)
    sums_ref[...] += jnp.where(lane == 0, squares, jnp.where(lane == 1, crosses, 0.0))

    @pl.when(g == pl.num_programs(1) - 1)
    def _():
        stats_ref[0] = sums_ref[...].T[:8]


def mix_blocks(x, gate, gno, wr, cols, rows, states, skip, gain):
    tokens, width = x.shape
    blocks, steps, heads = tokens // GROUP, width // LANES_STEP, rows.shape[1]
    wide = pl.BlockSpec((GROUP, LANES_STEP), lambda b, g: (b, g))
    line = pl.BlockSpec((1, LANES_STEP), lambda b, g: (0, g))
    return pl.pallas_call(
        functools.partial(mix_kernel, heads),
        grid=(blocks, steps),
        in_specs=[
            wide, wide, wide,
            pl.BlockSpec((GROUP, 2 * STATE), lambda b, g: (b, 0)),
            pl.BlockSpec((GROUP, 128), lambda b, g: (b, 0)),
            pl.BlockSpec((1, heads, GROUP), lambda b, g: (b, 0, 0)),
            pl.BlockSpec((1, STATE, LANES_STEP), lambda b, g: (b, 0, g)),
            line, line,
        ],
        out_specs=[wide, pl.BlockSpec((1, 8, GROUP), lambda b, g: (b, 0, 0))],
        out_shape=[
            jax.ShapeDtypeStruct((tokens, width), F32),
            jax.ShapeDtypeStruct((blocks, 8, GROUP), F32),
        ],
        scratch_shapes=[pltpu.VMEM((GROUP, GROUP), F32), pltpu.VMEM((GROUP, 128), F32)],
        cost_estimate=pl.CostEstimate(
            flops=2 * tokens * width * (2 * GROUP + 2 * STATE) * 2,
            bytes_accessed=tokens * width * 10,
            transcendentals=tokens * GROUP * width // HEADDIM,
        ),
        name="mix_blocks",
    )(x, gate, gno, wr, cols, rows, states, skip, gain)


def gate_kernel(
    heads,
    mixed_ref, gate_ref, gno_ref, x_ref, stats_ref, gain_ref, wr_ref, cols_ref,
    normed_ref, ggate_ref, gdiag_ref, gain_sum_ref, skip_sum_ref, flow_ref, scaled_ref,
):
    @pl.when(pl.program_id(1) == 0)
    def _():
        gain_sum_ref[...] = jnp.zeros_like(gain_sum_ref)
        skip_sum_ref[...] = jnp.zeros_like(skip_sum_ref)

    stats = stats_ref[0].T
    scale = lax.rsqrt(stats[:, 0:1] / INNER + EPSILON)
    cross = scale * stats[:, 1:2] / INNER
    grown = jnp.exp(turned(cols_ref[...], pl.program_id(0) * HEADS_STEP))
    low_half = low_lanes(GROUP)
    for pair in range(HEADS_STEP // 2):
        lanes = slice(PAIR * pair, PAIR * (pair + 1))
        mixed = mixed_ref[:, lanes]
        gate = gate_ref[:, lanes].astype(F32)
        gno = gno_ref[:, lanes].astype(F32)
        gain = gain_ref[:, lanes]
        sig = jax.nn.sigmoid(gate)
        act = gate * sig
        hat = mixed * act * scale
        normed_ref[:, lanes] = (hat * gain).astype(BF16)
        gain_sum_ref[:, lanes] += jnp.sum(gno * hat, axis=0, keepdims=True)
        grad_gated = scale * (gno * gain - hat * cross)
        grad_mixed = grad_gated * act
        ggate_ref[:, lanes] = (grad_gated * mixed * sig * (1.0 + gate * (1.0 - sig))).astype(BF16)
        skip_sum_ref[:, lanes] += jnp.sum(grad_mixed * x_ref[:, lanes].astype(F32), axis=0, keepdims=True)
        diag = grad_mixed.astype(BF16)
        gdiag_ref[:, lanes] = diag
        scaled = diag.astype(F32) * spread_heads(grown, heads + 2 * pair, low_half)
        scaled_ref[:, lanes] = scaled.astype(BF16)
    flow_ref[0] = dot(wr_ref[...], scaled_ref[...], 0, 0)


def gate_blocks(mixed, gate, gno, x, stats, gain, wr, cols, heads):
    tokens, width = x.shape
    blocks, steps = tokens // GROUP, width // LANES_STEP
    wide = pl.BlockSpec((GROUP, LANES_STEP), lambda g, b: (b, g))
    line = pl.BlockSpec((1, LANES_STEP), lambda g, b: (0, g))
    return pl.pallas_call(
        functools.partial(gate_kernel, heads),
        grid=(steps, blocks),
        in_specs=[
            wide, wide, wide, wide,
            pl.BlockSpec((1, 8, GROUP), lambda g, b: (b, 0, 0)),
            line,
            pl.BlockSpec((GROUP, STATE), lambda g, b: (b, 1)),
            pl.BlockSpec((GROUP, 128), lambda g, b: (b, 0)),
        ],
        out_specs=[
            wide, wide, wide, line, line,
            pl.BlockSpec((1, STATE, LANES_STEP), lambda g, b: (b, 0, g)),
        ],
        out_shape=[
            jax.ShapeDtypeStruct((tokens, width), BF16),
            jax.ShapeDtypeStruct((tokens, width), BF16),
            jax.ShapeDtypeStruct((tokens, width), BF16),
            jax.ShapeDtypeStruct((1, width), F32),
            jax.ShapeDtypeStruct((1, width), F32),
            jax.ShapeDtypeStruct((blocks, STATE, width), F32),
        ],
        scratch_shapes=[pltpu.VMEM((GROUP, LANES_STEP), BF16)],
        cost_estimate=pl.CostEstimate(
            flops=2 * tokens * STATE * width,
            bytes_accessed=tokens * width * 16 + blocks * STATE * width * 4,
            transcendentals=tokens * width,
        ),
        name="gate_blocks",
    )(mixed, gate, gno, x, stats, gain, wr, cols)


def back_kernel(
    groups, heads,
    x_ref, mixed_ref, grad_ref, slope_ref, pre_ref, rim_ref, wr_ref, nslope_ref, npre_ref, nrim_ref,
    cols_ref, rows_ref, state_ref, flow_ref, skip_ref, taps_ref, ntaps_ref, rate_ref,
    gpre_ref, gnarrow_ref, sums_ref, nsums_ref, hsums_ref, halo_ref, nhalo_ref,
    scores_ref, gscores_ref, prod_ref, gw_ref, gr_ref, u_ref, v_ref, i_ref, e_ref, ext_ref, next_ref, head_ref,
):
    step_id, g = pl.program_id(0), pl.program_id(1)
    block = pl.num_programs(0) - 1 - step_id
    last_of_slot = lax.rem(block, groups) == groups - 1
    first_of_slot = lax.rem(block, groups) == 0

    @pl.when(g == 0)
    def _():
        scores_ref[...] = dot(wr_ref[:, STATE:], wr_ref[:, :STATE], 1, 1)
        for ref in (gscores_ref, gw_ref, gr_ref, u_ref, v_ref, i_ref, e_ref):
            ref[...] = jnp.zeros_like(ref)

    @pl.when(jnp.logical_and(g == 0, step_id == 0))
    def _():
        sums_ref[...] = jnp.zeros_like(sums_ref)
        nsums_ref[...] = jnp.zeros_like(nsums_ref)
        hsums_ref[...] = jnp.zeros_like(hsums_ref)

    @pl.when(last_of_slot)
    def _():
        ext_ref[g, GROUP : GROUP + 8, :] = jnp.zeros((8, LANES_STEP), F32)
        next_ref[GROUP : GROUP + 8, :] = jnp.zeros((8, 2 * STATE), F32)

    @pl.when(jnp.logical_not(last_of_slot))
    def _():
        ext_ref[g, GROUP : GROUP + 8, :] = ext_ref[g, 0:8, :]

        @pl.when(g == 0)
        def _():
            next_ref[GROUP : GROUP + 8, :] = next_ref[0:8, :]

    cols = turned(cols_ref[...], g * HEADS_STEP)
    grown = jnp.exp(cols)
    shrunk = jnp.exp(cols[GROUP - 1 : GROUP, :] - cols)
    low_half = low_lanes(GROUP)
    lower = lower_mask()
    grad_write = jnp.zeros((GROUP, STATE), F32)
    grad_read = jnp.zeros((GROUP, STATE), F32)
    for pair in range(HEADS_STEP // 2):
        lanes = slice(PAIR * pair, PAIR * (pair + 1))
        x = x_ref[:, lanes].astype(F32)
        grad = grad_ref[:, lanes]
        grad_f = grad.astype(F32)
        skip = skip_ref[:, lanes]
        steps = spread_heads(cols, 2 * pair, low_half)
        tail = spread_heads(shrunk, heads + 2 * pair, low_half)
        stepped = x * steps
        x_halves = (
            jnp.where(low_half, stepped, 0.0).astype(BF16),
            jnp.where(low_half, 0.0, stepped).astype(BF16),
        )
        g_halves = (
            jnp.where(low_half, grad_f, 0.0).astype(BF16),
            jnp.where(low_half, 0.0, grad_f).astype(BF16),
        )
        flow = flow_ref[0, :, lanes]
        state = state_ref[0, :, lanes]
        e_ref[0:1, lanes] = jnp.sum(flow.astype(F32) * state.astype(F32), axis=0, keepdims=True)
        scaled = (grad_f * spread_heads(grown, heads + 2 * pair, low_half)).astype(BF16)
        grad_read = grad_read + dot(scaled, state, 1, 1)
        grad_write = grad_write + dot((stepped * tail).astype(BF16), flow, 1, 1)
        stepped_low = stepped.astype(BF16).astype(F32)
        inter = dot(wr_ref[:, :STATE], flow, 1, 0) * tail
        total = jnp.zeros_like(inter)
        for side in range(2):
            head = 2 * pair + side
            row = rows_ref[0, pl.ds(g * HEADS_STEP + head, 1), :]
            decay = jnp.exp(jnp.where(lower, cols[:, heads + head : heads + head + 1] - row, -1e30))
            weights = (scores_ref[...] * decay).astype(BF16)
            total = total + dot(weights, g_halves[side], 0, 0)
            gscores_ref[...] += dot(grad, x_halves[side], 1, 1) * decay
        both = total + inter
        prod_ref[0, :, lanes] = x * both
        prod_ref[1, :, lanes] = grad_f * (mixed_ref[:, lanes] - skip * x) - stepped_low * total
        prod_ref[2, :, lanes] = stepped_low * inter
        grad_conv = (steps * both + skip * grad_f) * slope_ref[:, lanes].astype(F32)
        ext_ref[g, 0:GROUP, lanes] = grad_conv
        pre = pre_ref[:, lanes].astype(F32)
        total_pre = jnp.zeros_like(grad_conv)
        for j in range(CONV):
            moved = ext_ref[g, j : j + GROUP, lanes]
            total_pre = total_pre + taps_ref[CONV - 1 - j : CONV - j, lanes] * moved
            sums_ref[g, CONV - 1 - j : CONV - j, lanes] += jnp.sum(pre * moved, axis=0, keepdims=True)
        sums_ref[g, CONV : CONV + 1, lanes] += jnp.sum(grad_conv, axis=0, keepdims=True)
        gpre_ref[:, lanes] = total_pre.astype(BF16)

    @pl.when(first_of_slot)
    def _():
        head_ref[0:8, :LANES_STEP] = jnp.zeros((8, LANES_STEP), F32)
        head_ref[8:16, :LANES_STEP] = ext_ref[g, 0:8, :]
        halo = jnp.zeros((8, LANES_STEP), F32)
        for j in range(CONV):
            moved = head_ref[j : j + 8, :LANES_STEP]
            halo = halo + taps_ref[CONV - 1 - j : CONV - j, :] * moved
            sums_ref[g, CONV - 1 - j : CONV - j, :] += jnp.sum(
                rim_ref[0].astype(F32) * moved[5:8], axis=0, keepdims=True
            )
        halo_ref[0] = halo

    chosen_rows = lax.broadcasted_iota(jnp.int32, (LANES_STEP, 128), 0) // HEADDIM + g * HEADS_STEP
    chosen = (chosen_rows == lax.broadcasted_iota(jnp.int32, (LANES_STEP, 128), 1)).astype(BF16)

    def sums_of(values, terms):
        total, rest = None, values
        for _ in range(terms):
            part = rest.astype(BF16)
            rest = rest - part.astype(F32)
            piece = dot(part, chosen, 1, 0)
            total = piece if total is None else total + piece
        return total

    u_ref[...] += sums_of(prod_ref[0], 2)
    v_ref[...] += sums_of(prod_ref[1], 2)
    i_ref[...] += sums_of(prod_ref[2], 2)
    e_ref[8:16, 0:128] += sums_of(e_ref[0:8, :], 2)
    gw_ref[...] += grad_write
    gr_ref[...] += grad_read

    @pl.when(g == pl.num_programs(1) - 1)
    def _():
        low = gscores_ref[...].astype(BF16)
        gradient = (
            gw_ref[...] + dot(low, wr_ref[:, STATE:], 0, 0),
            gr_ref[...] + dot(low, wr_ref[:, :STATE], 1, 0),
        )
        for part in range(2):
            lanes = slice(STATE * part, STATE * (part + 1))
            grad_conv = gradient[part] * nslope_ref[:, lanes]
            next_ref[0:GROUP, lanes] = grad_conv
            pre = npre_ref[:, lanes].astype(BF16).astype(F32)
            total_pre = jnp.zeros_like(grad_conv)
            for j in range(CONV):
                moved = next_ref[j : j + GROUP, lanes]
                total_pre = total_pre + ntaps_ref[CONV - 1 - j : CONV - j, lanes] * moved
                nsums_ref[CONV - 1 - j : CONV - j, lanes] += jnp.sum(pre * moved, axis=0, keepdims=True)
            nsums_ref[CONV : CONV + 1, lanes] += jnp.sum(grad_conv, axis=0, keepdims=True)
            gnarrow_ref[:, lanes] = total_pre.astype(BF16)

        @pl.when(first_of_slot)
        def _():
            head_ref[0:8, : 2 * STATE] = jnp.zeros((8, 2 * STATE), F32)
            head_ref[8:16, : 2 * STATE] = next_ref[0:8, :]
            halo = jnp.zeros((8, 2 * STATE), F32)
            for j in range(CONV):
                moved = head_ref[j : j + 8, : 2 * STATE]
                halo = halo + ntaps_ref[CONV - 1 - j : CONV - j, :] * moved
                nsums_ref[CONV - 1 - j : CONV - j, :] += jnp.sum(
                    nrim_ref[0].astype(F32) * moved[5:8], axis=0, keepdims=True
                )
            nhalo_ref[0] = halo

        own = cols_ref[...]
        lane = lax.broadcasted_iota(jnp.int32, (GROUP, 128), 1)
        step = jnp.where(lane < heads, own, 0.0)
        cum = pltpu.roll(own, 128 - heads, 1)
        sig = jnp.where(lane < heads, pltpu.roll(own, 128 - 2 * heads, 1), 0.0)
        strict = lax.broadcasted_iota(jnp.int32, (GROUP, GROUP), 0) > lax.broadcasted_iota(
            jnp.int32, (GROUP, GROUP), 1
        )
        reverse_sum = (
            split_dot(lower.astype(BF16), v_ref[...], 2, 0)
            + split_dot(strict.astype(BF16), i_ref[...], 2, 1)
            + jnp.exp(cum[GROUP - 1 : GROUP, :]) * e_ref[8:9, 0:128]
        )
        grad_raw = (u_ref[...] + rate_ref[...] * reverse_sum) * sig
        gnarrow_ref[:, 2 * STATE :] = grad_raw.astype(BF16)
        hsums_ref[0:1, :] += jnp.sum(grad_raw, axis=0, keepdims=True)
        hsums_ref[1:2, :] += jnp.sum(reverse_sum * step, axis=0, keepdims=True) * rate_ref[...]


def back_blocks(
    x, mixed, grad, slope, pre, rim, wr, nslope, npre, nrim, cols, rows, states, flows, skip, taps, ntaps, rate, groups
):
    tokens, width = x.shape
    blocks, steps, heads, slots = tokens // GROUP, width // LANES_STEP, rows.shape[1], rim.shape[0]
    at = lambda b: blocks - 1 - b
    wide = pl.BlockSpec((GROUP, LANES_STEP), lambda b, g: (at(b), g))
    narrow = lambda w: pl.BlockSpec((GROUP, w), lambda b, g: (at(b), 0))
    state = pl.BlockSpec((1, STATE, LANES_STEP), lambda b, g: (at(b), 0, g))
    line = lambda n: pl.BlockSpec((n, LANES_STEP), lambda b, g: (0, g))
    whole = lambda shape: pl.BlockSpec(shape, lambda b, g: (0,) * len(shape))
    return pl.pallas_call(
        functools.partial(back_kernel, groups, heads),
        grid=(blocks, steps),
        in_specs=[
            wide, wide, wide, wide, wide,
            pl.BlockSpec((1, CONV - 1, LANES_STEP), lambda b, g: (at(b) // groups, 0, g)),
            narrow(2 * STATE), narrow(2 * STATE), narrow(npre.shape[1]),
            pl.BlockSpec((1, CONV - 1, 2 * STATE), lambda b, g: (at(b) // groups, 0, 0)),
            narrow(128),
            pl.BlockSpec((1, heads, GROUP), lambda b, g: (at(b), 0, 0)),
            state, state, line(1), line(CONV), whole((CONV, 2 * STATE)), whole((1, 128)),
        ],
        out_specs=[
            wide, narrow(2 * STATE + 128),
            whole((steps, 8, LANES_STEP)), whole((8, 2 * STATE)), whole((8, 128)),
            pl.BlockSpec((1, 8, LANES_STEP), lambda b, g: (at(b) // groups, 0, g)),
            pl.BlockSpec((1, 8, 2 * STATE), lambda b, g: (at(b) // groups, 0, 0)),
        ],
        out_shape=[
            jax.ShapeDtypeStruct((tokens, width), BF16),
            jax.ShapeDtypeStruct((tokens, 2 * STATE + 128), BF16),
            jax.ShapeDtypeStruct((steps, 8, LANES_STEP), F32),
            jax.ShapeDtypeStruct((8, 2 * STATE), F32),
            jax.ShapeDtypeStruct((8, 128), F32),
            jax.ShapeDtypeStruct((slots, 8, width), F32),
            jax.ShapeDtypeStruct((slots, 8, 2 * STATE), F32),
        ],
        scratch_shapes=[
            pltpu.VMEM((GROUP, GROUP), F32),
            pltpu.VMEM((GROUP, GROUP), F32),
            pltpu.VMEM((3, GROUP, LANES_STEP), F32),
            pltpu.VMEM((GROUP, STATE), F32),
            pltpu.VMEM((GROUP, STATE), F32),
            pltpu.VMEM((GROUP, 128), F32),
            pltpu.VMEM((GROUP, 128), F32),
            pltpu.VMEM((GROUP, 128), F32),
            pltpu.VMEM((16, LANES_STEP), F32),
            pltpu.VMEM((steps, GROUP + 8, LANES_STEP), F32),
            pltpu.VMEM((GROUP + 8, 2 * STATE), F32),
            pltpu.VMEM((16, max(LANES_STEP, 2 * STATE)), F32),
        ],
        cost_estimate=pl.CostEstimate(
            flops=2 * tokens * width * (4 * GROUP + 4 * STATE) * 2,
            bytes_accessed=tokens * width * 14,
            transcendentals=tokens * GROUP * width // HEADDIM,
        ),
        name="back_blocks",
    )(x, mixed, grad, slope, pre, rim, wr, nslope, npre, nrim, cols, rows, states, flows, skip, taps, ntaps, rate)


MESH = pl.DeviceIdType.MESH
FAR_PARTS = 4


def fetch_kernel(
    x_ref, inner_ref, gate_ref, step_ref, wr_ref, out_ref, small_ref,
    full_x, full_inner, full_gate, full_step, full_wr, out_far, full_small,
    x_own, inner_own, gate_own, step_own, wr_own, small_own, send_sem, recv_sem, local_sem,
):
    f, c, z = lax.axis_index("fsdp"), lax.axis_index("ctx"), lax.axis_index("tp")
    half = z // 2
    slots, seq, cols = full_x.shape[0], full_x.shape[1], x_ref.shape[2]
    depth = inner_ref.shape[0]
    partners = (
        {"fsdp": f ^ 1}, {"fsdp": f ^ 2}, {"fsdp": f ^ 3}, {"ctx": c ^ 1}, {"tp": z ^ 1}, {"tp": z ^ 2},
    )
    barrier = pltpu.get_barrier_semaphore()
    for partner in partners:
        pl.semaphore_signal(barrier, inc=1, device_id=partner, device_id_type=MESH)
    pl.semaphore_wait(barrier, len(partners))

    copies = []

    def send(src, dst, partner):
        at = len(copies)
        copy = pltpu.make_async_remote_copy(
            src_ref=src, dst_ref=dst, send_sem=send_sem.at[at], recv_sem=recv_sem.at[at],
            device_id=partners[partner], device_id_type=MESH,
        )
        copy.start()
        copies.append([copy, False])
        return at

    def arrived(at):
        copies[at][0].wait_recv()
        copies[at][1] = True

    def feature(which):
        return pl.ds(pl.multiple_of(which * cols, 128), cols)

    def shard(full, row_f, far):
        wide = full.shape[1] // 2
        start = pl.multiple_of((row_f * 2 + c) * depth, depth)
        return full.at[pl.ds(start, depth), pl.ds(far * wide, wide)]

    def shard_one(full, row_f, far):
        start = pl.multiple_of((row_f * 2 + c) * depth, depth)
        return full.at[pl.ds(start, depth), :]

    def spread(full, src, far, part=shard):
        dst = part(full, f, far)
        near = [send(src, dst, k) for k in range(3)]
        send(src, dst, 3)
        return near

    def relay(full, near, far, part=shard):
        for k in range(3):
            arrived(near[k])
            row = part(full, f ^ (k + 1), far)
            send(row, row, 3)

    mine = pl.ds(half * slots, slots)
    other = pl.ds((1 - half) * slots, slots)
    send(small_ref, full_small.at[z], 4)
    far_small = send(small_ref, full_small.at[z], 5)
    send(x_ref.at[mine], full_x.at[:, :, feature(z)], 4)
    far_inner = send(inner_ref, shard(full_inner, f, 1), 5)
    far_step = send(step_ref, shard(full_step, f, 1), 5)
    piece = seq // FAR_PARTS
    far_x = [
        send(x_ref.at[other, pl.ds(piece * i, piece)], full_x.at[:, pl.ds(piece * i, piece), feature(z)], 5)
        for i in range(FAR_PARTS)
    ]
    far_gate = send(gate_ref, shard(full_gate, f, 1), 5)
    send(out_ref, out_far, 5)
    own_inner = spread(full_inner, inner_ref, 0)
    own_step = spread(full_step, step_ref, 0)
    own_wr = spread(full_wr, wr_ref, 0, shard_one)

    staged = (
        (x_ref.at[mine], x_own, full_x.at[:, :, feature(z)]),
        (inner_ref, inner_own, shard(full_inner, f, 0)),
        (gate_ref, gate_own, shard(full_gate, f, 0)),
        (step_ref, step_own, shard(full_step, f, 0)),
        (wr_ref, wr_own, shard_one(full_wr, f, 0)),
        (small_ref, small_own, full_small.at[z]),
    )
    loads = [pltpu.make_async_copy(src, buf, local_sem.at[0, i]) for i, (src, buf, _) in enumerate(staged)]
    stores = [pltpu.make_async_copy(buf, dst, local_sem.at[1, i]) for i, (_, buf, dst) in enumerate(staged)]
    for load in loads:
        load.start()
    for load, store in zip(loads, stores):
        load.wait()
        store.start()

    arrived(far_small)
    send(full_small.at[z ^ 2], full_small.at[z ^ 2], 4)
    arrived(far_inner)
    away_inner = spread(full_inner, shard(full_inner, f, 1), 1)
    arrived(far_step)
    away_step = spread(full_step, shard(full_step, f, 1), 1)
    own_gate = spread(full_gate, gate_ref, 0)

    def both(i):
        arrived(far_x[i])
        part = full_x.at[:, pl.ds(piece * i, piece), feature(z ^ 2)]
        send(part, part, 4)

    relay(full_inner, own_inner, 0)
    relay(full_step, own_step, 0)
    relay(full_wr, own_wr, 0, shard_one)
    both(0)
    relay(full_inner, away_inner, 1)
    relay(full_step, away_step, 1)
    both(1)
    both(2)
    relay(full_gate, own_gate, 0)
    both(3)
    arrived(far_gate)
    away_gate = spread(full_gate, shard(full_gate, f, 1), 1)
    relay(full_gate, away_gate, 1)
    for store in stores:
        store.wait()
    for copy, done in copies:
        if not done:
            copy.wait_recv()
        copy.wait_send()


def fetch(hidden, inner, gate, step, wr, out, small):
    slot_count, seq, cols = hidden.shape
    slots, depth = slot_count // 2, inner.shape[0]
    total = 8 * depth
    count = 1 + 2 * FAR_PARTS + 3 + 7 * 7 + 4
    anywhere = pl.BlockSpec(memory_space=pl.ANY)
    full = lambda x: jax.ShapeDtypeStruct((total, 2 * x.shape[1]), BF16)
    return pl.pallas_call(
        fetch_kernel,
        in_specs=[anywhere] * 7,
        out_specs=[anywhere] * 7,
        out_shape=[
            jax.ShapeDtypeStruct((slots, seq, 4 * cols), BF16),
            full(inner), full(gate), full(step),
            jax.ShapeDtypeStruct((total, wr.shape[1]), BF16),
            jax.ShapeDtypeStruct(out.shape, BF16),
            jax.ShapeDtypeStruct((4,) + small.shape, F32),
        ],
        scratch_shapes=[
            pltpu.VMEM((slots, seq, cols), BF16),
            pltpu.VMEM(inner.shape, BF16),
            pltpu.VMEM(gate.shape, BF16),
            pltpu.VMEM(step.shape, BF16),
            pltpu.VMEM(wr.shape, BF16),
            pltpu.VMEM(small.shape, F32),
            pltpu.SemaphoreType.DMA((count,)),
            pltpu.SemaphoreType.DMA((count,)),
            pltpu.SemaphoreType.DMA((2, 6)),
        ],
        compiler_params=pltpu.CompilerParams(collective_id=0, has_side_effects=True),
        name="fetch",
    )(hidden, inner, gate, step, wr, out, small)


def finish_kernel(
    part_ref, grad_ref, small_ref, cross_ref,
    near_out, other_out, home_out, narrow_out, small_out, small_far, cross_out, cross_far,
    relay_buf, part_buf, sum_buf, core_buf, own_buf, plane_buf, got_buf, sent_buf, home_buf, wr_send, wr_got,
    small_got, cross_got, send_sem, recv_sem, load_sem,
):
    f, c, z = lax.axis_index("fsdp"), lax.axis_index("ctx"), lax.axis_index("tp")
    tokens, cols = near_out.shape
    depth, inner = home_out.shape
    partners = (
        {"fsdp": f ^ 1}, {"fsdp": f ^ 2}, {"fsdp": f ^ 3}, {"ctx": c ^ 1}, {"tp": z ^ 1}, {"tp": z ^ 2},
    )
    barrier = pltpu.get_barrier_semaphore()
    for partner in partners:
        pl.semaphore_signal(barrier, inc=1, device_id=partner, device_id_type=MESH)

    def feature(which):
        return pl.ds(pl.multiple_of(which * cols, 128), cols)

    def rows_of(row_f, core):
        return pl.ds(pl.multiple_of((row_f * 2 + core) * depth, depth), depth)

    piece = tokens // FAR_PARTS
    loads = [
        pltpu.make_async_copy(grad_ref.at[rows_of(f ^ k, c)], own_buf.at[k], load_sem.at[k]) for k in range(4)
    ] + [
        pltpu.make_async_copy(
            part_ref.at[pl.ds(piece * i, piece), feature(z ^ 2)], part_buf.at[i], load_sem.at[4 + i]
        )
        for i in range(FAR_PARTS)
    ]
    for load in loads:
        load.start()
    pl.semaphore_wait(barrier, len(partners))

    copies = []

    def send(src, dst, partner):
        at = len(copies)
        copy = pltpu.make_async_remote_copy(
            src_ref=src, dst_ref=dst, send_sem=send_sem.at[at], recv_sem=recv_sem.at[at],
            device_id=partners[partner], device_id_type=MESH,
        )
        copy.start()
        copies.append([copy, False])
        return at

    def arrived(at):
        copies[at][0].wait_recv()
        copies[at][1] = True

    core = [send(grad_ref.at[rows_of(f ^ k, c ^ 1)], core_buf.at[k], 3) for k in (1, 2, 3, 0)]
    core_of = {1: core[0], 2: core[1], 3: core[2], 0: core[3]}
    small = [send(small_ref, small_got.at[0], 3)]
    cross = [send(cross_ref, cross_got, 4)]
    relays = [
        send(part_ref.at[pl.ds(piece * i, piece), feature(z ^ 3)], relay_buf.at[i], 4) for i in range(FAR_PARTS)
    ]
    for load in loads[:4]:
        load.wait()
    plane = []
    for k in (1, 2, 3):
        arrived(core_of[k])
        sent_buf[k - 1] = (own_buf[k].astype(F32) + core_buf[k].astype(F32)).astype(BF16)
        plane.append(send(sent_buf.at[k - 1], plane_buf.at[k - 1], k - 1))
    arrived(cross[0])
    cross_out[...] = cross_ref[...] + cross_got[...]
    arrived(small[0])
    small_out[...] = small_ref[...] + small_got[0]
    small.append(send(small_out, small_got.at[1], 0))
    cross.append(send(cross_out, cross_far, 5))

    def passed_on(i):
        loads[4 + i].wait()
        arrived(relays[i])
        sum_buf[i] = (part_buf[i].astype(F32) + relay_buf[i].astype(F32)).astype(BF16)
        send(sum_buf.at[i], other_out.at[pl.ds(piece * i, piece)], 5)

    passed_on(0)
    arrived(small[1])
    copies[small[1]][0].wait_send()
    small_out[...] = small_out[...] + small_got[1]
    small.append(send(small_out, small_got.at[2], 1))
    passed_on(1)
    arrived(core_of[0])
    passed_on(2)
    arrived(small[2])
    copies[small[2]][0].wait_send()
    small_out[...] = small_out[...] + small_got[2]
    small.append(send(small_out, small_got.at[3], 4))
    passed_on(3)
    total = own_buf[0].astype(F32) + core_buf[0].astype(F32)
    for at in plane:
        arrived(at)
    for k in range(3):
        total = total + plane_buf[k].astype(F32)
    wr_send[...] = total[:, 2 * inner : 2 * inner + 2 * STATE]
    wr = send(wr_send, wr_got, 4)
    send(part_ref.at[:, feature(z ^ 1)], near_out, 4)
    home_out[...] = total[:, :inner]
    home_buf[:, :inner] = total[:, inner : 2 * inner].astype(BF16)
    narrow_out[:, 2 * STATE : 2 * STATE + 128] = total[:, 2 * inner + 2 * STATE :]
    home_buf[:, inner + 2 * STATE :] = total[:, 2 * inner + 2 * STATE :].astype(BF16)
    arrived(small[3])
    copies[small[3]][0].wait_send()
    shared = small_out.shape[0] // 2
    small_out[shared:, :] = small_out[shared:, :] + small_got[3, shared:, :]
    small.append(send(small_out, small_far, 5))
    arrived(wr)
    both = wr_send[...] + wr_got[...]
    narrow_out[:, : 2 * STATE] = both
    home_buf[:, inner : inner + 2 * STATE] = both.astype(BF16)
    last = send(home_buf, got_buf, 5)
    arrived(last)
    home_out[...] += got_buf[:, :inner].astype(F32)
    narrow_out[:, : 2 * STATE] += got_buf[:, inner : inner + 2 * STATE].astype(F32)
    steps = got_buf[:, inner + 2 * STATE :].astype(F32)
    narrow_out[:, 2 * STATE + 128 :] = steps
    for copy, done in copies:
        if not done:
            copy.wait_recv()
    waited = {small[1], small[2], small[3]}
    for at, (copy, done) in enumerate(copies):
        if at not in waited:
            copy.wait_send()


def finish(part, grad, small, cross, depth):
    tokens, width = part.shape
    cols, total = width // 4, grad.shape[1]
    rest = 2 * STATE + 128
    inner = (total - rest) // 2
    anywhere = pl.BlockSpec(memory_space=pl.ANY)
    vmem = pl.BlockSpec(memory_space=pltpu.VMEM)
    count = 4 + 5 + 2 + FAR_PARTS * 2 + 1 + 3 + 2
    return pl.pallas_call(
        finish_kernel,
        in_specs=[anywhere, anywhere, vmem, vmem],
        out_specs=[anywhere, anywhere, vmem, vmem, vmem, vmem, vmem, vmem],
        out_shape=[
            jax.ShapeDtypeStruct((tokens, cols), BF16),
            jax.ShapeDtypeStruct((tokens, cols), BF16),
            jax.ShapeDtypeStruct((depth, inner), F32),
            jax.ShapeDtypeStruct((depth, rest + 128), F32),
            jax.ShapeDtypeStruct(small.shape, F32),
            jax.ShapeDtypeStruct(small.shape, F32),
            jax.ShapeDtypeStruct(cross.shape, F32),
            jax.ShapeDtypeStruct(cross.shape, F32),
        ],
        scratch_shapes=[
            pltpu.VMEM((FAR_PARTS, tokens // FAR_PARTS, cols), BF16),
            pltpu.VMEM((FAR_PARTS, tokens // FAR_PARTS, cols), BF16),
            pltpu.VMEM((FAR_PARTS, tokens // FAR_PARTS, cols), BF16),
            pltpu.VMEM((4, depth, total), BF16),
            pltpu.VMEM((4, depth, total), BF16),
            pltpu.VMEM((3, depth, total), BF16),
            pltpu.VMEM((depth, inner + rest), BF16),
            pltpu.VMEM((3, depth, total), BF16),
            pltpu.VMEM((depth, inner + rest), BF16),
            pltpu.VMEM((depth, 2 * STATE), F32),
            pltpu.VMEM((depth, 2 * STATE), F32),
            pltpu.VMEM((4,) + small.shape, F32),
            pltpu.VMEM(cross.shape, F32),
            pltpu.SemaphoreType.DMA((count,)),
            pltpu.SemaphoreType.DMA((count,)),
            pltpu.SemaphoreType.DMA((4 + FAR_PARTS,)),
        ],
        compiler_params=pltpu.CompilerParams(collective_id=1, has_side_effects=True),
        name="finish",
    )(part, grad, small, cross)


def after(x, other):
    return lax.optimization_barrier((x, other))[0]


def everywhere(x):
    for axis in ("ctx", "fsdp"):
        count, bit = lax.axis_size(axis), 1
        if count & (count - 1):
            x = lax.psum(x, axis)
            continue
        while bit < count:
            x = x + lax.ppermute(x, axis, [(i, i ^ bit) for i in range(count)])
            bit *= 2
    return x


def pack(parts):
    return jnp.concatenate([part.reshape(-1) for part in parts])


def unpack(vector, shapes):
    parts, at = [], 0
    for shape in shapes:
        size = 1
        for dim in shape:
            size *= dim
        parts.append(vector[at : at + size].reshape(shape))
        at += size
    return parts


def on_device(
    hidden_in,
    lengths,
    norm_gain,
    proj_gate_inner,
    proj_write_read,
    proj_step,
    conv_inner,
    conv_inner_bias,
    conv_write_read,
    conv_write_read_bias,
    step_bias,
    log_rate,
    skip_gain,
    gate_gain,
    proj_out,
    out_cotangent,
):
    slot_count, seq_here, width_here = hidden_in.shape
    slots = slot_count // 2
    tokens = slots * seq_here
    heads_own = step_bias.shape[0]
    inner_own = gate_gain.shape[0]
    heads = 2 * heads_own
    inner = 2 * inner_own
    tp_count = lax.axis_size("tp")
    width = tp_count * width_here
    groups = seq_here // GROUP
    blocks = slots * groups
    head_steps = heads // HEADS_STEP
    rim_rows = CONV - 1
    place = lax.axis_index("tp")
    far_half, near_side = place // 2, place % 2

    def half_of(whole, which):
        return lax.dynamic_slice_in_dim(whole, which * slots, slots, 0)

    def ordered(own, near, far, both, axis):
        first = lambda a, b: jnp.where(near_side == 0, a, b)
        a0, a1, b0, b1 = first(own, near), first(near, own), first(far, both), first(both, far)
        lower = lambda a, b: jnp.where(far_half == 0, a, b)
        return jnp.concatenate(
            [lower(a0, b0), lower(a1, b1), lower(b0, a0), lower(b1, a1)], axis=axis
        )

    def own_features(piece):
        relay = swap(piece(place ^ 3).astype(BF16), 1)
        keep = swap(piece(place ^ 1).astype(BF16), 1)
        sent = swap((piece(place ^ 2) + relay.astype(F32)).astype(BF16), 2)
        kept = (piece(place) + keep.astype(F32)).reshape(slots, seq_here, width_here)
        other = sent.astype(F32).reshape(slots, seq_here, width_here)
        return both_halves(kept, other)

    def both_halves(kept, other):
        return jnp.where(
            far_half == 0,
            jnp.concatenate([kept, other], axis=0),
            jnp.concatenate([other, kept], axis=0),
        )

    small_shapes = [(CONV, inner_own), (inner_own,), (inner_own,), (heads_own,), (heads_own,), (heads_own,)]
    def gathered(x):
        return lax.all_gather(x, ("fsdp", "ctx"), axis=0, tiled=True)

    own_small = pack([conv_inner, conv_inner_bias, gate_gain, step_bias, log_rate, skip_gain])
    cot_mine, cot_other = half_of(out_cotangent, far_half), half_of(out_cotangent, 1 - far_half)
    narrow_cols = 2 * STATE + heads
    narrow_pad = -narrow_cols % 128
    zeros = lambda x, extra: jnp.zeros((x.shape[0], extra), BF16)
    inner_shard, gate_shard = proj_gate_inner[:, 1], proj_gate_inner[:, 0]
    if lax.axis_size("fsdp") == 4 and lax.axis_size("ctx") == 2:
        step_shard = jnp.concatenate([proj_step, zeros(proj_step, 128 - heads_own)], axis=1)
        small = pack([norm_gain.astype(F32), own_small])
        small = jnp.pad(small, (0, -small.size % 1024)).reshape(-1, 128)
        full_x, full_inner, full_gate, full_step, full_wr, out_far, full_small = fetch(
            hidden_in, inner_shard, gate_shard, step_shard, proj_write_read, proj_out, small
        )
        full_small = full_small.reshape(tp_count, -1)
        full_gain = full_small[:, :width_here].reshape(width)
        far_row = lax.dynamic_slice_in_dim(full_small, place ^ 2, 1, 0)[0, width_here:]
        far_small = unpack(far_row, small_shapes)
        full_narrow = jnp.concatenate(
            [full_wr, full_step[:, :heads_own], full_step[:, 128 : 128 + heads_own], zeros(full_wr, narrow_pad)],
            axis=1,
        )
        cot_dep = full_x
    else:
        x_mine, x_other = half_of(hidden_in, far_half), half_of(hidden_in, 1 - far_half)
        narrow_shard = jnp.concatenate(
            [proj_write_read, proj_step, swap(proj_step, 2), zeros(proj_step, narrow_pad)], axis=1
        )
        inner_far = swap(inner_shard, 2)
        x_near = swap(x_mine, 1)
        x_far = swap(after(x_other, inner_far), 2)
        gate_far = swap(after(gate_shard, x_far), 2)
        x_both = swap(x_far, 1)
        cot_dep = after(x_both, gate_far)
        full_narrow = gathered(narrow_shard)
        full_inner = gathered(jnp.concatenate([inner_shard, inner_far], axis=1))
        full_gate = gathered(jnp.concatenate([after(gate_shard, full_inner), gate_far], axis=1))
        full_x = ordered(x_mine, x_near, x_far, x_both, 2)
        out_far = swap(after(proj_out, cot_dep), 2)
        gain = norm_gain.astype(F32)
        full_gain = ordered(gain, swap(gain, 1), swap(gain, 2), swap(gain, 3), 0)
        far_small = unpack(swap(own_small, 2), small_shapes)
    full_x = full_x.reshape(tokens, width)
    cot_near = swap(after(cot_mine, cot_dep), 1)
    cot_far = swap(after(cot_other, cot_dep), 2)
    cot_both = swap(cot_far, 1)
    full_out = gathered(jnp.concatenate([after(proj_out, full_gate), out_far], axis=1))
    full_cot = ordered(cot_mine, cot_near, cot_far, cot_both, 2).reshape(tokens, width)

    taps = jnp.concatenate([conv_inner, far_small[0]], axis=1)
    taps_bias = jnp.concatenate([conv_inner_bias, far_small[1]])
    gain_gate = jnp.concatenate([gate_gain, far_small[2]])
    bias_step = jnp.concatenate([step_bias, far_small[3]])
    rate_log = jnp.concatenate([log_rate, far_small[4]])
    gain_skip = jnp.concatenate([skip_gain, far_small[5]])
    rate = -jnp.exp(rate_log)
    skip_lanes = jnp.repeat(gain_skip, HEADDIM)[None]

    in_float = full_x.astype(F32)
    in_scale = lax.rsqrt(jnp.mean(in_float * in_float, axis=-1, keepdims=True) + EPSILON)
    normed = (in_float * in_scale * full_gain.astype(F32)).astype(BF16)
    narrow_pre = dot(normed, full_narrow, 1, 0)
    inner_pre = dot(normed, full_inner, 1, 0).astype(BF16)
    gate_pre = dot(normed, full_gate, 1, 0).astype(BF16)

    def rim_of(pre):
        by_slot = pre.reshape(slots, seq_here, pre.shape[-1])
        return passed_along(by_slot[:, seq_here - rim_rows :].astype(BF16), "ctx", 1)

    inner_rim, narrow_rim = rim_of(inner_pre), rim_of(narrow_pre[:, : 2 * STATE])
    lane_pad = lambda x: jnp.pad(x, (0, 128 - heads))[None]
    rate_row = lane_pad(rate)
    inner_act, slope, write_read, narrow_slope, cols, cum_rows, local_state, decay_lanes = start_blocks(
        inner_pre, inner_rim, narrow_pre, narrow_rim, taps, taps_bias[None], conv_write_read,
        conv_write_read_bias[None], lane_pad(bias_step), rate_row, groups, heads,
    )
    local_state = local_state.reshape(slots, groups, STATE, inner)
    decay_lanes = decay_lanes.reshape(slots, groups, 1, inner)
    carried = local_state[:, 0]
    device_decay = decay_lanes[:, 0]
    for position in range(1, groups):
        carried = decay_lanes[:, position] * carried + local_state[:, position]
        device_decay = device_decay * decay_lanes[:, position]
    current = carried_in(device_decay, carried, None, False)
    state_list = []
    for position in range(groups):
        state_list.append(current)
        current = decay_lanes[:, position] * current + local_state[:, position]
    states = jnp.stack(state_list, axis=1)
    states_low = states.astype(BF16).reshape(blocks, STATE, inner)

    position_ids = lax.axis_index("ctx") * seq_here + jnp.arange(seq_here)
    valid_rows = (position_ids[None, :] < lengths[:, None]).astype(F32)
    valid_here = half_of(valid_rows, far_half).reshape(tokens, 1)
    masked = (full_cot.astype(F32) * valid_here).astype(BF16)
    grad_normed_out = dot(masked, full_out, 1, 0).astype(BF16)
    mixed_out, stats = mix_blocks(
        inner_act, gate_pre, grad_normed_out, write_read, cols, cum_rows, states_low, skip_lanes, gain_gate[None],
    )
    stats = stats + swap(stats, 1)
    normed_out, grad_gate_pre, grad_diag, grad_gate_gain, grad_skip_lanes, local_grad = gate_blocks(
        mixed_out, gate_pre, grad_normed_out, inner_act, stats, gain_gate[None], write_read, cols, heads
    )
    local_grad = local_grad.reshape(slots, groups, STATE, inner)

    def branch_piece(which):
        rows = lax.dynamic_slice_in_dim(full_out, which * width_here, width_here, 0)
        return dot(normed_out, rows, 1, 1)

    branch = own_features(branch_piece)
    hidden_out = (hidden_in.astype(F32) + valid_rows[..., None] * branch).astype(BF16)
    grad_proj_out = dot(masked, normed_out, 0, 0).astype(BF16)
    grad_gate_w = dot(normed, grad_gate_pre, 0, 0).astype(BF16)
    grad_by_gate = dot(grad_gate_pre, full_gate, 1, 1)
    other_scale = swap(in_scale.reshape(-1, 128), 2)

    flowing = local_grad[:, groups - 1]
    for position in reversed(range(groups - 1)):
        flowing = decay_lanes[:, position] * flowing + local_grad[:, position]
    flowing = carried_in(device_decay, flowing, None, True)
    flow_list = []
    for position in reversed(range(groups)):
        flow_list.insert(0, flowing)
        flowing = decay_lanes[:, position] * flowing + local_grad[:, position]
    flows = jnp.stack(flow_list, axis=1)
    flows_low = flows.astype(BF16).reshape(blocks, STATE, inner)
    flows_low = after(flows_low, (grad_proj_out, grad_gate_w))

    grad_inner_pre, grad_narrow, tap_sums, narrow_sums, head_sums, halo, narrow_halo = back_blocks(
        inner_act, mixed_out, grad_diag, slope, inner_pre, inner_rim, write_read, narrow_slope, narrow_pre,
        narrow_rim, cols, cum_rows, states_low, flows_low, skip_lanes, taps, conv_write_read, rate_row, groups,
    )
    tap_sums = tap_sums.transpose(1, 0, 2).reshape(8, inner)
    grad_taps, grad_taps_bias = tap_sums[:CONV], tap_sums[CONV]
    grad_conv_write_read, grad_conv_write_read_bias = narrow_sums[:CONV], narrow_sums[CONV]
    grad_step_bias, grad_log_rate = head_sums[0, :heads], head_sums[1, :heads]

    def completed(grad, halo):
        back = passed_along(halo, "ctx", -1)
        for slot in range(slots):
            ends = (slot + 1) * seq_here
            rows = grad[ends - 8 : ends, : halo.shape[-1]].astype(F32) + back[slot]
            grad = lax.dynamic_update_slice(grad, rows.astype(BF16), (ends - 8, 0))
        return grad

    grad_inner_pre, grad_narrow = completed(grad_inner_pre, halo), completed(grad_narrow, narrow_halo)
    def reduced(x):
        return lax.psum_scatter(x, ("fsdp", "ctx"), scatter_dimension=0, tiled=True)

    early = reduced(jnp.concatenate([grad_proj_out, grad_gate_w], axis=1))
    early_far = swap(jnp.concatenate([early[:, inner_own:inner], early[:, inner + inner_own :]], axis=1), 2)
    grad_out_home = early[:, :inner_own].astype(F32) + early_far[:, :inner_own].astype(F32)
    grad_gate_home = early[:, inner : inner + inner_own].astype(F32) + early_far[:, inner_own:].astype(F32)

    grad_inner_pre, hidden_out = lax.optimization_barrier((grad_inner_pre, hidden_out))
    late = jnp.concatenate([grad_inner_pre, grad_narrow], axis=1)
    grad_late_w = dot(normed, late, 0, 0).astype(BF16)
    partial_normed = (
        grad_by_gate + dot(grad_inner_pre, full_inner, 1, 1) + dot(grad_narrow, full_narrow, 1, 1)
    )
    by_hat = partial_normed * (full_x.astype(F32) * in_scale)
    grad_gain_full = jnp.sum(by_hat, axis=0)
    cross_part = jnp.sum(by_hat * full_gain.astype(F32), axis=1)
    partial_low = partial_normed.astype(BF16)

    grad_skip_gain = jnp.sum(grad_skip_lanes.reshape(heads, HEADDIM), axis=1)
    shared_shapes = [(CONV, 2 * STATE), (2 * STATE,), (width,)]
    head_shapes = [(CONV, inner), (inner,), (inner,), (heads,), (heads,), (heads,)]
    by_head = pack([grad_taps, grad_taps_bias, grad_gate_gain, grad_step_bias, grad_log_rate, grad_skip_gain])
    by_all = pack([grad_conv_write_read, grad_conv_write_read_bias, grad_gain_full])

    if lax.axis_size("fsdp") == 4 and lax.axis_size("ctx") == 2:
        lines = -(-max(by_head.size, by_all.size) // 1024) * 8
        filled = lambda v: jnp.pad(v, (0, lines * 128 - v.size)).reshape(lines, 128)
        near, other, grad_inner_home, narrow_sum, small_own, small_far, cross_rows, cross_far = finish(
            partial_low,
            after(grad_late_w, early_far),
            jnp.concatenate([filled(by_head), filled(by_all)]),
            cross_part.reshape(-1, 128),
            proj_write_read.shape[0],
        )
        kept = lax.dynamic_slice_in_dim(partial_normed, place * width_here, width_here, 1) + near.astype(F32)
        grad_normed = both_halves(
            kept.reshape(slots, seq_here, width_here), other.astype(F32).reshape(slots, seq_here, width_here)
        )
        write_read_home = narrow_sum[:, : 2 * STATE]
        step_home = (
            narrow_sum[:, 2 * STATE : 2 * STATE + heads_own]
            + narrow_sum[:, 2 * STATE + 128 + heads_own : 2 * STATE + 128 + heads]
        )
        cross_rows, cross_far = cross_rows.reshape(-1), cross_far.reshape(-1)
        parts = unpack(small_own[:lines].reshape(-1), head_shapes)
        far_parts = unpack(small_far[:lines].reshape(-1), head_shapes)
        far_parts = [lax.slice_in_dim(p, p.shape[-1] // 2, p.shape[-1], axis=p.ndim - 1) for p in far_parts]
        shared = (small_own[lines:] + small_far[lines:]).reshape(-1)
    else:

        def normed_piece(which):
            return lax.dynamic_slice_in_dim(partial_normed, which * width_here, width_here, 1)

        grad_normed = own_features(normed_piece)
        late_sum = reduced(grad_late_w)
        late_far = swap(late_sum, 2).astype(F32)
        late_sum = late_sum.astype(F32)
        grad_inner_home = late_sum[:, :inner_own] + late_far[:, inner_own:inner]
        write_read_home = late_sum[:, inner : inner + 2 * STATE] + late_far[:, inner : inner + 2 * STATE]
        write_read_home = write_read_home + swap(write_read_home, 1)
        steps_at = inner + 2 * STATE
        step_home = late_sum[:, steps_at : steps_at + heads_own] + late_far[:, steps_at + heads_own : steps_at + heads]
        cross_rows = cross_part + swap(cross_part, 1)
        cross_far = swap(cross_rows, 2)
        smalls = everywhere(pack([by_head, by_all]))
        parts = unpack(smalls[: by_head.size], head_shapes)
        away = [lax.slice_in_dim(p, p.shape[-1] // 2, p.shape[-1], axis=p.ndim - 1) for p in parts]
        far_parts = unpack(swap(pack(away), 2), small_shapes)
        shared = smalls[by_head.size :]
        shared = shared + swap(shared, 1)
        shared = shared + swap(shared, 2)

    homes = [
        lax.slice_in_dim(p, 0, p.shape[-1] // 2, axis=p.ndim - 1) + a for p, a in zip(parts, far_parts)
    ]
    wr_taps, wr_bias, gain_all = unpack(shared, shared_shapes)
    grad_norm_gain = lax.dynamic_slice_in_dim(gain_all, place * width_here, width_here, 0)

    own_gain = norm_gain.astype(F32)
    own_scale = both_halves(
        in_scale.reshape(slots, seq_here, 1), other_scale.reshape(slots, seq_here, 1)
    )
    own_hat = hidden_in.astype(F32) * own_scale
    grad_hat_in = grad_normed * own_gain
    cross_in = both_halves(
        cross_rows.reshape(slots, seq_here, 1), cross_far.reshape(slots, seq_here, 1)
    ) / width
    grad_hidden_in = own_scale * (grad_hat_in - own_hat * cross_in) + out_cotangent.astype(F32)
    return (
        hidden_out,
        grad_hidden_in,
        grad_norm_gain,
        jnp.stack([grad_gate_home, grad_inner_home], axis=1),
        write_read_home,
        step_home,
        homes[0],
        homes[1],
        wr_taps,
        wr_bias,
        homes[3],
        homes[4],
        homes[5],
        homes[2],
        grad_out_home,
    )


def solution(mesh):
    rows = ("fsdp", "ctx")
    acts = P("fsdp", "ctx", "tp")
    placed = (
        acts,
        P("fsdp"),
        P("tp"),
        P(rows, None, "tp"),
        P(rows, None),
        P(rows, "tp"),
        P(None, "tp"),
        P("tp"),
        P(),
        P(),
        P("tp"),
        P("tp"),
        P("tp"),
        P("tp"),
        P(rows, "tp"),
        acts,
    )
    return jax.shard_map(
        on_device,
        mesh=mesh,
        in_specs=placed,
        out_specs=(
            acts,
            acts,
            P("tp"),
            P(rows, None, "tp"),
            P(rows, None),
            P(rows, "tp"),
            P(None, "tp"),
            P("tp"),
            P(),
            P(),
            P("tp"),
            P("tp"),
            P("tp"),
            P("tp"),
            P(rows, "tp"),
        ),
        check_vma=False,
    )
```

```python
import functools

import jax
import jax.numpy as jnp
from jax import lax
from jax.experimental import pallas as pl
from jax.experimental.pallas import tpu as pltpu
from jax.sharding import PartitionSpec as P

HEADDIM = 64
STATE = 128
CONV = 4
GROUP = 256
INNER = 3072
EPSILON = 1e-05
PAIR = 2 * HEADDIM
HEADS_STEP = 6
LANES_STEP = HEADS_STEP * HEADDIM
F32 = jnp.float32
BF16 = jnp.bfloat16
HIGHEST = lax.Precision.HIGHEST


def swap(x, bit):
    count = lax.axis_size("tp")
    return lax.ppermute(x, "tp", [(i, i ^ bit) for i in range(count)])


def passed_along(x, axis, by):
    count = lax.axis_size(axis)
    pairs = [(i, i + by) for i in range(count) if 0 <= i + by < count]
    return lax.ppermute(x, axis, pairs)


def carried_in(decay, final, combine, reverse):
    count, position = (lax.axis_size("ctx"), lax.axis_index("ctx"))
    if count == 2:
        return passed_along(final.astype(BF16), "ctx", -1 if reverse else 1).astype(F32)
    decays = lax.all_gather(decay.astype(BF16), "ctx").astype(F32)
    finals = lax.all_gather(final.astype(BF16), "ctx")
    start = jnp.zeros_like(final)

    def lap(k, before):
        at = count - 1 - k if reverse else k
        reached = at > position if reverse else at < position
        new = decays[at] * before + finals[at].astype(F32)
        return jnp.where(reached, new, before)

    return lax.fori_loop(0, count, lap, start)


def dot(a, b, da, db):
    return lax.dot_general(a, b, (((da,), (db,)), ((), ())), preferred_element_type=F32)


def low_lanes(rows):
    return lax.broadcasted_iota(jnp.int32, (rows, PAIR), 1) < HEADDIM


def spread_heads(cols, first, low_half):
    return jnp.where(low_half, cols[:, first : first + 1], cols[:, first + 1 : first + 2])


def lower_mask():
    return lax.broadcasted_iota(jnp.int32, (GROUP, GROUP), 0) >= lax.broadcasted_iota(
        jnp.int32, (GROUP, GROUP), 1
    )


def split_dot(ones, values, terms, contract):
    total, rest = None, values
    for _ in range(terms):
        part = rest.astype(BF16)
        rest = rest - part.astype(F32)
        piece = dot(ones, part, contract, 0)
        total = piece if total is None else total + piece
    return total


def turned(cols, heads_before):
    return pltpu.roll(cols, lax.rem(128 - heads_before, 128), 1)


def start_kernel(
    groups, heads,
    inner_ref, rim_ref, narrow_ref, nrim_ref, taps_ref, bias_ref, ntaps_ref, nbias_ref, sbias_ref, rate_ref,
    x_ref, slope_ref, wr_ref, nslope_ref, cols_ref, rows_ref, local_ref, decay_ref,
    ext_ref, next_ref, scaled_ref,
):
    first = lax.rem(pl.program_id(0), groups) == 0

    @pl.when(first)
    def _():
        ext_ref[5:8, :] = rim_ref[0].astype(F32)
        next_ref[5:8, :] = nrim_ref[0].astype(F32)

    @pl.when(jnp.logical_not(first))
    def _():
        ext_ref[0:8, :] = ext_ref[GROUP : GROUP + 8, :]
        next_ref[0:8, :] = next_ref[GROUP : GROUP + 8, :]

    def conv(source, taps, bias, lanes):
        total = bias[:, lanes]
        for k in range(CONV):
            total = total + taps[k : k + 1, lanes] * source[5 + k : 5 + k + GROUP, lanes]
        sig = jax.nn.sigmoid(total)
        return total * sig, sig * (1.0 + total * (1.0 - sig))

    for part in range(2 * STATE // 128):
        lanes = slice(128 * part, 128 * (part + 1))
        next_ref[8 : GROUP + 8, lanes] = narrow_ref[:, lanes].astype(BF16).astype(F32)
        act, slope = conv(next_ref, ntaps_ref, nbias_ref, lanes)
        wr_ref[:, lanes] = act.astype(BF16)
        nslope_ref[:, lanes] = slope

    raw = narrow_ref[:, 2 * STATE :] + sbias_ref[...]
    lane = lax.broadcasted_iota(jnp.int32, (GROUP, 128), 1)
    step = jnp.maximum(raw, 0.0) + jnp.log1p(jnp.exp(-jnp.abs(raw)))
    step = jnp.where(lane < heads, step, 0.0)
    sig = jnp.where(lane < heads, jax.nn.sigmoid(raw), 0.0)
    cum = split_dot(lower_mask().astype(BF16), step * rate_ref[...], 3, 1)
    cols = step + pltpu.roll(cum, heads, 1) + pltpu.roll(sig, 2 * heads, 1)
    cols_ref[...] = cols
    rows_ref[0] = cum.T[:heads]
    last = cum[GROUP - 1 : GROUP, :]
    scale = jnp.exp(last - cum) * step
    decay = jnp.exp(last)
    low_half, low_row = low_lanes(GROUP), low_lanes(1)
    for pair in range(heads // 2):
        lanes = slice(PAIR * pair, PAIR * (pair + 1))
        ext_ref[8 : GROUP + 8, lanes] = inner_ref[:, lanes].astype(F32)
        act, slope = conv(ext_ref, taps_ref, bias_ref, lanes)
        x = act.astype(BF16)
        x_ref[:, lanes] = x
        slope_ref[:, lanes] = slope.astype(BF16)
        scaled_ref[:, lanes] = (x.astype(F32) * spread_heads(scale, 2 * pair, low_half)).astype(BF16)
        decay_ref[0, :, lanes] = spread_heads(decay, 2 * pair, low_row)
    local_ref[0] = dot(wr_ref[:, :STATE], scaled_ref[...], 0, 0)


def start_blocks(inner_pre, rim, narrow, nrim, taps, bias, ntaps, nbias, sbias, rate, groups, heads):
    tokens, width = inner_pre.shape
    blocks = tokens // GROUP
    rows = lambda w: pl.BlockSpec((GROUP, w), lambda b: (b, 0))
    whole = lambda x: pl.BlockSpec(x.shape, lambda b: (0,) * x.ndim)
    return pl.pallas_call(
        functools.partial(start_kernel, groups, heads),
        grid=(blocks,),
        in_specs=[
            rows(width),
            pl.BlockSpec((1, CONV - 1, width), lambda b: (b // groups, 0, 0)),
            rows(narrow.shape[1]),
            pl.BlockSpec((1, CONV - 1, 2 * STATE), lambda b: (b // groups, 0, 0)),
            whole(taps), whole(bias), whole(ntaps), whole(nbias), whole(sbias), whole(rate),
        ],
        out_specs=[
            rows(width), rows(width), rows(2 * STATE), rows(2 * STATE), rows(128),
            pl.BlockSpec((1, heads, GROUP), lambda b: (b, 0, 0)),
            pl.BlockSpec((1, STATE, width), lambda b: (b, 0, 0)),
            pl.BlockSpec((1, 1, width), lambda b: (b, 0, 0)),
        ],
        out_shape=[
            jax.ShapeDtypeStruct((tokens, width), BF16),
            jax.ShapeDtypeStruct((tokens, width), BF16),
            jax.ShapeDtypeStruct((tokens, 2 * STATE), BF16),
            jax.ShapeDtypeStruct((tokens, 2 * STATE), F32),
            jax.ShapeDtypeStruct((tokens, 128), F32),
            jax.ShapeDtypeStruct((blocks, heads, GROUP), F32),
            jax.ShapeDtypeStruct((blocks, STATE, width), F32),
            jax.ShapeDtypeStruct((blocks, 1, width), F32),
        ],
        scratch_shapes=[
            pltpu.VMEM((GROUP + 8, width), F32),
            pltpu.VMEM((GROUP + 8, 2 * STATE), F32),
            pltpu.VMEM((GROUP, width), BF16),
        ],
        cost_estimate=pl.CostEstimate(
            flops=2 * tokens * STATE * width + 20 * tokens * width,
            bytes_accessed=tokens * width * 6 + blocks * STATE * width * 4,
            transcendentals=tokens * width,
        ),
        name="start_blocks",
    )(inner_pre, rim, narrow, nrim, taps, bias, ntaps, nbias, sbias, rate)


def mix_kernel(
    heads,
    x_ref, gate_ref, gno_ref, wr_ref, cols_ref, rows_ref, state_ref, skip_ref, gain_ref,
    mixed_ref, stats_ref, scores_ref, sums_ref,
):
    g = pl.program_id(1)

    @pl.when(g == 0)
    def _():
        scores_ref[...] = dot(wr_ref[:, STATE:], wr_ref[:, :STATE], 1, 1)
        sums_ref[...] = jnp.zeros_like(sums_ref)

    cols = turned(cols_ref[...], g * HEADS_STEP)
    grown = jnp.exp(cols)
    low_half = low_lanes(GROUP)
    lower = lower_mask()
    squares = jnp.zeros((GROUP, 1), F32)
    crosses = jnp.zeros((GROUP, 1), F32)
    for pair in range(HEADS_STEP // 2):
        lanes = slice(PAIR * pair, PAIR * (pair + 1))
        x = x_ref[:, lanes].astype(F32)
        stepped = x * spread_heads(cols, 2 * pair, low_half)
        halves = (
            jnp.where(low_half, stepped, 0.0).astype(BF16),
            jnp.where(low_half, 0.0, stepped).astype(BF16),
        )
        total = dot(wr_ref[:, STATE:], state_ref[0, :, lanes], 1, 0)
        total = total * spread_heads(grown, heads + 2 * pair, low_half)
        for side in range(2):
            head = 2 * pair + side
            row = rows_ref[0, pl.ds(g * HEADS_STEP + head, 1), :]
            spread = jnp.where(lower, cols[:, heads + head : heads + head + 1] - row, -1e30)
            weights = (scores_ref[...] * jnp.exp(spread)).astype(BF16)
            total = total + dot(weights, halves[side], 1, 0)
        mixed = total + skip_ref[:, lanes] * x
        mixed_ref[:, lanes] = mixed
        gate = gate_ref[:, lanes].astype(F32)
        gated = mixed * (gate * jax.nn.sigmoid(gate))
        squares = squares + jnp.sum(gated * gated, axis=1, keepdims=True)
        grad_hat = gno_ref[:, lanes].astype(F32) * gain_ref[:, lanes]
        crosses = crosses + jnp.sum(gated * grad_hat, axis=1, keepdims=True)
    lane = lax.broadcasted_iota(jnp.int32, (GROUP, 128), 1)
    sums_ref[...] += jnp.where(lane == 0, squares, jnp.where(lane == 1, crosses, 0.0))

    @pl.when(g == pl.num_programs(1) - 1)
    def _():
        stats_ref[0] = sums_ref[...].T[:8]


def mix_blocks(x, gate, gno, wr, cols, rows, states, skip, gain):
    tokens, width = x.shape
    blocks, steps, heads = tokens // GROUP, width // LANES_STEP, rows.shape[1]
    wide = pl.BlockSpec((GROUP, LANES_STEP), lambda b, g: (b, g))
    line = pl.BlockSpec((1, LANES_STEP), lambda b, g: (0, g))
    return pl.pallas_call(
        functools.partial(mix_kernel, heads),
        grid=(blocks, steps),
        in_specs=[
            wide, wide, wide,
            pl.BlockSpec((GROUP, 2 * STATE), lambda b, g: (b, 0)),
            pl.BlockSpec((GROUP, 128), lambda b, g: (b, 0)),
            pl.BlockSpec((1, heads, GROUP), lambda b, g: (b, 0, 0)),
            pl.BlockSpec((1, STATE, LANES_STEP), lambda b, g: (b, 0, g)),
            line, line,
        ],
        out_specs=[wide, pl.BlockSpec((1, 8, GROUP), lambda b, g: (b, 0, 0))],
        out_shape=[
            jax.ShapeDtypeStruct((tokens, width), F32),
            jax.ShapeDtypeStruct((blocks, 8, GROUP), F32),
        ],
        scratch_shapes=[pltpu.VMEM((GROUP, GROUP), F32), pltpu.VMEM((GROUP, 128), F32)],
        cost_estimate=pl.CostEstimate(
            flops=2 * tokens * width * (2 * GROUP + 2 * STATE) * 2,
            bytes_accessed=tokens * width * 10,
            transcendentals=tokens * GROUP * width // HEADDIM,
        ),
        name="mix_blocks",
    )(x, gate, gno, wr, cols, rows, states, skip, gain)


def gate_kernel(
    heads,
    mixed_ref, gate_ref, gno_ref, x_ref, stats_ref, gain_ref, wr_ref, cols_ref,
    normed_ref, ggate_ref, gdiag_ref, gain_sum_ref, skip_sum_ref, flow_ref, scaled_ref,
):
    @pl.when(pl.program_id(1) == 0)
    def _():
        gain_sum_ref[...] = jnp.zeros_like(gain_sum_ref)
        skip_sum_ref[...] = jnp.zeros_like(skip_sum_ref)

    stats = stats_ref[0].T
    scale = lax.rsqrt(stats[:, 0:1] / INNER + EPSILON)
    cross = scale * stats[:, 1:2] / INNER
    grown = jnp.exp(turned(cols_ref[...], pl.program_id(0) * HEADS_STEP))
    low_half = low_lanes(GROUP)
    for pair in range(HEADS_STEP // 2):
        lanes = slice(PAIR * pair, PAIR * (pair + 1))
        mixed = mixed_ref[:, lanes]
        gate = gate_ref[:, lanes].astype(F32)
        gno = gno_ref[:, lanes].astype(F32)
        gain = gain_ref[:, lanes]
        sig = jax.nn.sigmoid(gate)
        act = gate * sig
        hat = mixed * act * scale
        normed_ref[:, lanes] = (hat * gain).astype(BF16)
        gain_sum_ref[:, lanes] += jnp.sum(gno * hat, axis=0, keepdims=True)
        grad_gated = scale * (gno * gain - hat * cross)
        grad_mixed = grad_gated * act
        ggate_ref[:, lanes] = (grad_gated * mixed * sig * (1.0 + gate * (1.0 - sig))).astype(BF16)
        skip_sum_ref[:, lanes] += jnp.sum(grad_mixed * x_ref[:, lanes].astype(F32), axis=0, keepdims=True)
        diag = grad_mixed.astype(BF16)
        gdiag_ref[:, lanes] = diag
        scaled = diag.astype(F32) * spread_heads(grown, heads + 2 * pair, low_half)
        scaled_ref[:, lanes] = scaled.astype(BF16)
    flow_ref[0] = dot(wr_ref[...], scaled_ref[...], 0, 0)


def gate_blocks(mixed, gate, gno, x, stats, gain, wr, cols, heads):
    tokens, width = x.shape
    blocks, steps = tokens // GROUP, width // LANES_STEP
    wide = pl.BlockSpec((GROUP, LANES_STEP), lambda g, b: (b, g))
    line = pl.BlockSpec((1, LANES_STEP), lambda g, b: (0, g))
    return pl.pallas_call(
        functools.partial(gate_kernel, heads),
        grid=(steps, blocks),
        in_specs=[
            wide, wide, wide, wide,
            pl.BlockSpec((1, 8, GROUP), lambda g, b: (b, 0, 0)),
            line,
            pl.BlockSpec((GROUP, STATE), lambda g, b: (b, 1)),
            pl.BlockSpec((GROUP, 128), lambda g, b: (b, 0)),
        ],
        out_specs=[
            wide, wide, wide, line, line,
            pl.BlockSpec((1, STATE, LANES_STEP), lambda g, b: (b, 0, g)),
        ],
        out_shape=[
            jax.ShapeDtypeStruct((tokens, width), BF16),
            jax.ShapeDtypeStruct((tokens, width), BF16),
            jax.ShapeDtypeStruct((tokens, width), BF16),
            jax.ShapeDtypeStruct((1, width), F32),
            jax.ShapeDtypeStruct((1, width), F32),
            jax.ShapeDtypeStruct((blocks, STATE, width), F32),
        ],
        scratch_shapes=[pltpu.VMEM((GROUP, LANES_STEP), BF16)],
        cost_estimate=pl.CostEstimate(
            flops=2 * tokens * STATE * width,
            bytes_accessed=tokens * width * 16 + blocks * STATE * width * 4,
            transcendentals=tokens * width,
        ),
        name="gate_blocks",
    )(mixed, gate, gno, x, stats, gain, wr, cols)


def back_kernel(
    groups, heads,
    x_ref, mixed_ref, grad_ref, slope_ref, pre_ref, rim_ref, wr_ref, nslope_ref, npre_ref, nrim_ref,
    cols_ref, rows_ref, state_ref, flow_ref, skip_ref, taps_ref, ntaps_ref, rate_ref,
    gpre_ref, gnarrow_ref, sums_ref, nsums_ref, hsums_ref, halo_ref, nhalo_ref,
    scores_ref, gscores_ref, prod_ref, gw_ref, gr_ref, u_ref, v_ref, i_ref, e_ref, ext_ref, next_ref, head_ref,
):
    step_id, g = pl.program_id(0), pl.program_id(1)
    block = pl.num_programs(0) - 1 - step_id
    last_of_slot = lax.rem(block, groups) == groups - 1
    first_of_slot = lax.rem(block, groups) == 0

    @pl.when(g == 0)
    def _():
        scores_ref[...] = dot(wr_ref[:, STATE:], wr_ref[:, :STATE], 1, 1)
        for ref in (gscores_ref, gw_ref, gr_ref, u_ref, v_ref, i_ref, e_ref):
            ref[...] = jnp.zeros_like(ref)

    @pl.when(jnp.logical_and(g == 0, step_id == 0))
    def _():
        sums_ref[...] = jnp.zeros_like(sums_ref)
        nsums_ref[...] = jnp.zeros_like(nsums_ref)
        hsums_ref[...] = jnp.zeros_like(hsums_ref)

    @pl.when(last_of_slot)
    def _():
        ext_ref[g, GROUP : GROUP + 8, :] = jnp.zeros((8, LANES_STEP), F32)
        next_ref[GROUP : GROUP + 8, :] = jnp.zeros((8, 2 * STATE), F32)

    @pl.when(jnp.logical_not(last_of_slot))
    def _():
        ext_ref[g, GROUP : GROUP + 8, :] = ext_ref[g, 0:8, :]

        @pl.when(g == 0)
        def _():
            next_ref[GROUP : GROUP + 8, :] = next_ref[0:8, :]

    cols = turned(cols_ref[...], g * HEADS_STEP)
    grown = jnp.exp(cols)
    shrunk = jnp.exp(cols[GROUP - 1 : GROUP, :] - cols)
    low_half = low_lanes(GROUP)
    lower = lower_mask()
    grad_write = jnp.zeros((GROUP, STATE), F32)
    grad_read = jnp.zeros((GROUP, STATE), F32)
    for pair in range(HEADS_STEP // 2):
        lanes = slice(PAIR * pair, PAIR * (pair + 1))
        x = x_ref[:, lanes].astype(F32)
        grad = grad_ref[:, lanes]
        grad_f = grad.astype(F32)
        skip = skip_ref[:, lanes]
        steps = spread_heads(cols, 2 * pair, low_half)
        tail = spread_heads(shrunk, heads + 2 * pair, low_half)
        stepped = x * steps
        x_halves = (
            jnp.where(low_half, stepped, 0.0).astype(BF16),
            jnp.where(low_half, 0.0, stepped).astype(BF16),
        )
        g_halves = (
            jnp.where(low_half, grad_f, 0.0).astype(BF16),
            jnp.where(low_half, 0.0, grad_f).astype(BF16),
        )
        flow = flow_ref[0, :, lanes]
        state = state_ref[0, :, lanes]
        e_ref[0:1, lanes] = jnp.sum(flow.astype(F32) * state.astype(F32), axis=0, keepdims=True)
        scaled = (grad_f * spread_heads(grown, heads + 2 * pair, low_half)).astype(BF16)
        grad_read = grad_read + dot(scaled, state, 1, 1)
        grad_write = grad_write + dot((stepped * tail).astype(BF16), flow, 1, 1)
        stepped_low = stepped.astype(BF16).astype(F32)
        inter = dot(wr_ref[:, :STATE], flow, 1, 0) * tail
        total = jnp.zeros_like(inter)
        for side in range(2):
            head = 2 * pair + side
            row = rows_ref[0, pl.ds(g * HEADS_STEP + head, 1), :]
            decay = jnp.exp(jnp.where(lower, cols[:, heads + head : heads + head + 1] - row, -1e30))
            weights = (scores_ref[...] * decay).astype(BF16)
            total = total + dot(weights, g_halves[side], 0, 0)
            gscores_ref[...] += dot(grad, x_halves[side], 1, 1) * decay
        both = total + inter
        prod_ref[0, :, lanes] = x * both
        prod_ref[1, :, lanes] = grad_f * (mixed_ref[:, lanes] - skip * x) - stepped_low * total
        prod_ref[2, :, lanes] = stepped_low * inter
        grad_conv = (steps * both + skip * grad_f) * slope_ref[:, lanes].astype(F32)
        ext_ref[g, 0:GROUP, lanes] = grad_conv
        pre = pre_ref[:, lanes].astype(F32)
        total_pre = jnp.zeros_like(grad_conv)
        for j in range(CONV):
            moved = ext_ref[g, j : j + GROUP, lanes]
            total_pre = total_pre + taps_ref[CONV - 1 - j : CONV - j, lanes] * moved
            sums_ref[g, CONV - 1 - j : CONV - j, lanes] += jnp.sum(pre * moved, axis=0, keepdims=True)
        sums_ref[g, CONV : CONV + 1, lanes] += jnp.sum(grad_conv, axis=0, keepdims=True)
        gpre_ref[:, lanes] = total_pre.astype(BF16)

    @pl.when(first_of_slot)
    def _():
        head_ref[0:8, :LANES_STEP] = jnp.zeros((8, LANES_STEP), F32)
        head_ref[8:16, :LANES_STEP] = ext_ref[g, 0:8, :]
        halo = jnp.zeros((8, LANES_STEP), F32)
        for j in range(CONV):
            moved = head_ref[j : j + 8, :LANES_STEP]
            halo = halo + taps_ref[CONV - 1 - j : CONV - j, :] * moved
            sums_ref[g, CONV - 1 - j : CONV - j, :] += jnp.sum(
                rim_ref[0].astype(F32) * moved[5:8], axis=0, keepdims=True
            )
        halo_ref[0] = halo

    chosen_rows = lax.broadcasted_iota(jnp.int32, (LANES_STEP, 128), 0) // HEADDIM + g * HEADS_STEP
    chosen = (chosen_rows == lax.broadcasted_iota(jnp.int32, (LANES_STEP, 128), 1)).astype(BF16)

    def sums_of(values, terms):
        total, rest = None, values
        for _ in range(terms):
            part = rest.astype(BF16)
            rest = rest - part.astype(F32)
            piece = dot(part, chosen, 1, 0)
            total = piece if total is None else total + piece
        return total

    u_ref[...] += sums_of(prod_ref[0], 2)
    v_ref[...] += sums_of(prod_ref[1], 2)
    i_ref[...] += sums_of(prod_ref[2], 2)
    e_ref[8:16, 0:128] += sums_of(e_ref[0:8, :], 2)
    gw_ref[...] += grad_write
    gr_ref[...] += grad_read

    @pl.when(g == pl.num_programs(1) - 1)
    def _():
        low = gscores_ref[...].astype(BF16)
        gradient = (
            gw_ref[...] + dot(low, wr_ref[:, STATE:], 0, 0),
            gr_ref[...] + dot(low, wr_ref[:, :STATE], 1, 0),
        )
        for part in range(2):
            lanes = slice(STATE * part, STATE * (part + 1))
            grad_conv = gradient[part] * nslope_ref[:, lanes]
            next_ref[0:GROUP, lanes] = grad_conv
            pre = npre_ref[:, lanes].astype(BF16).astype(F32)
            total_pre = jnp.zeros_like(grad_conv)
            for j in range(CONV):
                moved = next_ref[j : j + GROUP, lanes]
                total_pre = total_pre + ntaps_ref[CONV - 1 - j : CONV - j, lanes] * moved
                nsums_ref[CONV - 1 - j : CONV - j, lanes] += jnp.sum(pre * moved, axis=0, keepdims=True)
            nsums_ref[CONV : CONV + 1, lanes] += jnp.sum(grad_conv, axis=0, keepdims=True)
            gnarrow_ref[:, lanes] = total_pre.astype(BF16)

        @pl.when(first_of_slot)
        def _():
            head_ref[0:8, : 2 * STATE] = jnp.zeros((8, 2 * STATE), F32)
            head_ref[8:16, : 2 * STATE] = next_ref[0:8, :]
            halo = jnp.zeros((8, 2 * STATE), F32)
            for j in range(CONV):
                moved = head_ref[j : j + 8, : 2 * STATE]
                halo = halo + ntaps_ref[CONV - 1 - j : CONV - j, :] * moved
                nsums_ref[CONV - 1 - j : CONV - j, :] += jnp.sum(
                    nrim_ref[0].astype(F32) * moved[5:8], axis=0, keepdims=True
                )
            nhalo_ref[0] = halo

        own = cols_ref[...]
        lane = lax.broadcasted_iota(jnp.int32, (GROUP, 128), 1)
        step = jnp.where(lane < heads, own, 0.0)
        cum = pltpu.roll(own, 128 - heads, 1)
        sig = jnp.where(lane < heads, pltpu.roll(own, 128 - 2 * heads, 1), 0.0)
        strict = lax.broadcasted_iota(jnp.int32, (GROUP, GROUP), 0) > lax.broadcasted_iota(
            jnp.int32, (GROUP, GROUP), 1
        )
        reverse_sum = (
            split_dot(lower.astype(BF16), v_ref[...], 2, 0)
            + split_dot(strict.astype(BF16), i_ref[...], 2, 1)
            + jnp.exp(cum[GROUP - 1 : GROUP, :]) * e_ref[8:9, 0:128]
        )
        grad_raw = (u_ref[...] + rate_ref[...] * reverse_sum) * sig
        gnarrow_ref[:, 2 * STATE :] = grad_raw.astype(BF16)
        hsums_ref[0:1, :] += jnp.sum(grad_raw, axis=0, keepdims=True)
        hsums_ref[1:2, :] += jnp.sum(reverse_sum * step, axis=0, keepdims=True) * rate_ref[...]


def back_blocks(
    x, mixed, grad, slope, pre, rim, wr, nslope, npre, nrim, cols, rows, states, flows, skip, taps, ntaps, rate, groups
):
    tokens, width = x.shape
    blocks, steps, heads, slots = tokens // GROUP, width // LANES_STEP, rows.shape[1], rim.shape[0]
    at = lambda b: blocks - 1 - b
    wide = pl.BlockSpec((GROUP, LANES_STEP), lambda b, g: (at(b), g))
    narrow = lambda w: pl.BlockSpec((GROUP, w), lambda b, g: (at(b), 0))
    state = pl.BlockSpec((1, STATE, LANES_STEP), lambda b, g: (at(b), 0, g))
    line = lambda n: pl.BlockSpec((n, LANES_STEP), lambda b, g: (0, g))
    whole = lambda shape: pl.BlockSpec(shape, lambda b, g: (0,) * len(shape))
    return pl.pallas_call(
        functools.partial(back_kernel, groups, heads),
        grid=(blocks, steps),
        in_specs=[
            wide, wide, wide, wide, wide,
            pl.BlockSpec((1, CONV - 1, LANES_STEP), lambda b, g: (at(b) // groups, 0, g)),
            narrow(2 * STATE), narrow(2 * STATE), narrow(npre.shape[1]),
            pl.BlockSpec((1, CONV - 1, 2 * STATE), lambda b, g: (at(b) // groups, 0, 0)),
            narrow(128),
            pl.BlockSpec((1, heads, GROUP), lambda b, g: (at(b), 0, 0)),
            state, state, line(1), line(CONV), whole((CONV, 2 * STATE)), whole((1, 128)),
        ],
        out_specs=[
            wide, narrow(2 * STATE + 128),
            whole((steps, 8, LANES_STEP)), whole((8, 2 * STATE)), whole((8, 128)),
            pl.BlockSpec((1, 8, LANES_STEP), lambda b, g: (at(b) // groups, 0, g)),
            pl.BlockSpec((1, 8, 2 * STATE), lambda b, g: (at(b) // groups, 0, 0)),
        ],
        out_shape=[
            jax.ShapeDtypeStruct((tokens, width), BF16),
            jax.ShapeDtypeStruct((tokens, 2 * STATE + 128), BF16),
            jax.ShapeDtypeStruct((steps, 8, LANES_STEP), F32),
            jax.ShapeDtypeStruct((8, 2 * STATE), F32),
            jax.ShapeDtypeStruct((8, 128), F32),
            jax.ShapeDtypeStruct((slots, 8, width), F32),
            jax.ShapeDtypeStruct((slots, 8, 2 * STATE), F32),
        ],
        scratch_shapes=[
            pltpu.VMEM((GROUP, GROUP), F32),
            pltpu.VMEM((GROUP, GROUP), F32),
            pltpu.VMEM((3, GROUP, LANES_STEP), F32),
            pltpu.VMEM((GROUP, STATE), F32),
            pltpu.VMEM((GROUP, STATE), F32),
            pltpu.VMEM((GROUP, 128), F32),
            pltpu.VMEM((GROUP, 128), F32),
            pltpu.VMEM((GROUP, 128), F32),
            pltpu.VMEM((16, LANES_STEP), F32),
            pltpu.VMEM((steps, GROUP + 8, LANES_STEP), F32),
            pltpu.VMEM((GROUP + 8, 2 * STATE), F32),
            pltpu.VMEM((16, max(LANES_STEP, 2 * STATE)), F32),
        ],
        cost_estimate=pl.CostEstimate(
            flops=2 * tokens * width * (4 * GROUP + 4 * STATE) * 2,
            bytes_accessed=tokens * width * 14,
            transcendentals=tokens * GROUP * width // HEADDIM,
        ),
        name="back_blocks",
    )(x, mixed, grad, slope, pre, rim, wr, nslope, npre, nrim, cols, rows, states, flows, skip, taps, ntaps, rate)


MESH = pl.DeviceIdType.MESH
FAR_PARTS = 4


def fetch_kernel(
    x_ref, inner_ref, late_ref, step_ref, wr_ref, small_ref,
    full_x, full_inner, late_far, full_step, full_wr, full_small,
    x_own, inner_own, step_own, wr_own, small_own, send_sem, recv_sem, local_sem,
):
    f, c, z = lax.axis_index("fsdp"), lax.axis_index("ctx"), lax.axis_index("tp")
    half = z // 2
    slots, seq, cols = full_x.shape[0], full_x.shape[1], x_ref.shape[2]
    depth = inner_ref.shape[0]
    partners = (
        {"fsdp": f ^ 1}, {"fsdp": f ^ 2}, {"fsdp": f ^ 3}, {"ctx": c ^ 1}, {"tp": z ^ 1}, {"tp": z ^ 2},
    )
    barrier = pltpu.get_barrier_semaphore()
    for partner in partners:
        pl.semaphore_signal(barrier, inc=1, device_id=partner, device_id_type=MESH)
    pl.semaphore_wait(barrier, len(partners))

    copies = []

    def send(src, dst, partner):
        at = len(copies)
        copy = pltpu.make_async_remote_copy(
            src_ref=src, dst_ref=dst, send_sem=send_sem.at[at], recv_sem=recv_sem.at[at],
            device_id=partners[partner], device_id_type=MESH,
        )
        copy.start()
        copies.append([copy, False])
        return at

    def arrived(at):
        copies[at][0].wait_recv()
        copies[at][1] = True

    def feature(which):
        return pl.ds(pl.multiple_of(which * cols, 128), cols)

    def shard(full, row_f, far):
        wide = full.shape[1] // 2
        start = pl.multiple_of((row_f * 2 + c) * depth, depth)
        return full.at[pl.ds(start, depth), pl.ds(far * wide, wide)]

    def shard_one(full, row_f, far):
        start = pl.multiple_of((row_f * 2 + c) * depth, depth)
        return full.at[pl.ds(start, depth), :]

    def spread(full, src, far, part=shard):
        dst = part(full, f, far)
        near = [send(src, dst, k) for k in range(3)]
        send(src, dst, 3)
        return near

    def relay(full, near, far, part=shard):
        for k in range(3):
            arrived(near[k])
            row = part(full, f ^ (k + 1), far)
            send(row, row, 3)

    mine = pl.ds(half * slots, slots)
    other = pl.ds((1 - half) * slots, slots)
    send(small_ref, full_small.at[z], 4)
    far_small = send(small_ref, full_small.at[z], 5)
    send(x_ref.at[mine], full_x.at[:, :, feature(z)], 4)
    far_inner = send(inner_ref, shard(full_inner, f, 1), 5)
    far_step = send(step_ref, shard(full_step, f, 1), 5)
    piece = seq // FAR_PARTS
    far_x = [
        send(x_ref.at[other, pl.ds(piece * i, piece)], full_x.at[:, pl.ds(piece * i, piece), feature(z)], 5)
        for i in range(FAR_PARTS)
    ]
    send(late_ref, late_far, 5)
    own_inner = spread(full_inner, inner_ref, 0)
    own_step = spread(full_step, step_ref, 0)
    own_wr = spread(full_wr, wr_ref, 0, shard_one)

    staged = (
        (x_ref.at[mine], x_own, full_x.at[:, :, feature(z)]),
        (inner_ref, inner_own, shard(full_inner, f, 0)),
        (step_ref, step_own, shard(full_step, f, 0)),
        (wr_ref, wr_own, shard_one(full_wr, f, 0)),
        (small_ref, small_own, full_small.at[z]),
    )
    loads = [pltpu.make_async_copy(src, buf, local_sem.at[0, i]) for i, (src, buf, _) in enumerate(staged)]
    stores = [pltpu.make_async_copy(buf, dst, local_sem.at[1, i]) for i, (_, buf, dst) in enumerate(staged)]
    for load in loads:
        load.start()
    for load, store in zip(loads, stores):
        load.wait()
        store.start()

    arrived(far_small)
    send(full_small.at[z ^ 2], full_small.at[z ^ 2], 4)
    arrived(far_inner)
    away_inner = spread(full_inner, shard(full_inner, f, 1), 1)
    arrived(far_step)
    away_step = spread(full_step, shard(full_step, f, 1), 1)

    def both(i):
        arrived(far_x[i])
        part = full_x.at[:, pl.ds(piece * i, piece), feature(z ^ 2)]
        send(part, part, 4)

    relay(full_inner, own_inner, 0)
    relay(full_step, own_step, 0)
    relay(full_wr, own_wr, 0, shard_one)
    both(0)
    relay(full_inner, away_inner, 1)
    relay(full_step, away_step, 1)
    both(1)
    both(2)
    both(3)
    for store in stores:
        store.wait()
    for copy, done in copies:
        if not done:
            copy.wait_recv()
        copy.wait_send()


def fetch(hidden, inner, late, step, wr, small):
    slot_count, seq, cols = hidden.shape
    slots, depth = slot_count // 2, inner.shape[0]
    total = 8 * depth
    count = 1 + 2 * FAR_PARTS + 3 + 5 * 7 + 3
    anywhere = pl.BlockSpec(memory_space=pl.ANY)
    full = lambda x: jax.ShapeDtypeStruct((total, 2 * x.shape[1]), BF16)
    return pl.pallas_call(
        fetch_kernel,
        in_specs=[anywhere] * 6,
        out_specs=[anywhere] * 6,
        out_shape=[
            jax.ShapeDtypeStruct((slots, seq, 4 * cols), BF16),
            full(inner), jax.ShapeDtypeStruct(late.shape, BF16), full(step),
            jax.ShapeDtypeStruct((total, wr.shape[1]), BF16),
            jax.ShapeDtypeStruct((4,) + small.shape, F32),
        ],
        scratch_shapes=[
            pltpu.VMEM((slots, seq, cols), BF16),
            pltpu.VMEM(inner.shape, BF16),
            pltpu.VMEM(step.shape, BF16),
            pltpu.VMEM(wr.shape, BF16),
            pltpu.VMEM(small.shape, F32),
            pltpu.SemaphoreType.DMA((count,)),
            pltpu.SemaphoreType.DMA((count,)),
            pltpu.SemaphoreType.DMA((2, 5)),
        ],
        compiler_params=pltpu.CompilerParams(collective_id=0, has_side_effects=True),
        name="fetch",
    )(hidden, inner, late, step, wr, small)


def finish_kernel(
    part_ref, grad_ref, small_ref, cross_ref,
    near_out, other_out, home_out, narrow_out, small_out, small_far, cross_out, cross_far,
    relay_buf, part_buf, sum_buf, core_buf, own_buf, plane_buf, got_buf, sent_buf, home_buf, wr_send, wr_got,
    small_got, cross_got, send_sem, recv_sem, load_sem,
):
    f, c, z = lax.axis_index("fsdp"), lax.axis_index("ctx"), lax.axis_index("tp")
    tokens, cols = near_out.shape
    depth, inner = home_out.shape
    partners = (
        {"fsdp": f ^ 1}, {"fsdp": f ^ 2}, {"fsdp": f ^ 3}, {"ctx": c ^ 1}, {"tp": z ^ 1}, {"tp": z ^ 2},
    )
    barrier = pltpu.get_barrier_semaphore()
    for partner in partners:
        pl.semaphore_signal(barrier, inc=1, device_id=partner, device_id_type=MESH)

    def feature(which):
        return pl.ds(pl.multiple_of(which * cols, 128), cols)

    def rows_of(row_f, core):
        return pl.ds(pl.multiple_of((row_f * 2 + core) * depth, depth), depth)

    piece = tokens // FAR_PARTS
    loads = [
        pltpu.make_async_copy(grad_ref.at[rows_of(f ^ k, c)], own_buf.at[k], load_sem.at[k]) for k in range(4)
    ] + [
        pltpu.make_async_copy(
            part_ref.at[pl.ds(piece * i, piece), feature(z ^ 2)], part_buf.at[i], load_sem.at[4 + i]
        )
        for i in range(FAR_PARTS)
    ]
    for load in loads:
        load.start()
    pl.semaphore_wait(barrier, len(partners))

    copies = []

    def send(src, dst, partner):
        at = len(copies)
        copy = pltpu.make_async_remote_copy(
            src_ref=src, dst_ref=dst, send_sem=send_sem.at[at], recv_sem=recv_sem.at[at],
            device_id=partners[partner], device_id_type=MESH,
        )
        copy.start()
        copies.append([copy, False])
        return at

    def arrived(at):
        copies[at][0].wait_recv()
        copies[at][1] = True

    core = [send(grad_ref.at[rows_of(f ^ k, c ^ 1)], core_buf.at[k], 3) for k in (1, 2, 3, 0)]
    core_of = {1: core[0], 2: core[1], 3: core[2], 0: core[3]}
    small = [send(small_ref, small_got.at[0], 3)]
    cross = [send(cross_ref, cross_got, 4)]
    relays = [
        send(part_ref.at[pl.ds(piece * i, piece), feature(z ^ 3)], relay_buf.at[i], 4) for i in range(FAR_PARTS)
    ]
    def passed_on(i):
        loads[4 + i].wait()
        arrived(relays[i])
        sum_buf[i] = (part_buf[i].astype(F32) + relay_buf[i].astype(F32)).astype(BF16)
        send(sum_buf.at[i], other_out.at[pl.ds(piece * i, piece)], 5)

    arrived(small[0])
    small_out[...] = small_ref[...] + small_got[0]
    small.append(send(small_out, small_got.at[1], 0))
    arrived(cross[0])
    cross_out[...] = cross_ref[...] + cross_got[...]
    cross.append(send(cross_out, cross_far, 5))
    for load in loads[:4]:
        load.wait()
    for k in (1, 2):
        arrived(core_of[k])
        sent_buf[k - 1] = (own_buf[k].astype(F32) + core_buf[k].astype(F32)).astype(BF16)
    arrived(small[1])
    copies[small[1]][0].wait_send()
    small_out[...] = small_out[...] + small_got[1]
    small.append(send(small_out, small_got.at[2], 1))
    plane = [send(sent_buf.at[0], plane_buf.at[0], 0)]
    arrived(core_of[3])
    sent_buf[2] = (own_buf[3].astype(F32) + core_buf[3].astype(F32)).astype(BF16)
    plane.append(send(sent_buf.at[1], plane_buf.at[1], 1))
    plane.append(send(sent_buf.at[2], plane_buf.at[2], 2))
    arrived(small[2])
    copies[small[2]][0].wait_send()
    small_out[...] = small_out[...] + small_got[2]
    small.append(send(small_out, small_got.at[3], 4))
    for i in range(FAR_PARTS):
        passed_on(i)
    arrived(core_of[0])
    arrived(small[3])
    copies[small[3]][0].wait_send()
    shared = small_out.shape[0] // 2
    small_out[shared:, :] = small_out[shared:, :] + small_got[3, shared:, :]
    small.append(send(small_out, small_far, 5))
    total = own_buf[0].astype(F32) + core_buf[0].astype(F32)
    for at in plane:
        arrived(at)
    for k in range(3):
        total = total + plane_buf[k].astype(F32)
    wr_send[...] = total[:, 2 * inner : 2 * inner + 2 * STATE]
    wr = send(wr_send, wr_got, 4)
    middle = tokens // 2
    send(part_ref.at[pl.ds(0, middle), feature(z ^ 1)], near_out.at[pl.ds(0, middle)], 4)
    home_out[...] = total[:, :inner]
    home_buf[:, :inner] = total[:, inner : 2 * inner].astype(BF16)
    narrow_out[:, 2 * STATE : 2 * STATE + 128] = total[:, 2 * inner + 2 * STATE :]
    home_buf[:, inner + 2 * STATE :] = total[:, 2 * inner + 2 * STATE :].astype(BF16)
    arrived(wr)
    both = wr_send[...] + wr_got[...]
    narrow_out[:, : 2 * STATE] = both
    home_buf[:, inner : inner + 2 * STATE] = both.astype(BF16)
    last = send(home_buf, got_buf, 5)
    send(part_ref.at[pl.ds(middle, middle), feature(z ^ 1)], near_out.at[pl.ds(middle, middle)], 4)
    arrived(last)
    home_out[...] += got_buf[:, :inner].astype(F32)
    narrow_out[:, : 2 * STATE] += got_buf[:, inner : inner + 2 * STATE].astype(F32)
    steps = got_buf[:, inner + 2 * STATE :].astype(F32)
    narrow_out[:, 2 * STATE + 128 :] = steps
    for copy, done in copies:
        if not done:
            copy.wait_recv()
    waited = {small[1], small[2], small[3]}
    for at, (copy, done) in enumerate(copies):
        if at not in waited:
            copy.wait_send()


def finish(part, grad, small, cross, depth):
    tokens, width = part.shape
    cols, total = width // 4, grad.shape[1]
    rest = 2 * STATE + 128
    inner = (total - rest) // 2
    anywhere = pl.BlockSpec(memory_space=pl.ANY)
    vmem = pl.BlockSpec(memory_space=pltpu.VMEM)
    count = 4 + 5 + 2 + FAR_PARTS * 2 + 2 + 3 + 2
    return pl.pallas_call(
        finish_kernel,
        in_specs=[anywhere, anywhere, vmem, vmem],
        out_specs=[anywhere, anywhere, vmem, vmem, vmem, vmem, vmem, vmem],
        out_shape=[
            jax.ShapeDtypeStruct((tokens, cols), BF16),
            jax.ShapeDtypeStruct((tokens, cols), BF16),
            jax.ShapeDtypeStruct((depth, inner), F32),
            jax.ShapeDtypeStruct((depth, rest + 128), F32),
            jax.ShapeDtypeStruct(small.shape, F32),
            jax.ShapeDtypeStruct(small.shape, F32),
            jax.ShapeDtypeStruct(cross.shape, F32),
            jax.ShapeDtypeStruct(cross.shape, F32),
        ],
        scratch_shapes=[
            pltpu.VMEM((FAR_PARTS, tokens // FAR_PARTS, cols), BF16),
            pltpu.VMEM((FAR_PARTS, tokens // FAR_PARTS, cols), BF16),
            pltpu.VMEM((FAR_PARTS, tokens // FAR_PARTS, cols), BF16),
            pltpu.VMEM((4, depth, total), BF16),
            pltpu.VMEM((4, depth, total), BF16),
            pltpu.VMEM((3, depth, total), BF16),
            pltpu.VMEM((depth, inner + rest), BF16),
            pltpu.VMEM((3, depth, total), BF16),
            pltpu.VMEM((depth, inner + rest), BF16),
            pltpu.VMEM((depth, 2 * STATE), F32),
            pltpu.VMEM((depth, 2 * STATE), F32),
            pltpu.VMEM((4,) + small.shape, F32),
            pltpu.VMEM(cross.shape, F32),
            pltpu.SemaphoreType.DMA((count,)),
            pltpu.SemaphoreType.DMA((count,)),
            pltpu.SemaphoreType.DMA((4 + FAR_PARTS,)),
        ],
        compiler_params=pltpu.CompilerParams(collective_id=1, has_side_effects=True),
        name="finish",
    )(part, grad, small, cross)


def after(x, other):
    return lax.optimization_barrier((x, other))[0]


def everywhere(x):
    for axis in ("ctx", "fsdp"):
        count, bit = lax.axis_size(axis), 1
        if count & (count - 1):
            x = lax.psum(x, axis)
            continue
        while bit < count:
            x = x + lax.ppermute(x, axis, [(i, i ^ bit) for i in range(count)])
            bit *= 2
    return x


def pack(parts):
    return jnp.concatenate([part.reshape(-1) for part in parts])


def unpack(vector, shapes):
    parts, at = [], 0
    for shape in shapes:
        size = 1
        for dim in shape:
            size *= dim
        parts.append(vector[at : at + size].reshape(shape))
        at += size
    return parts


def on_device(
    hidden_in,
    lengths,
    norm_gain,
    proj_gate_inner,
    proj_write_read,
    proj_step,
    conv_inner,
    conv_inner_bias,
    conv_write_read,
    conv_write_read_bias,
    step_bias,
    log_rate,
    skip_gain,
    gate_gain,
    proj_out,
    out_cotangent,
):
    slot_count, seq_here, width_here = hidden_in.shape
    slots = slot_count // 2
    tokens = slots * seq_here
    heads_own = step_bias.shape[0]
    inner_own = gate_gain.shape[0]
    heads = 2 * heads_own
    inner = 2 * inner_own
    tp_count = lax.axis_size("tp")
    width = tp_count * width_here
    groups = seq_here // GROUP
    blocks = slots * groups
    head_steps = heads // HEADS_STEP
    rim_rows = CONV - 1
    place = lax.axis_index("tp")
    far_half, near_side = place // 2, place % 2

    def half_of(whole, which):
        return lax.dynamic_slice_in_dim(whole, which * slots, slots, 0)

    def ordered(own, near, far, both, axis):
        first = lambda a, b: jnp.where(near_side == 0, a, b)
        a0, a1, b0, b1 = first(own, near), first(near, own), first(far, both), first(both, far)
        lower = lambda a, b: jnp.where(far_half == 0, a, b)
        return jnp.concatenate(
            [lower(a0, b0), lower(a1, b1), lower(b0, a0), lower(b1, a1)], axis=axis
        )

    ready = []

    def own_features(piece):
        first, second = piece(place ^ 3).astype(BF16), piece(place ^ 1).astype(BF16)
        relay = swap(first, 1)
        keep = swap(second, 1)
        summed = (piece(place ^ 2) + relay.astype(F32)).astype(BF16)
        ready.extend([first, second, summed])
        sent = swap(summed, 2)
        kept = (piece(place) + keep.astype(F32)).reshape(slots, seq_here, width_here)
        other = sent.astype(F32).reshape(slots, seq_here, width_here)
        return both_halves(kept, other)

    def both_halves(kept, other):
        return jnp.where(
            far_half == 0,
            jnp.concatenate([kept, other], axis=0),
            jnp.concatenate([other, kept], axis=0),
        )

    small_shapes = [(CONV, inner_own), (inner_own,), (inner_own,), (heads_own,), (heads_own,), (heads_own,)]
    def gathered(x):
        return lax.all_gather(x, ("fsdp", "ctx"), axis=0, tiled=True)

    own_small = pack([conv_inner, conv_inner_bias, gate_gain, step_bias, log_rate, skip_gain])
    cot_mine, cot_other = half_of(out_cotangent, far_half), half_of(out_cotangent, 1 - far_half)
    narrow_cols = 2 * STATE + heads
    narrow_pad = -narrow_cols % 128
    zeros = lambda x, extra: jnp.zeros((x.shape[0], extra), BF16)
    inner_shard, gate_shard = proj_gate_inner[:, 1], proj_gate_inner[:, 0]
    if lax.axis_size("fsdp") == 4 and lax.axis_size("ctx") == 2:
        step_shard = jnp.concatenate([proj_step, zeros(proj_step, 128 - heads_own)], axis=1)
        small = pack([norm_gain.astype(F32), own_small])
        small = jnp.pad(small, (0, -small.size % 1024)).reshape(-1, 128)
        late_shard = jnp.concatenate([gate_shard, proj_out], axis=1)
        full_x, full_inner, late_far, full_step, full_wr, full_small = fetch(
            hidden_in, inner_shard, late_shard, step_shard, proj_write_read, small
        )
        gate_far, out_far = late_far[:, :inner_own], late_far[:, inner_own:]
        full_small = full_small.reshape(tp_count, -1)
        full_gain = full_small[:, :width_here].reshape(width)
        far_row = lax.dynamic_slice_in_dim(full_small, place ^ 2, 1, 0)[0, width_here:]
        far_small = unpack(far_row, small_shapes)
        full_narrow = jnp.concatenate(
            [full_wr, full_step[:, :heads_own], full_step[:, 128 : 128 + heads_own], zeros(full_wr, narrow_pad)],
            axis=1,
        )
        cot_dep = full_x
    else:
        x_mine, x_other = half_of(hidden_in, far_half), half_of(hidden_in, 1 - far_half)
        narrow_shard = jnp.concatenate(
            [proj_write_read, proj_step, swap(proj_step, 2), zeros(proj_step, narrow_pad)], axis=1
        )
        inner_far = swap(inner_shard, 2)
        x_near = swap(x_mine, 1)
        x_far = swap(after(x_other, inner_far), 2)
        gate_far = swap(after(gate_shard, x_far), 2)
        x_both = swap(x_far, 1)
        cot_dep = after(x_both, gate_far)
        out_far = swap(after(proj_out, cot_dep), 2)
        full_narrow = gathered(narrow_shard)
        full_inner = gathered(jnp.concatenate([inner_shard, inner_far], axis=1))
        full_x = ordered(x_mine, x_near, x_far, x_both, 2)
        gain = norm_gain.astype(F32)
        full_gain = ordered(gain, swap(gain, 1), swap(gain, 2), swap(gain, 3), 0)
        far_small = unpack(swap(own_small, 2), small_shapes)
    full_x = full_x.reshape(tokens, width)
    full_late = gathered(jnp.concatenate([gate_shard, gate_far, proj_out, out_far], axis=1))
    full_gate, full_out = full_late[:, :inner], full_late[:, inner:]
    cot_mine, cot_other, cot_dep = lax.optimization_barrier((cot_mine, cot_other, cot_dep))
    cot_near, cot_far, cot_both = swap(cot_mine, 1), swap(cot_other, 2), swap(cot_other, 3)
    full_cot = ordered(cot_mine, cot_near, cot_far, cot_both, 2).reshape(tokens, width)

    taps = jnp.concatenate([conv_inner, far_small[0]], axis=1)
    taps_bias = jnp.concatenate([conv_inner_bias, far_small[1]])
    gain_gate = jnp.concatenate([gate_gain, far_small[2]])
    bias_step = jnp.concatenate([step_bias, far_small[3]])
    rate_log = jnp.concatenate([log_rate, far_small[4]])
    gain_skip = jnp.concatenate([skip_gain, far_small[5]])
    rate = -jnp.exp(rate_log)
    skip_lanes = jnp.repeat(gain_skip, HEADDIM)[None]

    in_float = full_x.astype(F32)
    in_scale = lax.rsqrt(jnp.mean(in_float * in_float, axis=-1, keepdims=True) + EPSILON)
    normed = (in_float * in_scale * full_gain.astype(F32)).astype(BF16)
    narrow_pre = dot(normed, full_narrow, 1, 0)
    inner_pre = dot(normed, full_inner, 1, 0).astype(BF16)
    gate_pre = dot(normed, full_gate, 1, 0).astype(BF16)

    def rim_of(pre):
        by_slot = pre.reshape(slots, seq_here, pre.shape[-1])
        return passed_along(by_slot[:, seq_here - rim_rows :].astype(BF16), "ctx", 1)

    inner_rim, narrow_rim = rim_of(inner_pre), rim_of(narrow_pre[:, : 2 * STATE])
    lane_pad = lambda x: jnp.pad(x, (0, 128 - heads))[None]
    rate_row = lane_pad(rate)
    inner_act, slope, write_read, narrow_slope, cols, cum_rows, local_state, decay_lanes = start_blocks(
        inner_pre, inner_rim, narrow_pre, narrow_rim, taps, taps_bias[None], conv_write_read,
        conv_write_read_bias[None], lane_pad(bias_step), rate_row, groups, heads,
    )
    local_state = local_state.reshape(slots, groups, STATE, inner)
    decay_lanes = decay_lanes.reshape(slots, groups, 1, inner)
    carried = local_state[:, 0]
    device_decay = decay_lanes[:, 0]
    for position in range(1, groups):
        carried = decay_lanes[:, position] * carried + local_state[:, position]
        device_decay = device_decay * decay_lanes[:, position]
    current = carried_in(device_decay, carried, None, False)
    state_list = []
    for position in range(groups):
        state_list.append(current)
        current = decay_lanes[:, position] * current + local_state[:, position]
    states = jnp.stack(state_list, axis=1)
    states_low = states.astype(BF16).reshape(blocks, STATE, inner)

    position_ids = lax.axis_index("ctx") * seq_here + jnp.arange(seq_here)
    valid_rows = (position_ids[None, :] < lengths[:, None]).astype(F32)
    valid_here = half_of(valid_rows, far_half).reshape(tokens, 1)
    masked = (full_cot.astype(F32) * valid_here).astype(BF16)
    grad_normed_out = dot(masked, full_out, 1, 0).astype(BF16)
    mixed_out, stats = mix_blocks(
        inner_act, gate_pre, grad_normed_out, write_read, cols, cum_rows, states_low, skip_lanes, gain_gate[None],
    )
    stats = stats + swap(stats, 1)
    normed_out, grad_gate_pre, grad_diag, grad_gate_gain, grad_skip_lanes, local_grad = gate_blocks(
        mixed_out, gate_pre, grad_normed_out, inner_act, stats, gain_gate[None], write_read, cols, heads
    )
    local_grad = local_grad.reshape(slots, groups, STATE, inner)

    def branch_piece(which):
        rows = lax.dynamic_slice_in_dim(full_out, which * width_here, width_here, 0)
        return dot(normed_out, rows, 1, 1)

    branch = own_features(branch_piece)
    hidden_out = (hidden_in.astype(F32) + valid_rows[..., None] * branch).astype(BF16)
    normed_out, grad_gate_pre, *_ = lax.optimization_barrier((normed_out, grad_gate_pre, ready[0], ready[1]))
    grad_proj_out = dot(masked, normed_out, 0, 0).astype(BF16)
    grad_gate_w = dot(normed, grad_gate_pre, 0, 0).astype(BF16)
    grad_by_gate = dot(grad_gate_pre, full_gate, 1, 1)
    other_scale = swap(in_scale.reshape(-1, 128), 2)

    flowing = local_grad[:, groups - 1]
    for position in reversed(range(groups - 1)):
        flowing = decay_lanes[:, position] * flowing + local_grad[:, position]
    flowing = carried_in(device_decay, flowing, None, True)
    flow_list = []
    for position in reversed(range(groups)):
        flow_list.insert(0, flowing)
        flowing = decay_lanes[:, position] * flowing + local_grad[:, position]
    flows = jnp.stack(flow_list, axis=1)
    flows_low = flows.astype(BF16).reshape(blocks, STATE, inner)
    flows_low = after(flows_low, (grad_proj_out, grad_gate_w, ready[2]))

    grad_inner_pre, grad_narrow, tap_sums, narrow_sums, head_sums, halo, narrow_halo = back_blocks(
        inner_act, mixed_out, grad_diag, slope, inner_pre, inner_rim, write_read, narrow_slope, narrow_pre,
        narrow_rim, cols, cum_rows, states_low, flows_low, skip_lanes, taps, conv_write_read, rate_row, groups,
    )
    tap_sums = tap_sums.transpose(1, 0, 2).reshape(8, inner)
    grad_taps, grad_taps_bias = tap_sums[:CONV], tap_sums[CONV]
    grad_conv_write_read, grad_conv_write_read_bias = narrow_sums[:CONV], narrow_sums[CONV]
    grad_step_bias, grad_log_rate = head_sums[0, :heads], head_sums[1, :heads]

    def completed(grad, halo):
        back = passed_along(halo, "ctx", -1)
        for slot in range(slots):
            ends = (slot + 1) * seq_here
            rows = grad[ends - 8 : ends, : halo.shape[-1]].astype(F32) + back[slot]
            grad = lax.dynamic_update_slice(grad, rows.astype(BF16), (ends - 8, 0))
        return grad

    grad_inner_pre, grad_narrow = completed(grad_inner_pre, halo), completed(grad_narrow, narrow_halo)
    def reduced(x):
        return lax.psum_scatter(x, ("fsdp", "ctx"), scatter_dimension=0, tiled=True)

    early = reduced(jnp.concatenate([grad_proj_out, grad_gate_w], axis=1))
    grad_inner_pre, hidden_out, early = lax.optimization_barrier((grad_inner_pre, hidden_out, early))
    early_far = swap(jnp.concatenate([early[:, inner_own:inner], early[:, inner + inner_own :]], axis=1), 2)
    grad_out_home = early[:, :inner_own].astype(F32) + early_far[:, :inner_own].astype(F32)
    grad_gate_home = early[:, inner : inner + inner_own].astype(F32) + early_far[:, inner_own:].astype(F32)

    late = jnp.concatenate([grad_inner_pre, grad_narrow], axis=1)
    grad_late_w = dot(normed, late, 0, 0).astype(BF16)
    partial_normed = (
        grad_by_gate + dot(grad_inner_pre, full_inner, 1, 1) + dot(grad_narrow, full_narrow, 1, 1)
    )
    by_hat = partial_normed * (full_x.astype(F32) * in_scale)
    grad_gain_full = jnp.sum(by_hat, axis=0)
    cross_part = jnp.sum(by_hat * full_gain.astype(F32), axis=1)
    partial_low = partial_normed.astype(BF16)

    grad_skip_gain = jnp.sum(grad_skip_lanes.reshape(heads, HEADDIM), axis=1)
    shared_shapes = [(CONV, 2 * STATE), (2 * STATE,), (width,)]
    head_shapes = [(CONV, inner), (inner,), (inner,), (heads,), (heads,), (heads,)]
    by_head = pack([grad_taps, grad_taps_bias, grad_gate_gain, grad_step_bias, grad_log_rate, grad_skip_gain])
    by_all = pack([grad_conv_write_read, grad_conv_write_read_bias, grad_gain_full])

    if lax.axis_size("fsdp") == 4 and lax.axis_size("ctx") == 2:
        lines = -(-max(by_head.size, by_all.size) // 1024) * 8
        filled = lambda v: jnp.pad(v, (0, lines * 128 - v.size)).reshape(lines, 128)
        near, other, grad_inner_home, narrow_sum, small_own, small_far, cross_rows, cross_far = finish(
            partial_low,
            after(grad_late_w, early_far),
            jnp.concatenate([filled(by_head), filled(by_all)]),
            cross_part.reshape(-1, 128),
            proj_write_read.shape[0],
        )
        kept = lax.dynamic_slice_in_dim(partial_normed, place * width_here, width_here, 1) + near.astype(F32)
        grad_normed = both_halves(
            kept.reshape(slots, seq_here, width_here), other.astype(F32).reshape(slots, seq_here, width_here)
        )
        write_read_home = narrow_sum[:, : 2 * STATE]
        step_home = (
            narrow_sum[:, 2 * STATE : 2 * STATE + heads_own]
            + narrow_sum[:, 2 * STATE + 128 + heads_own : 2 * STATE + 128 + heads]
        )
        cross_rows, cross_far = cross_rows.reshape(-1), cross_far.reshape(-1)
        parts = unpack(small_own[:lines].reshape(-1), head_shapes)
        far_parts = unpack(small_far[:lines].reshape(-1), head_shapes)
        far_parts = [lax.slice_in_dim(p, p.shape[-1] // 2, p.shape[-1], axis=p.ndim - 1) for p in far_parts]
        shared = (small_own[lines:] + small_far[lines:]).reshape(-1)
    else:

        def normed_piece(which):
            return lax.dynamic_slice_in_dim(partial_normed, which * width_here, width_here, 1)

        grad_normed = own_features(normed_piece)
        late_sum = reduced(grad_late_w)
        late_far = swap(late_sum, 2).astype(F32)
        late_sum = late_sum.astype(F32)
        grad_inner_home = late_sum[:, :inner_own] + late_far[:, inner_own:inner]
        write_read_home = late_sum[:, inner : inner + 2 * STATE] + late_far[:, inner : inner + 2 * STATE]
        write_read_home = write_read_home + swap(write_read_home, 1)
        steps_at = inner + 2 * STATE
        step_home = late_sum[:, steps_at : steps_at + heads_own] + late_far[:, steps_at + heads_own : steps_at + heads]
        cross_rows = cross_part + swap(cross_part, 1)
        cross_far = swap(cross_rows, 2)
        smalls = everywhere(pack([by_head, by_all]))
        parts = unpack(smalls[: by_head.size], head_shapes)
        away = [lax.slice_in_dim(p, p.shape[-1] // 2, p.shape[-1], axis=p.ndim - 1) for p in parts]
        far_parts = unpack(swap(pack(away), 2), small_shapes)
        shared = smalls[by_head.size :]
        shared = shared + swap(shared, 1)
        shared = shared + swap(shared, 2)

    homes = [
        lax.slice_in_dim(p, 0, p.shape[-1] // 2, axis=p.ndim - 1) + a for p, a in zip(parts, far_parts)
    ]
    wr_taps, wr_bias, gain_all = unpack(shared, shared_shapes)
    grad_norm_gain = lax.dynamic_slice_in_dim(gain_all, place * width_here, width_here, 0)

    own_gain = norm_gain.astype(F32)
    own_scale = both_halves(
        in_scale.reshape(slots, seq_here, 1), other_scale.reshape(slots, seq_here, 1)
    )
    own_hat = hidden_in.astype(F32) * own_scale
    grad_hat_in = grad_normed * own_gain
    cross_in = both_halves(
        cross_rows.reshape(slots, seq_here, 1), cross_far.reshape(slots, seq_here, 1)
    ) / width
    grad_hidden_in = own_scale * (grad_hat_in - own_hat * cross_in) + out_cotangent.astype(F32)
    return (
        hidden_out,
        grad_hidden_in,
        grad_norm_gain,
        jnp.stack([grad_gate_home, grad_inner_home], axis=1),
        write_read_home,
        step_home,
        homes[0],
        homes[1],
        wr_taps,
        wr_bias,
        homes[3],
        homes[4],
        homes[5],
        homes[2],
        grad_out_home,
    )


def solution(mesh):
    rows = ("fsdp", "ctx")
    acts = P("fsdp", "ctx", "tp")
    placed = (
        acts,
        P("fsdp"),
        P("tp"),
        P(rows, None, "tp"),
        P(rows, None),
        P(rows, "tp"),
        P(None, "tp"),
        P("tp"),
        P(),
        P(),
        P("tp"),
        P("tp"),
        P("tp"),
        P("tp"),
        P(rows, "tp"),
        acts,
    )
    return jax.shard_map(
        on_device,
        mesh=mesh,
        in_specs=placed,
        out_specs=(
            acts,
            acts,
            P("tp"),
            P(rows, None, "tp"),
            P(rows, None),
            P(rows, "tp"),
            P(None, "tp"),
            P("tp"),
            P(),
            P(),
            P("tp"),
            P("tp"),
            P("tp"),
            P("tp"),
            P(rows, "tp"),
        ),
        check_vma=False,
    )
```

```python
import functools

import jax
import jax.numpy as jnp
from jax import lax
from jax.experimental import pallas as pl
from jax.experimental.pallas import tpu as pltpu
from jax.sharding import PartitionSpec as P

HEADDIM = 64
STATE = 128
CONV = 4
GROUP = 256
INNER = 3072
EPSILON = 1e-05
PAIR = 2 * HEADDIM
HEADS_STEP = 6
LANES_STEP = HEADS_STEP * HEADDIM
GATE_HEADS = 12
GATE_LANES = GATE_HEADS * HEADDIM
F32 = jnp.float32
BF16 = jnp.bfloat16
HIGHEST = lax.Precision.HIGHEST


def swap(x, bit):
    count = lax.axis_size("tp")
    return lax.ppermute(x, "tp", [(i, i ^ bit) for i in range(count)])


def passed_along(x, axis, by):
    count = lax.axis_size(axis)
    pairs = [(i, i + by) for i in range(count) if 0 <= i + by < count]
    return lax.ppermute(x, axis, pairs)


def carried_in(decay, final, combine, reverse):
    count, position = (lax.axis_size("ctx"), lax.axis_index("ctx"))
    if count == 2:
        return passed_along(final.astype(BF16), "ctx", -1 if reverse else 1).astype(F32)
    decays = lax.all_gather(decay.astype(BF16), "ctx").astype(F32)
    finals = lax.all_gather(final.astype(BF16), "ctx")
    start = jnp.zeros_like(final)

    def lap(k, before):
        at = count - 1 - k if reverse else k
        reached = at > position if reverse else at < position
        new = decays[at] * before + finals[at].astype(F32)
        return jnp.where(reached, new, before)

    return lax.fori_loop(0, count, lap, start)


def dot(a, b, da, db):
    return lax.dot_general(a, b, (((da,), (db,)), ((), ())), preferred_element_type=F32)


def low_lanes(rows):
    return lax.broadcasted_iota(jnp.int32, (rows, PAIR), 1) < HEADDIM


def spread_heads(cols, first, low_half):
    return jnp.where(low_half, cols[:, first : first + 1], cols[:, first + 1 : first + 2])


def lower_mask():
    return lax.broadcasted_iota(jnp.int32, (GROUP, GROUP), 0) >= lax.broadcasted_iota(
        jnp.int32, (GROUP, GROUP), 1
    )


def split_dot(ones, values, terms, contract):
    total, rest = None, values
    for _ in range(terms):
        part = rest.astype(BF16)
        rest = rest - part.astype(F32)
        piece = dot(ones, part, contract, 0)
        total = piece if total is None else total + piece
    return total


def turned(cols, heads_before):
    return pltpu.roll(cols, lax.rem(128 - heads_before, 128), 1)


def start_kernel(
    groups, heads,
    inner_ref, rim_ref, narrow_ref, nrim_ref, taps_ref, bias_ref, ntaps_ref, nbias_ref, sbias_ref, rate_ref,
    x_ref, slope_ref, wr_ref, nslope_ref, cols_ref, rows_ref, local_ref, decay_ref,
    ext_ref, next_ref, scaled_ref,
):
    first = lax.rem(pl.program_id(0), groups) == 0

    @pl.when(first)
    def _():
        ext_ref[5:8, :] = rim_ref[0].astype(F32)
        next_ref[5:8, :] = nrim_ref[0].astype(F32)

    @pl.when(jnp.logical_not(first))
    def _():
        ext_ref[0:8, :] = ext_ref[GROUP : GROUP + 8, :]
        next_ref[0:8, :] = next_ref[GROUP : GROUP + 8, :]

    def conv(source, taps, bias, lanes):
        total = bias[:, lanes]
        for k in range(CONV):
            total = total + taps[k : k + 1, lanes] * source[5 + k : 5 + k + GROUP, lanes]
        sig = jax.nn.sigmoid(total)
        return total * sig, sig * (1.0 + total * (1.0 - sig))

    for part in range(2 * STATE // 128):
        lanes = slice(128 * part, 128 * (part + 1))
        next_ref[8 : GROUP + 8, lanes] = narrow_ref[:, lanes].astype(BF16).astype(F32)
        act, slope = conv(next_ref, ntaps_ref, nbias_ref, lanes)
        wr_ref[:, lanes] = act.astype(BF16)
        nslope_ref[:, lanes] = slope

    raw = narrow_ref[:, 2 * STATE :] + sbias_ref[...]
    lane = lax.broadcasted_iota(jnp.int32, (GROUP, 128), 1)
    step = jnp.maximum(raw, 0.0) + jnp.log1p(jnp.exp(-jnp.abs(raw)))
    step = jnp.where(lane < heads, step, 0.0)
    sig = jnp.where(lane < heads, jax.nn.sigmoid(raw), 0.0)
    cum = split_dot(lower_mask().astype(BF16), step * rate_ref[...], 3, 1)
    cols = step + pltpu.roll(cum, heads, 1) + pltpu.roll(sig, 2 * heads, 1)
    cols_ref[...] = cols
    rows_ref[0] = cum.T[:heads]
    last = cum[GROUP - 1 : GROUP, :]
    scale = jnp.exp(last - cum) * step
    decay = jnp.exp(last)
    low_half, low_row = low_lanes(GROUP), low_lanes(1)
    for pair in range(heads // 2):
        lanes = slice(PAIR * pair, PAIR * (pair + 1))
        ext_ref[8 : GROUP + 8, lanes] = inner_ref[:, lanes].astype(F32)
        act, slope = conv(ext_ref, taps_ref, bias_ref, lanes)
        x = act.astype(BF16)
        x_ref[:, lanes] = x
        slope_ref[:, lanes] = slope.astype(BF16)
        scaled_ref[:, lanes] = (x.astype(F32) * spread_heads(scale, 2 * pair, low_half)).astype(BF16)
        decay_ref[0, :, lanes] = spread_heads(decay, 2 * pair, low_row)
    local_ref[0] = dot(wr_ref[:, :STATE], scaled_ref[...], 0, 0)


def start_blocks(inner_pre, rim, narrow, nrim, taps, bias, ntaps, nbias, sbias, rate, groups, heads):
    tokens, width = inner_pre.shape
    blocks = tokens // GROUP
    rows = lambda w: pl.BlockSpec((GROUP, w), lambda b: (b, 0))
    whole = lambda x: pl.BlockSpec(x.shape, lambda b: (0,) * x.ndim)
    return pl.pallas_call(
        functools.partial(start_kernel, groups, heads),
        grid=(blocks,),
        in_specs=[
            rows(width),
            pl.BlockSpec((1, CONV - 1, width), lambda b: (b // groups, 0, 0)),
            rows(narrow.shape[1]),
            pl.BlockSpec((1, CONV - 1, 2 * STATE), lambda b: (b // groups, 0, 0)),
            whole(taps), whole(bias), whole(ntaps), whole(nbias), whole(sbias), whole(rate),
        ],
        out_specs=[
            rows(width), rows(width), rows(2 * STATE), rows(2 * STATE), rows(128),
            pl.BlockSpec((1, heads, GROUP), lambda b: (b, 0, 0)),
            pl.BlockSpec((1, STATE, width), lambda b: (b, 0, 0)),
            pl.BlockSpec((1, 1, width), lambda b: (b, 0, 0)),
        ],
        out_shape=[
            jax.ShapeDtypeStruct((tokens, width), BF16),
            jax.ShapeDtypeStruct((tokens, width), BF16),
            jax.ShapeDtypeStruct((tokens, 2 * STATE), BF16),
            jax.ShapeDtypeStruct((tokens, 2 * STATE), F32),
            jax.ShapeDtypeStruct((tokens, 128), F32),
            jax.ShapeDtypeStruct((blocks, heads, GROUP), F32),
            jax.ShapeDtypeStruct((blocks, STATE, width), F32),
            jax.ShapeDtypeStruct((blocks, 1, width), F32),
        ],
        scratch_shapes=[
            pltpu.VMEM((GROUP + 8, width), F32),
            pltpu.VMEM((GROUP + 8, 2 * STATE), F32),
            pltpu.VMEM((GROUP, width), BF16),
        ],
        cost_estimate=pl.CostEstimate(
            flops=2 * tokens * STATE * width + 20 * tokens * width,
            bytes_accessed=tokens * width * 6 + blocks * STATE * width * 4,
            transcendentals=tokens * width,
        ),
        name="start_blocks",
    )(inner_pre, rim, narrow, nrim, taps, bias, ntaps, nbias, sbias, rate)


def mix_kernel(
    heads,
    x_ref, gate_ref, gno_ref, wr_ref, cols_ref, rows_ref, state_ref, skip_ref, gain_ref,
    mixed_ref, stats_ref, scores_ref, sums_ref,
):
    g = pl.program_id(1)

    @pl.when(g == 0)
    def _():
        scores_ref[...] = dot(wr_ref[:, STATE:], wr_ref[:, :STATE], 1, 1)
        sums_ref[...] = jnp.zeros_like(sums_ref)

    cols = turned(cols_ref[...], g * HEADS_STEP)
    grown = jnp.exp(cols)
    low_half = low_lanes(GROUP)
    lower = lower_mask()
    squares = jnp.zeros((GROUP, 1), F32)
    crosses = jnp.zeros((GROUP, 1), F32)
    for pair in range(HEADS_STEP // 2):
        lanes = slice(PAIR * pair, PAIR * (pair + 1))
        x = x_ref[:, lanes].astype(F32)
        stepped = x * spread_heads(cols, 2 * pair, low_half)
        halves = (
            jnp.where(low_half, stepped, 0.0).astype(BF16),
            jnp.where(low_half, 0.0, stepped).astype(BF16),
        )
        total = dot(wr_ref[:, STATE:], state_ref[0, :, lanes], 1, 0)
        total = total * spread_heads(grown, heads + 2 * pair, low_half)
        for side in range(2):
            head = 2 * pair + side
            row = rows_ref[0, pl.ds(g * HEADS_STEP + head, 1), :]
            spread = jnp.where(lower, cols[:, heads + head : heads + head + 1] - row, -1e30)
            weights = (scores_ref[...] * jnp.exp(spread)).astype(BF16)
            total = total + dot(weights, halves[side], 1, 0)
        mixed = total + skip_ref[:, lanes] * x
        mixed_ref[:, lanes] = mixed
        gate = gate_ref[:, lanes].astype(F32)
        gated = mixed * (gate * jax.nn.sigmoid(gate))
        squares = squares + jnp.sum(gated * gated, axis=1, keepdims=True)
        grad_hat = gno_ref[:, lanes].astype(F32) * gain_ref[:, lanes]
        crosses = crosses + jnp.sum(gated * grad_hat, axis=1, keepdims=True)
    lane = lax.broadcasted_iota(jnp.int32, (GROUP, 128), 1)
    sums_ref[...] += jnp.where(lane == 0, squares, jnp.where(lane == 1, crosses, 0.0))

    @pl.when(g == pl.num_programs(1) - 1)
    def _():
        stats_ref[0] = sums_ref[...].T[:8]


def mix_blocks(x, gate, gno, wr, cols, rows, states, skip, gain):
    tokens, width = x.shape
    blocks, steps, heads = tokens // GROUP, width // LANES_STEP, rows.shape[1]
    wide = pl.BlockSpec((GROUP, LANES_STEP), lambda b, g: (b, g))
    line = pl.BlockSpec((1, LANES_STEP), lambda b, g: (0, g))
    return pl.pallas_call(
        functools.partial(mix_kernel, heads),
        grid=(blocks, steps),
        in_specs=[
            wide, wide, wide,
            pl.BlockSpec((GROUP, 2 * STATE), lambda b, g: (b, 0)),
            pl.BlockSpec((GROUP, 128), lambda b, g: (b, 0)),
            pl.BlockSpec((1, heads, GROUP), lambda b, g: (b, 0, 0)),
            pl.BlockSpec((1, STATE, LANES_STEP), lambda b, g: (b, 0, g)),
            line, line,
        ],
        out_specs=[wide, pl.BlockSpec((1, 8, GROUP), lambda b, g: (b, 0, 0))],
        out_shape=[
            jax.ShapeDtypeStruct((tokens, width), F32),
            jax.ShapeDtypeStruct((blocks, 8, GROUP), F32),
        ],
        scratch_shapes=[pltpu.VMEM((GROUP, GROUP), F32), pltpu.VMEM((GROUP, 128), F32)],
        cost_estimate=pl.CostEstimate(
            flops=2 * tokens * width * (2 * GROUP + 2 * STATE) * 2,
            bytes_accessed=tokens * width * 10,
            transcendentals=tokens * GROUP * width // HEADDIM,
        ),
        name="mix_blocks",
    )(x, gate, gno, wr, cols, rows, states, skip, gain)


def gate_kernel(
    heads,
    mixed_ref, gate_ref, gno_ref, x_ref, stats_ref, gain_ref, wr_ref, cols_ref,
    normed_ref, ggate_ref, gdiag_ref, gain_sum_ref, skip_sum_ref, flow_ref, scaled_ref,
):
    @pl.when(pl.program_id(1) == 0)
    def _():
        gain_sum_ref[...] = jnp.zeros_like(gain_sum_ref)
        skip_sum_ref[...] = jnp.zeros_like(skip_sum_ref)

    stats = stats_ref[0].T
    scale = lax.rsqrt(stats[:, 0:1] / INNER + EPSILON)
    cross = scale * stats[:, 1:2] / INNER
    grown = jnp.exp(turned(cols_ref[...], pl.program_id(0) * GATE_HEADS))
    low_half = low_lanes(GROUP)
    for pair in range(GATE_HEADS // 2):
        lanes = slice(PAIR * pair, PAIR * (pair + 1))
        mixed = mixed_ref[:, lanes]
        gate = gate_ref[:, lanes].astype(F32)
        gno = gno_ref[:, lanes].astype(F32)
        gain = gain_ref[:, lanes]
        sig = jax.nn.sigmoid(gate)
        act = gate * sig
        hat = mixed * act * scale
        normed_ref[:, lanes] = (hat * gain).astype(BF16)
        gain_sum_ref[:, lanes] += jnp.sum(gno * hat, axis=0, keepdims=True)
        grad_gated = scale * (gno * gain - hat * cross)
        grad_mixed = grad_gated * act
        ggate_ref[:, lanes] = (grad_gated * mixed * sig * (1.0 + gate * (1.0 - sig))).astype(BF16)
        skip_sum_ref[:, lanes] += jnp.sum(grad_mixed * x_ref[:, lanes].astype(F32), axis=0, keepdims=True)
        diag = grad_mixed.astype(BF16)
        gdiag_ref[:, lanes] = diag
        scaled = diag.astype(F32) * spread_heads(grown, heads + 2 * pair, low_half)
        scaled_ref[:, lanes] = scaled.astype(BF16)
    flow_ref[0] = dot(wr_ref[...], scaled_ref[...], 0, 0)


def gate_blocks(mixed, gate, gno, x, stats, gain, wr, cols, heads):
    tokens, width = x.shape
    blocks, steps = tokens // GROUP, width // GATE_LANES
    wide = pl.BlockSpec((GROUP, GATE_LANES), lambda g, b: (b, g))
    line = pl.BlockSpec((1, GATE_LANES), lambda g, b: (0, g))
    return pl.pallas_call(
        functools.partial(gate_kernel, heads),
        grid=(steps, blocks),
        in_specs=[
            wide, wide, wide, wide,
            pl.BlockSpec((1, 8, GROUP), lambda g, b: (b, 0, 0)),
            line,
            pl.BlockSpec((GROUP, STATE), lambda g, b: (b, 1)),
            pl.BlockSpec((GROUP, 128), lambda g, b: (b, 0)),
        ],
        out_specs=[
            wide, wide, wide, line, line,
            pl.BlockSpec((1, STATE, GATE_LANES), lambda g, b: (b, 0, g)),
        ],
        out_shape=[
            jax.ShapeDtypeStruct((tokens, width), BF16),
            jax.ShapeDtypeStruct((tokens, width), BF16),
            jax.ShapeDtypeStruct((tokens, width), BF16),
            jax.ShapeDtypeStruct((1, width), F32),
            jax.ShapeDtypeStruct((1, width), F32),
            jax.ShapeDtypeStruct((blocks, STATE, width), F32),
        ],
        scratch_shapes=[pltpu.VMEM((GROUP, GATE_LANES), BF16)],
        cost_estimate=pl.CostEstimate(
            flops=2 * tokens * STATE * width,
            bytes_accessed=tokens * width * 16 + blocks * STATE * width * 4,
            transcendentals=tokens * width,
        ),
        name="gate_blocks",
    )(mixed, gate, gno, x, stats, gain, wr, cols)


def back_kernel(
    groups, heads,
    x_ref, mixed_ref, grad_ref, slope_ref, pre_ref, rim_ref, wr_ref, nslope_ref, npre_ref, nrim_ref,
    cols_ref, rows_ref, state_ref, flow_ref, skip_ref, taps_ref, ntaps_ref, rate_ref,
    gpre_ref, gnarrow_ref, sums_ref, nsums_ref, hsums_ref, halo_ref, nhalo_ref,
    scores_ref, gscores_ref, prod_ref, gw_ref, gr_ref, u_ref, v_ref, i_ref, e_ref, ext_ref, next_ref, head_ref,
):
    step_id, g = pl.program_id(0), pl.program_id(1)
    block = pl.num_programs(0) - 1 - step_id
    last_of_slot = lax.rem(block, groups) == groups - 1
    first_of_slot = lax.rem(block, groups) == 0

    @pl.when(g == 0)
    def _():
        scores_ref[...] = dot(wr_ref[:, STATE:], wr_ref[:, :STATE], 1, 1)
        for ref in (gscores_ref, gw_ref, gr_ref, u_ref, v_ref, i_ref, e_ref):
            ref[...] = jnp.zeros_like(ref)

    @pl.when(jnp.logical_and(g == 0, step_id == 0))
    def _():
        sums_ref[...] = jnp.zeros_like(sums_ref)
        nsums_ref[...] = jnp.zeros_like(nsums_ref)
        hsums_ref[...] = jnp.zeros_like(hsums_ref)

    @pl.when(last_of_slot)
    def _():
        ext_ref[g, GROUP : GROUP + 8, :] = jnp.zeros((8, LANES_STEP), F32)
        next_ref[GROUP : GROUP + 8, :] = jnp.zeros((8, 2 * STATE), F32)

    @pl.when(jnp.logical_not(last_of_slot))
    def _():
        ext_ref[g, GROUP : GROUP + 8, :] = ext_ref[g, 0:8, :]

        @pl.when(g == 0)
        def _():
            next_ref[GROUP : GROUP + 8, :] = next_ref[0:8, :]

    cols = turned(cols_ref[...], g * HEADS_STEP)
    grown = jnp.exp(cols)
    shrunk = jnp.exp(cols[GROUP - 1 : GROUP, :] - cols)
    low_half = low_lanes(GROUP)
    lower = lower_mask()
    grad_write = jnp.zeros((GROUP, STATE), F32)
    grad_read = jnp.zeros((GROUP, STATE), F32)
    for pair in range(HEADS_STEP // 2):
        lanes = slice(PAIR * pair, PAIR * (pair + 1))
        x = x_ref[:, lanes].astype(F32)
        grad = grad_ref[:, lanes]
        grad_f = grad.astype(F32)
        skip = skip_ref[:, lanes]
        steps = spread_heads(cols, 2 * pair, low_half)
        tail = spread_heads(shrunk, heads + 2 * pair, low_half)
        stepped = x * steps
        x_halves = (
            jnp.where(low_half, stepped, 0.0).astype(BF16),
            jnp.where(low_half, 0.0, stepped).astype(BF16),
        )
        g_halves = (
            jnp.where(low_half, grad_f, 0.0).astype(BF16),
            jnp.where(low_half, 0.0, grad_f).astype(BF16),
        )
        flow = flow_ref[0, :, lanes]
        state = state_ref[0, :, lanes]
        e_ref[0:1, lanes] = jnp.sum(flow.astype(F32) * state.astype(F32), axis=0, keepdims=True)
        scaled = (grad_f * spread_heads(grown, heads + 2 * pair, low_half)).astype(BF16)
        grad_read = grad_read + dot(scaled, state, 1, 1)
        grad_write = grad_write + dot((stepped * tail).astype(BF16), flow, 1, 1)
        stepped_low = stepped.astype(BF16).astype(F32)
        inter = dot(wr_ref[:, :STATE], flow, 1, 0) * tail
        total = jnp.zeros_like(inter)
        for side in range(2):
            head = 2 * pair + side
            row = rows_ref[0, pl.ds(g * HEADS_STEP + head, 1), :]
            decay = jnp.exp(jnp.where(lower, cols[:, heads + head : heads + head + 1] - row, -1e30))
            weights = (scores_ref[...] * decay).astype(BF16)
            total = total + dot(weights, g_halves[side], 0, 0)
            gscores_ref[...] += dot(grad, x_halves[side], 1, 1) * decay
        both = total + inter
        prod_ref[0, :, lanes] = x * both
        prod_ref[1, :, lanes] = grad_f * (mixed_ref[:, lanes] - skip * x) - stepped_low * total
        prod_ref[2, :, lanes] = stepped_low * inter
        grad_conv = (steps * both + skip * grad_f) * slope_ref[:, lanes].astype(F32)
        ext_ref[g, 0:GROUP, lanes] = grad_conv
        pre = pre_ref[:, lanes].astype(F32)
        total_pre = jnp.zeros_like(grad_conv)
        for j in range(CONV):
            moved = ext_ref[g, j : j + GROUP, lanes]
            total_pre = total_pre + taps_ref[CONV - 1 - j : CONV - j, lanes] * moved
            sums_ref[g, CONV - 1 - j : CONV - j, lanes] += jnp.sum(pre * moved, axis=0, keepdims=True)
        sums_ref[g, CONV : CONV + 1, lanes] += jnp.sum(grad_conv, axis=0, keepdims=True)
        gpre_ref[:, lanes] = total_pre.astype(BF16)

    @pl.when(first_of_slot)
    def _():
        head_ref[0:8, :LANES_STEP] = jnp.zeros((8, LANES_STEP), F32)
        head_ref[8:16, :LANES_STEP] = ext_ref[g, 0:8, :]
        halo = jnp.zeros((8, LANES_STEP), F32)
        for j in range(CONV):
            moved = head_ref[j : j + 8, :LANES_STEP]
            halo = halo + taps_ref[CONV - 1 - j : CONV - j, :] * moved
            sums_ref[g, CONV - 1 - j : CONV - j, :] += jnp.sum(
                rim_ref[0].astype(F32) * moved[5:8], axis=0, keepdims=True
            )
        halo_ref[0] = halo

    chosen_rows = lax.broadcasted_iota(jnp.int32, (LANES_STEP, 128), 0) // HEADDIM + g * HEADS_STEP
    chosen = (chosen_rows == lax.broadcasted_iota(jnp.int32, (LANES_STEP, 128), 1)).astype(BF16)

    def sums_of(values, terms):
        total, rest = None, values
        for _ in range(terms):
            part = rest.astype(BF16)
            rest = rest - part.astype(F32)
            piece = dot(part, chosen, 1, 0)
            total = piece if total is None else total + piece
        return total

    u_ref[...] += sums_of(prod_ref[0], 2)
    v_ref[...] += sums_of(prod_ref[1], 2)
    i_ref[...] += sums_of(prod_ref[2], 2)
    e_ref[8:16, 0:128] += sums_of(e_ref[0:8, :], 2)
    gw_ref[...] += grad_write
    gr_ref[...] += grad_read

    @pl.when(g == pl.num_programs(1) - 1)
    def _():
        low = gscores_ref[...].astype(BF16)
        gradient = (
            gw_ref[...] + dot(low, wr_ref[:, STATE:], 0, 0),
            gr_ref[...] + dot(low, wr_ref[:, :STATE], 1, 0),
        )
        for part in range(2):
            lanes = slice(STATE * part, STATE * (part + 1))
            grad_conv = gradient[part] * nslope_ref[:, lanes]
            next_ref[0:GROUP, lanes] = grad_conv
            pre = npre_ref[:, lanes].astype(BF16).astype(F32)
            total_pre = jnp.zeros_like(grad_conv)
            for j in range(CONV):
                moved = next_ref[j : j + GROUP, lanes]
                total_pre = total_pre + ntaps_ref[CONV - 1 - j : CONV - j, lanes] * moved
                nsums_ref[CONV - 1 - j : CONV - j, lanes] += jnp.sum(pre * moved, axis=0, keepdims=True)
            nsums_ref[CONV : CONV + 1, lanes] += jnp.sum(grad_conv, axis=0, keepdims=True)
            gnarrow_ref[:, lanes] = total_pre.astype(BF16)

        @pl.when(first_of_slot)
        def _():
            head_ref[0:8, : 2 * STATE] = jnp.zeros((8, 2 * STATE), F32)
            head_ref[8:16, : 2 * STATE] = next_ref[0:8, :]
            halo = jnp.zeros((8, 2 * STATE), F32)
            for j in range(CONV):
                moved = head_ref[j : j + 8, : 2 * STATE]
                halo = halo + ntaps_ref[CONV - 1 - j : CONV - j, :] * moved
                nsums_ref[CONV - 1 - j : CONV - j, :] += jnp.sum(
                    nrim_ref[0].astype(F32) * moved[5:8], axis=0, keepdims=True
                )
            nhalo_ref[0] = halo

        own = cols_ref[...]
        lane = lax.broadcasted_iota(jnp.int32, (GROUP, 128), 1)
        step = jnp.where(lane < heads, own, 0.0)
        cum = pltpu.roll(own, 128 - heads, 1)
        sig = jnp.where(lane < heads, pltpu.roll(own, 128 - 2 * heads, 1), 0.0)
        strict = lax.broadcasted_iota(jnp.int32, (GROUP, GROUP), 0) > lax.broadcasted_iota(
            jnp.int32, (GROUP, GROUP), 1
        )
        reverse_sum = (
            split_dot(lower.astype(BF16), v_ref[...], 2, 0)
            + split_dot(strict.astype(BF16), i_ref[...], 2, 1)
            + jnp.exp(cum[GROUP - 1 : GROUP, :]) * e_ref[8:9, 0:128]
        )
        grad_raw = (u_ref[...] + rate_ref[...] * reverse_sum) * sig
        gnarrow_ref[:, 2 * STATE :] = grad_raw.astype(BF16)
        hsums_ref[0:1, :] += jnp.sum(grad_raw, axis=0, keepdims=True)
        hsums_ref[1:2, :] += jnp.sum(reverse_sum * step, axis=0, keepdims=True) * rate_ref[...]


def back_blocks(
    x, mixed, grad, slope, pre, rim, wr, nslope, npre, nrim, cols, rows, states, flows, skip, taps, ntaps, rate, groups
):
    tokens, width = x.shape
    blocks, steps, heads, slots = tokens // GROUP, width // LANES_STEP, rows.shape[1], rim.shape[0]
    at = lambda b: blocks - 1 - b
    wide = pl.BlockSpec((GROUP, LANES_STEP), lambda b, g: (at(b), g))
    narrow = lambda w: pl.BlockSpec((GROUP, w), lambda b, g: (at(b), 0))
    state = pl.BlockSpec((1, STATE, LANES_STEP), lambda b, g: (at(b), 0, g))
    line = lambda n: pl.BlockSpec((n, LANES_STEP), lambda b, g: (0, g))
    whole = lambda shape: pl.BlockSpec(shape, lambda b, g: (0,) * len(shape))
    return pl.pallas_call(
        functools.partial(back_kernel, groups, heads),
        grid=(blocks, steps),
        in_specs=[
            wide, wide, wide, wide, wide,
            pl.BlockSpec((1, CONV - 1, LANES_STEP), lambda b, g: (at(b) // groups, 0, g)),
            narrow(2 * STATE), narrow(2 * STATE), narrow(npre.shape[1]),
            pl.BlockSpec((1, CONV - 1, 2 * STATE), lambda b, g: (at(b) // groups, 0, 0)),
            narrow(128),
            pl.BlockSpec((1, heads, GROUP), lambda b, g: (at(b), 0, 0)),
            state, state, line(1), line(CONV), whole((CONV, 2 * STATE)), whole((1, 128)),
        ],
        out_specs=[
            wide, narrow(2 * STATE + 128),
            whole((steps, 8, LANES_STEP)), whole((8, 2 * STATE)), whole((8, 128)),
            pl.BlockSpec((1, 8, LANES_STEP), lambda b, g: (at(b) // groups, 0, g)),
            pl.BlockSpec((1, 8, 2 * STATE), lambda b, g: (at(b) // groups, 0, 0)),
        ],
        out_shape=[
            jax.ShapeDtypeStruct((tokens, width), BF16),
            jax.ShapeDtypeStruct((tokens, 2 * STATE + 128), BF16),
            jax.ShapeDtypeStruct((steps, 8, LANES_STEP), F32),
            jax.ShapeDtypeStruct((8, 2 * STATE), F32),
            jax.ShapeDtypeStruct((8, 128), F32),
            jax.ShapeDtypeStruct((slots, 8, width), F32),
            jax.ShapeDtypeStruct((slots, 8, 2 * STATE), F32),
        ],
        scratch_shapes=[
            pltpu.VMEM((GROUP, GROUP), F32),
            pltpu.VMEM((GROUP, GROUP), F32),
            pltpu.VMEM((3, GROUP, LANES_STEP), F32),
            pltpu.VMEM((GROUP, STATE), F32),
            pltpu.VMEM((GROUP, STATE), F32),
            pltpu.VMEM((GROUP, 128), F32),
            pltpu.VMEM((GROUP, 128), F32),
            pltpu.VMEM((GROUP, 128), F32),
            pltpu.VMEM((16, LANES_STEP), F32),
            pltpu.VMEM((steps, GROUP + 8, LANES_STEP), F32),
            pltpu.VMEM((GROUP + 8, 2 * STATE), F32),
            pltpu.VMEM((16, max(LANES_STEP, 2 * STATE)), F32),
        ],
        cost_estimate=pl.CostEstimate(
            flops=2 * tokens * width * (4 * GROUP + 4 * STATE) * 2,
            bytes_accessed=tokens * width * 14,
            transcendentals=tokens * GROUP * width // HEADDIM,
        ),
        name="back_blocks",
    )(x, mixed, grad, slope, pre, rim, wr, nslope, npre, nrim, cols, rows, states, flows, skip, taps, ntaps, rate)


MESH = pl.DeviceIdType.MESH
FAR_PARTS = 4


def fetch_kernel(
    x_ref, inner_ref, late_ref, step_ref, wr_ref, small_ref,
    full_x, full_inner, late_far, full_step, full_wr, full_small,
    x_own, inner_own, step_own, wr_own, small_own, send_sem, recv_sem, local_sem,
):
    f, c, z = lax.axis_index("fsdp"), lax.axis_index("ctx"), lax.axis_index("tp")
    half = z // 2
    slots, seq, cols = full_x.shape[0], full_x.shape[1], x_ref.shape[2]
    depth = inner_ref.shape[0]
    partners = (
        {"fsdp": f ^ 1}, {"fsdp": f ^ 2}, {"fsdp": f ^ 3}, {"ctx": c ^ 1}, {"tp": z ^ 1}, {"tp": z ^ 2},
    )
    barrier = pltpu.get_barrier_semaphore()
    for partner in partners:
        pl.semaphore_signal(barrier, inc=1, device_id=partner, device_id_type=MESH)
    pl.semaphore_wait(barrier, len(partners))

    copies = []

    def send(src, dst, partner):
        at = len(copies)
        copy = pltpu.make_async_remote_copy(
            src_ref=src, dst_ref=dst, send_sem=send_sem.at[at], recv_sem=recv_sem.at[at],
            device_id=partners[partner], device_id_type=MESH,
        )
        copy.start()
        copies.append([copy, False])
        return at

    def arrived(at):
        copies[at][0].wait_recv()
        copies[at][1] = True

    def feature(which):
        return pl.ds(pl.multiple_of(which * cols, 128), cols)

    def shard(full, row_f, far):
        wide = full.shape[1] // 2
        start = pl.multiple_of((row_f * 2 + c) * depth, depth)
        return full.at[pl.ds(start, depth), pl.ds(far * wide, wide)]

    def shard_one(full, row_f, far):
        start = pl.multiple_of((row_f * 2 + c) * depth, depth)
        return full.at[pl.ds(start, depth), :]

    def spread(full, src, far, part=shard):
        dst = part(full, f, far)
        near = [send(src, dst, k) for k in range(3)]
        send(src, dst, 3)
        return near

    def relay(full, near, far, part=shard):
        for k in range(3):
            arrived(near[k])
            row = part(full, f ^ (k + 1), far)
            send(row, row, 3)

    mine = pl.ds(half * slots, slots)
    other = pl.ds((1 - half) * slots, slots)
    send(small_ref, full_small.at[z], 4)
    far_small = send(small_ref, full_small.at[z], 5)
    send(x_ref.at[mine], full_x.at[:, :, feature(z)], 4)
    far_inner = send(inner_ref, shard(full_inner, f, 1), 5)
    far_step = send(step_ref, shard(full_step, f, 1), 5)
    piece = seq // FAR_PARTS
    far_x = [
        send(x_ref.at[other, pl.ds(piece * i, piece)], full_x.at[:, pl.ds(piece * i, piece), feature(z)], 5)
        for i in range(FAR_PARTS)
    ]
    send(late_ref, late_far, 5)
    own_inner = spread(full_inner, inner_ref, 0)
    own_step = spread(full_step, step_ref, 0)
    own_wr = spread(full_wr, wr_ref, 0, shard_one)

    staged = (
        (x_ref.at[mine], x_own, full_x.at[:, :, feature(z)]),
        (inner_ref, inner_own, shard(full_inner, f, 0)),
        (step_ref, step_own, shard(full_step, f, 0)),
        (wr_ref, wr_own, shard_one(full_wr, f, 0)),
        (small_ref, small_own, full_small.at[z]),
    )
    loads = [pltpu.make_async_copy(src, buf, local_sem.at[0, i]) for i, (src, buf, _) in enumerate(staged)]
    stores = [pltpu.make_async_copy(buf, dst, local_sem.at[1, i]) for i, (_, buf, dst) in enumerate(staged)]
    for load in loads:
        load.start()
    for load, store in zip(loads, stores):
        load.wait()
        store.start()

    arrived(far_small)
    send(full_small.at[z ^ 2], full_small.at[z ^ 2], 4)
    arrived(far_inner)
    away_inner = spread(full_inner, shard(full_inner, f, 1), 1)
    arrived(far_step)
    away_step = spread(full_step, shard(full_step, f, 1), 1)

    def both(i):
        arrived(far_x[i])
        part = full_x.at[:, pl.ds(piece * i, piece), feature(z ^ 2)]
        send(part, part, 4)

    relay(full_inner, own_inner, 0)
    relay(full_step, own_step, 0)
    relay(full_wr, own_wr, 0, shard_one)
    both(0)
    relay(full_inner, away_inner, 1)
    relay(full_step, away_step, 1)
    both(1)
    both(2)
    both(3)
    for store in stores:
        store.wait()
    for copy, done in copies:
        if not done:
            copy.wait_recv()
        copy.wait_send()


def fetch(hidden, inner, late, step, wr, small):
    slot_count, seq, cols = hidden.shape
    slots, depth = slot_count // 2, inner.shape[0]
    total = 8 * depth
    count = 1 + 2 * FAR_PARTS + 3 + 5 * 7 + 3
    anywhere = pl.BlockSpec(memory_space=pl.ANY)
    full = lambda x: jax.ShapeDtypeStruct((total, 2 * x.shape[1]), BF16)
    return pl.pallas_call(
        fetch_kernel,
        in_specs=[anywhere] * 6,
        out_specs=[anywhere] * 6,
        out_shape=[
            jax.ShapeDtypeStruct((slots, seq, 4 * cols), BF16),
            full(inner), jax.ShapeDtypeStruct(late.shape, BF16), full(step),
            jax.ShapeDtypeStruct((total, wr.shape[1]), BF16),
            jax.ShapeDtypeStruct((4,) + small.shape, F32),
        ],
        scratch_shapes=[
            pltpu.VMEM((slots, seq, cols), BF16),
            pltpu.VMEM(inner.shape, BF16),
            pltpu.VMEM(step.shape, BF16),
            pltpu.VMEM(wr.shape, BF16),
            pltpu.VMEM(small.shape, F32),
            pltpu.SemaphoreType.DMA((count,)),
            pltpu.SemaphoreType.DMA((count,)),
            pltpu.SemaphoreType.DMA((2, 5)),
        ],
        compiler_params=pltpu.CompilerParams(collective_id=0, has_side_effects=True),
        name="fetch",
    )(hidden, inner, late, step, wr, small)


def finish_kernel(
    part_ref, relay_ref, grad_ref, core_ref, small_ref, cross_ref,
    near_out, other_out, home_out, narrow_out, small_out, small_far, cross_out, cross_far,
    relay_buf, part_buf, sum_buf, core_buf, own_buf, plane_buf, got_buf, sent_buf, home_buf, wr_send, wr_got,
    small_got, cross_got, send_sem, recv_sem, load_sem,
):
    f, c, z = lax.axis_index("fsdp"), lax.axis_index("ctx"), lax.axis_index("tp")
    tokens, cols = near_out.shape
    depth, inner = home_out.shape
    partners = (
        {"fsdp": f ^ 1}, {"fsdp": f ^ 2}, {"fsdp": f ^ 3}, {"ctx": c ^ 1}, {"tp": z ^ 1}, {"tp": z ^ 2},
    )
    barrier = pltpu.get_barrier_semaphore()
    for partner in partners:
        pl.semaphore_signal(barrier, inc=1, device_id=partner, device_id_type=MESH)

    def feature(which):
        return pl.ds(pl.multiple_of(which * cols, 128), cols)

    def rows_of(row_f, core):
        return pl.ds(pl.multiple_of((row_f * 2 + core) * depth, depth), depth)

    piece = tokens // FAR_PARTS
    loads = [
        pltpu.make_async_copy(grad_ref.at[rows_of(f ^ k, c)], own_buf.at[k], load_sem.at[k]) for k in range(4)
    ] + [
        pltpu.make_async_copy(core_ref.at[f ^ k], core_buf.at[k], load_sem.at[4 + k]) for k in range(4)
    ] + [
        pltpu.make_async_copy(relay_ref.at[pl.ds(piece * i, piece)], relay_buf.at[i], load_sem.at[8 + i])
        for i in range(FAR_PARTS)
    ] + [
        pltpu.make_async_copy(
            part_ref.at[pl.ds(piece * i, piece), feature(z ^ 2)], part_buf.at[i], load_sem.at[8 + FAR_PARTS + i]
        )
        for i in range(FAR_PARTS)
    ]
    for load in loads:
        load.start()
    pl.semaphore_wait(barrier, len(partners))

    copies = []

    def send(src, dst, partner):
        at = len(copies)
        copy = pltpu.make_async_remote_copy(
            src_ref=src, dst_ref=dst, send_sem=send_sem.at[at], recv_sem=recv_sem.at[at],
            device_id=partners[partner], device_id_type=MESH,
        )
        copy.start()
        copies.append([copy, False])
        return at

    def arrived(at):
        copies[at][0].wait_recv()
        copies[at][1] = True

    small = [send(small_ref, small_got.at[0], 3)]
    cross = [send(cross_ref, cross_got, 4)]
    def passed_on(i):
        loads[8 + i].wait()
        loads[8 + FAR_PARTS + i].wait()
        sum_buf[i] = (part_buf[i].astype(F32) + relay_buf[i].astype(F32)).astype(BF16)
        send(sum_buf.at[i], other_out.at[pl.ds(piece * i, piece)], 5)

    for load in loads[:8]:
        load.wait()
    arrived(small[0])
    small_out[...] = small_ref[...] + small_got[0]
    small.append(send(small_out, small_got.at[1], 0))
    arrived(cross[0])
    cross_out[...] = cross_ref[...] + cross_got[...]
    cross.append(send(cross_out, cross_far, 5))
    for k in (1, 2, 3):
        sent_buf[k - 1] = (own_buf[k].astype(F32) + core_buf[k].astype(F32)).astype(BF16)
    passed_on(0)
    arrived(small[1])
    copies[small[1]][0].wait_send()
    small_out[...] = small_out[...] + small_got[1]
    small.append(send(small_out, small_got.at[2], 1))
    plane = [send(sent_buf.at[k], plane_buf.at[k], k) for k in range(3)]
    for i in range(1, FAR_PARTS):
        passed_on(i)
    arrived(small[2])
    copies[small[2]][0].wait_send()
    small_out[...] = small_out[...] + small_got[2]
    small.append(send(small_out, small_got.at[3], 4))
    middle = tokens // 2
    send(part_ref.at[pl.ds(0, middle), feature(z ^ 1)], near_out.at[pl.ds(0, middle)], 4)
    arrived(small[3])
    copies[small[3]][0].wait_send()
    shared = small_out.shape[0] // 2
    small_out[shared:, :] = small_out[shared:, :] + small_got[3, shared:, :]
    small.append(send(small_out, small_far, 5))
    total = own_buf[0].astype(F32) + core_buf[0].astype(F32)
    for at in plane:
        arrived(at)
    for k in range(3):
        total = total + plane_buf[k].astype(F32)
    wr_send[...] = total[:, 2 * inner : 2 * inner + 2 * STATE]
    wr = send(wr_send, wr_got, 4)
    home_out[...] = total[:, :inner]
    home_buf[:, :inner] = total[:, inner : 2 * inner].astype(BF16)
    narrow_out[:, 2 * STATE : 2 * STATE + 128] = total[:, 2 * inner + 2 * STATE :]
    home_buf[:, inner + 2 * STATE :] = total[:, 2 * inner + 2 * STATE :].astype(BF16)
    arrived(wr)
    both = wr_send[...] + wr_got[...]
    narrow_out[:, : 2 * STATE] = both
    home_buf[:, inner : inner + 2 * STATE] = both.astype(BF16)
    last = send(home_buf, got_buf, 5)
    send(part_ref.at[pl.ds(middle, middle), feature(z ^ 1)], near_out.at[pl.ds(middle, middle)], 4)
    arrived(last)
    home_out[...] += got_buf[:, :inner].astype(F32)
    narrow_out[:, : 2 * STATE] += got_buf[:, inner : inner + 2 * STATE].astype(F32)
    steps = got_buf[:, inner + 2 * STATE :].astype(F32)
    narrow_out[:, 2 * STATE + 128 :] = steps
    for copy, done in copies:
        if not done:
            copy.wait_recv()
    waited = {small[1], small[2], small[3]}
    for at, (copy, done) in enumerate(copies):
        if at not in waited:
            copy.wait_send()


def finish(part, relay, grad, core, small, cross, depth):
    tokens, width = part.shape
    cols, total = width // 4, grad.shape[1]
    rest = 2 * STATE + 128
    inner = (total - rest) // 2
    anywhere = pl.BlockSpec(memory_space=pl.ANY)
    vmem = pl.BlockSpec(memory_space=pltpu.VMEM)
    count = 5 + 2 + FAR_PARTS + 2 + 3 + 2
    return pl.pallas_call(
        finish_kernel,
        in_specs=[anywhere, anywhere, anywhere, anywhere, vmem, vmem],
        out_specs=[anywhere, anywhere, vmem, vmem, vmem, vmem, vmem, vmem],
        out_shape=[
            jax.ShapeDtypeStruct((tokens, cols), BF16),
            jax.ShapeDtypeStruct((tokens, cols), BF16),
            jax.ShapeDtypeStruct((depth, inner), F32),
            jax.ShapeDtypeStruct((depth, rest + 128), F32),
            jax.ShapeDtypeStruct(small.shape, F32),
            jax.ShapeDtypeStruct(small.shape, F32),
            jax.ShapeDtypeStruct(cross.shape, F32),
            jax.ShapeDtypeStruct(cross.shape, F32),
        ],
        scratch_shapes=[
            pltpu.VMEM((FAR_PARTS, tokens // FAR_PARTS, cols), BF16),
            pltpu.VMEM((FAR_PARTS, tokens // FAR_PARTS, cols), BF16),
            pltpu.VMEM((FAR_PARTS, tokens // FAR_PARTS, cols), BF16),
            pltpu.VMEM((4, depth, total), BF16),
            pltpu.VMEM((4, depth, total), BF16),
            pltpu.VMEM((3, depth, total), BF16),
            pltpu.VMEM((depth, inner + rest), BF16),
            pltpu.VMEM((3, depth, total), BF16),
            pltpu.VMEM((depth, inner + rest), BF16),
            pltpu.VMEM((depth, 2 * STATE), F32),
            pltpu.VMEM((depth, 2 * STATE), F32),
            pltpu.VMEM((4,) + small.shape, F32),
            pltpu.VMEM(cross.shape, F32),
            pltpu.SemaphoreType.DMA((count,)),
            pltpu.SemaphoreType.DMA((count,)),
            pltpu.SemaphoreType.DMA((8 + 2 * FAR_PARTS,)),
        ],
        compiler_params=pltpu.CompilerParams(collective_id=1, has_side_effects=True),
        name="finish",
    )(part, relay, grad, core, small, cross)


def after(x, other):
    return lax.optimization_barrier((x, other))[0]


def everywhere(x):
    for axis in ("ctx", "fsdp"):
        count, bit = lax.axis_size(axis), 1
        if count & (count - 1):
            x = lax.psum(x, axis)
            continue
        while bit < count:
            x = x + lax.ppermute(x, axis, [(i, i ^ bit) for i in range(count)])
            bit *= 2
    return x


def pack(parts):
    return jnp.concatenate([part.reshape(-1) for part in parts])


def unpack(vector, shapes):
    parts, at = [], 0
    for shape in shapes:
        size = 1
        for dim in shape:
            size *= dim
        parts.append(vector[at : at + size].reshape(shape))
        at += size
    return parts


def on_device(
    hidden_in,
    lengths,
    norm_gain,
    proj_gate_inner,
    proj_write_read,
    proj_step,
    conv_inner,
    conv_inner_bias,
    conv_write_read,
    conv_write_read_bias,
    step_bias,
    log_rate,
    skip_gain,
    gate_gain,
    proj_out,
    out_cotangent,
):
    slot_count, seq_here, width_here = hidden_in.shape
    slots = slot_count // 2
    tokens = slots * seq_here
    heads_own = step_bias.shape[0]
    inner_own = gate_gain.shape[0]
    heads = 2 * heads_own
    inner = 2 * inner_own
    tp_count = lax.axis_size("tp")
    width = tp_count * width_here
    groups = seq_here // GROUP
    blocks = slots * groups
    head_steps = heads // HEADS_STEP
    rim_rows = CONV - 1
    place = lax.axis_index("tp")
    far_half, near_side = place // 2, place % 2

    def half_of(whole, which):
        return lax.dynamic_slice_in_dim(whole, which * slots, slots, 0)

    def ordered(own, near, far, both, axis):
        first = lambda a, b: jnp.where(near_side == 0, a, b)
        a0, a1, b0, b1 = first(own, near), first(near, own), first(far, both), first(both, far)
        lower = lambda a, b: jnp.where(far_half == 0, a, b)
        return jnp.concatenate(
            [lower(a0, b0), lower(a1, b1), lower(b0, a0), lower(b1, a1)], axis=axis
        )

    ready = []

    def own_features(piece):
        first, second = piece(place ^ 3).astype(BF16), piece(place ^ 1).astype(BF16)
        relay = swap(first, 1)
        keep = swap(second, 1)
        summed = (piece(place ^ 2) + relay.astype(F32)).astype(BF16)
        ready.extend([first, second, summed])
        sent = swap(summed, 2)
        kept = (piece(place) + keep.astype(F32)).reshape(slots, seq_here, width_here)
        other = sent.astype(F32).reshape(slots, seq_here, width_here)
        return both_halves(kept, other)

    def both_halves(kept, other):
        return jnp.where(
            far_half == 0,
            jnp.concatenate([kept, other], axis=0),
            jnp.concatenate([other, kept], axis=0),
        )

    small_shapes = [(CONV, inner_own), (inner_own,), (inner_own,), (heads_own,), (heads_own,), (heads_own,)]
    def gathered(x):
        return lax.all_gather(x, ("fsdp", "ctx"), axis=0, tiled=True)

    own_small = pack([conv_inner, conv_inner_bias, gate_gain, step_bias, log_rate, skip_gain])
    cot_mine, cot_other = half_of(out_cotangent, far_half), half_of(out_cotangent, 1 - far_half)
    narrow_cols = 2 * STATE + heads
    narrow_pad = -narrow_cols % 128
    zeros = lambda x, extra: jnp.zeros((x.shape[0], extra), BF16)
    inner_shard, gate_shard = proj_gate_inner[:, 1], proj_gate_inner[:, 0]
    if lax.axis_size("fsdp") == 4 and lax.axis_size("ctx") == 2:
        step_shard = jnp.concatenate([proj_step, zeros(proj_step, 128 - heads_own)], axis=1)
        small = pack([norm_gain.astype(F32), own_small])
        small = jnp.pad(small, (0, -small.size % 1024)).reshape(-1, 128)
        late_shard = jnp.concatenate([gate_shard, proj_out], axis=1)
        full_x, full_inner, late_far, full_step, full_wr, full_small = fetch(
            hidden_in, inner_shard, late_shard, step_shard, proj_write_read, small
        )
        gate_far, out_far = late_far[:, :inner_own], late_far[:, inner_own:]
        full_small = full_small.reshape(tp_count, -1)
        full_gain = full_small[:, :width_here].reshape(width)
        far_row = lax.dynamic_slice_in_dim(full_small, place ^ 2, 1, 0)[0, width_here:]
        far_small = unpack(far_row, small_shapes)
        full_narrow = jnp.concatenate(
            [full_wr, full_step[:, :heads_own], full_step[:, 128 : 128 + heads_own], zeros(full_wr, narrow_pad)],
            axis=1,
        )
        cot_dep = full_x
    else:
        x_mine, x_other = half_of(hidden_in, far_half), half_of(hidden_in, 1 - far_half)
        narrow_shard = jnp.concatenate(
            [proj_write_read, proj_step, swap(proj_step, 2), zeros(proj_step, narrow_pad)], axis=1
        )
        inner_far = swap(inner_shard, 2)
        x_near = swap(x_mine, 1)
        x_far = swap(after(x_other, inner_far), 2)
        gate_far = swap(after(gate_shard, x_far), 2)
        x_both = swap(x_far, 1)
        cot_dep = after(x_both, gate_far)
        out_far = swap(after(proj_out, cot_dep), 2)
        full_narrow = gathered(narrow_shard)
        full_inner = gathered(jnp.concatenate([inner_shard, inner_far], axis=1))
        full_x = ordered(x_mine, x_near, x_far, x_both, 2)
        gain = norm_gain.astype(F32)
        full_gain = ordered(gain, swap(gain, 1), swap(gain, 2), swap(gain, 3), 0)
        far_small = unpack(swap(own_small, 2), small_shapes)
    full_x = full_x.reshape(tokens, width)
    full_late = gathered(jnp.concatenate([gate_shard, gate_far, proj_out, out_far], axis=1))
    full_gate, full_out = full_late[:, :inner], full_late[:, inner:]
    cot_mine, cot_other, cot_dep = lax.optimization_barrier((cot_mine, cot_other, cot_dep))
    cot_near, cot_far, cot_both = swap(cot_mine, 1), swap(cot_other, 2), swap(cot_other, 3)
    taps = jnp.concatenate([conv_inner, far_small[0]], axis=1)
    taps_bias = jnp.concatenate([conv_inner_bias, far_small[1]])
    gain_gate = jnp.concatenate([gate_gain, far_small[2]])
    bias_step = jnp.concatenate([step_bias, far_small[3]])
    rate_log = jnp.concatenate([log_rate, far_small[4]])
    gain_skip = jnp.concatenate([skip_gain, far_small[5]])
    rate = -jnp.exp(rate_log)
    skip_lanes = jnp.repeat(gain_skip, HEADDIM)[None]

    in_float = full_x.astype(F32)
    in_scale = lax.rsqrt(jnp.mean(in_float * in_float, axis=-1, keepdims=True) + EPSILON)
    normed = (in_float * in_scale * full_gain.astype(F32)).astype(BF16)
    narrow_pre = dot(normed, full_narrow, 1, 0)
    inner_pre = dot(normed, full_inner, 1, 0).astype(BF16)
    gate_pre = dot(normed, full_gate, 1, 0).astype(BF16)
    cot_near, cot_far, cot_both, gate_pre = lax.optimization_barrier((cot_near, cot_far, cot_both, gate_pre))
    full_cot = ordered(cot_mine, cot_near, cot_far, cot_both, 2).reshape(tokens, width)

    def rim_of(pre):
        by_slot = pre.reshape(slots, seq_here, pre.shape[-1])
        return passed_along(by_slot[:, seq_here - rim_rows :].astype(BF16), "ctx", 1)

    inner_rim, narrow_rim = rim_of(inner_pre), rim_of(narrow_pre[:, : 2 * STATE])
    lane_pad = lambda x: jnp.pad(x, (0, 128 - heads))[None]
    rate_row = lane_pad(rate)
    inner_act, slope, write_read, narrow_slope, cols, cum_rows, local_state, decay_lanes = start_blocks(
        inner_pre, inner_rim, narrow_pre, narrow_rim, taps, taps_bias[None], conv_write_read,
        conv_write_read_bias[None], lane_pad(bias_step), rate_row, groups, heads,
    )
    local_state = local_state.reshape(slots, groups, STATE, inner)
    decay_lanes = decay_lanes.reshape(slots, groups, 1, inner)
    carried = local_state[:, 0]
    device_decay = decay_lanes[:, 0]
    for position in range(1, groups):
        carried = decay_lanes[:, position] * carried + local_state[:, position]
        device_decay = device_decay * decay_lanes[:, position]
    current = carried_in(device_decay, carried, None, False)
    state_list = []
    for position in range(groups):
        state_list.append(current)
        current = decay_lanes[:, position] * current + local_state[:, position]
    states = jnp.stack(state_list, axis=1)
    states_low = states.astype(BF16).reshape(blocks, STATE, inner)

    position_ids = lax.axis_index("ctx") * seq_here + jnp.arange(seq_here)
    valid_rows = (position_ids[None, :] < lengths[:, None]).astype(F32)
    valid_here = half_of(valid_rows, far_half).reshape(tokens, 1)
    masked = (full_cot.astype(F32) * valid_here).astype(BF16)
    grad_normed_out = dot(masked, full_out, 1, 0).astype(BF16)
    mixed_out, stats = mix_blocks(
        inner_act, gate_pre, grad_normed_out, write_read, cols, cum_rows, states_low, skip_lanes, gain_gate[None],
    )
    stats = stats + swap(stats, 1)
    normed_out, grad_gate_pre, grad_diag, grad_gate_gain, grad_skip_lanes, local_grad = gate_blocks(
        mixed_out, gate_pre, grad_normed_out, inner_act, stats, gain_gate[None], write_read, cols, heads
    )
    local_grad = local_grad.reshape(slots, groups, STATE, inner)

    def branch_piece(which):
        rows = lax.dynamic_slice(full_late, (which * width_here, inner), (width_here, inner))
        return dot(normed_out, rows, 1, 1)

    branch = own_features(branch_piece)
    hidden_out = (hidden_in.astype(F32) + valid_rows[..., None] * branch).astype(BF16)
    normed_out, grad_gate_pre, *_ = lax.optimization_barrier((normed_out, grad_gate_pre, ready[0], ready[1]))
    grad_proj_out = dot(masked, normed_out, 0, 0).astype(BF16)
    grad_gate_w = dot(normed, grad_gate_pre, 0, 0).astype(BF16)
    grad_by_gate = dot(grad_gate_pre, full_gate, 1, 1)
    other_scale = swap(in_scale.reshape(-1, 128), 2)

    flowing = local_grad[:, groups - 1]
    for position in reversed(range(groups - 1)):
        flowing = decay_lanes[:, position] * flowing + local_grad[:, position]
    flowing = carried_in(device_decay, flowing, None, True)
    flow_list = []
    for position in reversed(range(groups)):
        flow_list.insert(0, flowing)
        flowing = decay_lanes[:, position] * flowing + local_grad[:, position]
    flows = jnp.stack(flow_list, axis=1)
    flows_low = flows.astype(BF16).reshape(blocks, STATE, inner)
    flows_low = after(flows_low, (grad_proj_out, grad_gate_w, ready[2]))

    grad_inner_pre, grad_narrow, tap_sums, narrow_sums, head_sums, halo, narrow_halo = back_blocks(
        inner_act, mixed_out, grad_diag, slope, inner_pre, inner_rim, write_read, narrow_slope, narrow_pre,
        narrow_rim, cols, cum_rows, states_low, flows_low, skip_lanes, taps, conv_write_read, rate_row, groups,
    )
    tap_sums = tap_sums.transpose(1, 0, 2).reshape(8, inner)
    grad_taps, grad_taps_bias = tap_sums[:CONV], tap_sums[CONV]
    grad_conv_write_read, grad_conv_write_read_bias = narrow_sums[:CONV], narrow_sums[CONV]
    grad_step_bias, grad_log_rate = head_sums[0, :heads], head_sums[1, :heads]

    def completed(grad, halo):
        back = passed_along(halo, "ctx", -1)
        for slot in range(slots):
            ends = (slot + 1) * seq_here
            rows = grad[ends - 8 : ends, : halo.shape[-1]].astype(F32) + back[slot]
            grad = lax.dynamic_update_slice(grad, rows.astype(BF16), (ends - 8, 0))
        return grad

    grad_inner_pre, grad_narrow = completed(grad_inner_pre, halo), completed(grad_narrow, narrow_halo)
    def reduced(x):
        return lax.psum_scatter(x, ("fsdp", "ctx"), scatter_dimension=0, tiled=True)

    early = reduced(jnp.concatenate([grad_proj_out, grad_gate_w], axis=1))
    early_away = jnp.concatenate([early[:, inner_own:inner], early[:, inner + inner_own :]], axis=1)
    grad_inner_pre, hidden_out, early_away = lax.optimization_barrier((grad_inner_pre, hidden_out, early_away))
    early_far = swap(early_away, 2)
    by_kernel = lax.axis_size("fsdp") == 4 and lax.axis_size("ctx") == 2
    late = jnp.concatenate([grad_inner_pre, grad_narrow], axis=1)
    if by_kernel:
        which = (place ^ 3) * width_here
        rows_at = lambda full: lax.dynamic_slice_in_dim(full, which, width_here, 0)
        relay_piece = (
            lax.dynamic_slice_in_dim(grad_by_gate, which, width_here, 1)
            + dot(grad_inner_pre, rows_at(full_inner), 1, 1)
            + dot(grad_narrow, rows_at(full_narrow), 1, 1)
        ).astype(BF16)
        relay = swap(relay_piece, 1)
        late = after(late, relay_piece)
    grad_late_w = dot(normed, late, 0, 0).astype(BF16)
    if by_kernel:
        by_core = grad_late_w.reshape(4, 2, -1, grad_late_w.shape[1])
        away = lax.dynamic_index_in_dim(by_core, 1 - lax.axis_index("ctx"), 1, keepdims=False)
        core = lax.ppermute(away, "ctx", [(0, 1), (1, 0)])
        grad_inner_pre, grad_narrow, *_ = lax.optimization_barrier(
            (grad_inner_pre, grad_narrow, away, early_far)
        )
    by_inner = dot(grad_inner_pre, full_inner, 1, 1)
    partial_normed = grad_by_gate + by_inner + dot(grad_narrow, full_narrow, 1, 1)
    grad_out_home = early[:, :inner_own].astype(F32) + early_far[:, :inner_own].astype(F32)
    grad_gate_home = early[:, inner : inner + inner_own].astype(F32) + early_far[:, inner_own:].astype(F32)
    by_hat = partial_normed * (full_x.astype(F32) * in_scale)
    grad_gain_full = jnp.sum(by_hat, axis=0)
    cross_part = jnp.sum(by_hat * full_gain.astype(F32), axis=1)
    partial_low = partial_normed.astype(BF16)

    grad_skip_gain = jnp.sum(grad_skip_lanes.reshape(heads, HEADDIM), axis=1)
    shared_shapes = [(CONV, 2 * STATE), (2 * STATE,), (width,)]
    head_shapes = [(CONV, inner), (inner,), (inner,), (heads,), (heads,), (heads,)]
    by_head = pack([grad_taps, grad_taps_bias, grad_gate_gain, grad_step_bias, grad_log_rate, grad_skip_gain])
    by_all = pack([grad_conv_write_read, grad_conv_write_read_bias, grad_gain_full])

    if by_kernel:
        span = max(inner, width, (CONV + 1) * 2 * STATE)
        line = lambda v: jnp.pad(v.reshape(-1, v.shape[-1]), ((0, 0), (0, span - v.shape[-1])))
        by_lines = jnp.concatenate(
            [
                line(tap_sums[: CONV + 1]),
                line(grad_gate_gain),
                line(jnp.concatenate([grad_step_bias, grad_log_rate, grad_skip_gain])),
                jnp.zeros((1, span), F32),
                line(grad_gain_full),
                line(narrow_sums[: CONV + 1].reshape(-1)),
                jnp.zeros((6, span), F32),
            ]
        )
        near, other, grad_inner_home, narrow_sum, small_own, small_far, cross_rows, cross_far = finish(
            partial_low,
            relay,
            grad_late_w,
            core,
            by_lines,
            cross_part.reshape(-1, 128),
            proj_write_read.shape[0],
        )
        kept = lax.dynamic_slice_in_dim(partial_normed, place * width_here, width_here, 1) + near.astype(F32)
        grad_normed = both_halves(
            kept.reshape(slots, seq_here, width_here), other.astype(F32).reshape(slots, seq_here, width_here)
        )
        write_read_home = narrow_sum[:, : 2 * STATE]
        step_home = (
            narrow_sum[:, 2 * STATE : 2 * STATE + heads_own]
            + narrow_sum[:, 2 * STATE + 128 + heads_own : 2 * STATE + 128 + heads]
        )
        cross_rows, cross_far = cross_rows.reshape(-1), cross_far.reshape(-1)
        homes = [
            small_own[at, :inner_own] + small_far[at, inner_own:inner] for at in (slice(0, CONV), CONV, CONV + 1)
        ] + [
            small_own[CONV + 2, k * heads : k * heads + heads_own]
            + small_far[CONV + 2, k * heads + heads_own : (k + 1) * heads]
            for k in range(3)
        ]
        shared = small_own[8:] + small_far[8:]
        grad_norm_gain = lax.dynamic_slice_in_dim(shared[0], place * width_here, width_here, 0)
        wr_sums = shared[1, : (CONV + 1) * 2 * STATE].reshape(CONV + 1, 2 * STATE)
        wr_taps, wr_bias = wr_sums[:CONV], wr_sums[CONV]
    else:

        def normed_piece(which):
            return lax.dynamic_slice_in_dim(partial_normed, which * width_here, width_here, 1)

        grad_normed = own_features(normed_piece)
        late_sum = reduced(grad_late_w)
        late_far = swap(late_sum, 2).astype(F32)
        late_sum = late_sum.astype(F32)
        grad_inner_home = late_sum[:, :inner_own] + late_far[:, inner_own:inner]
        write_read_home = late_sum[:, inner : inner + 2 * STATE] + late_far[:, inner : inner + 2 * STATE]
        write_read_home = write_read_home + swap(write_read_home, 1)
        steps_at = inner + 2 * STATE
        step_home = late_sum[:, steps_at : steps_at + heads_own] + late_far[:, steps_at + heads_own : steps_at + heads]
        cross_rows = cross_part + swap(cross_part, 1)
        cross_far = swap(cross_rows, 2)
        smalls = everywhere(pack([by_head, by_all]))
        parts = unpack(smalls[: by_head.size], head_shapes)
        away = [lax.slice_in_dim(p, p.shape[-1] // 2, p.shape[-1], axis=p.ndim - 1) for p in parts]
        far_parts = unpack(swap(pack(away), 2), small_shapes)
        shared = smalls[by_head.size :]
        shared = shared + swap(shared, 1)
        shared = shared + swap(shared, 2)
        homes = [
            lax.slice_in_dim(p, 0, p.shape[-1] // 2, axis=p.ndim - 1) + a for p, a in zip(parts, far_parts)
        ]
        wr_taps, wr_bias, gain_all = unpack(shared, shared_shapes)
        grad_norm_gain = lax.dynamic_slice_in_dim(gain_all, place * width_here, width_here, 0)

    own_gain = norm_gain.astype(F32)
    own_scale = both_halves(
        in_scale.reshape(slots, seq_here, 1), other_scale.reshape(slots, seq_here, 1)
    )
    own_hat = hidden_in.astype(F32) * own_scale
    grad_hat_in = grad_normed * own_gain
    cross_in = both_halves(
        cross_rows.reshape(slots, seq_here, 1), cross_far.reshape(slots, seq_here, 1)
    ) / width
    grad_hidden_in = own_scale * (grad_hat_in - own_hat * cross_in) + out_cotangent.astype(F32)
    return (
        hidden_out,
        grad_hidden_in,
        grad_norm_gain,
        jnp.stack([grad_gate_home, grad_inner_home], axis=1),
        write_read_home,
        step_home,
        homes[0],
        homes[1],
        wr_taps,
        wr_bias,
        homes[3],
        homes[4],
        homes[5],
        homes[2],
        grad_out_home,
    )


def solution(mesh):
    rows = ("fsdp", "ctx")
    acts = P("fsdp", "ctx", "tp")
    placed = (
        acts,
        P("fsdp"),
        P("tp"),
        P(rows, None, "tp"),
        P(rows, None),
        P(rows, "tp"),
        P(None, "tp"),
        P("tp"),
        P(),
        P(),
        P("tp"),
        P("tp"),
        P("tp"),
        P("tp"),
        P(rows, "tp"),
        acts,
    )
    return jax.shard_map(
        on_device,
        mesh=mesh,
        in_specs=placed,
        out_specs=(
            acts,
            acts,
            P("tp"),
            P(rows, None, "tp"),
            P(rows, None),
            P(rows, "tp"),
            P(None, "tp"),
            P("tp"),
            P(),
            P(),
            P("tp"),
            P("tp"),
            P("tp"),
            P("tp"),
            P(rows, "tp"),
        ),
        check_vma=False,
    )
```

```python
import functools

import jax
import jax.numpy as jnp
from jax import lax
from jax.experimental import pallas as pl
from jax.experimental.pallas import tpu as pltpu
from jax.sharding import PartitionSpec as P

HEADDIM = 64
STATE = 128
CONV = 4
GROUP = 256
INNER = 3072
EPSILON = 1e-05
PAIR = 2 * HEADDIM
HALF = GROUP // 2
HEADS_STEP = 6
LANES_STEP = HEADS_STEP * HEADDIM
GATE_HEADS = 12
GATE_LANES = GATE_HEADS * HEADDIM
F32 = jnp.float32
BF16 = jnp.bfloat16
HIGHEST = lax.Precision.HIGHEST


def swap(x, bit):
    count = lax.axis_size("tp")
    return lax.ppermute(x, "tp", [(i, i ^ bit) for i in range(count)])


def passed_along(x, axis, by):
    count = lax.axis_size(axis)
    pairs = [(i, i + by) for i in range(count) if 0 <= i + by < count]
    return lax.ppermute(x, axis, pairs)


def carried_in(decay, final, combine, reverse):
    count, position = (lax.axis_size("ctx"), lax.axis_index("ctx"))
    if count == 2:
        return passed_along(final.astype(BF16), "ctx", -1 if reverse else 1).astype(F32)
    decays = lax.all_gather(decay.astype(BF16), "ctx").astype(F32)
    finals = lax.all_gather(final.astype(BF16), "ctx")
    start = jnp.zeros_like(final)

    def lap(k, before):
        at = count - 1 - k if reverse else k
        reached = at > position if reverse else at < position
        new = decays[at] * before + finals[at].astype(F32)
        return jnp.where(reached, new, before)

    return lax.fori_loop(0, count, lap, start)


def dot(a, b, da, db):
    return lax.dot_general(a, b, (((da,), (db,)), ((), ())), preferred_element_type=F32)


def low_lanes(rows):
    return lax.broadcasted_iota(jnp.int32, (rows, PAIR), 1) < HEADDIM


def spread_heads(cols, first, low_half):
    return jnp.where(low_half, cols[:, first : first + 1], cols[:, first + 1 : first + 2])


def lower_mask():
    return lax.broadcasted_iota(jnp.int32, (GROUP, GROUP), 0) >= lax.broadcasted_iota(
        jnp.int32, (GROUP, GROUP), 1
    )


def quarter_mask():
    return lax.broadcasted_iota(jnp.int32, (HALF, HALF), 0) >= lax.broadcasted_iota(jnp.int32, (HALF, HALF), 1)


def decays(col, row, mask):
    early = jnp.exp(jnp.where(mask, col[:HALF] - row[:, :HALF], -1e30))
    cross = jnp.exp(col[HALF:] - row[:, :HALF])
    late = jnp.exp(jnp.where(mask, col[HALF:] - row[:, HALF:], -1e30))
    return early, cross, late


def split_dot(ones, values, terms, contract):
    total, rest = None, values
    for _ in range(terms):
        part = rest.astype(BF16)
        rest = rest - part.astype(F32)
        piece = dot(ones, part, contract, 0)
        total = piece if total is None else total + piece
    return total


def turned(cols, heads_before):
    return pltpu.roll(cols, lax.rem(128 - heads_before, 128), 1)


def start_kernel(
    groups, heads,
    inner_ref, rim_ref, narrow_ref, nrim_ref, taps_ref, bias_ref, ntaps_ref, nbias_ref, sbias_ref, rate_ref,
    x_ref, slope_ref, wr_ref, nslope_ref, cols_ref, rows_ref, local_ref, decay_ref,
    ext_ref, next_ref, scaled_ref,
):
    first = lax.rem(pl.program_id(0), groups) == 0

    @pl.when(first)
    def _():
        ext_ref[5:8, :] = rim_ref[0].astype(F32)
        next_ref[5:8, :] = nrim_ref[0].astype(F32)

    @pl.when(jnp.logical_not(first))
    def _():
        ext_ref[0:8, :] = ext_ref[GROUP : GROUP + 8, :]
        next_ref[0:8, :] = next_ref[GROUP : GROUP + 8, :]

    def conv(source, taps, bias, lanes):
        total = bias[:, lanes]
        for k in range(CONV):
            total = total + taps[k : k + 1, lanes] * source[5 + k : 5 + k + GROUP, lanes]
        sig = jax.nn.sigmoid(total)
        return total * sig, sig * (1.0 + total * (1.0 - sig))

    for part in range(2 * STATE // 128):
        lanes = slice(128 * part, 128 * (part + 1))
        next_ref[8 : GROUP + 8, lanes] = narrow_ref[:, lanes].astype(BF16).astype(F32)
        act, slope = conv(next_ref, ntaps_ref, nbias_ref, lanes)
        wr_ref[:, lanes] = act.astype(BF16)
        nslope_ref[:, lanes] = slope

    raw = narrow_ref[:, 2 * STATE :] + sbias_ref[...]
    lane = lax.broadcasted_iota(jnp.int32, (GROUP, 128), 1)
    step = jnp.maximum(raw, 0.0) + jnp.log1p(jnp.exp(-jnp.abs(raw)))
    step = jnp.where(lane < heads, step, 0.0)
    sig = jnp.where(lane < heads, jax.nn.sigmoid(raw), 0.0)
    cum = split_dot(lower_mask().astype(BF16), step * rate_ref[...], 3, 1)
    cols = step + pltpu.roll(cum, heads, 1) + pltpu.roll(sig, 2 * heads, 1)
    cols_ref[...] = cols
    rows_ref[0] = cum.T[:heads]
    last = cum[GROUP - 1 : GROUP, :]
    scale = jnp.exp(last - cum) * step
    decay = jnp.exp(last)
    low_half, low_row = low_lanes(GROUP), low_lanes(1)
    for pair in range(heads // 2):
        lanes = slice(PAIR * pair, PAIR * (pair + 1))
        ext_ref[8 : GROUP + 8, lanes] = inner_ref[:, lanes].astype(F32)
        act, slope = conv(ext_ref, taps_ref, bias_ref, lanes)
        x = act.astype(BF16)
        x_ref[:, lanes] = x
        slope_ref[:, lanes] = slope.astype(BF16)
        scaled_ref[:, lanes] = (x.astype(F32) * spread_heads(scale, 2 * pair, low_half)).astype(BF16)
        decay_ref[0, :, lanes] = spread_heads(decay, 2 * pair, low_row)
    local_ref[0] = dot(wr_ref[:, :STATE], scaled_ref[...], 0, 0)


def start_blocks(inner_pre, rim, narrow, nrim, taps, bias, ntaps, nbias, sbias, rate, groups, heads):
    tokens, width = inner_pre.shape
    blocks = tokens // GROUP
    rows = lambda w: pl.BlockSpec((GROUP, w), lambda b: (b, 0))
    whole = lambda x: pl.BlockSpec(x.shape, lambda b: (0,) * x.ndim)
    return pl.pallas_call(
        functools.partial(start_kernel, groups, heads),
        grid=(blocks,),
        in_specs=[
            rows(width),
            pl.BlockSpec((1, CONV - 1, width), lambda b: (b // groups, 0, 0)),
            rows(narrow.shape[1]),
            pl.BlockSpec((1, CONV - 1, 2 * STATE), lambda b: (b // groups, 0, 0)),
            whole(taps), whole(bias), whole(ntaps), whole(nbias), whole(sbias), whole(rate),
        ],
        out_specs=[
            rows(width), rows(width), rows(2 * STATE), rows(2 * STATE), rows(128),
            pl.BlockSpec((1, heads, GROUP), lambda b: (b, 0, 0)),
            pl.BlockSpec((1, STATE, width), lambda b: (b, 0, 0)),
            pl.BlockSpec((1, 1, width), lambda b: (b, 0, 0)),
        ],
        out_shape=[
            jax.ShapeDtypeStruct((tokens, width), BF16),
            jax.ShapeDtypeStruct((tokens, width), BF16),
            jax.ShapeDtypeStruct((tokens, 2 * STATE), BF16),
            jax.ShapeDtypeStruct((tokens, 2 * STATE), F32),
            jax.ShapeDtypeStruct((tokens, 128), F32),
            jax.ShapeDtypeStruct((blocks, heads, GROUP), F32),
            jax.ShapeDtypeStruct((blocks, STATE, width), F32),
            jax.ShapeDtypeStruct((blocks, 1, width), F32),
        ],
        scratch_shapes=[
            pltpu.VMEM((GROUP + 8, width), F32),
            pltpu.VMEM((GROUP + 8, 2 * STATE), F32),
            pltpu.VMEM((GROUP, width), BF16),
        ],
        cost_estimate=pl.CostEstimate(
            flops=2 * tokens * STATE * width + 20 * tokens * width,
            bytes_accessed=tokens * width * 6 + blocks * STATE * width * 4,
            transcendentals=tokens * width,
        ),
        name="start_blocks",
    )(inner_pre, rim, narrow, nrim, taps, bias, ntaps, nbias, sbias, rate)


def mix_kernel(
    heads,
    x_ref, gate_ref, gno_ref, wr_ref, cols_ref, rows_ref, state_ref, skip_ref, gain_ref,
    mixed_ref, stats_ref, scores_ref, sums_ref,
):
    g = pl.program_id(1)

    @pl.when(g == 0)
    def _():
        scores_ref[...] = dot(wr_ref[:, STATE:], wr_ref[:, :STATE], 1, 1)
        sums_ref[...] = jnp.zeros_like(sums_ref)

    cols = turned(cols_ref[...], g * GATE_HEADS)
    grown = jnp.exp(cols)
    low_half = low_lanes(GROUP)
    mask = quarter_mask()
    squares = jnp.zeros((GROUP, 1), F32)
    crosses = jnp.zeros((GROUP, 1), F32)
    for pair in range(GATE_HEADS // 2):
        lanes = slice(PAIR * pair, PAIR * (pair + 1))
        x = x_ref[:, lanes].astype(F32)
        stepped = x * spread_heads(cols, 2 * pair, low_half)
        halves = (
            jnp.where(low_half, stepped, 0.0).astype(BF16),
            jnp.where(low_half, 0.0, stepped).astype(BF16),
        )
        total = dot(wr_ref[:, STATE:], state_ref[0, :, lanes], 1, 0)
        total = total * spread_heads(grown, heads + 2 * pair, low_half)
        top = jnp.zeros((HALF, PAIR), F32)
        bottom = jnp.zeros((HALF, PAIR), F32)
        for side in range(2):
            head = 2 * pair + side
            row = rows_ref[0, pl.ds(g * GATE_HEADS + head, 1), :]
            early, cross, late = decays(cols[:, heads + head : heads + head + 1], row, mask)
            upper = (scores_ref[:HALF, :HALF] * early).astype(BF16)
            under = jnp.concatenate(
                [
                    (scores_ref[HALF:, :HALF] * cross).astype(BF16),
                    (scores_ref[HALF:, HALF:] * late).astype(BF16),
                ],
                axis=1,
            )
            top = top + dot(upper, halves[side][:HALF], 1, 0)
            bottom = bottom + dot(under, halves[side], 1, 0)
        total = total + jnp.concatenate([top, bottom], axis=0)
        mixed = total + skip_ref[:, lanes] * x
        mixed_ref[:, lanes] = mixed
        gate = gate_ref[:, lanes].astype(F32)
        gated = mixed * (gate * jax.nn.sigmoid(gate))
        squares = squares + jnp.sum(gated * gated, axis=1, keepdims=True)
        grad_hat = gno_ref[:, lanes].astype(F32) * gain_ref[:, lanes]
        crosses = crosses + jnp.sum(gated * grad_hat, axis=1, keepdims=True)
    lane = lax.broadcasted_iota(jnp.int32, (GROUP, 128), 1)
    sums_ref[...] += jnp.where(lane == 0, squares, jnp.where(lane == 1, crosses, 0.0))

    @pl.when(g == pl.num_programs(1) - 1)
    def _():
        stats_ref[0] = sums_ref[...].T[:8]


def mix_blocks(x, gate, gno, wr, cols, rows, states, skip, gain):
    tokens, width = x.shape
    blocks, steps, heads = tokens // GROUP, width // GATE_LANES, rows.shape[1]
    wide = pl.BlockSpec((GROUP, GATE_LANES), lambda b, g: (b, g))
    line = pl.BlockSpec((1, GATE_LANES), lambda b, g: (0, g))
    return pl.pallas_call(
        functools.partial(mix_kernel, heads),
        grid=(blocks, steps),
        in_specs=[
            wide, wide, wide,
            pl.BlockSpec((GROUP, 2 * STATE), lambda b, g: (b, 0)),
            pl.BlockSpec((GROUP, 128), lambda b, g: (b, 0)),
            pl.BlockSpec((1, heads, GROUP), lambda b, g: (b, 0, 0)),
            pl.BlockSpec((1, STATE, GATE_LANES), lambda b, g: (b, 0, g)),
            line, line,
        ],
        out_specs=[wide, pl.BlockSpec((1, 8, GROUP), lambda b, g: (b, 0, 0))],
        out_shape=[
            jax.ShapeDtypeStruct((tokens, width), F32),
            jax.ShapeDtypeStruct((blocks, 8, GROUP), F32),
        ],
        scratch_shapes=[pltpu.VMEM((GROUP, GROUP), F32), pltpu.VMEM((GROUP, 128), F32)],
        cost_estimate=pl.CostEstimate(
            flops=2 * tokens * width * (2 * GROUP + 2 * STATE) * 2,
            bytes_accessed=tokens * width * 10,
            transcendentals=tokens * GROUP * width // HEADDIM,
        ),
        name="mix_blocks",
    )(x, gate, gno, wr, cols, rows, states, skip, gain)


def gate_kernel(
    heads,
    mixed_ref, gate_ref, gno_ref, x_ref, stats_ref, gain_ref, wr_ref, cols_ref,
    normed_ref, ggate_ref, gdiag_ref, gain_sum_ref, skip_sum_ref, flow_ref, scaled_ref,
):
    @pl.when(pl.program_id(1) == 0)
    def _():
        gain_sum_ref[...] = jnp.zeros_like(gain_sum_ref)
        skip_sum_ref[...] = jnp.zeros_like(skip_sum_ref)

    stats = stats_ref[0].T
    scale = lax.rsqrt(stats[:, 0:1] / INNER + EPSILON)
    cross = scale * stats[:, 1:2] / INNER
    grown = jnp.exp(turned(cols_ref[...], pl.program_id(0) * GATE_HEADS))
    low_half = low_lanes(GROUP)
    for pair in range(GATE_HEADS // 2):
        lanes = slice(PAIR * pair, PAIR * (pair + 1))
        mixed = mixed_ref[:, lanes]
        gate = gate_ref[:, lanes].astype(F32)
        gno = gno_ref[:, lanes].astype(F32)
        gain = gain_ref[:, lanes]
        sig = jax.nn.sigmoid(gate)
        act = gate * sig
        hat = mixed * act * scale
        normed_ref[:, lanes] = (hat * gain).astype(BF16)
        gain_sum_ref[:, lanes] += jnp.sum(gno * hat, axis=0, keepdims=True)
        grad_gated = scale * (gno * gain - hat * cross)
        grad_mixed = grad_gated * act
        ggate_ref[:, lanes] = (grad_gated * mixed * sig * (1.0 + gate * (1.0 - sig))).astype(BF16)
        skip_sum_ref[:, lanes] += jnp.sum(grad_mixed * x_ref[:, lanes].astype(F32), axis=0, keepdims=True)
        diag = grad_mixed.astype(BF16)
        gdiag_ref[:, lanes] = diag
        scaled = diag.astype(F32) * spread_heads(grown, heads + 2 * pair, low_half)
        scaled_ref[:, lanes] = scaled.astype(BF16)
    flow_ref[0] = dot(wr_ref[...], scaled_ref[...], 0, 0)


def gate_blocks(mixed, gate, gno, x, stats, gain, wr, cols, heads):
    tokens, width = x.shape
    blocks, steps = tokens // GROUP, width // GATE_LANES
    wide = pl.BlockSpec((GROUP, GATE_LANES), lambda g, b: (b, g))
    line = pl.BlockSpec((1, GATE_LANES), lambda g, b: (0, g))
    return pl.pallas_call(
        functools.partial(gate_kernel, heads),
        grid=(steps, blocks),
        in_specs=[
            wide, wide, wide, wide,
            pl.BlockSpec((1, 8, GROUP), lambda g, b: (b, 0, 0)),
            line,
            pl.BlockSpec((GROUP, STATE), lambda g, b: (b, 1)),
            pl.BlockSpec((GROUP, 128), lambda g, b: (b, 0)),
        ],
        out_specs=[
            wide, wide, wide, line, line,
            pl.BlockSpec((1, STATE, GATE_LANES), lambda g, b: (b, 0, g)),
        ],
        out_shape=[
            jax.ShapeDtypeStruct((tokens, width), BF16),
            jax.ShapeDtypeStruct((tokens, width), BF16),
            jax.ShapeDtypeStruct((tokens, width), BF16),
            jax.ShapeDtypeStruct((1, width), F32),
            jax.ShapeDtypeStruct((1, width), F32),
            jax.ShapeDtypeStruct((blocks, STATE, width), F32),
        ],
        scratch_shapes=[pltpu.VMEM((GROUP, GATE_LANES), BF16)],
        cost_estimate=pl.CostEstimate(
            flops=2 * tokens * STATE * width,
            bytes_accessed=tokens * width * 16 + blocks * STATE * width * 4,
            transcendentals=tokens * width,
        ),
        name="gate_blocks",
    )(mixed, gate, gno, x, stats, gain, wr, cols)


def back_kernel(
    groups, heads,
    x_ref, mixed_ref, grad_ref, slope_ref, pre_ref, rim_ref, wr_ref, nslope_ref, npre_ref, nrim_ref,
    cols_ref, rows_ref, state_ref, flow_ref, skip_ref, taps_ref, ntaps_ref, rate_ref,
    gpre_ref, gnarrow_ref, sums_ref, nsums_ref, hsums_ref, halo_ref, nhalo_ref,
    scores_ref, gscores_ref, prod_ref, gw_ref, gr_ref, u_ref, v_ref, i_ref, e_ref, ext_ref, next_ref, head_ref,
):
    step_id, g = pl.program_id(0), pl.program_id(1)
    block = pl.num_programs(0) - 1 - step_id
    last_of_slot = lax.rem(block, groups) == groups - 1
    first_of_slot = lax.rem(block, groups) == 0

    @pl.when(g == 0)
    def _():
        scores_ref[...] = dot(wr_ref[:, STATE:], wr_ref[:, :STATE], 1, 1)
        for ref in (gscores_ref, gw_ref, gr_ref, u_ref, v_ref, i_ref, e_ref):
            ref[...] = jnp.zeros_like(ref)

    @pl.when(jnp.logical_and(g == 0, step_id == 0))
    def _():
        sums_ref[...] = jnp.zeros_like(sums_ref)
        nsums_ref[...] = jnp.zeros_like(nsums_ref)
        hsums_ref[...] = jnp.zeros_like(hsums_ref)

    @pl.when(last_of_slot)
    def _():
        ext_ref[g, GROUP : GROUP + 8, :] = jnp.zeros((8, LANES_STEP), F32)
        next_ref[GROUP : GROUP + 8, :] = jnp.zeros((8, 2 * STATE), F32)

    @pl.when(jnp.logical_not(last_of_slot))
    def _():
        ext_ref[g, GROUP : GROUP + 8, :] = ext_ref[g, 0:8, :]

        @pl.when(g == 0)
        def _():
            next_ref[GROUP : GROUP + 8, :] = next_ref[0:8, :]

    cols = turned(cols_ref[...], g * HEADS_STEP)
    grown = jnp.exp(cols)
    shrunk = jnp.exp(cols[GROUP - 1 : GROUP, :] - cols)
    low_half = low_lanes(GROUP)
    mask = quarter_mask()
    grad_write = jnp.zeros((GROUP, STATE), F32)
    grad_read = jnp.zeros((GROUP, STATE), F32)
    for pair in range(HEADS_STEP // 2):
        lanes = slice(PAIR * pair, PAIR * (pair + 1))
        x = x_ref[:, lanes].astype(F32)
        grad = grad_ref[:, lanes]
        grad_f = grad.astype(F32)
        skip = skip_ref[:, lanes]
        steps = spread_heads(cols, 2 * pair, low_half)
        tail = spread_heads(shrunk, heads + 2 * pair, low_half)
        stepped = x * steps
        x_halves = (
            jnp.where(low_half, stepped, 0.0).astype(BF16),
            jnp.where(low_half, 0.0, stepped).astype(BF16),
        )
        g_halves = (
            jnp.where(low_half, grad_f, 0.0).astype(BF16),
            jnp.where(low_half, 0.0, grad_f).astype(BF16),
        )
        flow = flow_ref[0, :, lanes]
        state = state_ref[0, :, lanes]
        e_ref[0:1, lanes] = jnp.sum(flow.astype(F32) * state.astype(F32), axis=0, keepdims=True)
        scaled = (grad_f * spread_heads(grown, heads + 2 * pair, low_half)).astype(BF16)
        grad_read = grad_read + dot(scaled, state, 1, 1)
        grad_write = grad_write + dot((stepped * tail).astype(BF16), flow, 1, 1)
        stepped_low = stepped.astype(BF16).astype(F32)
        inter = dot(wr_ref[:, :STATE], flow, 1, 0) * tail
        top = jnp.zeros((HALF, PAIR), F32)
        bottom = jnp.zeros((HALF, PAIR), F32)
        for side in range(2):
            head = 2 * pair + side
            row = rows_ref[0, pl.ds(g * HEADS_STEP + head, 1), :]
            early, cross, late = decays(cols[:, heads + head : heads + head + 1], row, mask)
            left = jnp.concatenate(
                [
                    (scores_ref[:HALF, :HALF] * early).astype(BF16),
                    (scores_ref[HALF:, :HALF] * cross).astype(BF16),
                ],
                axis=0,
            )
            right = (scores_ref[HALF:, HALF:] * late).astype(BF16)
            top = top + dot(left, g_halves[side], 0, 0)
            bottom = bottom + dot(right, g_halves[side][HALF:], 0, 0)
            under = dot(grad[HALF:], x_halves[side], 1, 1)
            terms = (
                dot(grad[:HALF], x_halves[side][:HALF], 1, 1) * early, under[:, :HALF] * cross, under[:, HALF:] * late,
            )
            quarters = terms if side == 0 else tuple(a + b for a, b in zip(quarters, terms))
        gscores_ref[:HALF, :HALF] += quarters[0]
        gscores_ref[HALF:, :HALF] += quarters[1]
        gscores_ref[HALF:, HALF:] += quarters[2]
        total = jnp.concatenate([top, bottom], axis=0)
        both = total + inter
        prod_ref[0, :, lanes] = x * both
        prod_ref[1, :, lanes] = grad_f * (mixed_ref[:, lanes] - skip * x) - stepped_low * total
        prod_ref[2, :, lanes] = stepped_low * inter
        grad_conv = (steps * both + skip * grad_f) * slope_ref[:, lanes].astype(F32)
        ext_ref[g, 0:GROUP, lanes] = grad_conv
        pre = pre_ref[:, lanes].astype(F32)
        total_pre = jnp.zeros_like(grad_conv)
        for j in range(CONV):
            moved = ext_ref[g, j : j + GROUP, lanes]
            total_pre = total_pre + taps_ref[CONV - 1 - j : CONV - j, lanes] * moved
            sums_ref[g, CONV - 1 - j : CONV - j, lanes] += jnp.sum(pre * moved, axis=0, keepdims=True)
        sums_ref[g, CONV : CONV + 1, lanes] += jnp.sum(grad_conv, axis=0, keepdims=True)
        gpre_ref[:, lanes] = total_pre.astype(BF16)

    @pl.when(first_of_slot)
    def _():
        head_ref[0:8, :LANES_STEP] = jnp.zeros((8, LANES_STEP), F32)
        head_ref[8:16, :LANES_STEP] = ext_ref[g, 0:8, :]
        halo = jnp.zeros((8, LANES_STEP), F32)
        for j in range(CONV):
            moved = head_ref[j : j + 8, :LANES_STEP]
            halo = halo + taps_ref[CONV - 1 - j : CONV - j, :] * moved
            sums_ref[g, CONV - 1 - j : CONV - j, :] += jnp.sum(
                rim_ref[0].astype(F32) * moved[5:8], axis=0, keepdims=True
            )
        halo_ref[0] = halo

    chosen_rows = lax.broadcasted_iota(jnp.int32, (LANES_STEP, 128), 0) // HEADDIM + g * HEADS_STEP
    chosen = (chosen_rows == lax.broadcasted_iota(jnp.int32, (LANES_STEP, 128), 1)).astype(BF16)

    def sums_of(values, terms):
        total, rest = None, values
        for _ in range(terms):
            part = rest.astype(BF16)
            rest = rest - part.astype(F32)
            piece = dot(part, chosen, 1, 0)
            total = piece if total is None else total + piece
        return total

    u_ref[...] += sums_of(prod_ref[0], 2)
    v_ref[...] += sums_of(prod_ref[1], 2)
    i_ref[...] += sums_of(prod_ref[2], 2)
    e_ref[8:16, 0:128] += sums_of(e_ref[0:8, :], 2)
    gw_ref[...] += grad_write
    gr_ref[...] += grad_read

    @pl.when(g == pl.num_programs(1) - 1)
    def _():
        low = gscores_ref[...].astype(BF16)
        gradient = (
            gw_ref[...] + dot(low, wr_ref[:, STATE:], 0, 0),
            gr_ref[...] + dot(low, wr_ref[:, :STATE], 1, 0),
        )
        for part in range(2):
            lanes = slice(STATE * part, STATE * (part + 1))
            grad_conv = gradient[part] * nslope_ref[:, lanes]
            next_ref[0:GROUP, lanes] = grad_conv
            pre = npre_ref[:, lanes].astype(BF16).astype(F32)
            total_pre = jnp.zeros_like(grad_conv)
            for j in range(CONV):
                moved = next_ref[j : j + GROUP, lanes]
                total_pre = total_pre + ntaps_ref[CONV - 1 - j : CONV - j, lanes] * moved
                nsums_ref[CONV - 1 - j : CONV - j, lanes] += jnp.sum(pre * moved, axis=0, keepdims=True)
            nsums_ref[CONV : CONV + 1, lanes] += jnp.sum(grad_conv, axis=0, keepdims=True)
            gnarrow_ref[:, lanes] = total_pre.astype(BF16)

        @pl.when(first_of_slot)
        def _():
            head_ref[0:8, : 2 * STATE] = jnp.zeros((8, 2 * STATE), F32)
            head_ref[8:16, : 2 * STATE] = next_ref[0:8, :]
            halo = jnp.zeros((8, 2 * STATE), F32)
            for j in range(CONV):
                moved = head_ref[j : j + 8, : 2 * STATE]
                halo = halo + ntaps_ref[CONV - 1 - j : CONV - j, :] * moved
                nsums_ref[CONV - 1 - j : CONV - j, :] += jnp.sum(
                    nrim_ref[0].astype(F32) * moved[5:8], axis=0, keepdims=True
                )
            nhalo_ref[0] = halo

        own = cols_ref[...]
        lane = lax.broadcasted_iota(jnp.int32, (GROUP, 128), 1)
        step = jnp.where(lane < heads, own, 0.0)
        cum = pltpu.roll(own, 128 - heads, 1)
        sig = jnp.where(lane < heads, pltpu.roll(own, 128 - 2 * heads, 1), 0.0)
        strict = lax.broadcasted_iota(jnp.int32, (GROUP, GROUP), 0) > lax.broadcasted_iota(
            jnp.int32, (GROUP, GROUP), 1
        )
        reverse_sum = (
            split_dot(lower_mask().astype(BF16), v_ref[...], 2, 0)
            + split_dot(strict.astype(BF16), i_ref[...], 2, 1)
            + jnp.exp(cum[GROUP - 1 : GROUP, :]) * e_ref[8:9, 0:128]
        )
        grad_raw = (u_ref[...] + rate_ref[...] * reverse_sum) * sig
        gnarrow_ref[:, 2 * STATE :] = grad_raw.astype(BF16)
        hsums_ref[0:1, :] += jnp.sum(grad_raw, axis=0, keepdims=True)
        hsums_ref[1:2, :] += jnp.sum(reverse_sum * step, axis=0, keepdims=True) * rate_ref[...]


def back_blocks(
    x, mixed, grad, slope, pre, rim, wr, nslope, npre, nrim, cols, rows, states, flows, skip, taps, ntaps, rate, groups
):
    tokens, width = x.shape
    blocks, steps, heads, slots = tokens // GROUP, width // LANES_STEP, rows.shape[1], rim.shape[0]
    at = lambda b: blocks - 1 - b
    wide = pl.BlockSpec((GROUP, LANES_STEP), lambda b, g: (at(b), g))
    narrow = lambda w: pl.BlockSpec((GROUP, w), lambda b, g: (at(b), 0))
    state = pl.BlockSpec((1, STATE, LANES_STEP), lambda b, g: (at(b), 0, g))
    line = lambda n: pl.BlockSpec((n, LANES_STEP), lambda b, g: (0, g))
    whole = lambda shape: pl.BlockSpec(shape, lambda b, g: (0,) * len(shape))
    return pl.pallas_call(
        functools.partial(back_kernel, groups, heads),
        grid=(blocks, steps),
        in_specs=[
            wide, wide, wide, wide, wide,
            pl.BlockSpec((1, CONV - 1, LANES_STEP), lambda b, g: (at(b) // groups, 0, g)),
            narrow(2 * STATE), narrow(2 * STATE), narrow(npre.shape[1]),
            pl.BlockSpec((1, CONV - 1, 2 * STATE), lambda b, g: (at(b) // groups, 0, 0)),
            narrow(128),
            pl.BlockSpec((1, heads, GROUP), lambda b, g: (at(b), 0, 0)),
            state, state, line(1), line(CONV), whole((CONV, 2 * STATE)), whole((1, 128)),
        ],
        out_specs=[
            wide, narrow(2 * STATE + 128),
            whole((steps, 8, LANES_STEP)), whole((8, 2 * STATE)), whole((8, 128)),
            pl.BlockSpec((1, 8, LANES_STEP), lambda b, g: (at(b) // groups, 0, g)),
            pl.BlockSpec((1, 8, 2 * STATE), lambda b, g: (at(b) // groups, 0, 0)),
        ],
        out_shape=[
            jax.ShapeDtypeStruct((tokens, width), BF16),
            jax.ShapeDtypeStruct((tokens, 2 * STATE + 128), BF16),
            jax.ShapeDtypeStruct((steps, 8, LANES_STEP), F32),
            jax.ShapeDtypeStruct((8, 2 * STATE), F32),
            jax.ShapeDtypeStruct((8, 128), F32),
            jax.ShapeDtypeStruct((slots, 8, width), F32),
            jax.ShapeDtypeStruct((slots, 8, 2 * STATE), F32),
        ],
        scratch_shapes=[
            pltpu.VMEM((GROUP, GROUP), F32),
            pltpu.VMEM((GROUP, GROUP), F32),
            pltpu.VMEM((3, GROUP, LANES_STEP), F32),
            pltpu.VMEM((GROUP, STATE), F32),
            pltpu.VMEM((GROUP, STATE), F32),
            pltpu.VMEM((GROUP, 128), F32),
            pltpu.VMEM((GROUP, 128), F32),
            pltpu.VMEM((GROUP, 128), F32),
            pltpu.VMEM((16, LANES_STEP), F32),
            pltpu.VMEM((steps, GROUP + 8, LANES_STEP), F32),
            pltpu.VMEM((GROUP + 8, 2 * STATE), F32),
            pltpu.VMEM((16, max(LANES_STEP, 2 * STATE)), F32),
        ],
        cost_estimate=pl.CostEstimate(
            flops=2 * tokens * width * (4 * GROUP + 4 * STATE) * 2,
            bytes_accessed=tokens * width * 14,
            transcendentals=tokens * GROUP * width // HEADDIM,
        ),
        name="back_blocks",
    )(x, mixed, grad, slope, pre, rim, wr, nslope, npre, nrim, cols, rows, states, flows, skip, taps, ntaps, rate)


MESH = pl.DeviceIdType.MESH
FAR_PARTS = 4


def fetch_kernel(
    x_ref, inner_ref, late_ref, step_ref, wr_ref, small_ref,
    full_x, full_inner, late_far, full_step, full_wr, full_small,
    x_own, inner_own, step_own, wr_own, small_own, send_sem, recv_sem, local_sem,
):
    f, c, z = lax.axis_index("fsdp"), lax.axis_index("ctx"), lax.axis_index("tp")
    half = z // 2
    slots, seq, cols = full_x.shape[0], full_x.shape[1], x_ref.shape[2]
    depth = inner_ref.shape[0]
    partners = (
        {"fsdp": f ^ 1}, {"fsdp": f ^ 2}, {"fsdp": f ^ 3}, {"ctx": c ^ 1}, {"tp": z ^ 1}, {"tp": z ^ 2},
    )
    barrier = pltpu.get_barrier_semaphore()
    for partner in partners:
        pl.semaphore_signal(barrier, inc=1, device_id=partner, device_id_type=MESH)
    pl.semaphore_wait(barrier, len(partners))

    copies = []

    def send(src, dst, partner):
        at = len(copies)
        copy = pltpu.make_async_remote_copy(
            src_ref=src, dst_ref=dst, send_sem=send_sem.at[at], recv_sem=recv_sem.at[at],
            device_id=partners[partner], device_id_type=MESH,
        )
        copy.start()
        copies.append([copy, False])
        return at

    def arrived(at):
        copies[at][0].wait_recv()
        copies[at][1] = True

    def feature(which):
        return pl.ds(pl.multiple_of(which * cols, 128), cols)

    def shard(full, row_f, far):
        wide = full.shape[1] // 2
        start = pl.multiple_of((row_f * 2 + c) * depth, depth)
        return full.at[pl.ds(start, depth), pl.ds(far * wide, wide)]

    def shard_one(full, row_f, far):
        start = pl.multiple_of((row_f * 2 + c) * depth, depth)
        return full.at[pl.ds(start, depth), :]

    def spread(full, src, far, part=shard):
        dst = part(full, f, far)
        near = [send(src, dst, k) for k in range(3)]
        send(src, dst, 3)
        return near

    def relay(full, near, far, part=shard):
        for k in range(3):
            arrived(near[k])
            row = part(full, f ^ (k + 1), far)
            send(row, row, 3)

    mine = pl.ds(half * slots, slots)
    other = pl.ds((1 - half) * slots, slots)
    send(small_ref, full_small.at[z], 4)
    far_small = send(small_ref, full_small.at[z], 5)
    send(x_ref.at[mine], full_x.at[:, :, feature(z)], 4)
    far_inner = send(inner_ref, shard(full_inner, f, 1), 5)
    far_step = send(step_ref, shard(full_step, f, 1), 5)
    piece = seq // FAR_PARTS
    far_x = [
        send(x_ref.at[other, pl.ds(piece * i, piece)], full_x.at[:, pl.ds(piece * i, piece), feature(z)], 5)
        for i in range(FAR_PARTS)
    ]
    send(late_ref, late_far, 5)
    own_inner = spread(full_inner, inner_ref, 0)
    own_step = spread(full_step, step_ref, 0)
    own_wr = spread(full_wr, wr_ref, 0, shard_one)

    staged = (
        (x_ref.at[mine], x_own, full_x.at[:, :, feature(z)]),
        (inner_ref, inner_own, shard(full_inner, f, 0)),
        (step_ref, step_own, shard(full_step, f, 0)),
        (wr_ref, wr_own, shard_one(full_wr, f, 0)),
        (small_ref, small_own, full_small.at[z]),
    )
    loads = [pltpu.make_async_copy(src, buf, local_sem.at[0, i]) for i, (src, buf, _) in enumerate(staged)]
    stores = [pltpu.make_async_copy(buf, dst, local_sem.at[1, i]) for i, (_, buf, dst) in enumerate(staged)]
    for load in loads:
        load.start()
    for load, store in zip(loads, stores):
        load.wait()
        store.start()

    arrived(far_small)
    send(full_small.at[z ^ 2], full_small.at[z ^ 2], 4)
    arrived(far_inner)
    away_inner = spread(full_inner, shard(full_inner, f, 1), 1)
    arrived(far_step)
    away_step = spread(full_step, shard(full_step, f, 1), 1)

    def both(i):
        arrived(far_x[i])
        part = full_x.at[:, pl.ds(piece * i, piece), feature(z ^ 2)]
        send(part, part, 4)

    relay(full_inner, own_inner, 0)
    relay(full_step, own_step, 0)
    relay(full_wr, own_wr, 0, shard_one)
    both(0)
    relay(full_inner, away_inner, 1)
    relay(full_step, away_step, 1)
    both(1)
    both(2)
    both(3)
    for store in stores:
        store.wait()
    for copy, done in copies:
        if not done:
            copy.wait_recv()
        copy.wait_send()


def fetch(hidden, inner, late, step, wr, small):
    slot_count, seq, cols = hidden.shape
    slots, depth = slot_count // 2, inner.shape[0]
    total = 8 * depth
    count = 1 + 2 * FAR_PARTS + 3 + 5 * 7 + 3
    anywhere = pl.BlockSpec(memory_space=pl.ANY)
    full = lambda x: jax.ShapeDtypeStruct((total, 2 * x.shape[1]), BF16)
    return pl.pallas_call(
        fetch_kernel,
        in_specs=[anywhere] * 6,
        out_specs=[anywhere] * 6,
        out_shape=[
            jax.ShapeDtypeStruct((slots, seq, 4 * cols), BF16),
            full(inner), jax.ShapeDtypeStruct(late.shape, BF16), full(step),
            jax.ShapeDtypeStruct((total, wr.shape[1]), BF16),
            jax.ShapeDtypeStruct((4,) + small.shape, F32),
        ],
        scratch_shapes=[
            pltpu.VMEM((slots, seq, cols), BF16),
            pltpu.VMEM(inner.shape, BF16),
            pltpu.VMEM(step.shape, BF16),
            pltpu.VMEM(wr.shape, BF16),
            pltpu.VMEM(small.shape, F32),
            pltpu.SemaphoreType.DMA((count,)),
            pltpu.SemaphoreType.DMA((count,)),
            pltpu.SemaphoreType.DMA((2, 5)),
        ],
        compiler_params=pltpu.CompilerParams(collective_id=0, has_side_effects=True),
        name="fetch",
    )(hidden, inner, late, step, wr, small)


def finish_kernel(
    part_ref, relay_ref, grad_ref, core_ref, small_ref, cross_ref,
    near_out, other_out, home_out, narrow_out, small_out, small_far, cross_out, cross_far,
    relay_buf, part_buf, sum_buf, core_buf, own_buf, plane_buf, got_buf, sent_buf, home_buf, wr_send, wr_got,
    small_got, cross_got, send_sem, recv_sem, load_sem,
):
    f, c, z = lax.axis_index("fsdp"), lax.axis_index("ctx"), lax.axis_index("tp")
    tokens, cols = near_out.shape
    depth, inner = home_out.shape
    partners = (
        {"fsdp": f ^ 1}, {"fsdp": f ^ 2}, {"fsdp": f ^ 3}, {"ctx": c ^ 1}, {"tp": z ^ 1}, {"tp": z ^ 2},
    )
    barrier = pltpu.get_barrier_semaphore()
    for partner in partners:
        pl.semaphore_signal(barrier, inc=1, device_id=partner, device_id_type=MESH)

    def feature(which):
        return pl.ds(pl.multiple_of(which * cols, 128), cols)

    def rows_of(row_f, core):
        return pl.ds(pl.multiple_of((row_f * 2 + core) * depth, depth), depth)

    piece = tokens // FAR_PARTS
    loads = [
        pltpu.make_async_copy(grad_ref.at[rows_of(f ^ k, c)], own_buf.at[k], load_sem.at[k]) for k in range(4)
    ] + [
        pltpu.make_async_copy(core_ref.at[f ^ k], core_buf.at[k], load_sem.at[4 + k]) for k in range(4)
    ] + [
        pltpu.make_async_copy(relay_ref.at[pl.ds(piece * i, piece)], relay_buf.at[i], load_sem.at[8 + i])
        for i in range(FAR_PARTS)
    ] + [
        pltpu.make_async_copy(
            part_ref.at[pl.ds(piece * i, piece), feature(z ^ 2)], part_buf.at[i], load_sem.at[8 + FAR_PARTS + i]
        )
        for i in range(FAR_PARTS)
    ]
    for load in loads:
        load.start()
    pl.semaphore_wait(barrier, len(partners))

    copies = []

    def send(src, dst, partner):
        at = len(copies)
        copy = pltpu.make_async_remote_copy(
            src_ref=src, dst_ref=dst, send_sem=send_sem.at[at], recv_sem=recv_sem.at[at],
            device_id=partners[partner], device_id_type=MESH,
        )
        copy.start()
        copies.append([copy, False])
        return at

    def arrived(at):
        copies[at][0].wait_recv()
        copies[at][1] = True

    small = [send(small_ref, small_got.at[0], 3)]
    cross = [send(cross_ref, cross_got, 4)]
    def passed_on(i):
        loads[8 + i].wait()
        loads[8 + FAR_PARTS + i].wait()
        sum_buf[i] = (part_buf[i].astype(F32) + relay_buf[i].astype(F32)).astype(BF16)
        send(sum_buf.at[i], other_out.at[pl.ds(piece * i, piece)], 5)

    for load in loads[:8]:
        load.wait()
    arrived(small[0])
    small_out[...] = small_ref[...] + small_got[0]
    small.append(send(small_out, small_got.at[1], 0))
    arrived(cross[0])
    cross_out[...] = cross_ref[...] + cross_got[...]
    cross.append(send(cross_out, cross_far, 5))
    for k in (1, 2, 3):
        sent_buf[k - 1] = (own_buf[k].astype(F32) + core_buf[k].astype(F32)).astype(BF16)
    passed_on(0)
    arrived(small[1])
    copies[small[1]][0].wait_send()
    small_out[...] = small_out[...] + small_got[1]
    small.append(send(small_out, small_got.at[2], 1))
    plane = [send(sent_buf.at[k], plane_buf.at[k], k) for k in range(3)]
    for i in range(1, FAR_PARTS):
        passed_on(i)
    arrived(small[2])
    copies[small[2]][0].wait_send()
    small_out[...] = small_out[...] + small_got[2]
    small.append(send(small_out, small_got.at[3], 4))
    middle = tokens // 2
    send(part_ref.at[pl.ds(0, middle), feature(z ^ 1)], near_out.at[pl.ds(0, middle)], 4)
    arrived(small[3])
    copies[small[3]][0].wait_send()
    shared = small_out.shape[0] // 2
    small_out[shared:, :] = small_out[shared:, :] + small_got[3, shared:, :]
    small.append(send(small_out, small_far, 5))
    total = own_buf[0].astype(F32) + core_buf[0].astype(F32)
    for at in plane:
        arrived(at)
    for k in range(3):
        total = total + plane_buf[k].astype(F32)
    wr_send[...] = total[:, 2 * inner : 2 * inner + 2 * STATE]
    wr = send(wr_send, wr_got, 4)
    home_out[...] = total[:, :inner]
    home_buf[:, :inner] = total[:, inner : 2 * inner].astype(BF16)
    narrow_out[:, 2 * STATE : 2 * STATE + 128] = total[:, 2 * inner + 2 * STATE :]
    home_buf[:, inner + 2 * STATE :] = total[:, 2 * inner + 2 * STATE :].astype(BF16)
    arrived(wr)
    both = wr_send[...] + wr_got[...]
    narrow_out[:, : 2 * STATE] = both
    home_buf[:, inner : inner + 2 * STATE] = both.astype(BF16)
    last = send(home_buf, got_buf, 5)
    send(part_ref.at[pl.ds(middle, middle), feature(z ^ 1)], near_out.at[pl.ds(middle, middle)], 4)
    arrived(last)
    home_out[...] += got_buf[:, :inner].astype(F32)
    narrow_out[:, : 2 * STATE] += got_buf[:, inner : inner + 2 * STATE].astype(F32)
    steps = got_buf[:, inner + 2 * STATE :].astype(F32)
    narrow_out[:, 2 * STATE + 128 :] = steps
    for copy, done in copies:
        if not done:
            copy.wait_recv()
    waited = {small[1], small[2], small[3]}
    for at, (copy, done) in enumerate(copies):
        if at not in waited:
            copy.wait_send()


def finish(part, relay, grad, core, small, cross, depth):
    tokens, width = part.shape
    cols, total = width // 4, grad.shape[1]
    rest = 2 * STATE + 128
    inner = (total - rest) // 2
    anywhere = pl.BlockSpec(memory_space=pl.ANY)
    vmem = pl.BlockSpec(memory_space=pltpu.VMEM)
    count = 5 + 2 + FAR_PARTS + 2 + 3 + 2
    return pl.pallas_call(
        finish_kernel,
        in_specs=[anywhere, anywhere, anywhere, anywhere, vmem, vmem],
        out_specs=[anywhere, anywhere, vmem, vmem, vmem, vmem, vmem, vmem],
        out_shape=[
            jax.ShapeDtypeStruct((tokens, cols), BF16),
            jax.ShapeDtypeStruct((tokens, cols), BF16),
            jax.ShapeDtypeStruct((depth, inner), F32),
            jax.ShapeDtypeStruct((depth, rest + 128), F32),
            jax.ShapeDtypeStruct(small.shape, F32),
            jax.ShapeDtypeStruct(small.shape, F32),
            jax.ShapeDtypeStruct(cross.shape, F32),
            jax.ShapeDtypeStruct(cross.shape, F32),
        ],
        scratch_shapes=[
            pltpu.VMEM((FAR_PARTS, tokens // FAR_PARTS, cols), BF16),
            pltpu.VMEM((FAR_PARTS, tokens // FAR_PARTS, cols), BF16),
            pltpu.VMEM((FAR_PARTS, tokens // FAR_PARTS, cols), BF16),
            pltpu.VMEM((4, depth, total), BF16),
            pltpu.VMEM((4, depth, total), BF16),
            pltpu.VMEM((3, depth, total), BF16),
            pltpu.VMEM((depth, inner + rest), BF16),
            pltpu.VMEM((3, depth, total), BF16),
            pltpu.VMEM((depth, inner + rest), BF16),
            pltpu.VMEM((depth, 2 * STATE), F32),
            pltpu.VMEM((depth, 2 * STATE), F32),
            pltpu.VMEM((4,) + small.shape, F32),
            pltpu.VMEM(cross.shape, F32),
            pltpu.SemaphoreType.DMA((count,)),
            pltpu.SemaphoreType.DMA((count,)),
            pltpu.SemaphoreType.DMA((8 + 2 * FAR_PARTS,)),
        ],
        compiler_params=pltpu.CompilerParams(collective_id=1, has_side_effects=True),
        name="finish",
    )(part, relay, grad, core, small, cross)


def after(x, other):
    return lax.optimization_barrier((x, other))[0]


def everywhere(x):
    for axis in ("ctx", "fsdp"):
        count, bit = lax.axis_size(axis), 1
        if count & (count - 1):
            x = lax.psum(x, axis)
            continue
        while bit < count:
            x = x + lax.ppermute(x, axis, [(i, i ^ bit) for i in range(count)])
            bit *= 2
    return x


def pack(parts):
    return jnp.concatenate([part.reshape(-1) for part in parts])


def unpack(vector, shapes):
    parts, at = [], 0
    for shape in shapes:
        size = 1
        for dim in shape:
            size *= dim
        parts.append(vector[at : at + size].reshape(shape))
        at += size
    return parts


def on_device(
    hidden_in,
    lengths,
    norm_gain,
    proj_gate_inner,
    proj_write_read,
    proj_step,
    conv_inner,
    conv_inner_bias,
    conv_write_read,
    conv_write_read_bias,
    step_bias,
    log_rate,
    skip_gain,
    gate_gain,
    proj_out,
    out_cotangent,
):
    slot_count, seq_here, width_here = hidden_in.shape
    slots = slot_count // 2
    tokens = slots * seq_here
    heads_own = step_bias.shape[0]
    inner_own = gate_gain.shape[0]
    heads = 2 * heads_own
    inner = 2 * inner_own
    tp_count = lax.axis_size("tp")
    width = tp_count * width_here
    groups = seq_here // GROUP
    blocks = slots * groups
    head_steps = heads // HEADS_STEP
    rim_rows = CONV - 1
    place = lax.axis_index("tp")
    far_half, near_side = place // 2, place % 2

    def half_of(whole, which):
        return lax.dynamic_slice_in_dim(whole, which * slots, slots, 0)

    def ordered(own, near, far, both, axis):
        first = lambda a, b: jnp.where(near_side == 0, a, b)
        a0, a1, b0, b1 = first(own, near), first(near, own), first(far, both), first(both, far)
        lower = lambda a, b: jnp.where(far_half == 0, a, b)
        return jnp.concatenate(
            [lower(a0, b0), lower(a1, b1), lower(b0, a0), lower(b1, a1)], axis=axis
        )

    ready = []

    def own_features(piece):
        first, second = piece(place ^ 3).astype(BF16), piece(place ^ 1).astype(BF16)
        relay = swap(first, 1)
        keep = swap(second, 1)
        summed = (piece(place ^ 2) + relay.astype(F32)).astype(BF16)
        ready.extend([first, second, summed])
        sent = swap(summed, 2)
        kept = (piece(place) + keep.astype(F32)).reshape(slots, seq_here, width_here)
        other = sent.astype(F32).reshape(slots, seq_here, width_here)
        return both_halves(kept, other)

    def both_halves(kept, other):
        return jnp.where(
            far_half == 0,
            jnp.concatenate([kept, other], axis=0),
            jnp.concatenate([other, kept], axis=0),
        )

    small_shapes = [(CONV, inner_own), (inner_own,), (inner_own,), (heads_own,), (heads_own,), (heads_own,)]
    def gathered(x):
        return lax.all_gather(x, ("fsdp", "ctx"), axis=0, tiled=True)

    own_small = pack([conv_inner, conv_inner_bias, gate_gain, step_bias, log_rate, skip_gain])
    cot_mine, cot_other = half_of(out_cotangent, far_half), half_of(out_cotangent, 1 - far_half)
    narrow_cols = 2 * STATE + heads
    narrow_pad = -narrow_cols % 128
    zeros = lambda x, extra: jnp.zeros((x.shape[0], extra), BF16)
    inner_shard, gate_shard = proj_gate_inner[:, 1], proj_gate_inner[:, 0]
    if lax.axis_size("fsdp") == 4 and lax.axis_size("ctx") == 2:
        step_shard = jnp.concatenate([proj_step, zeros(proj_step, 128 - heads_own)], axis=1)
        small = pack([norm_gain.astype(F32), own_small])
        small = jnp.pad(small, (0, -small.size % 1024)).reshape(-1, 128)
        late_shard = jnp.concatenate([gate_shard, proj_out], axis=1)
        full_x, full_inner, late_far, full_step, full_wr, full_small = fetch(
            hidden_in, inner_shard, late_shard, step_shard, proj_write_read, small
        )
        gate_far, out_far = late_far[:, :inner_own], late_far[:, inner_own:]
        full_small = full_small.reshape(tp_count, -1)
        full_gain = full_small[:, :width_here].reshape(width)
        far_row = lax.dynamic_slice_in_dim(full_small, place ^ 2, 1, 0)[0, width_here:]
        far_small = unpack(far_row, small_shapes)
        full_narrow = jnp.concatenate(
            [full_wr, full_step[:, :heads_own], full_step[:, 128 : 128 + heads_own], zeros(full_wr, narrow_pad)],
            axis=1,
        )
        cot_dep = full_x
    else:
        x_mine, x_other = half_of(hidden_in, far_half), half_of(hidden_in, 1 - far_half)
        narrow_shard = jnp.concatenate(
            [proj_write_read, proj_step, swap(proj_step, 2), zeros(proj_step, narrow_pad)], axis=1
        )
        inner_far = swap(inner_shard, 2)
        x_near = swap(x_mine, 1)
        x_far = swap(after(x_other, inner_far), 2)
        gate_far = swap(after(gate_shard, x_far), 2)
        x_both = swap(x_far, 1)
        cot_dep = after(x_both, gate_far)
        out_far = swap(after(proj_out, cot_dep), 2)
        full_narrow = gathered(narrow_shard)
        full_inner = gathered(jnp.concatenate([inner_shard, inner_far], axis=1))
        full_x = ordered(x_mine, x_near, x_far, x_both, 2)
        gain = norm_gain.astype(F32)
        full_gain = ordered(gain, swap(gain, 1), swap(gain, 2), swap(gain, 3), 0)
        far_small = unpack(swap(own_small, 2), small_shapes)
    full_x = full_x.reshape(tokens, width)
    full_late = gathered(jnp.concatenate([gate_shard, gate_far, proj_out, out_far], axis=1))
    full_gate, full_out = full_late[:, :inner], full_late[:, inner:]
    cot_mine, cot_other, cot_dep = lax.optimization_barrier((cot_mine, cot_other, cot_dep))
    cot_near, cot_far, cot_both = swap(cot_mine, 1), swap(cot_other, 2), swap(cot_other, 3)
    taps = jnp.concatenate([conv_inner, far_small[0]], axis=1)
    taps_bias = jnp.concatenate([conv_inner_bias, far_small[1]])
    gain_gate = jnp.concatenate([gate_gain, far_small[2]])
    bias_step = jnp.concatenate([step_bias, far_small[3]])
    rate_log = jnp.concatenate([log_rate, far_small[4]])
    gain_skip = jnp.concatenate([skip_gain, far_small[5]])
    rate = -jnp.exp(rate_log)
    skip_lanes = jnp.repeat(gain_skip, HEADDIM)[None]

    in_float = full_x.astype(F32)
    in_scale = lax.rsqrt(jnp.mean(in_float * in_float, axis=-1, keepdims=True) + EPSILON)
    normed = (in_float * in_scale * full_gain.astype(F32)).astype(BF16)
    narrow_pre = dot(normed, full_narrow, 1, 0)
    inner_pre = dot(normed, full_inner, 1, 0).astype(BF16)
    gate_pre = dot(normed, full_gate, 1, 0).astype(BF16)
    cot_near, cot_far, cot_both, gate_pre = lax.optimization_barrier((cot_near, cot_far, cot_both, gate_pre))
    full_cot = ordered(cot_mine, cot_near, cot_far, cot_both, 2).reshape(tokens, width)

    def rim_of(pre):
        by_slot = pre.reshape(slots, seq_here, pre.shape[-1])
        return passed_along(by_slot[:, seq_here - rim_rows :].astype(BF16), "ctx", 1)

    inner_rim, narrow_rim = rim_of(inner_pre), rim_of(narrow_pre[:, : 2 * STATE])
    lane_pad = lambda x: jnp.pad(x, (0, 128 - heads))[None]
    rate_row = lane_pad(rate)
    inner_act, slope, write_read, narrow_slope, cols, cum_rows, local_state, decay_lanes = start_blocks(
        inner_pre, inner_rim, narrow_pre, narrow_rim, taps, taps_bias[None], conv_write_read,
        conv_write_read_bias[None], lane_pad(bias_step), rate_row, groups, heads,
    )
    local_state = local_state.reshape(slots, groups, STATE, inner)
    decay_lanes = decay_lanes.reshape(slots, groups, 1, inner)
    carried = local_state[:, 0]
    device_decay = decay_lanes[:, 0]
    for position in range(1, groups):
        carried = decay_lanes[:, position] * carried + local_state[:, position]
        device_decay = device_decay * decay_lanes[:, position]
    current = carried_in(device_decay, carried, None, False)
    state_list = []
    for position in range(groups):
        state_list.append(current)
        current = decay_lanes[:, position] * current + local_state[:, position]
    states = jnp.stack(state_list, axis=1)
    states_low = states.astype(BF16).reshape(blocks, STATE, inner)

    position_ids = lax.axis_index("ctx") * seq_here + jnp.arange(seq_here)
    valid_rows = (position_ids[None, :] < lengths[:, None]).astype(F32)
    valid_here = half_of(valid_rows, far_half).reshape(tokens, 1)
    masked = (full_cot.astype(F32) * valid_here).astype(BF16)
    grad_normed_out = dot(masked, full_out, 1, 0).astype(BF16)
    mixed_out, stats = mix_blocks(
        inner_act, gate_pre, grad_normed_out, write_read, cols, cum_rows, states_low, skip_lanes, gain_gate[None],
    )
    stats = stats + swap(stats, 1)
    normed_out, grad_gate_pre, grad_diag, grad_gate_gain, grad_skip_lanes, local_grad = gate_blocks(
        mixed_out, gate_pre, grad_normed_out, inner_act, stats, gain_gate[None], write_read, cols, heads
    )
    local_grad = local_grad.reshape(slots, groups, STATE, inner)

    def branch_piece(which):
        rows = lax.dynamic_slice(full_late, (which * width_here, inner), (width_here, inner))
        return dot(normed_out, rows, 1, 1)

    branch = own_features(branch_piece)
    hidden_out = (hidden_in.astype(F32) + valid_rows[..., None] * branch).astype(BF16)
    normed_out, grad_gate_pre, *_ = lax.optimization_barrier((normed_out, grad_gate_pre, ready[0], ready[1]))
    grad_proj_out = dot(masked, normed_out, 0, 0).astype(BF16)
    grad_gate_w = dot(normed, grad_gate_pre, 0, 0).astype(BF16)
    grad_by_gate = dot(grad_gate_pre, full_gate, 1, 1).astype(BF16)
    other_scale = swap(in_scale.reshape(-1, 128), 2)

    flowing = local_grad[:, groups - 1]
    for position in reversed(range(groups - 1)):
        flowing = decay_lanes[:, position] * flowing + local_grad[:, position]
    flowing = carried_in(device_decay, flowing, None, True)
    flow_list = []
    for position in reversed(range(groups)):
        flow_list.insert(0, flowing)
        flowing = decay_lanes[:, position] * flowing + local_grad[:, position]
    flows = jnp.stack(flow_list, axis=1)
    flows_low = flows.astype(BF16).reshape(blocks, STATE, inner)
    flows_low = after(flows_low, (grad_proj_out, grad_gate_w, ready[2]))

    grad_inner_pre, grad_narrow, tap_sums, narrow_sums, head_sums, halo, narrow_halo = back_blocks(
        inner_act, mixed_out, grad_diag, slope, inner_pre, inner_rim, write_read, narrow_slope, narrow_pre,
        narrow_rim, cols, cum_rows, states_low, flows_low, skip_lanes, taps, conv_write_read, rate_row, groups,
    )
    tap_sums = tap_sums.transpose(1, 0, 2).reshape(8, inner)
    grad_taps, grad_taps_bias = tap_sums[:CONV], tap_sums[CONV]
    grad_conv_write_read, grad_conv_write_read_bias = narrow_sums[:CONV], narrow_sums[CONV]
    grad_step_bias, grad_log_rate = head_sums[0, :heads], head_sums[1, :heads]

    def completed(grad, halo):
        back = passed_along(halo, "ctx", -1)
        for slot in range(slots):
            ends = (slot + 1) * seq_here
            rows = grad[ends - 8 : ends, : halo.shape[-1]].astype(F32) + back[slot]
            grad = lax.dynamic_update_slice(grad, rows.astype(BF16), (ends - 8, 0))
        return grad

    grad_inner_pre, grad_narrow = completed(grad_inner_pre, halo), completed(grad_narrow, narrow_halo)
    def reduced(x):
        return lax.psum_scatter(x, ("fsdp", "ctx"), scatter_dimension=0, tiled=True)

    early = reduced(jnp.concatenate([grad_proj_out, grad_gate_w], axis=1))
    early_away = jnp.concatenate([early[:, inner_own:inner], early[:, inner + inner_own :]], axis=1)
    grad_inner_pre, hidden_out, early_away = lax.optimization_barrier((grad_inner_pre, hidden_out, early_away))
    early_far = swap(early_away, 2)
    by_kernel = lax.axis_size("fsdp") == 4 and lax.axis_size("ctx") == 2
    late = jnp.concatenate([grad_inner_pre, grad_narrow], axis=1)
    if by_kernel:
        which = (place ^ 3) * width_here
        rows_at = lambda full: lax.dynamic_slice_in_dim(full, which, width_here, 0)
        relay_piece = (
            lax.dynamic_slice_in_dim(grad_by_gate, which, width_here, 1)
            + dot(grad_inner_pre, rows_at(full_inner), 1, 1)
            + dot(grad_narrow, rows_at(full_narrow), 1, 1)
        ).astype(BF16)
        relay = swap(relay_piece, 1)
        late = after(late, relay_piece)
    grad_late_w = dot(normed, late, 0, 0).astype(BF16)
    if by_kernel:
        by_core = grad_late_w.reshape(4, 2, -1, grad_late_w.shape[1])
        away = lax.dynamic_index_in_dim(by_core, 1 - lax.axis_index("ctx"), 1, keepdims=False)
        core = lax.ppermute(away, "ctx", [(0, 1), (1, 0)])
        grad_inner_pre, grad_narrow, *_ = lax.optimization_barrier(
            (grad_inner_pre, grad_narrow, away, early_far)
        )
    by_inner = dot(grad_inner_pre, full_inner, 1, 1)
    partial_normed = grad_by_gate + by_inner + dot(grad_narrow, full_narrow, 1, 1)
    grad_out_home = early[:, :inner_own].astype(F32) + early_far[:, :inner_own].astype(F32)
    grad_gate_home = early[:, inner : inner + inner_own].astype(F32) + early_far[:, inner_own:].astype(F32)
    by_hat = partial_normed * (full_x.astype(F32) * in_scale)
    grad_gain_full = jnp.sum(by_hat, axis=0)
    cross_part = jnp.sum(by_hat * full_gain.astype(F32), axis=1)
    partial_low = partial_normed.astype(BF16)

    grad_skip_gain = jnp.sum(grad_skip_lanes.reshape(heads, HEADDIM), axis=1)
    shared_shapes = [(CONV, 2 * STATE), (2 * STATE,), (width,)]
    head_shapes = [(CONV, inner), (inner,), (inner,), (heads,), (heads,), (heads,)]
    by_head = pack([grad_taps, grad_taps_bias, grad_gate_gain, grad_step_bias, grad_log_rate, grad_skip_gain])
    by_all = pack([grad_conv_write_read, grad_conv_write_read_bias, grad_gain_full])

    if by_kernel:
        span = max(inner, width, (CONV + 1) * 2 * STATE)
        line = lambda v: jnp.pad(v.reshape(-1, v.shape[-1]), ((0, 0), (0, span - v.shape[-1])))
        by_lines = jnp.concatenate(
            [
                line(tap_sums[: CONV + 1]),
                line(grad_gate_gain),
                line(jnp.concatenate([grad_step_bias, grad_log_rate, grad_skip_gain])),
                jnp.zeros((1, span), F32),
                line(grad_gain_full),
                line(narrow_sums[: CONV + 1].reshape(-1)),
                jnp.zeros((6, span), F32),
            ]
        )
        near, other, grad_inner_home, narrow_sum, small_own, small_far, cross_rows, cross_far = finish(
            partial_low,
            relay,
            grad_late_w,
            core,
            by_lines,
            cross_part.reshape(-1, 128),
            proj_write_read.shape[0],
        )
        kept = lax.dynamic_slice_in_dim(partial_normed, place * width_here, width_here, 1) + near.astype(F32)
        grad_normed = both_halves(
            kept.reshape(slots, seq_here, width_here), other.astype(F32).reshape(slots, seq_here, width_here)
        )
        write_read_home = narrow_sum[:, : 2 * STATE]
        step_home = (
            narrow_sum[:, 2 * STATE : 2 * STATE + heads_own]
            + narrow_sum[:, 2 * STATE + 128 + heads_own : 2 * STATE + 128 + heads]
        )
        cross_rows, cross_far = cross_rows.reshape(-1), cross_far.reshape(-1)
        homes = [
            small_own[at, :inner_own] + small_far[at, inner_own:inner] for at in (slice(0, CONV), CONV, CONV + 1)
        ] + [
            small_own[CONV + 2, k * heads : k * heads + heads_own]
            + small_far[CONV + 2, k * heads + heads_own : (k + 1) * heads]
            for k in range(3)
        ]
        shared = small_own[8:] + small_far[8:]
        grad_norm_gain = lax.dynamic_slice_in_dim(shared[0], place * width_here, width_here, 0)
        wr_sums = shared[1, : (CONV + 1) * 2 * STATE].reshape(CONV + 1, 2 * STATE)
        wr_taps, wr_bias = wr_sums[:CONV], wr_sums[CONV]
    else:

        def normed_piece(which):
            return lax.dynamic_slice_in_dim(partial_normed, which * width_here, width_here, 1)

        grad_normed = own_features(normed_piece)
        late_sum = reduced(grad_late_w)
        late_far = swap(late_sum, 2).astype(F32)
        late_sum = late_sum.astype(F32)
        grad_inner_home = late_sum[:, :inner_own] + late_far[:, inner_own:inner]
        write_read_home = late_sum[:, inner : inner + 2 * STATE] + late_far[:, inner : inner + 2 * STATE]
        write_read_home = write_read_home + swap(write_read_home, 1)
        steps_at = inner + 2 * STATE
        step_home = late_sum[:, steps_at : steps_at + heads_own] + late_far[:, steps_at + heads_own : steps_at + heads]
        cross_rows = cross_part + swap(cross_part, 1)
        cross_far = swap(cross_rows, 2)
        smalls = everywhere(pack([by_head, by_all]))
        parts = unpack(smalls[: by_head.size], head_shapes)
        away = [lax.slice_in_dim(p, p.shape[-1] // 2, p.shape[-1], axis=p.ndim - 1) for p in parts]
        far_parts = unpack(swap(pack(away), 2), small_shapes)
        shared = smalls[by_head.size :]
        shared = shared + swap(shared, 1)
        shared = shared + swap(shared, 2)
        homes = [
            lax.slice_in_dim(p, 0, p.shape[-1] // 2, axis=p.ndim - 1) + a for p, a in zip(parts, far_parts)
        ]
        wr_taps, wr_bias, gain_all = unpack(shared, shared_shapes)
        grad_norm_gain = lax.dynamic_slice_in_dim(gain_all, place * width_here, width_here, 0)

    own_gain = norm_gain.astype(F32)
    own_scale = both_halves(
        in_scale.reshape(slots, seq_here, 1), other_scale.reshape(slots, seq_here, 1)
    )
    own_hat = hidden_in.astype(F32) * own_scale
    grad_hat_in = grad_normed * own_gain
    cross_in = both_halves(
        cross_rows.reshape(slots, seq_here, 1), cross_far.reshape(slots, seq_here, 1)
    ) / width
    grad_hidden_in = own_scale * (grad_hat_in - own_hat * cross_in) + out_cotangent.astype(F32)
    return (
        hidden_out,
        grad_hidden_in,
        grad_norm_gain,
        jnp.stack([grad_gate_home, grad_inner_home], axis=1),
        write_read_home,
        step_home,
        homes[0],
        homes[1],
        wr_taps,
        wr_bias,
        homes[3],
        homes[4],
        homes[5],
        homes[2],
        grad_out_home,
    )


def solution(mesh):
    rows = ("fsdp", "ctx")
    acts = P("fsdp", "ctx", "tp")
    placed = (
        acts,
        P("fsdp"),
        P("tp"),
        P(rows, None, "tp"),
        P(rows, None),
        P(rows, "tp"),
        P(None, "tp"),
        P("tp"),
        P(),
        P(),
        P("tp"),
        P("tp"),
        P("tp"),
        P("tp"),
        P(rows, "tp"),
        acts,
    )
    return jax.shard_map(
        on_device,
        mesh=mesh,
        in_specs=placed,
        out_specs=(
            acts,
            acts,
            P("tp"),
            P(rows, None, "tp"),
            P(rows, None),
            P(rows, "tp"),
            P(None, "tp"),
            P("tp"),
            P(),
            P(),
            P("tp"),
            P("tp"),
            P("tp"),
            P("tp"),
            P(rows, "tp"),
        ),
        check_vma=False,
    )
```

```python
import functools

import jax
import jax.numpy as jnp
from jax import lax
from jax.experimental import pallas as pl
from jax.experimental.pallas import tpu as pltpu
from jax.sharding import PartitionSpec as P

HEADDIM = 64
STATE = 128
CONV = 4
GROUP = 256
INNER = 3072
EPSILON = 1e-05
PAIR = 2 * HEADDIM
HALF = GROUP // 2
HEADS_STEP = 6
LANES_STEP = HEADS_STEP * HEADDIM
GATE_HEADS = 12
GATE_LANES = GATE_HEADS * HEADDIM
F32 = jnp.float32
BF16 = jnp.bfloat16
HIGHEST = lax.Precision.HIGHEST


def swap(x, bit):
    count = lax.axis_size("tp")
    return lax.ppermute(x, "tp", [(i, i ^ bit) for i in range(count)])


def passed_along(x, axis, by):
    count = lax.axis_size(axis)
    pairs = [(i, i + by) for i in range(count) if 0 <= i + by < count]
    return lax.ppermute(x, axis, pairs)


def carried_in(decay, final, combine, reverse):
    count, position = (lax.axis_size("ctx"), lax.axis_index("ctx"))
    if count == 2:
        return passed_along(final.astype(BF16), "ctx", -1 if reverse else 1).astype(F32)
    decays = lax.all_gather(decay.astype(BF16), "ctx").astype(F32)
    finals = lax.all_gather(final.astype(BF16), "ctx")
    start = jnp.zeros_like(final)

    def lap(k, before):
        at = count - 1 - k if reverse else k
        reached = at > position if reverse else at < position
        new = decays[at] * before + finals[at].astype(F32)
        return jnp.where(reached, new, before)

    return lax.fori_loop(0, count, lap, start)


def dot(a, b, da, db):
    return lax.dot_general(a, b, (((da,), (db,)), ((), ())), preferred_element_type=F32)


def low_lanes(rows):
    return lax.broadcasted_iota(jnp.int32, (rows, PAIR), 1) < HEADDIM


def spread_heads(cols, first, low_half):
    return jnp.where(low_half, cols[:, first : first + 1], cols[:, first + 1 : first + 2])


def lower_mask():
    return lax.broadcasted_iota(jnp.int32, (GROUP, GROUP), 0) >= lax.broadcasted_iota(
        jnp.int32, (GROUP, GROUP), 1
    )


def quarter_mask():
    return lax.broadcasted_iota(jnp.int32, (HALF, HALF), 0) >= lax.broadcasted_iota(jnp.int32, (HALF, HALF), 1)


def decays(col, row, mask):
    early = jnp.exp(jnp.where(mask, col[:HALF] - row[:, :HALF], -1e30))
    cross = jnp.exp(col[HALF:] - row[:, :HALF])
    late = jnp.exp(jnp.where(mask, col[HALF:] - row[:, HALF:], -1e30))
    return early, cross, late


def split_dot(ones, values, terms, contract):
    total, rest = None, values
    for _ in range(terms):
        part = rest.astype(BF16)
        rest = rest - part.astype(F32)
        piece = dot(ones, part, contract, 0)
        total = piece if total is None else total + piece
    return total


def turned(cols, heads_before):
    return pltpu.roll(cols, lax.rem(128 - heads_before, 128), 1)


def start_kernel(
    groups, heads,
    inner_ref, rim_ref, narrow_ref, nrim_ref, taps_ref, bias_ref, ntaps_ref, nbias_ref, sbias_ref, rate_ref,
    x_ref, slope_ref, wr_ref, nslope_ref, cols_ref, rows_ref, local_ref, decay_ref,
    ext_ref, next_ref, scaled_ref,
):
    first = lax.rem(pl.program_id(0), groups) == 0

    @pl.when(first)
    def _():
        ext_ref[5:8, :] = rim_ref[0].astype(F32)
        next_ref[5:8, :] = nrim_ref[0].astype(F32)

    @pl.when(jnp.logical_not(first))
    def _():
        ext_ref[0:8, :] = ext_ref[GROUP : GROUP + 8, :]
        next_ref[0:8, :] = next_ref[GROUP : GROUP + 8, :]

    def conv(source, taps, bias, lanes):
        total = bias[:, lanes]
        for k in range(CONV):
            total = total + taps[k : k + 1, lanes] * source[5 + k : 5 + k + GROUP, lanes]
        sig = jax.nn.sigmoid(total)
        return total * sig, sig * (1.0 + total * (1.0 - sig))

    for part in range(2 * STATE // 128):
        lanes = slice(128 * part, 128 * (part + 1))
        next_ref[8 : GROUP + 8, lanes] = narrow_ref[:, lanes].astype(BF16).astype(F32)
        act, slope = conv(next_ref, ntaps_ref, nbias_ref, lanes)
        wr_ref[:, lanes] = act.astype(BF16)
        nslope_ref[:, lanes] = slope

    raw = narrow_ref[:, 2 * STATE :] + sbias_ref[...]
    lane = lax.broadcasted_iota(jnp.int32, (GROUP, 128), 1)
    step = jnp.maximum(raw, 0.0) + jnp.log1p(jnp.exp(-jnp.abs(raw)))
    step = jnp.where(lane < heads, step, 0.0)
    sig = jnp.where(lane < heads, jax.nn.sigmoid(raw), 0.0)
    cum = split_dot(lower_mask().astype(BF16), step * rate_ref[...], 3, 1)
    cols = step + pltpu.roll(cum, heads, 1) + pltpu.roll(sig, 2 * heads, 1)
    cols_ref[...] = cols
    rows_ref[0] = cum.T[:heads]
    last = cum[GROUP - 1 : GROUP, :]
    scale = jnp.exp(last - cum) * step
    decay = jnp.exp(last)
    low_half, low_row = low_lanes(GROUP), low_lanes(1)
    for pair in range(heads // 2):
        lanes = slice(PAIR * pair, PAIR * (pair + 1))
        ext_ref[8 : GROUP + 8, lanes] = inner_ref[:, lanes].astype(F32)
        act, slope = conv(ext_ref, taps_ref, bias_ref, lanes)
        x = act.astype(BF16)
        x_ref[:, lanes] = x
        slope_ref[:, lanes] = slope.astype(BF16)
        scaled_ref[:, lanes] = (x.astype(F32) * spread_heads(scale, 2 * pair, low_half)).astype(BF16)
        decay_ref[0, :, lanes] = spread_heads(decay, 2 * pair, low_row)
    local_ref[0] = dot(wr_ref[:, :STATE], scaled_ref[...], 0, 0)


def start_blocks(inner_pre, rim, narrow, nrim, taps, bias, ntaps, nbias, sbias, rate, groups, heads):
    tokens, width = inner_pre.shape
    blocks = tokens // GROUP
    rows = lambda w: pl.BlockSpec((GROUP, w), lambda b: (b, 0))
    whole = lambda x: pl.BlockSpec(x.shape, lambda b: (0,) * x.ndim)
    return pl.pallas_call(
        functools.partial(start_kernel, groups, heads),
        grid=(blocks,),
        in_specs=[
            rows(width),
            pl.BlockSpec((1, CONV - 1, width), lambda b: (b // groups, 0, 0)),
            rows(narrow.shape[1]),
            pl.BlockSpec((1, CONV - 1, 2 * STATE), lambda b: (b // groups, 0, 0)),
            whole(taps), whole(bias), whole(ntaps), whole(nbias), whole(sbias), whole(rate),
        ],
        out_specs=[
            rows(width), rows(width), rows(2 * STATE), rows(2 * STATE), rows(128),
            pl.BlockSpec((1, heads, GROUP), lambda b: (b, 0, 0)),
            pl.BlockSpec((1, STATE, width), lambda b: (b, 0, 0)),
            pl.BlockSpec((1, 1, width), lambda b: (b, 0, 0)),
        ],
        out_shape=[
            jax.ShapeDtypeStruct((tokens, width), BF16),
            jax.ShapeDtypeStruct((tokens, width), BF16),
            jax.ShapeDtypeStruct((tokens, 2 * STATE), BF16),
            jax.ShapeDtypeStruct((tokens, 2 * STATE), F32),
            jax.ShapeDtypeStruct((tokens, 128), F32),
            jax.ShapeDtypeStruct((blocks, heads, GROUP), F32),
            jax.ShapeDtypeStruct((blocks, STATE, width), F32),
            jax.ShapeDtypeStruct((blocks, 1, width), F32),
        ],
        scratch_shapes=[
            pltpu.VMEM((GROUP + 8, width), F32),
            pltpu.VMEM((GROUP + 8, 2 * STATE), F32),
            pltpu.VMEM((GROUP, width), BF16),
        ],
        cost_estimate=pl.CostEstimate(
            flops=2 * tokens * STATE * width + 20 * tokens * width,
            bytes_accessed=tokens * width * 6 + blocks * STATE * width * 4,
            transcendentals=tokens * width,
        ),
        name="start_blocks",
    )(inner_pre, rim, narrow, nrim, taps, bias, ntaps, nbias, sbias, rate)


def mix_kernel(
    heads,
    x_ref, gate_ref, gno_ref, wr_ref, cols_ref, rows_ref, state_ref, skip_ref, gain_ref,
    mixed_ref, stats_ref, scores_ref, sums_ref,
):
    g = pl.program_id(1)

    @pl.when(g == 0)
    def _():
        scores_ref[...] = dot(wr_ref[:, STATE:], wr_ref[:, :STATE], 1, 1)
        sums_ref[...] = jnp.zeros_like(sums_ref)

    cols = turned(cols_ref[...], g * GATE_HEADS)
    grown = jnp.exp(cols)
    low_half = low_lanes(GROUP)
    mask = quarter_mask()
    squares = jnp.zeros((GROUP, 1), F32)
    crosses = jnp.zeros((GROUP, 1), F32)
    for pair in range(GATE_HEADS // 2):
        lanes = slice(PAIR * pair, PAIR * (pair + 1))
        x = x_ref[:, lanes].astype(F32)
        stepped = x * spread_heads(cols, 2 * pair, low_half)
        halves = (
            jnp.where(low_half, stepped, 0.0).astype(BF16),
            jnp.where(low_half, 0.0, stepped).astype(BF16),
        )
        total = dot(wr_ref[:, STATE:], state_ref[0, :, lanes], 1, 0)
        total = total * spread_heads(grown, heads + 2 * pair, low_half)
        top = jnp.zeros((HALF, PAIR), F32)
        bottom = jnp.zeros((HALF, PAIR), F32)
        for side in range(2):
            head = 2 * pair + side
            row = rows_ref[0, pl.ds(g * GATE_HEADS + head, 1), :]
            early, cross, late = decays(cols[:, heads + head : heads + head + 1], row, mask)
            upper = (scores_ref[:HALF, :HALF] * early).astype(BF16)
            under = jnp.concatenate(
                [
                    (scores_ref[HALF:, :HALF] * cross).astype(BF16),
                    (scores_ref[HALF:, HALF:] * late).astype(BF16),
                ],
                axis=1,
            )
            top = top + dot(upper, halves[side][:HALF], 1, 0)
            bottom = bottom + dot(under, halves[side], 1, 0)
        total = total + jnp.concatenate([top, bottom], axis=0)
        mixed = total + skip_ref[:, lanes] * x
        mixed_ref[:, lanes] = mixed
        gate = gate_ref[:, lanes].astype(F32)
        gated = mixed * (gate * jax.nn.sigmoid(gate))
        squares = squares + jnp.sum(gated * gated, axis=1, keepdims=True)
        grad_hat = gno_ref[:, lanes].astype(F32) * gain_ref[:, lanes]
        crosses = crosses + jnp.sum(gated * grad_hat, axis=1, keepdims=True)
    lane = lax.broadcasted_iota(jnp.int32, (GROUP, 128), 1)
    sums_ref[...] += jnp.where(lane == 0, squares, jnp.where(lane == 1, crosses, 0.0))

    @pl.when(g == pl.num_programs(1) - 1)
    def _():
        stats_ref[0] = sums_ref[...].T[:8]


def mix_blocks(x, gate, gno, wr, cols, rows, states, skip, gain):
    tokens, width = x.shape
    blocks, steps, heads = tokens // GROUP, width // GATE_LANES, rows.shape[1]
    wide = pl.BlockSpec((GROUP, GATE_LANES), lambda b, g: (b, g))
    line = pl.BlockSpec((1, GATE_LANES), lambda b, g: (0, g))
    return pl.pallas_call(
        functools.partial(mix_kernel, heads),
        grid=(blocks, steps),
        in_specs=[
            wide, wide, wide,
            pl.BlockSpec((GROUP, 2 * STATE), lambda b, g: (b, 0)),
            pl.BlockSpec((GROUP, 128), lambda b, g: (b, 0)),
            pl.BlockSpec((1, heads, GROUP), lambda b, g: (b, 0, 0)),
            pl.BlockSpec((1, STATE, GATE_LANES), lambda b, g: (b, 0, g)),
            line, line,
        ],
        out_specs=[wide, pl.BlockSpec((1, 8, GROUP), lambda b, g: (b, 0, 0))],
        out_shape=[
            jax.ShapeDtypeStruct((tokens, width), F32),
            jax.ShapeDtypeStruct((blocks, 8, GROUP), F32),
        ],
        scratch_shapes=[pltpu.VMEM((GROUP, GROUP), F32), pltpu.VMEM((GROUP, 128), F32)],
        cost_estimate=pl.CostEstimate(
            flops=2 * tokens * width * (2 * GROUP + 2 * STATE) * 2,
            bytes_accessed=tokens * width * 10,
            transcendentals=tokens * GROUP * width // HEADDIM,
        ),
        name="mix_blocks",
    )(x, gate, gno, wr, cols, rows, states, skip, gain)


def gate_kernel(
    heads,
    mixed_ref, gate_ref, gno_ref, x_ref, stats_ref, gain_ref, wr_ref, cols_ref,
    normed_ref, ggate_ref, gdiag_ref, gain_sum_ref, skip_sum_ref, flow_ref, scaled_ref,
):
    @pl.when(pl.program_id(1) == 0)
    def _():
        gain_sum_ref[...] = jnp.zeros_like(gain_sum_ref)
        skip_sum_ref[...] = jnp.zeros_like(skip_sum_ref)

    stats = stats_ref[0].T
    scale = lax.rsqrt(stats[:, 0:1] / INNER + EPSILON)
    cross = scale * stats[:, 1:2] / INNER
    grown = jnp.exp(turned(cols_ref[...], pl.program_id(0) * GATE_HEADS))
    low_half = low_lanes(GROUP)
    for pair in range(GATE_HEADS // 2):
        lanes = slice(PAIR * pair, PAIR * (pair + 1))
        mixed = mixed_ref[:, lanes]
        gate = gate_ref[:, lanes].astype(F32)
        gno = gno_ref[:, lanes].astype(F32)
        gain = gain_ref[:, lanes]
        sig = jax.nn.sigmoid(gate)
        act = gate * sig
        hat = mixed * act * scale
        normed_ref[:, lanes] = (hat * gain).astype(BF16)
        gain_sum_ref[:, lanes] += jnp.sum(gno * hat, axis=0, keepdims=True)
        grad_gated = scale * (gno * gain - hat * cross)
        grad_mixed = grad_gated * act
        ggate_ref[:, lanes] = (grad_gated * mixed * sig * (1.0 + gate * (1.0 - sig))).astype(BF16)
        skip_sum_ref[:, lanes] += jnp.sum(grad_mixed * x_ref[:, lanes].astype(F32), axis=0, keepdims=True)
        diag = grad_mixed.astype(BF16)
        gdiag_ref[:, lanes] = diag
        scaled = diag.astype(F32) * spread_heads(grown, heads + 2 * pair, low_half)
        scaled_ref[:, lanes] = scaled.astype(BF16)
    flow_ref[0] = dot(wr_ref[...], scaled_ref[...], 0, 0)


def gate_blocks(mixed, gate, gno, x, stats, gain, wr, cols, heads):
    tokens, width = x.shape
    blocks, steps = tokens // GROUP, width // GATE_LANES
    wide = pl.BlockSpec((GROUP, GATE_LANES), lambda g, b: (b, g))
    line = pl.BlockSpec((1, GATE_LANES), lambda g, b: (0, g))
    return pl.pallas_call(
        functools.partial(gate_kernel, heads),
        grid=(steps, blocks),
        in_specs=[
            wide, wide, wide, wide,
            pl.BlockSpec((1, 8, GROUP), lambda g, b: (b, 0, 0)),
            line,
            pl.BlockSpec((GROUP, STATE), lambda g, b: (b, 1)),
            pl.BlockSpec((GROUP, 128), lambda g, b: (b, 0)),
        ],
        out_specs=[
            wide, wide, wide, line, line,
            pl.BlockSpec((1, STATE, GATE_LANES), lambda g, b: (b, 0, g)),
        ],
        out_shape=[
            jax.ShapeDtypeStruct((tokens, width), BF16),
            jax.ShapeDtypeStruct((tokens, width), BF16),
            jax.ShapeDtypeStruct((tokens, width), BF16),
            jax.ShapeDtypeStruct((1, width), F32),
            jax.ShapeDtypeStruct((1, width), F32),
            jax.ShapeDtypeStruct((blocks, STATE, width), F32),
        ],
        scratch_shapes=[pltpu.VMEM((GROUP, GATE_LANES), BF16)],
        cost_estimate=pl.CostEstimate(
            flops=2 * tokens * STATE * width,
            bytes_accessed=tokens * width * 16 + blocks * STATE * width * 4,
            transcendentals=tokens * width,
        ),
        name="gate_blocks",
    )(mixed, gate, gno, x, stats, gain, wr, cols)


def back_kernel(
    groups, heads,
    x_ref, mixed_ref, grad_ref, slope_ref, pre_ref, rim_ref, wr_ref, nslope_ref, npre_ref, nrim_ref,
    cols_ref, rows_ref, state_ref, flow_ref, skip_ref, taps_ref, ntaps_ref, rate_ref,
    gpre_ref, gnarrow_ref, sums_ref, nsums_ref, hsums_ref, halo_ref, nhalo_ref,
    scores_ref, gscores_ref, prod_ref, gw_ref, gr_ref, u_ref, v_ref, i_ref, e_ref, ext_ref, next_ref, head_ref,
):
    step_id, g = pl.program_id(0), pl.program_id(1)
    block = pl.num_programs(0) - 1 - step_id
    last_of_slot = lax.rem(block, groups) == groups - 1
    first_of_slot = lax.rem(block, groups) == 0

    @pl.when(g == 0)
    def _():
        scores_ref[...] = dot(wr_ref[:, STATE:], wr_ref[:, :STATE], 1, 1)
        for ref in (gscores_ref, gw_ref, gr_ref, u_ref, v_ref, i_ref, e_ref):
            ref[...] = jnp.zeros_like(ref)

    @pl.when(jnp.logical_and(g == 0, step_id == 0))
    def _():
        sums_ref[...] = jnp.zeros_like(sums_ref)
        nsums_ref[...] = jnp.zeros_like(nsums_ref)
        hsums_ref[...] = jnp.zeros_like(hsums_ref)

    @pl.when(last_of_slot)
    def _():
        ext_ref[g, GROUP : GROUP + 8, :] = jnp.zeros((8, LANES_STEP), F32)
        next_ref[GROUP : GROUP + 8, :] = jnp.zeros((8, 2 * STATE), F32)

    @pl.when(jnp.logical_not(last_of_slot))
    def _():
        ext_ref[g, GROUP : GROUP + 8, :] = ext_ref[g, 0:8, :]

        @pl.when(g == 0)
        def _():
            next_ref[GROUP : GROUP + 8, :] = next_ref[0:8, :]

    cols = turned(cols_ref[...], g * HEADS_STEP)
    grown = jnp.exp(cols)
    shrunk = jnp.exp(cols[GROUP - 1 : GROUP, :] - cols)
    low_half = low_lanes(GROUP)
    mask = quarter_mask()
    grad_write = jnp.zeros((GROUP, STATE), F32)
    grad_read = jnp.zeros((GROUP, STATE), F32)
    for pair in range(HEADS_STEP // 2):
        lanes = slice(PAIR * pair, PAIR * (pair + 1))
        x = x_ref[:, lanes].astype(F32)
        grad = grad_ref[:, lanes]
        grad_f = grad.astype(F32)
        skip = skip_ref[:, lanes]
        steps = spread_heads(cols, 2 * pair, low_half)
        tail = spread_heads(shrunk, heads + 2 * pair, low_half)
        stepped = x * steps
        x_halves = (
            jnp.where(low_half, stepped, 0.0).astype(BF16),
            jnp.where(low_half, 0.0, stepped).astype(BF16),
        )
        g_halves = (
            jnp.where(low_half, grad_f, 0.0).astype(BF16),
            jnp.where(low_half, 0.0, grad_f).astype(BF16),
        )
        flow = flow_ref[0, :, lanes]
        state = state_ref[0, :, lanes]
        e_ref[0:1, lanes] = jnp.sum(flow.astype(F32) * state.astype(F32), axis=0, keepdims=True)
        scaled = (grad_f * spread_heads(grown, heads + 2 * pair, low_half)).astype(BF16)
        grad_read = grad_read + dot(scaled, state, 1, 1)
        grad_write = grad_write + dot((stepped * tail).astype(BF16), flow, 1, 1)
        stepped_low = stepped.astype(BF16).astype(F32)
        inter = dot(wr_ref[:, :STATE], flow, 1, 0) * tail
        top = jnp.zeros((HALF, PAIR), F32)
        bottom = jnp.zeros((HALF, PAIR), F32)
        for side in range(2):
            head = 2 * pair + side
            row = rows_ref[0, pl.ds(g * HEADS_STEP + head, 1), :]
            early, cross, late = decays(cols[:, heads + head : heads + head + 1], row, mask)
            left = jnp.concatenate(
                [
                    (scores_ref[:HALF, :HALF] * early).astype(BF16),
                    (scores_ref[HALF:, :HALF] * cross).astype(BF16),
                ],
                axis=0,
            )
            right = (scores_ref[HALF:, HALF:] * late).astype(BF16)
            top = top + dot(left, g_halves[side], 0, 0)
            bottom = bottom + dot(right, g_halves[side][HALF:], 0, 0)
            under = dot(grad[HALF:], x_halves[side], 1, 1)
            terms = (
                dot(grad[:HALF], x_halves[side][:HALF], 1, 1) * early, under[:, :HALF] * cross, under[:, HALF:] * late,
            )
            quarters = terms if side == 0 else tuple(a + b for a, b in zip(quarters, terms))
        gscores_ref[:HALF, :HALF] += quarters[0]
        gscores_ref[HALF:, :HALF] += quarters[1]
        gscores_ref[HALF:, HALF:] += quarters[2]
        total = jnp.concatenate([top, bottom], axis=0)
        both = total + inter
        prod_ref[0, :, lanes] = x * both
        prod_ref[1, :, lanes] = grad_f * (mixed_ref[:, lanes] - skip * x) - stepped_low * total
        prod_ref[2, :, lanes] = stepped_low * inter
        grad_conv = (steps * both + skip * grad_f) * slope_ref[:, lanes].astype(F32)
        ext_ref[g, 0:GROUP, lanes] = grad_conv
        pre = pre_ref[:, lanes].astype(F32)
        total_pre = jnp.zeros_like(grad_conv)
        for j in range(CONV):
            moved = ext_ref[g, j : j + GROUP, lanes]
            total_pre = total_pre + taps_ref[CONV - 1 - j : CONV - j, lanes] * moved
            sums_ref[g, CONV - 1 - j : CONV - j, lanes] += jnp.sum(pre * moved, axis=0, keepdims=True)
        sums_ref[g, CONV : CONV + 1, lanes] += jnp.sum(grad_conv, axis=0, keepdims=True)
        gpre_ref[:, lanes] = total_pre.astype(BF16)

    @pl.when(first_of_slot)
    def _():
        head_ref[0:8, :LANES_STEP] = jnp.zeros((8, LANES_STEP), F32)
        head_ref[8:16, :LANES_STEP] = ext_ref[g, 0:8, :]
        halo = jnp.zeros((8, LANES_STEP), F32)
        for j in range(CONV):
            moved = head_ref[j : j + 8, :LANES_STEP]
            halo = halo + taps_ref[CONV - 1 - j : CONV - j, :] * moved
            sums_ref[g, CONV - 1 - j : CONV - j, :] += jnp.sum(
                rim_ref[0].astype(F32) * moved[5:8], axis=0, keepdims=True
            )
        halo_ref[0] = halo

    chosen_rows = lax.broadcasted_iota(jnp.int32, (LANES_STEP, 128), 0) // HEADDIM + g * HEADS_STEP
    chosen = (chosen_rows == lax.broadcasted_iota(jnp.int32, (LANES_STEP, 128), 1)).astype(BF16)

    def sums_of(values, terms):
        total, rest = None, values
        for _ in range(terms):
            part = rest.astype(BF16)
            rest = rest - part.astype(F32)
            piece = dot(part, chosen, 1, 0)
            total = piece if total is None else total + piece
        return total

    u_ref[...] += sums_of(prod_ref[0], 2)
    v_ref[...] += sums_of(prod_ref[1], 2)
    i_ref[...] += sums_of(prod_ref[2], 2)
    e_ref[8:16, 0:128] += sums_of(e_ref[0:8, :], 2)
    gw_ref[...] += grad_write
    gr_ref[...] += grad_read

    @pl.when(g == pl.num_programs(1) - 1)
    def _():
        low = gscores_ref[...].astype(BF16)
        gradient = (
            gw_ref[...] + dot(low, wr_ref[:, STATE:], 0, 0),
            gr_ref[...] + dot(low, wr_ref[:, :STATE], 1, 0),
        )
        for part in range(2):
            lanes = slice(STATE * part, STATE * (part + 1))
            grad_conv = gradient[part] * nslope_ref[:, lanes]
            next_ref[0:GROUP, lanes] = grad_conv
            pre = npre_ref[:, lanes].astype(BF16).astype(F32)
            total_pre = jnp.zeros_like(grad_conv)
            for j in range(CONV):
                moved = next_ref[j : j + GROUP, lanes]
                total_pre = total_pre + ntaps_ref[CONV - 1 - j : CONV - j, lanes] * moved
                nsums_ref[CONV - 1 - j : CONV - j, lanes] += jnp.sum(pre * moved, axis=0, keepdims=True)
            nsums_ref[CONV : CONV + 1, lanes] += jnp.sum(grad_conv, axis=0, keepdims=True)
            gnarrow_ref[:, lanes] = total_pre.astype(BF16)

        @pl.when(first_of_slot)
        def _():
            head_ref[0:8, : 2 * STATE] = jnp.zeros((8, 2 * STATE), F32)
            head_ref[8:16, : 2 * STATE] = next_ref[0:8, :]
            halo = jnp.zeros((8, 2 * STATE), F32)
            for j in range(CONV):
                moved = head_ref[j : j + 8, : 2 * STATE]
                halo = halo + ntaps_ref[CONV - 1 - j : CONV - j, :] * moved
                nsums_ref[CONV - 1 - j : CONV - j, :] += jnp.sum(
                    nrim_ref[0].astype(F32) * moved[5:8], axis=0, keepdims=True
                )
            nhalo_ref[0] = halo

        own = cols_ref[...]
        lane = lax.broadcasted_iota(jnp.int32, (GROUP, 128), 1)
        step = jnp.where(lane < heads, own, 0.0)
        cum = pltpu.roll(own, 128 - heads, 1)
        sig = jnp.where(lane < heads, pltpu.roll(own, 128 - 2 * heads, 1), 0.0)
        strict = lax.broadcasted_iota(jnp.int32, (GROUP, GROUP), 0) > lax.broadcasted_iota(
            jnp.int32, (GROUP, GROUP), 1
        )
        reverse_sum = (
            split_dot(lower_mask().astype(BF16), v_ref[...], 2, 0)
            + split_dot(strict.astype(BF16), i_ref[...], 2, 1)
            + jnp.exp(cum[GROUP - 1 : GROUP, :]) * e_ref[8:9, 0:128]
        )
        grad_raw = (u_ref[...] + rate_ref[...] * reverse_sum) * sig
        gnarrow_ref[:, 2 * STATE :] = grad_raw.astype(BF16)
        hsums_ref[0:1, :] += jnp.sum(grad_raw, axis=0, keepdims=True)
        hsums_ref[1:2, :] += jnp.sum(reverse_sum * step, axis=0, keepdims=True) * rate_ref[...]


def back_blocks(
    x, mixed, grad, slope, pre, rim, wr, nslope, npre, nrim, cols, rows, states, flows, skip, taps, ntaps, rate, groups
):
    tokens, width = x.shape
    blocks, steps, heads, slots = tokens // GROUP, width // LANES_STEP, rows.shape[1], rim.shape[0]
    at = lambda b: blocks - 1 - b
    wide = pl.BlockSpec((GROUP, LANES_STEP), lambda b, g: (at(b), g))
    narrow = lambda w: pl.BlockSpec((GROUP, w), lambda b, g: (at(b), 0))
    state = pl.BlockSpec((1, STATE, LANES_STEP), lambda b, g: (at(b), 0, g))
    line = lambda n: pl.BlockSpec((n, LANES_STEP), lambda b, g: (0, g))
    whole = lambda shape: pl.BlockSpec(shape, lambda b, g: (0,) * len(shape))
    return pl.pallas_call(
        functools.partial(back_kernel, groups, heads),
        grid=(blocks, steps),
        in_specs=[
            wide, wide, wide, wide, wide,
            pl.BlockSpec((1, CONV - 1, LANES_STEP), lambda b, g: (at(b) // groups, 0, g)),
            narrow(2 * STATE), narrow(2 * STATE), narrow(npre.shape[1]),
            pl.BlockSpec((1, CONV - 1, 2 * STATE), lambda b, g: (at(b) // groups, 0, 0)),
            narrow(128),
            pl.BlockSpec((1, heads, GROUP), lambda b, g: (at(b), 0, 0)),
            state, state, line(1), line(CONV), whole((CONV, 2 * STATE)), whole((1, 128)),
        ],
        out_specs=[
            wide, narrow(2 * STATE + 128),
            whole((steps, 8, LANES_STEP)), whole((8, 2 * STATE)), whole((8, 128)),
            pl.BlockSpec((1, 8, LANES_STEP), lambda b, g: (at(b) // groups, 0, g)),
            pl.BlockSpec((1, 8, 2 * STATE), lambda b, g: (at(b) // groups, 0, 0)),
        ],
        out_shape=[
            jax.ShapeDtypeStruct((tokens, width), BF16),
            jax.ShapeDtypeStruct((tokens, 2 * STATE + 128), BF16),
            jax.ShapeDtypeStruct((steps, 8, LANES_STEP), F32),
            jax.ShapeDtypeStruct((8, 2 * STATE), F32),
            jax.ShapeDtypeStruct((8, 128), F32),
            jax.ShapeDtypeStruct((slots, 8, width), F32),
            jax.ShapeDtypeStruct((slots, 8, 2 * STATE), F32),
        ],
        scratch_shapes=[
            pltpu.VMEM((GROUP, GROUP), F32),
            pltpu.VMEM((GROUP, GROUP), F32),
            pltpu.VMEM((3, GROUP, LANES_STEP), F32),
            pltpu.VMEM((GROUP, STATE), F32),
            pltpu.VMEM((GROUP, STATE), F32),
            pltpu.VMEM((GROUP, 128), F32),
            pltpu.VMEM((GROUP, 128), F32),
            pltpu.VMEM((GROUP, 128), F32),
            pltpu.VMEM((16, LANES_STEP), F32),
            pltpu.VMEM((steps, GROUP + 8, LANES_STEP), F32),
            pltpu.VMEM((GROUP + 8, 2 * STATE), F32),
            pltpu.VMEM((16, max(LANES_STEP, 2 * STATE)), F32),
        ],
        cost_estimate=pl.CostEstimate(
            flops=2 * tokens * width * (4 * GROUP + 4 * STATE) * 2,
            bytes_accessed=tokens * width * 14,
            transcendentals=tokens * GROUP * width // HEADDIM,
        ),
        name="back_blocks",
    )(x, mixed, grad, slope, pre, rim, wr, nslope, npre, nrim, cols, rows, states, flows, skip, taps, ntaps, rate)


MESH = pl.DeviceIdType.MESH
FAR_PARTS = 4


def fetch_kernel(
    x_ref, inner_ref, late_ref, step_ref, wr_ref, small_ref,
    full_x, full_inner, late_far, full_step, full_wr, full_small,
    x_own, inner_own, step_own, wr_own, small_own, send_sem, recv_sem, local_sem,
):
    f, c, z = lax.axis_index("fsdp"), lax.axis_index("ctx"), lax.axis_index("tp")
    half = z // 2
    slots, seq, cols = full_x.shape[0], full_x.shape[1], x_ref.shape[2]
    depth = inner_ref.shape[0]
    partners = (
        {"fsdp": f ^ 1}, {"fsdp": f ^ 2}, {"fsdp": f ^ 3}, {"ctx": c ^ 1}, {"tp": z ^ 1}, {"tp": z ^ 2},
    )
    barrier = pltpu.get_barrier_semaphore()
    for partner in partners:
        pl.semaphore_signal(barrier, inc=1, device_id=partner, device_id_type=MESH)
    pl.semaphore_wait(barrier, len(partners))

    copies = []

    def send(src, dst, partner):
        at = len(copies)
        copy = pltpu.make_async_remote_copy(
            src_ref=src, dst_ref=dst, send_sem=send_sem.at[at], recv_sem=recv_sem.at[at],
            device_id=partners[partner], device_id_type=MESH,
        )
        copy.start()
        copies.append([copy, False])
        return at

    def arrived(at):
        copies[at][0].wait_recv()
        copies[at][1] = True

    def feature(which):
        return pl.ds(pl.multiple_of(which * cols, 128), cols)

    def shard(full, row_f, far):
        wide = full.shape[1] // 2
        start = pl.multiple_of((row_f * 2 + c) * depth, depth)
        return full.at[pl.ds(start, depth), pl.ds(far * wide, wide)]

    def shard_one(full, row_f, far):
        start = pl.multiple_of((row_f * 2 + c) * depth, depth)
        return full.at[pl.ds(start, depth), :]

    def spread(full, src, far, part=shard):
        dst = part(full, f, far)
        near = [send(src, dst, k) for k in range(3)]
        send(src, dst, 3)
        return near

    def relay(full, near, far, part=shard):
        for k in range(3):
            arrived(near[k])
            row = part(full, f ^ (k + 1), far)
            send(row, row, 3)

    mine = pl.ds(half * slots, slots)
    other = pl.ds((1 - half) * slots, slots)
    send(small_ref, full_small.at[z], 4)
    far_small = send(small_ref, full_small.at[z], 5)
    send(x_ref.at[mine], full_x.at[:, :, feature(z)], 4)
    far_inner = send(inner_ref, shard(full_inner, f, 1), 5)
    far_step = send(step_ref, shard(full_step, f, 1), 5)
    piece = seq // FAR_PARTS
    far_x = [
        send(x_ref.at[other, pl.ds(piece * i, piece)], full_x.at[:, pl.ds(piece * i, piece), feature(z)], 5)
        for i in range(FAR_PARTS)
    ]
    send(late_ref, late_far, 5)
    own_inner = spread(full_inner, inner_ref, 0)
    own_step = spread(full_step, step_ref, 0)
    own_wr = spread(full_wr, wr_ref, 0, shard_one)

    staged = (
        (x_ref.at[mine], x_own, full_x.at[:, :, feature(z)]),
        (inner_ref, inner_own, shard(full_inner, f, 0)),
        (step_ref, step_own, shard(full_step, f, 0)),
        (wr_ref, wr_own, shard_one(full_wr, f, 0)),
        (small_ref, small_own, full_small.at[z]),
    )
    loads = [pltpu.make_async_copy(src, buf, local_sem.at[0, i]) for i, (src, buf, _) in enumerate(staged)]
    stores = [pltpu.make_async_copy(buf, dst, local_sem.at[1, i]) for i, (_, buf, dst) in enumerate(staged)]
    for load in loads:
        load.start()
    for load, store in zip(loads, stores):
        load.wait()
        store.start()

    arrived(far_small)
    send(full_small.at[z ^ 2], full_small.at[z ^ 2], 4)
    arrived(far_inner)
    away_inner = spread(full_inner, shard(full_inner, f, 1), 1)
    arrived(far_step)
    away_step = spread(full_step, shard(full_step, f, 1), 1)

    def both(i):
        arrived(far_x[i])
        part = full_x.at[:, pl.ds(piece * i, piece), feature(z ^ 2)]
        send(part, part, 4)

    relay(full_inner, own_inner, 0)
    relay(full_step, own_step, 0)
    relay(full_wr, own_wr, 0, shard_one)
    both(0)
    relay(full_inner, away_inner, 1)
    relay(full_step, away_step, 1)
    both(1)
    both(2)
    both(3)
    for store in stores:
        store.wait()
    for copy, done in copies:
        if not done:
            copy.wait_recv()
        copy.wait_send()


def fetch(hidden, inner, late, step, wr, small):
    slot_count, seq, cols = hidden.shape
    slots, depth = slot_count // 2, inner.shape[0]
    total = 8 * depth
    count = 1 + 2 * FAR_PARTS + 3 + 5 * 7 + 3
    anywhere = pl.BlockSpec(memory_space=pl.ANY)
    full = lambda x: jax.ShapeDtypeStruct((total, 2 * x.shape[1]), BF16)
    return pl.pallas_call(
        fetch_kernel,
        in_specs=[anywhere] * 6,
        out_specs=[anywhere] * 6,
        out_shape=[
            jax.ShapeDtypeStruct((slots, seq, 4 * cols), BF16),
            full(inner), jax.ShapeDtypeStruct(late.shape, BF16), full(step),
            jax.ShapeDtypeStruct((total, wr.shape[1]), BF16),
            jax.ShapeDtypeStruct((4,) + small.shape, F32),
        ],
        scratch_shapes=[
            pltpu.VMEM((slots, seq, cols), BF16),
            pltpu.VMEM(inner.shape, BF16),
            pltpu.VMEM(step.shape, BF16),
            pltpu.VMEM(wr.shape, BF16),
            pltpu.VMEM(small.shape, F32),
            pltpu.SemaphoreType.DMA((count,)),
            pltpu.SemaphoreType.DMA((count,)),
            pltpu.SemaphoreType.DMA((2, 5)),
        ],
        compiler_params=pltpu.CompilerParams(collective_id=0, has_side_effects=True),
        name="fetch",
    )(hidden, inner, late, step, wr, small)


def finish_kernel(
    part_ref, relay_ref, grad_ref, core_ref, small_ref, cross_ref,
    near_out, other_out, home_out, narrow_out, small_out, small_far, cross_out, cross_far,
    relay_buf, part_buf, sum_buf, core_buf, own_buf, plane_buf, got_buf, sent_buf, home_buf, wr_send, wr_got,
    small_got, cross_got, send_sem, recv_sem, load_sem,
):
    f, c, z = lax.axis_index("fsdp"), lax.axis_index("ctx"), lax.axis_index("tp")
    tokens, cols = near_out.shape
    depth, inner = home_out.shape
    partners = (
        {"fsdp": f ^ 1}, {"fsdp": f ^ 2}, {"fsdp": f ^ 3}, {"ctx": c ^ 1}, {"tp": z ^ 1}, {"tp": z ^ 2},
    )
    barrier = pltpu.get_barrier_semaphore()
    for partner in partners:
        pl.semaphore_signal(barrier, inc=1, device_id=partner, device_id_type=MESH)

    def feature(which):
        return pl.ds(pl.multiple_of(which * cols, 128), cols)

    def rows_of(row_f, core):
        return pl.ds(pl.multiple_of((row_f * 2 + core) * depth, depth), depth)

    piece = tokens // FAR_PARTS
    loads = [
        pltpu.make_async_copy(grad_ref.at[rows_of(f ^ k, c)], own_buf.at[k], load_sem.at[k]) for k in range(4)
    ] + [
        pltpu.make_async_copy(core_ref.at[f ^ k], core_buf.at[k], load_sem.at[4 + k]) for k in range(4)
    ] + [
        pltpu.make_async_copy(relay_ref.at[pl.ds(piece * i, piece)], relay_buf.at[i], load_sem.at[8 + i])
        for i in range(FAR_PARTS)
    ] + [
        pltpu.make_async_copy(
            part_ref.at[pl.ds(piece * i, piece), feature(z ^ 2)], part_buf.at[i], load_sem.at[8 + FAR_PARTS + i]
        )
        for i in range(FAR_PARTS)
    ]
    for load in loads:
        load.start()
    pl.semaphore_wait(barrier, len(partners))

    copies = []

    def send(src, dst, partner):
        at = len(copies)
        copy = pltpu.make_async_remote_copy(
            src_ref=src, dst_ref=dst, send_sem=send_sem.at[at], recv_sem=recv_sem.at[at],
            device_id=partners[partner], device_id_type=MESH,
        )
        copy.start()
        copies.append([copy, False])
        return at

    def arrived(at):
        copies[at][0].wait_recv()
        copies[at][1] = True

    small = [send(small_ref, small_got.at[0], 3)]
    cross = [send(cross_ref, cross_got, 4)]
    def passed_on(i):
        loads[8 + i].wait()
        loads[8 + FAR_PARTS + i].wait()
        sum_buf[i] = (part_buf[i].astype(F32) + relay_buf[i].astype(F32)).astype(BF16)
        send(sum_buf.at[i], other_out.at[pl.ds(piece * i, piece)], 5)

    for load in loads[:8]:
        load.wait()
    arrived(small[0])
    small_out[...] = small_ref[...] + small_got[0]
    small.append(send(small_out, small_got.at[1], 0))
    arrived(cross[0])
    cross_out[...] = cross_ref[...] + cross_got[...]
    cross.append(send(cross_out, cross_far, 5))
    for k in (1, 2, 3):
        sent_buf[k - 1] = (own_buf[k].astype(F32) + core_buf[k].astype(F32)).astype(BF16)
    passed_on(0)
    arrived(small[1])
    copies[small[1]][0].wait_send()
    small_out[...] = small_out[...] + small_got[1]
    small.append(send(small_out, small_got.at[2], 1))
    plane = [send(sent_buf.at[k], plane_buf.at[k], k) for k in range(3)]
    for i in range(1, FAR_PARTS):
        passed_on(i)
    arrived(small[2])
    copies[small[2]][0].wait_send()
    small_out[...] = small_out[...] + small_got[2]
    small.append(send(small_out, small_got.at[3], 4))
    middle = tokens // 2
    send(part_ref.at[pl.ds(0, middle), feature(z ^ 1)], near_out.at[pl.ds(0, middle)], 4)
    arrived(small[3])
    copies[small[3]][0].wait_send()
    shared = small_out.shape[0] // 2
    small_out[shared:, :] = small_out[shared:, :] + small_got[3, shared:, :]
    small.append(send(small_out, small_far, 5))
    total = own_buf[0].astype(F32) + core_buf[0].astype(F32)
    for at in plane:
        arrived(at)
    for k in range(3):
        total = total + plane_buf[k].astype(F32)
    wr_send[...] = total[:, 2 * inner : 2 * inner + 2 * STATE]
    wr = send(wr_send, wr_got, 4)
    home_out[...] = total[:, :inner]
    home_buf[:, :inner] = total[:, inner : 2 * inner].astype(BF16)
    narrow_out[:, 2 * STATE : 2 * STATE + 128] = total[:, 2 * inner + 2 * STATE :]
    home_buf[:, inner + 2 * STATE :] = total[:, 2 * inner + 2 * STATE :].astype(BF16)
    arrived(wr)
    both = wr_send[...] + wr_got[...]
    narrow_out[:, : 2 * STATE] = both
    home_buf[:, inner : inner + 2 * STATE] = both.astype(BF16)
    last = send(home_buf, got_buf, 5)
    send(part_ref.at[pl.ds(middle, middle), feature(z ^ 1)], near_out.at[pl.ds(middle, middle)], 4)
    arrived(last)
    home_out[...] += got_buf[:, :inner].astype(F32)
    narrow_out[:, : 2 * STATE] += got_buf[:, inner : inner + 2 * STATE].astype(F32)
    steps = got_buf[:, inner + 2 * STATE :].astype(F32)
    narrow_out[:, 2 * STATE + 128 :] = steps
    for copy, done in copies:
        if not done:
            copy.wait_recv()
    waited = {small[1], small[2], small[3]}
    for at, (copy, done) in enumerate(copies):
        if at not in waited:
            copy.wait_send()


def finish(part, relay, grad, core, small, cross, depth):
    tokens, width = part.shape
    cols, total = width // 4, grad.shape[1]
    rest = 2 * STATE + 128
    inner = (total - rest) // 2
    anywhere = pl.BlockSpec(memory_space=pl.ANY)
    vmem = pl.BlockSpec(memory_space=pltpu.VMEM)
    count = 5 + 2 + FAR_PARTS + 2 + 3 + 2
    return pl.pallas_call(
        finish_kernel,
        in_specs=[anywhere, anywhere, anywhere, anywhere, vmem, vmem],
        out_specs=[anywhere, anywhere, vmem, vmem, vmem, vmem, vmem, vmem],
        out_shape=[
            jax.ShapeDtypeStruct((tokens, cols), BF16),
            jax.ShapeDtypeStruct((tokens, cols), BF16),
            jax.ShapeDtypeStruct((depth, inner), F32),
            jax.ShapeDtypeStruct((depth, rest + 128), F32),
            jax.ShapeDtypeStruct(small.shape, F32),
            jax.ShapeDtypeStruct(small.shape, F32),
            jax.ShapeDtypeStruct(cross.shape, F32),
            jax.ShapeDtypeStruct(cross.shape, F32),
        ],
        scratch_shapes=[
            pltpu.VMEM((FAR_PARTS, tokens // FAR_PARTS, cols), BF16),
            pltpu.VMEM((FAR_PARTS, tokens // FAR_PARTS, cols), BF16),
            pltpu.VMEM((FAR_PARTS, tokens // FAR_PARTS, cols), BF16),
            pltpu.VMEM((4, depth, total), BF16),
            pltpu.VMEM((4, depth, total), BF16),
            pltpu.VMEM((3, depth, total), BF16),
            pltpu.VMEM((depth, inner + rest), BF16),
            pltpu.VMEM((3, depth, total), BF16),
            pltpu.VMEM((depth, inner + rest), BF16),
            pltpu.VMEM((depth, 2 * STATE), F32),
            pltpu.VMEM((depth, 2 * STATE), F32),
            pltpu.VMEM((4,) + small.shape, F32),
            pltpu.VMEM(cross.shape, F32),
            pltpu.SemaphoreType.DMA((count,)),
            pltpu.SemaphoreType.DMA((count,)),
            pltpu.SemaphoreType.DMA((8 + 2 * FAR_PARTS,)),
        ],
        compiler_params=pltpu.CompilerParams(collective_id=1, has_side_effects=True),
        name="finish",
    )(part, relay, grad, core, small, cross)


def after(x, other):
    return lax.optimization_barrier((x, other))[0]


def everywhere(x):
    for axis in ("ctx", "fsdp"):
        count, bit = lax.axis_size(axis), 1
        if count & (count - 1):
            x = lax.psum(x, axis)
            continue
        while bit < count:
            x = x + lax.ppermute(x, axis, [(i, i ^ bit) for i in range(count)])
            bit *= 2
    return x


def pack(parts):
    return jnp.concatenate([part.reshape(-1) for part in parts])


def unpack(vector, shapes):
    parts, at = [], 0
    for shape in shapes:
        size = 1
        for dim in shape:
            size *= dim
        parts.append(vector[at : at + size].reshape(shape))
        at += size
    return parts


def on_device(
    hidden_in,
    lengths,
    norm_gain,
    proj_gate_inner,
    proj_write_read,
    proj_step,
    conv_inner,
    conv_inner_bias,
    conv_write_read,
    conv_write_read_bias,
    step_bias,
    log_rate,
    skip_gain,
    gate_gain,
    proj_out,
    out_cotangent,
):
    slot_count, seq_here, width_here = hidden_in.shape
    slots = slot_count // 2
    tokens = slots * seq_here
    heads_own = step_bias.shape[0]
    inner_own = gate_gain.shape[0]
    heads = 2 * heads_own
    inner = 2 * inner_own
    tp_count = lax.axis_size("tp")
    width = tp_count * width_here
    groups = seq_here // GROUP
    blocks = slots * groups
    head_steps = heads // HEADS_STEP
    rim_rows = CONV - 1
    place = lax.axis_index("tp")
    far_half, near_side = place // 2, place % 2

    def half_of(whole, which):
        return lax.dynamic_slice_in_dim(whole, which * slots, slots, 0)

    def ordered(own, near, far, both, axis):
        first = lambda a, b: jnp.where(near_side == 0, a, b)
        a0, a1, b0, b1 = first(own, near), first(near, own), first(far, both), first(both, far)
        lower = lambda a, b: jnp.where(far_half == 0, a, b)
        return jnp.concatenate(
            [lower(a0, b0), lower(a1, b1), lower(b0, a0), lower(b1, a1)], axis=axis
        )

    ready = []

    def own_features(piece):
        first, second = piece(place ^ 3).astype(BF16), piece(place ^ 1).astype(BF16)
        relay = swap(first, 1)
        keep = swap(second, 1)
        summed = (piece(place ^ 2) + relay.astype(F32)).astype(BF16)
        ready.extend([first, second, summed])
        sent = swap(summed, 2)
        kept = (piece(place) + keep.astype(F32)).reshape(slots, seq_here, width_here)
        other = sent.astype(F32).reshape(slots, seq_here, width_here)
        return both_halves(kept, other)

    def both_halves(kept, other):
        return jnp.where(
            far_half == 0,
            jnp.concatenate([kept, other], axis=0),
            jnp.concatenate([other, kept], axis=0),
        )

    small_shapes = [(CONV, inner_own), (inner_own,), (inner_own,), (heads_own,), (heads_own,), (heads_own,)]
    def gathered(x):
        return lax.all_gather(x, ("fsdp", "ctx"), axis=0, tiled=True)

    own_small = pack([conv_inner, conv_inner_bias, gate_gain, step_bias, log_rate, skip_gain])
    cot_mine, cot_other = half_of(out_cotangent, far_half), half_of(out_cotangent, 1 - far_half)
    narrow_cols = 2 * STATE + heads
    narrow_pad = -narrow_cols % 128
    zeros = lambda x, extra: jnp.zeros((x.shape[0], extra), BF16)
    inner_shard, gate_shard = proj_gate_inner[:, 1], proj_gate_inner[:, 0]
    if lax.axis_size("fsdp") == 4 and lax.axis_size("ctx") == 2:
        step_shard = jnp.concatenate([proj_step, zeros(proj_step, 128 - heads_own)], axis=1)
        small = pack([norm_gain.astype(F32), own_small])
        small = jnp.pad(small, (0, -small.size % 1024)).reshape(-1, 128)
        late_shard = jnp.concatenate([gate_shard, proj_out], axis=1)
        full_x, full_inner, late_far, full_step, full_wr, full_small = fetch(
            hidden_in, inner_shard, late_shard, step_shard, proj_write_read, small
        )
        gate_far, out_far = late_far[:, :inner_own], late_far[:, inner_own:]
        full_small = full_small.reshape(tp_count, -1)
        full_gain = full_small[:, :width_here].reshape(width)
        far_row = lax.dynamic_slice_in_dim(full_small, place ^ 2, 1, 0)[0, width_here:]
        far_small = unpack(far_row, small_shapes)
        full_narrow = jnp.concatenate(
            [full_wr, full_step[:, :heads_own], full_step[:, 128 : 128 + heads_own], zeros(full_wr, narrow_pad)],
            axis=1,
        )
        cot_dep = full_x
    else:
        x_mine, x_other = half_of(hidden_in, far_half), half_of(hidden_in, 1 - far_half)
        narrow_shard = jnp.concatenate(
            [proj_write_read, proj_step, swap(proj_step, 2), zeros(proj_step, narrow_pad)], axis=1
        )
        inner_far = swap(inner_shard, 2)
        x_near = swap(x_mine, 1)
        x_far = swap(after(x_other, inner_far), 2)
        gate_far = swap(after(gate_shard, x_far), 2)
        x_both = swap(x_far, 1)
        cot_dep = after(x_both, gate_far)
        out_far = swap(after(proj_out, cot_dep), 2)
        full_narrow = gathered(narrow_shard)
        full_inner = gathered(jnp.concatenate([inner_shard, inner_far], axis=1))
        full_x = ordered(x_mine, x_near, x_far, x_both, 2)
        gain = norm_gain.astype(F32)
        full_gain = ordered(gain, swap(gain, 1), swap(gain, 2), swap(gain, 3), 0)
        far_small = unpack(swap(own_small, 2), small_shapes)
    full_x = full_x.reshape(tokens, width)
    full_late = gathered(jnp.concatenate([gate_shard, gate_far, proj_out, out_far], axis=1))
    full_gate, full_out = full_late[:, :inner], full_late[:, inner:]
    cot_mine, cot_other, cot_dep = lax.optimization_barrier((cot_mine, cot_other, cot_dep))
    cot_near, cot_far, cot_both = swap(cot_mine, 1), swap(cot_other, 2), swap(cot_other, 3)
    taps = jnp.concatenate([conv_inner, far_small[0]], axis=1)
    taps_bias = jnp.concatenate([conv_inner_bias, far_small[1]])
    gain_gate = jnp.concatenate([gate_gain, far_small[2]])
    bias_step = jnp.concatenate([step_bias, far_small[3]])
    rate_log = jnp.concatenate([log_rate, far_small[4]])
    gain_skip = jnp.concatenate([skip_gain, far_small[5]])
    rate = -jnp.exp(rate_log)
    skip_lanes = jnp.repeat(gain_skip, HEADDIM)[None]

    in_float = full_x.astype(F32)
    in_scale = lax.rsqrt(jnp.mean(in_float * in_float, axis=-1, keepdims=True) + EPSILON)
    normed = (in_float * in_scale * full_gain.astype(F32)).astype(BF16)
    narrow_pre = dot(normed, full_narrow, 1, 0)
    inner_pre = dot(normed, full_inner, 1, 0).astype(BF16)
    gate_pre = dot(normed, full_gate, 1, 0).astype(BF16)
    cot_near, cot_far, cot_both, gate_pre = lax.optimization_barrier((cot_near, cot_far, cot_both, gate_pre))
    full_cot = ordered(cot_mine, cot_near, cot_far, cot_both, 2).reshape(tokens, width)

    def rim_of(pre):
        by_slot = pre.reshape(slots, seq_here, pre.shape[-1])
        return passed_along(by_slot[:, seq_here - rim_rows :].astype(BF16), "ctx", 1)

    inner_rim, narrow_rim = rim_of(inner_pre), rim_of(narrow_pre[:, : 2 * STATE])
    lane_pad = lambda x: jnp.pad(x, (0, 128 - heads))[None]
    rate_row = lane_pad(rate)
    inner_act, slope, write_read, narrow_slope, cols, cum_rows, local_state, decay_lanes = start_blocks(
        inner_pre, inner_rim, narrow_pre, narrow_rim, taps, taps_bias[None], conv_write_read,
        conv_write_read_bias[None], lane_pad(bias_step), rate_row, groups, heads,
    )
    local_state = local_state.reshape(slots, groups, STATE, inner)
    decay_lanes = decay_lanes.reshape(slots, groups, 1, inner)
    carried = local_state[:, 0]
    device_decay = decay_lanes[:, 0]
    for position in range(1, groups):
        carried = decay_lanes[:, position] * carried + local_state[:, position]
        device_decay = device_decay * decay_lanes[:, position]
    current = carried_in(device_decay, carried, None, False)
    state_list = []
    for position in range(groups):
        state_list.append(current)
        current = decay_lanes[:, position] * current + local_state[:, position]
    states = jnp.stack(state_list, axis=1)
    states_low = states.astype(BF16).reshape(blocks, STATE, inner)

    position_ids = lax.axis_index("ctx") * seq_here + jnp.arange(seq_here)
    valid_rows = (position_ids[None, :] < lengths[:, None]).astype(F32)
    valid_here = half_of(valid_rows, far_half).reshape(tokens, 1)
    masked = (full_cot.astype(F32) * valid_here).astype(BF16)
    grad_normed_out = dot(masked, full_out, 1, 0).astype(BF16)
    mixed_out, stats = mix_blocks(
        inner_act, gate_pre, grad_normed_out, write_read, cols, cum_rows, states_low, skip_lanes, gain_gate[None],
    )
    stats = stats + swap(stats, 1)
    normed_out, grad_gate_pre, grad_diag, grad_gate_gain, grad_skip_lanes, local_grad = gate_blocks(
        mixed_out, gate_pre, grad_normed_out, inner_act, stats, gain_gate[None], write_read, cols, heads
    )
    local_grad = local_grad.reshape(slots, groups, STATE, inner)

    def branch_piece(which):
        rows = lax.dynamic_slice(full_late, (which * width_here, inner), (width_here, inner))
        return dot(normed_out, rows, 1, 1)

    branch = own_features(branch_piece)
    hidden_out = (hidden_in.astype(F32) + valid_rows[..., None] * branch).astype(BF16)
    normed_out, grad_gate_pre, *_ = lax.optimization_barrier((normed_out, grad_gate_pre, ready[0], ready[1]))
    grad_proj_out = dot(masked, normed_out, 0, 0).astype(BF16)
    grad_gate_w = dot(normed, grad_gate_pre, 0, 0).astype(BF16)
    grad_by_gate = dot(grad_gate_pre, full_gate, 1, 1).astype(BF16)
    other_scale = swap(in_scale.reshape(-1, 128), 2)

    flowing = local_grad[:, groups - 1]
    for position in reversed(range(groups - 1)):
        flowing = decay_lanes[:, position] * flowing + local_grad[:, position]
    flowing = carried_in(device_decay, flowing, None, True)
    flow_list = []
    for position in reversed(range(groups)):
        flow_list.insert(0, flowing)
        flowing = decay_lanes[:, position] * flowing + local_grad[:, position]
    flows = jnp.stack(flow_list, axis=1)
    flows_low = flows.astype(BF16).reshape(blocks, STATE, inner)
    flows_low = after(flows_low, (grad_proj_out, grad_gate_w, ready[2], other_scale))

    grad_inner_pre, grad_narrow, tap_sums, narrow_sums, head_sums, halo, narrow_halo = back_blocks(
        inner_act, mixed_out, grad_diag, slope, inner_pre, inner_rim, write_read, narrow_slope, narrow_pre,
        narrow_rim, cols, cum_rows, states_low, flows_low, skip_lanes, taps, conv_write_read, rate_row, groups,
    )
    tap_sums = tap_sums.transpose(1, 0, 2).reshape(8, inner)
    grad_taps, grad_taps_bias = tap_sums[:CONV], tap_sums[CONV]
    grad_conv_write_read, grad_conv_write_read_bias = narrow_sums[:CONV], narrow_sums[CONV]
    grad_step_bias, grad_log_rate = head_sums[0, :heads], head_sums[1, :heads]

    def completed(grad, halo):
        back = passed_along(halo, "ctx", -1)
        for slot in range(slots):
            ends = (slot + 1) * seq_here
            rows = grad[ends - 8 : ends, : halo.shape[-1]].astype(F32) + back[slot]
            grad = lax.dynamic_update_slice(grad, rows.astype(BF16), (ends - 8, 0))
        return grad

    grad_inner_pre, grad_narrow = completed(grad_inner_pre, halo), completed(grad_narrow, narrow_halo)
    def reduced(x):
        return lax.psum_scatter(x, ("fsdp", "ctx"), scatter_dimension=0, tiled=True)

    early = reduced(jnp.concatenate([grad_proj_out, grad_gate_w], axis=1))
    early_away = jnp.concatenate([early[:, inner_own:inner], early[:, inner + inner_own :]], axis=1)
    grad_inner_pre, hidden_out, early_away = lax.optimization_barrier((grad_inner_pre, hidden_out, early_away))
    early_far = swap(early_away, 2)
    by_kernel = lax.axis_size("fsdp") == 4 and lax.axis_size("ctx") == 2
    late = jnp.concatenate([grad_inner_pre, grad_narrow], axis=1)
    if by_kernel:
        which = (place ^ 3) * width_here
        rows_at = lambda full: lax.dynamic_slice_in_dim(full, which, width_here, 0)
        relay_piece = (
            lax.dynamic_slice_in_dim(grad_by_gate, which, width_here, 1)
            + dot(grad_inner_pre, rows_at(full_inner), 1, 1)
            + dot(grad_narrow, rows_at(full_narrow), 1, 1)
        ).astype(BF16)
        relay = swap(relay_piece, 1)
        late = after(late, relay_piece)
    grad_late_w = dot(normed, late, 0, 0).astype(BF16)
    if by_kernel:
        by_core = grad_late_w.reshape(4, 2, -1, grad_late_w.shape[1])
        away = lax.dynamic_index_in_dim(by_core, 1 - lax.axis_index("ctx"), 1, keepdims=False)
        core = lax.ppermute(away, "ctx", [(0, 1), (1, 0)])
        grad_inner_pre, grad_narrow, *_ = lax.optimization_barrier(
            (grad_inner_pre, grad_narrow, away, early_far)
        )
    by_inner = dot(grad_inner_pre, full_inner, 1, 1)
    partial_normed = grad_by_gate + by_inner + dot(grad_narrow, full_narrow, 1, 1)
    grad_out_home = early[:, :inner_own].astype(F32) + early_far[:, :inner_own].astype(F32)
    grad_gate_home = early[:, inner : inner + inner_own].astype(F32) + early_far[:, inner_own:].astype(F32)
    by_hat = partial_normed * (full_x.astype(F32) * in_scale)
    grad_gain_full = jnp.sum(by_hat, axis=0)
    cross_part = jnp.sum(by_hat * full_gain.astype(F32), axis=1)
    partial_low = partial_normed.astype(BF16)

    grad_skip_gain = jnp.sum(grad_skip_lanes.reshape(heads, HEADDIM), axis=1)
    shared_shapes = [(CONV, 2 * STATE), (2 * STATE,), (width,)]
    head_shapes = [(CONV, inner), (inner,), (inner,), (heads,), (heads,), (heads,)]
    by_head = pack([grad_taps, grad_taps_bias, grad_gate_gain, grad_step_bias, grad_log_rate, grad_skip_gain])
    by_all = pack([grad_conv_write_read, grad_conv_write_read_bias, grad_gain_full])

    if by_kernel:
        span = max(inner, width, (CONV + 1) * 2 * STATE)
        line = lambda v: jnp.pad(v.reshape(-1, v.shape[-1]), ((0, 0), (0, span - v.shape[-1])))
        by_lines = jnp.concatenate(
            [
                line(tap_sums[: CONV + 1]),
                line(grad_gate_gain),
                line(jnp.concatenate([grad_step_bias, grad_log_rate, grad_skip_gain])),
                jnp.zeros((1, span), F32),
                line(grad_gain_full),
                line(narrow_sums[: CONV + 1].reshape(-1)),
                jnp.zeros((6, span), F32),
            ]
        )
        near, other, grad_inner_home, narrow_sum, small_own, small_far, cross_rows, cross_far = finish(
            partial_low,
            relay,
            grad_late_w,
            core,
            by_lines,
            cross_part.reshape(-1, 128),
            proj_write_read.shape[0],
        )
        kept = lax.dynamic_slice_in_dim(partial_normed, place * width_here, width_here, 1) + near.astype(F32)
        grad_normed = both_halves(
            kept.reshape(slots, seq_here, width_here), other.astype(F32).reshape(slots, seq_here, width_here)
        )
        write_read_home = narrow_sum[:, : 2 * STATE]
        step_home = (
            narrow_sum[:, 2 * STATE : 2 * STATE + heads_own]
            + narrow_sum[:, 2 * STATE + 128 + heads_own : 2 * STATE + 128 + heads]
        )
        cross_rows, cross_far = cross_rows.reshape(-1), cross_far.reshape(-1)
        homes = [
            small_own[at, :inner_own] + small_far[at, inner_own:inner] for at in (slice(0, CONV), CONV, CONV + 1)
        ] + [
            small_own[CONV + 2, k * heads : k * heads + heads_own]
            + small_far[CONV + 2, k * heads + heads_own : (k + 1) * heads]
            for k in range(3)
        ]
        shared = small_own[8:] + small_far[8:]
        grad_norm_gain = lax.dynamic_slice_in_dim(shared[0], place * width_here, width_here, 0)
        wr_sums = shared[1, : (CONV + 1) * 2 * STATE].reshape(CONV + 1, 2 * STATE)
        wr_taps, wr_bias = wr_sums[:CONV], wr_sums[CONV]
    else:

        def normed_piece(which):
            return lax.dynamic_slice_in_dim(partial_normed, which * width_here, width_here, 1)

        grad_normed = own_features(normed_piece)
        late_sum = reduced(grad_late_w)
        late_far = swap(late_sum, 2).astype(F32)
        late_sum = late_sum.astype(F32)
        grad_inner_home = late_sum[:, :inner_own] + late_far[:, inner_own:inner]
        write_read_home = late_sum[:, inner : inner + 2 * STATE] + late_far[:, inner : inner + 2 * STATE]
        write_read_home = write_read_home + swap(write_read_home, 1)
        steps_at = inner + 2 * STATE
        step_home = late_sum[:, steps_at : steps_at + heads_own] + late_far[:, steps_at + heads_own : steps_at + heads]
        cross_rows = cross_part + swap(cross_part, 1)
        cross_far = swap(cross_rows, 2)
        smalls = everywhere(pack([by_head, by_all]))
        parts = unpack(smalls[: by_head.size], head_shapes)
        away = [lax.slice_in_dim(p, p.shape[-1] // 2, p.shape[-1], axis=p.ndim - 1) for p in parts]
        far_parts = unpack(swap(pack(away), 2), small_shapes)
        shared = smalls[by_head.size :]
        shared = shared + swap(shared, 1)
        shared = shared + swap(shared, 2)
        homes = [
            lax.slice_in_dim(p, 0, p.shape[-1] // 2, axis=p.ndim - 1) + a for p, a in zip(parts, far_parts)
        ]
        wr_taps, wr_bias, gain_all = unpack(shared, shared_shapes)
        grad_norm_gain = lax.dynamic_slice_in_dim(gain_all, place * width_here, width_here, 0)

    own_gain = norm_gain.astype(F32)
    own_scale = both_halves(
        in_scale.reshape(slots, seq_here, 1), other_scale.reshape(slots, seq_here, 1)
    )
    own_hat = hidden_in.astype(F32) * own_scale
    grad_hat_in = grad_normed * own_gain
    cross_in = both_halves(
        cross_rows.reshape(slots, seq_here, 1), cross_far.reshape(slots, seq_here, 1)
    ) / width
    grad_hidden_in = own_scale * (grad_hat_in - own_hat * cross_in) + out_cotangent.astype(F32)
    return (
        hidden_out,
        grad_hidden_in,
        grad_norm_gain,
        jnp.stack([grad_gate_home, grad_inner_home], axis=1),
        write_read_home,
        step_home,
        homes[0],
        homes[1],
        wr_taps,
        wr_bias,
        homes[3],
        homes[4],
        homes[5],
        homes[2],
        grad_out_home,
    )


def solution(mesh):
    rows = ("fsdp", "ctx")
    acts = P("fsdp", "ctx", "tp")
    placed = (
        acts,
        P("fsdp"),
        P("tp"),
        P(rows, None, "tp"),
        P(rows, None),
        P(rows, "tp"),
        P(None, "tp"),
        P("tp"),
        P(),
        P(),
        P("tp"),
        P("tp"),
        P("tp"),
        P("tp"),
        P(rows, "tp"),
        acts,
    )
    return jax.shard_map(
        on_device,
        mesh=mesh,
        in_specs=placed,
        out_specs=(
            acts,
            acts,
            P("tp"),
            P(rows, None, "tp"),
            P(rows, None),
            P(rows, "tp"),
            P(None, "tp"),
            P("tp"),
            P(),
            P(),
            P("tp"),
            P("tp"),
            P("tp"),
            P("tp"),
            P(rows, "tp"),
        ),
        check_vma=False,
    )
```

```python
import functools

import jax
import jax.numpy as jnp
from jax import lax
from jax.experimental import pallas as pl
from jax.experimental.pallas import tpu as pltpu
from jax.sharding import PartitionSpec as P

HEADDIM = 64
STATE = 128
CONV = 4
GROUP = 256
INNER = 3072
EPSILON = 1e-05
PAIR = 2 * HEADDIM
HALF = GROUP // 2
HEADS_STEP = 6
LANES_STEP = HEADS_STEP * HEADDIM
GATE_HEADS = 12
GATE_LANES = GATE_HEADS * HEADDIM
WIDE_HEADS = 24
WIDE_LANES = WIDE_HEADS * HEADDIM
F32 = jnp.float32
BF16 = jnp.bfloat16
HIGHEST = lax.Precision.HIGHEST


def swap(x, bit):
    count = lax.axis_size("tp")
    return lax.ppermute(x, "tp", [(i, i ^ bit) for i in range(count)])


def passed_along(x, axis, by):
    count = lax.axis_size(axis)
    pairs = [(i, i + by) for i in range(count) if 0 <= i + by < count]
    return lax.ppermute(x, axis, pairs)


def carried_in(decay, final, combine, reverse):
    count, position = (lax.axis_size("ctx"), lax.axis_index("ctx"))
    if count == 2:
        return passed_along(final.astype(BF16), "ctx", -1 if reverse else 1).astype(F32)
    decays = lax.all_gather(decay.astype(BF16), "ctx").astype(F32)
    finals = lax.all_gather(final.astype(BF16), "ctx")
    start = jnp.zeros_like(final)

    def lap(k, before):
        at = count - 1 - k if reverse else k
        reached = at > position if reverse else at < position
        new = decays[at] * before + finals[at].astype(F32)
        return jnp.where(reached, new, before)

    return lax.fori_loop(0, count, lap, start)


def dot(a, b, da, db):
    return lax.dot_general(a, b, (((da,), (db,)), ((), ())), preferred_element_type=F32)


def low_lanes(rows):
    return lax.broadcasted_iota(jnp.int32, (rows, PAIR), 1) < HEADDIM


def spread_heads(cols, first, low_half):
    return jnp.where(low_half, cols[:, first : first + 1], cols[:, first + 1 : first + 2])


def lower_mask():
    return lax.broadcasted_iota(jnp.int32, (GROUP, GROUP), 0) >= lax.broadcasted_iota(
        jnp.int32, (GROUP, GROUP), 1
    )


def quarter_mask():
    return lax.broadcasted_iota(jnp.int32, (HALF, HALF), 0) >= lax.broadcasted_iota(jnp.int32, (HALF, HALF), 1)


def decays(col, row, mask):
    early = jnp.exp(jnp.where(mask, col[:HALF] - row[:, :HALF], -1e30))
    cross = jnp.exp(col[HALF:] - row[:, :HALF])
    late = jnp.exp(jnp.where(mask, col[HALF:] - row[:, HALF:], -1e30))
    return early, cross, late


def split_dot(ones, values, terms, contract):
    total, rest = None, values
    for _ in range(terms):
        part = rest.astype(BF16)
        rest = rest - part.astype(F32)
        piece = dot(ones, part, contract, 0)
        total = piece if total is None else total + piece
    return total


def turned(cols, heads_before):
    return pltpu.roll(cols, lax.rem(128 - heads_before, 128), 1)


def start_kernel(
    groups, heads,
    inner_ref, rim_ref, narrow_ref, nrim_ref, taps_ref, bias_ref, ntaps_ref, nbias_ref, sbias_ref, rate_ref,
    x_ref, slope_ref, wr_ref, nslope_ref, cols_ref, rows_ref, local_ref, decay_ref,
    ext_ref, next_ref, scaled_ref,
):
    first = lax.rem(pl.program_id(0), groups) == 0

    @pl.when(first)
    def _():
        ext_ref[5:8, :] = rim_ref[0].astype(F32)
        next_ref[5:8, :] = nrim_ref[0].astype(F32)

    @pl.when(jnp.logical_not(first))
    def _():
        ext_ref[0:8, :] = ext_ref[GROUP : GROUP + 8, :]
        next_ref[0:8, :] = next_ref[GROUP : GROUP + 8, :]

    def conv(source, taps, bias, lanes):
        total = bias[:, lanes]
        for k in range(CONV):
            total = total + taps[k : k + 1, lanes] * source[5 + k : 5 + k + GROUP, lanes]
        sig = jax.nn.sigmoid(total)
        return total * sig, sig * (1.0 + total * (1.0 - sig))

    for part in range(2 * STATE // 128):
        lanes = slice(128 * part, 128 * (part + 1))
        next_ref[8 : GROUP + 8, lanes] = narrow_ref[:, lanes].astype(BF16).astype(F32)
        act, slope = conv(next_ref, ntaps_ref, nbias_ref, lanes)
        wr_ref[:, lanes] = act.astype(BF16)
        nslope_ref[:, lanes] = slope

    raw = narrow_ref[:, 2 * STATE :] + sbias_ref[...]
    lane = lax.broadcasted_iota(jnp.int32, (GROUP, 128), 1)
    step = jnp.maximum(raw, 0.0) + jnp.log1p(jnp.exp(-jnp.abs(raw)))
    step = jnp.where(lane < heads, step, 0.0)
    sig = jnp.where(lane < heads, jax.nn.sigmoid(raw), 0.0)
    cum = split_dot(lower_mask().astype(BF16), step * rate_ref[...], 3, 1)
    cols = step + pltpu.roll(cum, heads, 1) + pltpu.roll(sig, 2 * heads, 1)
    cols_ref[...] = cols
    rows_ref[0] = cum.T[:heads]
    last = cum[GROUP - 1 : GROUP, :]
    scale = jnp.exp(last - cum) * step
    decay = jnp.exp(last)
    low_half, low_row = low_lanes(GROUP), low_lanes(1)
    for pair in range(heads // 2):
        lanes = slice(PAIR * pair, PAIR * (pair + 1))
        ext_ref[8 : GROUP + 8, lanes] = inner_ref[:, lanes].astype(F32)
        act, slope = conv(ext_ref, taps_ref, bias_ref, lanes)
        x = act.astype(BF16)
        x_ref[:, lanes] = x
        slope_ref[:, lanes] = slope.astype(BF16)
        scaled_ref[:, lanes] = (x.astype(F32) * spread_heads(scale, 2 * pair, low_half)).astype(BF16)
        decay_ref[0, :, lanes] = spread_heads(decay, 2 * pair, low_row)
    local_ref[0] = dot(wr_ref[:, :STATE], scaled_ref[...], 0, 0)


def start_blocks(inner_pre, rim, narrow, nrim, taps, bias, ntaps, nbias, sbias, rate, groups, heads):
    tokens, width = inner_pre.shape
    blocks = tokens // GROUP
    rows = lambda w: pl.BlockSpec((GROUP, w), lambda b: (b, 0))
    whole = lambda x: pl.BlockSpec(x.shape, lambda b: (0,) * x.ndim)
    return pl.pallas_call(
        functools.partial(start_kernel, groups, heads),
        grid=(blocks,),
        in_specs=[
            rows(width),
            pl.BlockSpec((1, CONV - 1, width), lambda b: (b // groups, 0, 0)),
            rows(narrow.shape[1]),
            pl.BlockSpec((1, CONV - 1, 2 * STATE), lambda b: (b // groups, 0, 0)),
            whole(taps), whole(bias), whole(ntaps), whole(nbias), whole(sbias), whole(rate),
        ],
        out_specs=[
            rows(width), rows(width), rows(2 * STATE), rows(2 * STATE), rows(128),
            pl.BlockSpec((1, heads, GROUP), lambda b: (b, 0, 0)),
            pl.BlockSpec((1, STATE, width), lambda b: (b, 0, 0)),
            pl.BlockSpec((1, 1, width), lambda b: (b, 0, 0)),
        ],
        out_shape=[
            jax.ShapeDtypeStruct((tokens, width), BF16),
            jax.ShapeDtypeStruct((tokens, width), BF16),
            jax.ShapeDtypeStruct((tokens, 2 * STATE), BF16),
            jax.ShapeDtypeStruct((tokens, 2 * STATE), F32),
            jax.ShapeDtypeStruct((tokens, 128), F32),
            jax.ShapeDtypeStruct((blocks, heads, GROUP), F32),
            jax.ShapeDtypeStruct((blocks, STATE, width), F32),
            jax.ShapeDtypeStruct((blocks, 1, width), F32),
        ],
        scratch_shapes=[
            pltpu.VMEM((GROUP + 8, width), F32),
            pltpu.VMEM((GROUP + 8, 2 * STATE), F32),
            pltpu.VMEM((GROUP, width), BF16),
        ],
        cost_estimate=pl.CostEstimate(
            flops=2 * tokens * STATE * width + 20 * tokens * width,
            bytes_accessed=tokens * width * 6 + blocks * STATE * width * 4,
            transcendentals=tokens * width,
        ),
        name="start_blocks",
    )(inner_pre, rim, narrow, nrim, taps, bias, ntaps, nbias, sbias, rate)


def mix_kernel(
    heads,
    x_ref, gate_ref, gno_ref, wr_ref, cols_ref, rows_ref, state_ref, skip_ref, gain_ref,
    mixed_ref, stats_ref, scores_ref, sums_ref,
):
    g = pl.program_id(1)

    @pl.when(g == 0)
    def _():
        scores_ref[...] = dot(wr_ref[:, STATE:], wr_ref[:, :STATE], 1, 1)
        sums_ref[...] = jnp.zeros_like(sums_ref)

    cols = turned(cols_ref[...], g * GATE_HEADS)
    grown = jnp.exp(cols)
    low_half = low_lanes(GROUP)
    mask = quarter_mask()
    squares = jnp.zeros((GROUP, 1), F32)
    crosses = jnp.zeros((GROUP, 1), F32)
    for pair in range(GATE_HEADS // 2):
        lanes = slice(PAIR * pair, PAIR * (pair + 1))
        x = x_ref[:, lanes].astype(F32)
        stepped = x * spread_heads(cols, 2 * pair, low_half)
        halves = (
            jnp.where(low_half, stepped, 0.0).astype(BF16),
            jnp.where(low_half, 0.0, stepped).astype(BF16),
        )
        total = dot(wr_ref[:, STATE:], state_ref[0, :, lanes], 1, 0)
        total = total * spread_heads(grown, heads + 2 * pair, low_half)
        top = jnp.zeros((HALF, PAIR), F32)
        bottom = jnp.zeros((HALF, PAIR), F32)
        for side in range(2):
            head = 2 * pair + side
            row = rows_ref[0, pl.ds(g * GATE_HEADS + head, 1), :]
            early, cross, late = decays(cols[:, heads + head : heads + head + 1], row, mask)
            upper = (scores_ref[:HALF, :HALF] * early).astype(BF16)
            under = jnp.concatenate(
                [
                    (scores_ref[HALF:, :HALF] * cross).astype(BF16),
                    (scores_ref[HALF:, HALF:] * late).astype(BF16),
                ],
                axis=1,
            )
            top = top + dot(upper, halves[side][:HALF], 1, 0)
            bottom = bottom + dot(under, halves[side], 1, 0)
        total = total + jnp.concatenate([top, bottom], axis=0)
        mixed = total + skip_ref[:, lanes] * x
        mixed_ref[:, lanes] = mixed
        gate = gate_ref[:, lanes].astype(F32)
        gated = mixed * (gate * jax.nn.sigmoid(gate))
        squares = squares + jnp.sum(gated * gated, axis=1, keepdims=True)
        grad_hat = gno_ref[:, lanes].astype(F32) * gain_ref[:, lanes]
        crosses = crosses + jnp.sum(gated * grad_hat, axis=1, keepdims=True)
    lane = lax.broadcasted_iota(jnp.int32, (GROUP, 128), 1)
    sums_ref[...] += jnp.where(lane == 0, squares, jnp.where(lane == 1, crosses, 0.0))

    @pl.when(g == pl.num_programs(1) - 1)
    def _():
        stats_ref[0] = sums_ref[...].T[:8]


def mix_blocks(x, gate, gno, wr, cols, rows, states, skip, gain):
    tokens, width = x.shape
    blocks, steps, heads = tokens // GROUP, width // GATE_LANES, rows.shape[1]
    wide = pl.BlockSpec((GROUP, GATE_LANES), lambda b, g: (b, g))
    line = pl.BlockSpec((1, GATE_LANES), lambda b, g: (0, g))
    return pl.pallas_call(
        functools.partial(mix_kernel, heads),
        grid=(blocks, steps),
        in_specs=[
            wide, wide, wide,
            pl.BlockSpec((GROUP, 2 * STATE), lambda b, g: (b, 0)),
            pl.BlockSpec((GROUP, 128), lambda b, g: (b, 0)),
            pl.BlockSpec((1, heads, GROUP), lambda b, g: (b, 0, 0)),
            pl.BlockSpec((1, STATE, GATE_LANES), lambda b, g: (b, 0, g)),
            line, line,
        ],
        out_specs=[wide, pl.BlockSpec((1, 8, GROUP), lambda b, g: (b, 0, 0))],
        out_shape=[
            jax.ShapeDtypeStruct((tokens, width), F32),
            jax.ShapeDtypeStruct((blocks, 8, GROUP), F32),
        ],
        scratch_shapes=[pltpu.VMEM((GROUP, GROUP), F32), pltpu.VMEM((GROUP, 128), F32)],
        cost_estimate=pl.CostEstimate(
            flops=2 * tokens * width * (2 * GROUP + 2 * STATE) * 2,
            bytes_accessed=tokens * width * 10,
            transcendentals=tokens * GROUP * width // HEADDIM,
        ),
        name="mix_blocks",
    )(x, gate, gno, wr, cols, rows, states, skip, gain)


def gate_kernel(
    heads,
    mixed_ref, gate_ref, gno_ref, x_ref, stats_ref, gain_ref, wr_ref, cols_ref,
    normed_ref, ggate_ref, gdiag_ref, gain_sum_ref, skip_sum_ref, flow_ref, scaled_ref,
):
    @pl.when(pl.program_id(1) == 0)
    def _():
        gain_sum_ref[...] = jnp.zeros_like(gain_sum_ref)
        skip_sum_ref[...] = jnp.zeros_like(skip_sum_ref)

    stats = stats_ref[0].T
    scale = lax.rsqrt(stats[:, 0:1] / INNER + EPSILON)
    cross = scale * stats[:, 1:2] / INNER
    grown = jnp.exp(turned(cols_ref[...], pl.program_id(0) * WIDE_HEADS))
    low_half = low_lanes(GROUP)
    for pair in range(WIDE_HEADS // 2):
        lanes = slice(PAIR * pair, PAIR * (pair + 1))
        mixed = mixed_ref[:, lanes]
        gate = gate_ref[:, lanes].astype(F32)
        gno = gno_ref[:, lanes].astype(F32)
        gain = gain_ref[:, lanes]
        sig = jax.nn.sigmoid(gate)
        act = gate * sig
        hat = mixed * act * scale
        normed_ref[:, lanes] = (hat * gain).astype(BF16)
        gain_sum_ref[:, lanes] += jnp.sum(gno * hat, axis=0, keepdims=True)
        grad_gated = scale * (gno * gain - hat * cross)
        grad_mixed = grad_gated * act
        ggate_ref[:, lanes] = (grad_gated * mixed * sig * (1.0 + gate * (1.0 - sig))).astype(BF16)
        skip_sum_ref[:, lanes] += jnp.sum(grad_mixed * x_ref[:, lanes].astype(F32), axis=0, keepdims=True)
        diag = grad_mixed.astype(BF16)
        gdiag_ref[:, lanes] = diag
        scaled = diag.astype(F32) * spread_heads(grown, heads + 2 * pair, low_half)
        scaled_ref[:, lanes] = scaled.astype(BF16)
    flow_ref[0] = dot(wr_ref[...], scaled_ref[...], 0, 0)


def gate_blocks(mixed, gate, gno, x, stats, gain, wr, cols, heads):
    tokens, width = x.shape
    blocks, steps = tokens // GROUP, width // WIDE_LANES
    wide = pl.BlockSpec((GROUP, WIDE_LANES), lambda g, b: (b, g))
    line = pl.BlockSpec((1, WIDE_LANES), lambda g, b: (0, g))
    return pl.pallas_call(
        functools.partial(gate_kernel, heads),
        grid=(steps, blocks),
        in_specs=[
            wide, wide, wide, wide,
            pl.BlockSpec((1, 8, GROUP), lambda g, b: (b, 0, 0)),
            line,
            pl.BlockSpec((GROUP, STATE), lambda g, b: (b, 1)),
            pl.BlockSpec((GROUP, 128), lambda g, b: (b, 0)),
        ],
        out_specs=[
            wide, wide, wide, line, line,
            pl.BlockSpec((1, STATE, WIDE_LANES), lambda g, b: (b, 0, g)),
        ],
        out_shape=[
            jax.ShapeDtypeStruct((tokens, width), BF16),
            jax.ShapeDtypeStruct((tokens, width), BF16),
            jax.ShapeDtypeStruct((tokens, width), BF16),
            jax.ShapeDtypeStruct((1, width), F32),
            jax.ShapeDtypeStruct((1, width), F32),
            jax.ShapeDtypeStruct((blocks, STATE, width), F32),
        ],
        scratch_shapes=[pltpu.VMEM((GROUP, WIDE_LANES), BF16)],
        cost_estimate=pl.CostEstimate(
            flops=2 * tokens * STATE * width,
            bytes_accessed=tokens * width * 16 + blocks * STATE * width * 4,
            transcendentals=tokens * width,
        ),
        name="gate_blocks",
    )(mixed, gate, gno, x, stats, gain, wr, cols)


def back_kernel(
    groups, heads,
    x_ref, mixed_ref, grad_ref, slope_ref, pre_ref, rim_ref, wr_ref, nslope_ref, npre_ref, nrim_ref,
    cols_ref, rows_ref, state_ref, flow_ref, skip_ref, taps_ref, ntaps_ref, rate_ref,
    gpre_ref, gnarrow_ref, sums_ref, nsums_ref, hsums_ref, halo_ref, nhalo_ref,
    scores_ref, gscores_ref, prod_ref, gw_ref, gr_ref, u_ref, v_ref, i_ref, e_ref, ext_ref, next_ref, head_ref,
):
    step_id, g = pl.program_id(0), pl.program_id(1)
    block = pl.num_programs(0) - 1 - step_id
    last_of_slot = lax.rem(block, groups) == groups - 1
    first_of_slot = lax.rem(block, groups) == 0

    @pl.when(g == 0)
    def _():
        scores_ref[...] = dot(wr_ref[:, STATE:], wr_ref[:, :STATE], 1, 1)
        for ref in (gscores_ref, gw_ref, gr_ref, u_ref, v_ref, i_ref, e_ref):
            ref[...] = jnp.zeros_like(ref)

    @pl.when(jnp.logical_and(g == 0, step_id == 0))
    def _():
        sums_ref[...] = jnp.zeros_like(sums_ref)
        nsums_ref[...] = jnp.zeros_like(nsums_ref)
        hsums_ref[...] = jnp.zeros_like(hsums_ref)

    @pl.when(last_of_slot)
    def _():
        ext_ref[g, GROUP : GROUP + 8, :] = jnp.zeros((8, LANES_STEP), F32)
        next_ref[GROUP : GROUP + 8, :] = jnp.zeros((8, 2 * STATE), F32)

    @pl.when(jnp.logical_not(last_of_slot))
    def _():
        ext_ref[g, GROUP : GROUP + 8, :] = ext_ref[g, 0:8, :]

        @pl.when(g == 0)
        def _():
            next_ref[GROUP : GROUP + 8, :] = next_ref[0:8, :]

    cols = turned(cols_ref[...], g * HEADS_STEP)
    grown = jnp.exp(cols)
    shrunk = jnp.exp(cols[GROUP - 1 : GROUP, :] - cols)
    low_half = low_lanes(GROUP)
    mask = quarter_mask()
    grad_write = jnp.zeros((GROUP, STATE), F32)
    grad_read = jnp.zeros((GROUP, STATE), F32)
    for pair in range(HEADS_STEP // 2):
        lanes = slice(PAIR * pair, PAIR * (pair + 1))
        x = x_ref[:, lanes].astype(F32)
        grad = grad_ref[:, lanes]
        grad_f = grad.astype(F32)
        skip = skip_ref[:, lanes]
        steps = spread_heads(cols, 2 * pair, low_half)
        tail = spread_heads(shrunk, heads + 2 * pair, low_half)
        stepped = x * steps
        x_halves = (
            jnp.where(low_half, stepped, 0.0).astype(BF16),
            jnp.where(low_half, 0.0, stepped).astype(BF16),
        )
        g_halves = (
            jnp.where(low_half, grad_f, 0.0).astype(BF16),
            jnp.where(low_half, 0.0, grad_f).astype(BF16),
        )
        flow = flow_ref[0, :, lanes]
        state = state_ref[0, :, lanes]
        e_ref[0:1, lanes] = jnp.sum(flow.astype(F32) * state.astype(F32), axis=0, keepdims=True)
        scaled = (grad_f * spread_heads(grown, heads + 2 * pair, low_half)).astype(BF16)
        grad_read = grad_read + dot(scaled, state, 1, 1)
        grad_write = grad_write + dot((stepped * tail).astype(BF16), flow, 1, 1)
        stepped_low = stepped.astype(BF16).astype(F32)
        inter = dot(wr_ref[:, :STATE], flow, 1, 0) * tail
        top = jnp.zeros((HALF, PAIR), F32)
        bottom = jnp.zeros((HALF, PAIR), F32)
        for side in range(2):
            head = 2 * pair + side
            row = rows_ref[0, pl.ds(g * HEADS_STEP + head, 1), :]
            early, cross, late = decays(cols[:, heads + head : heads + head + 1], row, mask)
            left = jnp.concatenate(
                [
                    (scores_ref[:HALF, :HALF] * early).astype(BF16),
                    (scores_ref[HALF:, :HALF] * cross).astype(BF16),
                ],
                axis=0,
            )
            right = (scores_ref[HALF:, HALF:] * late).astype(BF16)
            top = top + dot(left, g_halves[side], 0, 0)
            bottom = bottom + dot(right, g_halves[side][HALF:], 0, 0)
            under = dot(grad[HALF:], x_halves[side], 1, 1)
            terms = (
                dot(grad[:HALF], x_halves[side][:HALF], 1, 1) * early, under[:, :HALF] * cross, under[:, HALF:] * late,
            )
            quarters = terms if side == 0 else tuple(a + b for a, b in zip(quarters, terms))
        gscores_ref[:HALF, :HALF] += quarters[0]
        gscores_ref[HALF:, :HALF] += quarters[1]
        gscores_ref[HALF:, HALF:] += quarters[2]
        total = jnp.concatenate([top, bottom], axis=0)
        both = total + inter
        prod_ref[0, :, lanes] = x * both
        prod_ref[1, :, lanes] = grad_f * (mixed_ref[:, lanes] - skip * x) - stepped_low * total
        prod_ref[2, :, lanes] = stepped_low * inter
        grad_conv = (steps * both + skip * grad_f) * slope_ref[:, lanes].astype(F32)
        ext_ref[g, 0:GROUP, lanes] = grad_conv
        pre = pre_ref[:, lanes].astype(F32)
        total_pre = jnp.zeros_like(grad_conv)
        for j in range(CONV):
            moved = ext_ref[g, j : j + GROUP, lanes]
            total_pre = total_pre + taps_ref[CONV - 1 - j : CONV - j, lanes] * moved
            sums_ref[g, CONV - 1 - j : CONV - j, lanes] += jnp.sum(pre * moved, axis=0, keepdims=True)
        sums_ref[g, CONV : CONV + 1, lanes] += jnp.sum(grad_conv, axis=0, keepdims=True)
        gpre_ref[:, lanes] = total_pre.astype(BF16)

    @pl.when(first_of_slot)
    def _():
        head_ref[0:8, :LANES_STEP] = jnp.zeros((8, LANES_STEP), F32)
        head_ref[8:16, :LANES_STEP] = ext_ref[g, 0:8, :]
        halo = jnp.zeros((8, LANES_STEP), F32)
        for j in range(CONV):
            moved = head_ref[j : j + 8, :LANES_STEP]
            halo = halo + taps_ref[CONV - 1 - j : CONV - j, :] * moved
            sums_ref[g, CONV - 1 - j : CONV - j, :] += jnp.sum(
                rim_ref[0].astype(F32) * moved[5:8], axis=0, keepdims=True
            )
        halo_ref[0] = halo

    chosen_rows = lax.broadcasted_iota(jnp.int32, (LANES_STEP, 128), 0) // HEADDIM + g * HEADS_STEP
    chosen = (chosen_rows == lax.broadcasted_iota(jnp.int32, (LANES_STEP, 128), 1)).astype(BF16)

    def sums_of(values, terms):
        total, rest = None, values
        for _ in range(terms):
            part = rest.astype(BF16)
            rest = rest - part.astype(F32)
            piece = dot(part, chosen, 1, 0)
            total = piece if total is None else total + piece
        return total

    u_ref[...] += sums_of(prod_ref[0], 2)
    v_ref[...] += sums_of(prod_ref[1], 2)
    i_ref[...] += sums_of(prod_ref[2], 2)
    e_ref[8:16, 0:128] += sums_of(e_ref[0:8, :], 2)
    gw_ref[...] += grad_write
    gr_ref[...] += grad_read

    @pl.when(g == pl.num_programs(1) - 1)
    def _():
        low = gscores_ref[...].astype(BF16)
        gradient = (
            gw_ref[...] + dot(low, wr_ref[:, STATE:], 0, 0),
            gr_ref[...] + dot(low, wr_ref[:, :STATE], 1, 0),
        )
        for part in range(2):
            lanes = slice(STATE * part, STATE * (part + 1))
            grad_conv = gradient[part] * nslope_ref[:, lanes]
            next_ref[0:GROUP, lanes] = grad_conv
            pre = npre_ref[:, lanes].astype(BF16).astype(F32)
            total_pre = jnp.zeros_like(grad_conv)
            for j in range(CONV):
                moved = next_ref[j : j + GROUP, lanes]
                total_pre = total_pre + ntaps_ref[CONV - 1 - j : CONV - j, lanes] * moved
                nsums_ref[CONV - 1 - j : CONV - j, lanes] += jnp.sum(pre * moved, axis=0, keepdims=True)
            nsums_ref[CONV : CONV + 1, lanes] += jnp.sum(grad_conv, axis=0, keepdims=True)
            gnarrow_ref[:, lanes] = total_pre.astype(BF16)

        @pl.when(first_of_slot)
        def _():
            head_ref[0:8, : 2 * STATE] = jnp.zeros((8, 2 * STATE), F32)
            head_ref[8:16, : 2 * STATE] = next_ref[0:8, :]
            halo = jnp.zeros((8, 2 * STATE), F32)
            for j in range(CONV):
                moved = head_ref[j : j + 8, : 2 * STATE]
                halo = halo + ntaps_ref[CONV - 1 - j : CONV - j, :] * moved
                nsums_ref[CONV - 1 - j : CONV - j, :] += jnp.sum(
                    nrim_ref[0].astype(F32) * moved[5:8], axis=0, keepdims=True
                )
            nhalo_ref[0] = halo

        own = cols_ref[...]
        lane = lax.broadcasted_iota(jnp.int32, (GROUP, 128), 1)
        step = jnp.where(lane < heads, own, 0.0)
        cum = pltpu.roll(own, 128 - heads, 1)
        sig = jnp.where(lane < heads, pltpu.roll(own, 128 - 2 * heads, 1), 0.0)
        strict = lax.broadcasted_iota(jnp.int32, (GROUP, GROUP), 0) > lax.broadcasted_iota(
            jnp.int32, (GROUP, GROUP), 1
        )
        reverse_sum = (
            split_dot(lower_mask().astype(BF16), v_ref[...], 2, 0)
            + split_dot(strict.astype(BF16), i_ref[...], 2, 1)
            + jnp.exp(cum[GROUP - 1 : GROUP, :]) * e_ref[8:9, 0:128]
        )
        grad_raw = (u_ref[...] + rate_ref[...] * reverse_sum) * sig
        gnarrow_ref[:, 2 * STATE :] = grad_raw.astype(BF16)
        hsums_ref[0:1, :] += jnp.sum(grad_raw, axis=0, keepdims=True)
        hsums_ref[1:2, :] += jnp.sum(reverse_sum * step, axis=0, keepdims=True) * rate_ref[...]


def back_blocks(
    x, mixed, grad, slope, pre, rim, wr, nslope, npre, nrim, cols, rows, states, flows, skip, taps, ntaps, rate, groups
):
    tokens, width = x.shape
    blocks, steps, heads, slots = tokens // GROUP, width // LANES_STEP, rows.shape[1], rim.shape[0]
    at = lambda b: blocks - 1 - b
    wide = pl.BlockSpec((GROUP, LANES_STEP), lambda b, g: (at(b), g))
    narrow = lambda w: pl.BlockSpec((GROUP, w), lambda b, g: (at(b), 0))
    state = pl.BlockSpec((1, STATE, LANES_STEP), lambda b, g: (at(b), 0, g))
    line = lambda n: pl.BlockSpec((n, LANES_STEP), lambda b, g: (0, g))
    whole = lambda shape: pl.BlockSpec(shape, lambda b, g: (0,) * len(shape))
    return pl.pallas_call(
        functools.partial(back_kernel, groups, heads),
        grid=(blocks, steps),
        in_specs=[
            wide, wide, wide, wide, wide,
            pl.BlockSpec((1, CONV - 1, LANES_STEP), lambda b, g: (at(b) // groups, 0, g)),
            narrow(2 * STATE), narrow(2 * STATE), narrow(npre.shape[1]),
            pl.BlockSpec((1, CONV - 1, 2 * STATE), lambda b, g: (at(b) // groups, 0, 0)),
            narrow(128),
            pl.BlockSpec((1, heads, GROUP), lambda b, g: (at(b), 0, 0)),
            state, state, line(1), line(CONV), whole((CONV, 2 * STATE)), whole((1, 128)),
        ],
        out_specs=[
            wide, narrow(2 * STATE + 128),
            whole((steps, 8, LANES_STEP)), whole((8, 2 * STATE)), whole((8, 128)),
            pl.BlockSpec((1, 8, LANES_STEP), lambda b, g: (at(b) // groups, 0, g)),
            pl.BlockSpec((1, 8, 2 * STATE), lambda b, g: (at(b) // groups, 0, 0)),
        ],
        out_shape=[
            jax.ShapeDtypeStruct((tokens, width), BF16),
            jax.ShapeDtypeStruct((tokens, 2 * STATE + 128), BF16),
            jax.ShapeDtypeStruct((steps, 8, LANES_STEP), F32),
            jax.ShapeDtypeStruct((8, 2 * STATE), F32),
            jax.ShapeDtypeStruct((8, 128), F32),
            jax.ShapeDtypeStruct((slots, 8, width), F32),
            jax.ShapeDtypeStruct((slots, 8, 2 * STATE), F32),
        ],
        scratch_shapes=[
            pltpu.VMEM((GROUP, GROUP), F32),
            pltpu.VMEM((GROUP, GROUP), F32),
            pltpu.VMEM((3, GROUP, LANES_STEP), F32),
            pltpu.VMEM((GROUP, STATE), F32),
            pltpu.VMEM((GROUP, STATE), F32),
            pltpu.VMEM((GROUP, 128), F32),
            pltpu.VMEM((GROUP, 128), F32),
            pltpu.VMEM((GROUP, 128), F32),
            pltpu.VMEM((16, LANES_STEP), F32),
            pltpu.VMEM((steps, GROUP + 8, LANES_STEP), F32),
            pltpu.VMEM((GROUP + 8, 2 * STATE), F32),
            pltpu.VMEM((16, max(LANES_STEP, 2 * STATE)), F32),
        ],
        cost_estimate=pl.CostEstimate(
            flops=2 * tokens * width * (4 * GROUP + 4 * STATE) * 2,
            bytes_accessed=tokens * width * 14,
            transcendentals=tokens * GROUP * width // HEADDIM,
        ),
        name="back_blocks",
    )(x, mixed, grad, slope, pre, rim, wr, nslope, npre, nrim, cols, rows, states, flows, skip, taps, ntaps, rate)


MESH = pl.DeviceIdType.MESH
FAR_PARTS = 4


def fetch_kernel(
    x_ref, inner_ref, late_ref, step_ref, wr_ref, small_ref,
    full_x, full_inner, late_far, full_step, full_wr, full_small,
    x_own, inner_own, step_own, wr_own, small_own, send_sem, recv_sem, local_sem,
):
    f, c, z = lax.axis_index("fsdp"), lax.axis_index("ctx"), lax.axis_index("tp")
    half = z // 2
    slots, seq, cols = full_x.shape[0], full_x.shape[1], x_ref.shape[2]
    depth = inner_ref.shape[0]
    partners = (
        {"fsdp": f ^ 1}, {"fsdp": f ^ 2}, {"fsdp": f ^ 3}, {"ctx": c ^ 1}, {"tp": z ^ 1}, {"tp": z ^ 2},
    )
    barrier = pltpu.get_barrier_semaphore()
    for partner in partners:
        pl.semaphore_signal(barrier, inc=1, device_id=partner, device_id_type=MESH)
    pl.semaphore_wait(barrier, len(partners))

    copies = []

    def send(src, dst, partner):
        at = len(copies)
        copy = pltpu.make_async_remote_copy(
            src_ref=src, dst_ref=dst, send_sem=send_sem.at[at], recv_sem=recv_sem.at[at],
            device_id=partners[partner], device_id_type=MESH,
        )
        copy.start()
        copies.append([copy, False])
        return at

    def arrived(at):
        copies[at][0].wait_recv()
        copies[at][1] = True

    def feature(which):
        return pl.ds(pl.multiple_of(which * cols, 128), cols)

    def shard(full, row_f, far):
        wide = full.shape[1] // 2
        start = pl.multiple_of((row_f * 2 + c) * depth, depth)
        return full.at[pl.ds(start, depth), pl.ds(far * wide, wide)]

    def shard_one(full, row_f, far):
        start = pl.multiple_of((row_f * 2 + c) * depth, depth)
        return full.at[pl.ds(start, depth), :]

    def spread(full, src, far, part=shard):
        dst = part(full, f, far)
        near = [send(src, dst, k) for k in range(3)]
        send(src, dst, 3)
        return near

    def relay(full, near, far, part=shard):
        for k in range(3):
            arrived(near[k])
            row = part(full, f ^ (k + 1), far)
            send(row, row, 3)

    mine = pl.ds(half * slots, slots)
    other = pl.ds((1 - half) * slots, slots)
    send(small_ref, full_small.at[z], 4)
    far_small = send(small_ref, full_small.at[z], 5)
    send(x_ref.at[mine], full_x.at[:, :, feature(z)], 4)
    far_inner = send(inner_ref, shard(full_inner, f, 1), 5)
    far_step = send(step_ref, shard(full_step, f, 1), 5)
    piece = seq // FAR_PARTS
    far_x = [
        send(x_ref.at[other, pl.ds(piece * i, piece)], full_x.at[:, pl.ds(piece * i, piece), feature(z)], 5)
        for i in range(FAR_PARTS)
    ]
    send(late_ref, late_far, 5)
    own_inner = spread(full_inner, inner_ref, 0)
    own_step = spread(full_step, step_ref, 0)
    own_wr = spread(full_wr, wr_ref, 0, shard_one)

    staged = (
        (x_ref.at[mine], x_own, full_x.at[:, :, feature(z)]),
        (inner_ref, inner_own, shard(full_inner, f, 0)),
        (step_ref, step_own, shard(full_step, f, 0)),
        (wr_ref, wr_own, shard_one(full_wr, f, 0)),
        (small_ref, small_own, full_small.at[z]),
    )
    loads = [pltpu.make_async_copy(src, buf, local_sem.at[0, i]) for i, (src, buf, _) in enumerate(staged)]
    stores = [pltpu.make_async_copy(buf, dst, local_sem.at[1, i]) for i, (_, buf, dst) in enumerate(staged)]
    for load in loads:
        load.start()
    for load, store in zip(loads, stores):
        load.wait()
        store.start()

    arrived(far_small)
    send(full_small.at[z ^ 2], full_small.at[z ^ 2], 4)
    arrived(far_inner)
    away_inner = spread(full_inner, shard(full_inner, f, 1), 1)
    arrived(far_step)
    away_step = spread(full_step, shard(full_step, f, 1), 1)

    def both(i):
        arrived(far_x[i])
        part = full_x.at[:, pl.ds(piece * i, piece), feature(z ^ 2)]
        send(part, part, 4)

    relay(full_inner, own_inner, 0)
    relay(full_step, own_step, 0)
    relay(full_wr, own_wr, 0, shard_one)
    both(0)
    relay(full_inner, away_inner, 1)
    relay(full_step, away_step, 1)
    both(1)
    both(2)
    both(3)
    for store in stores:
        store.wait()
    for copy, done in copies:
        if not done:
            copy.wait_recv()
        copy.wait_send()


def fetch(hidden, inner, late, step, wr, small):
    slot_count, seq, cols = hidden.shape
    slots, depth = slot_count // 2, inner.shape[0]
    total = 8 * depth
    count = 1 + 2 * FAR_PARTS + 3 + 5 * 7 + 3
    anywhere = pl.BlockSpec(memory_space=pl.ANY)
    full = lambda x: jax.ShapeDtypeStruct((total, 2 * x.shape[1]), BF16)
    return pl.pallas_call(
        fetch_kernel,
        in_specs=[anywhere] * 6,
        out_specs=[anywhere] * 6,
        out_shape=[
            jax.ShapeDtypeStruct((slots, seq, 4 * cols), BF16),
            full(inner), jax.ShapeDtypeStruct(late.shape, BF16), full(step),
            jax.ShapeDtypeStruct((total, wr.shape[1]), BF16),
            jax.ShapeDtypeStruct((4,) + small.shape, F32),
        ],
        scratch_shapes=[
            pltpu.VMEM((slots, seq, cols), BF16),
            pltpu.VMEM(inner.shape, BF16),
            pltpu.VMEM(step.shape, BF16),
            pltpu.VMEM(wr.shape, BF16),
            pltpu.VMEM(small.shape, F32),
            pltpu.SemaphoreType.DMA((count,)),
            pltpu.SemaphoreType.DMA((count,)),
            pltpu.SemaphoreType.DMA((2, 5)),
        ],
        compiler_params=pltpu.CompilerParams(collective_id=0, has_side_effects=True),
        name="fetch",
    )(hidden, inner, late, step, wr, small)


def finish_kernel(
    part_ref, relay_ref, grad_ref, core_ref, small_ref, cross_ref,
    near_out, other_out, home_out, narrow_out, small_out, small_far, cross_out, cross_far,
    relay_buf, part_buf, sum_buf, core_buf, own_buf, plane_buf, got_buf, sent_buf, home_buf, wr_send, wr_got,
    small_got, cross_got, send_sem, recv_sem, load_sem,
):
    f, c, z = lax.axis_index("fsdp"), lax.axis_index("ctx"), lax.axis_index("tp")
    tokens, cols = near_out.shape
    depth, inner = home_out.shape
    partners = (
        {"fsdp": f ^ 1}, {"fsdp": f ^ 2}, {"fsdp": f ^ 3}, {"ctx": c ^ 1}, {"tp": z ^ 1}, {"tp": z ^ 2},
    )
    barrier = pltpu.get_barrier_semaphore()
    for partner in partners:
        pl.semaphore_signal(barrier, inc=1, device_id=partner, device_id_type=MESH)

    def feature(which):
        return pl.ds(pl.multiple_of(which * cols, 128), cols)

    def rows_of(row_f, core):
        return pl.ds(pl.multiple_of((row_f * 2 + core) * depth, depth), depth)

    piece = tokens // FAR_PARTS
    loads = [
        pltpu.make_async_copy(grad_ref.at[rows_of(f ^ k, c)], own_buf.at[k], load_sem.at[k]) for k in range(4)
    ] + [
        pltpu.make_async_copy(core_ref.at[f ^ k], core_buf.at[k], load_sem.at[4 + k]) for k in range(4)
    ] + [
        pltpu.make_async_copy(relay_ref.at[pl.ds(piece * i, piece)], relay_buf.at[i], load_sem.at[8 + i])
        for i in range(FAR_PARTS)
    ] + [
        pltpu.make_async_copy(
            part_ref.at[pl.ds(piece * i, piece), feature(z ^ 2)], part_buf.at[i], load_sem.at[8 + FAR_PARTS + i]
        )
        for i in range(FAR_PARTS)
    ]
    for load in loads:
        load.start()
    pl.semaphore_wait(barrier, len(partners))

    copies = []

    def send(src, dst, partner):
        at = len(copies)
        copy = pltpu.make_async_remote_copy(
            src_ref=src, dst_ref=dst, send_sem=send_sem.at[at], recv_sem=recv_sem.at[at],
            device_id=partners[partner], device_id_type=MESH,
        )
        copy.start()
        copies.append([copy, False])
        return at

    def arrived(at):
        copies[at][0].wait_recv()
        copies[at][1] = True

    small = [send(small_ref, small_got.at[0], 3)]
    cross = [send(cross_ref, cross_got, 4)]
    def passed_on(i):
        loads[8 + i].wait()
        loads[8 + FAR_PARTS + i].wait()
        sum_buf[i] = (part_buf[i].astype(F32) + relay_buf[i].astype(F32)).astype(BF16)
        send(sum_buf.at[i], other_out.at[pl.ds(piece * i, piece)], 5)

    for load in loads[:8]:
        load.wait()
    arrived(small[0])
    small_out[...] = small_ref[...] + small_got[0]
    small.append(send(small_out, small_got.at[1], 0))
    arrived(cross[0])
    cross_out[...] = cross_ref[...] + cross_got[...]
    cross.append(send(cross_out, cross_far, 5))
    for k in (1, 2, 3):
        sent_buf[k - 1] = (own_buf[k].astype(F32) + core_buf[k].astype(F32)).astype(BF16)
    passed_on(0)
    arrived(small[1])
    copies[small[1]][0].wait_send()
    small_out[...] = small_out[...] + small_got[1]
    small.append(send(small_out, small_got.at[2], 1))
    plane = [send(sent_buf.at[k], plane_buf.at[k], k) for k in range(3)]
    for i in range(1, FAR_PARTS):
        passed_on(i)
    arrived(small[2])
    copies[small[2]][0].wait_send()
    small_out[...] = small_out[...] + small_got[2]
    small.append(send(small_out, small_got.at[3], 4))
    middle = tokens // 2
    send(part_ref.at[pl.ds(0, middle), feature(z ^ 1)], near_out.at[pl.ds(0, middle)], 4)
    arrived(small[3])
    copies[small[3]][0].wait_send()
    shared = small_out.shape[0] // 2
    small_out[shared:, :] = small_out[shared:, :] + small_got[3, shared:, :]
    small.append(send(small_out, small_far, 5))
    total = own_buf[0].astype(F32) + core_buf[0].astype(F32)
    for at in plane:
        arrived(at)
    for k in range(3):
        total = total + plane_buf[k].astype(F32)
    wr_send[...] = total[:, 2 * inner : 2 * inner + 2 * STATE]
    wr = send(wr_send, wr_got, 4)
    home_out[...] = total[:, :inner]
    home_buf[:, :inner] = total[:, inner : 2 * inner].astype(BF16)
    narrow_out[:, 2 * STATE : 2 * STATE + 128] = total[:, 2 * inner + 2 * STATE :]
    home_buf[:, inner + 2 * STATE :] = total[:, 2 * inner + 2 * STATE :].astype(BF16)
    arrived(wr)
    both = wr_send[...] + wr_got[...]
    narrow_out[:, : 2 * STATE] = both
    home_buf[:, inner : inner + 2 * STATE] = both.astype(BF16)
    last = send(home_buf, got_buf, 5)
    send(part_ref.at[pl.ds(middle, middle), feature(z ^ 1)], near_out.at[pl.ds(middle, middle)], 4)
    arrived(last)
    home_out[...] += got_buf[:, :inner].astype(F32)
    narrow_out[:, : 2 * STATE] += got_buf[:, inner : inner + 2 * STATE].astype(F32)
    steps = got_buf[:, inner + 2 * STATE :].astype(F32)
    narrow_out[:, 2 * STATE + 128 :] = steps
    for copy, done in copies:
        if not done:
            copy.wait_recv()
    waited = {small[1], small[2], small[3]}
    for at, (copy, done) in enumerate(copies):
        if at not in waited:
            copy.wait_send()


def finish(part, relay, grad, core, small, cross, depth):
    tokens, width = part.shape
    cols, total = width // 4, grad.shape[1]
    rest = 2 * STATE + 128
    inner = (total - rest) // 2
    anywhere = pl.BlockSpec(memory_space=pl.ANY)
    vmem = pl.BlockSpec(memory_space=pltpu.VMEM)
    count = 5 + 2 + FAR_PARTS + 2 + 3 + 2
    return pl.pallas_call(
        finish_kernel,
        in_specs=[anywhere, anywhere, anywhere, anywhere, vmem, vmem],
        out_specs=[anywhere, anywhere, vmem, vmem, vmem, vmem, vmem, vmem],
        out_shape=[
            jax.ShapeDtypeStruct((tokens, cols), BF16),
            jax.ShapeDtypeStruct((tokens, cols), BF16),
            jax.ShapeDtypeStruct((depth, inner), F32),
            jax.ShapeDtypeStruct((depth, rest + 128), F32),
            jax.ShapeDtypeStruct(small.shape, F32),
            jax.ShapeDtypeStruct(small.shape, F32),
            jax.ShapeDtypeStruct(cross.shape, F32),
            jax.ShapeDtypeStruct(cross.shape, F32),
        ],
        scratch_shapes=[
            pltpu.VMEM((FAR_PARTS, tokens // FAR_PARTS, cols), BF16),
            pltpu.VMEM((FAR_PARTS, tokens // FAR_PARTS, cols), BF16),
            pltpu.VMEM((FAR_PARTS, tokens // FAR_PARTS, cols), BF16),
            pltpu.VMEM((4, depth, total), BF16),
            pltpu.VMEM((4, depth, total), BF16),
            pltpu.VMEM((3, depth, total), BF16),
            pltpu.VMEM((depth, inner + rest), BF16),
            pltpu.VMEM((3, depth, total), BF16),
            pltpu.VMEM((depth, inner + rest), BF16),
            pltpu.VMEM((depth, 2 * STATE), F32),
            pltpu.VMEM((depth, 2 * STATE), F32),
            pltpu.VMEM((4,) + small.shape, F32),
            pltpu.VMEM(cross.shape, F32),
            pltpu.SemaphoreType.DMA((count,)),
            pltpu.SemaphoreType.DMA((count,)),
            pltpu.SemaphoreType.DMA((8 + 2 * FAR_PARTS,)),
        ],
        compiler_params=pltpu.CompilerParams(collective_id=1, has_side_effects=True),
        name="finish",
    )(part, relay, grad, core, small, cross)


def after(x, other):
    return lax.optimization_barrier((x, other))[0]


def everywhere(x):
    for axis in ("ctx", "fsdp"):
        count, bit = lax.axis_size(axis), 1
        if count & (count - 1):
            x = lax.psum(x, axis)
            continue
        while bit < count:
            x = x + lax.ppermute(x, axis, [(i, i ^ bit) for i in range(count)])
            bit *= 2
    return x


def pack(parts):
    return jnp.concatenate([part.reshape(-1) for part in parts])


def unpack(vector, shapes):
    parts, at = [], 0
    for shape in shapes:
        size = 1
        for dim in shape:
            size *= dim
        parts.append(vector[at : at + size].reshape(shape))
        at += size
    return parts


def on_device(
    hidden_in,
    lengths,
    norm_gain,
    proj_gate_inner,
    proj_write_read,
    proj_step,
    conv_inner,
    conv_inner_bias,
    conv_write_read,
    conv_write_read_bias,
    step_bias,
    log_rate,
    skip_gain,
    gate_gain,
    proj_out,
    out_cotangent,
):
    slot_count, seq_here, width_here = hidden_in.shape
    slots = slot_count // 2
    tokens = slots * seq_here
    heads_own = step_bias.shape[0]
    inner_own = gate_gain.shape[0]
    heads = 2 * heads_own
    inner = 2 * inner_own
    tp_count = lax.axis_size("tp")
    width = tp_count * width_here
    groups = seq_here // GROUP
    blocks = slots * groups
    head_steps = heads // HEADS_STEP
    rim_rows = CONV - 1
    place = lax.axis_index("tp")
    far_half, near_side = place // 2, place % 2

    def half_of(whole, which):
        return lax.dynamic_slice_in_dim(whole, which * slots, slots, 0)

    def ordered(own, near, far, both, axis):
        first = lambda a, b: jnp.where(near_side == 0, a, b)
        a0, a1, b0, b1 = first(own, near), first(near, own), first(far, both), first(both, far)
        lower = lambda a, b: jnp.where(far_half == 0, a, b)
        return jnp.concatenate(
            [lower(a0, b0), lower(a1, b1), lower(b0, a0), lower(b1, a1)], axis=axis
        )

    ready = []

    def own_features(piece):
        first, second = piece(place ^ 3).astype(BF16), piece(place ^ 1).astype(BF16)
        relay = swap(first, 1)
        keep = swap(second, 1)
        summed = (piece(place ^ 2) + relay.astype(F32)).astype(BF16)
        ready.extend([first, second, summed])
        sent = swap(summed, 2)
        kept = (piece(place) + keep.astype(F32)).reshape(slots, seq_here, width_here)
        other = sent.astype(F32).reshape(slots, seq_here, width_here)
        return both_halves(kept, other)

    def both_halves(kept, other):
        return jnp.where(
            far_half == 0,
            jnp.concatenate([kept, other], axis=0),
            jnp.concatenate([other, kept], axis=0),
        )

    small_shapes = [(CONV, inner_own), (inner_own,), (inner_own,), (heads_own,), (heads_own,), (heads_own,)]
    def gathered(x):
        return lax.all_gather(x, ("fsdp", "ctx"), axis=0, tiled=True)

    own_small = pack([conv_inner, conv_inner_bias, gate_gain, step_bias, log_rate, skip_gain])
    cot_mine, cot_other = half_of(out_cotangent, far_half), half_of(out_cotangent, 1 - far_half)
    narrow_cols = 2 * STATE + heads
    narrow_pad = -narrow_cols % 128
    zeros = lambda x, extra: jnp.zeros((x.shape[0], extra), BF16)
    inner_shard, gate_shard = proj_gate_inner[:, 1], proj_gate_inner[:, 0]
    if lax.axis_size("fsdp") == 4 and lax.axis_size("ctx") == 2:
        step_shard = jnp.concatenate([proj_step, zeros(proj_step, 128 - heads_own)], axis=1)
        small = pack([norm_gain.astype(F32), own_small])
        small = jnp.pad(small, (0, -small.size % 1024)).reshape(-1, 128)
        late_shard = jnp.concatenate([gate_shard, proj_out], axis=1)
        full_x, full_inner, late_far, full_step, full_wr, full_small = fetch(
            hidden_in, inner_shard, late_shard, step_shard, proj_write_read, small
        )
        gate_far, out_far = late_far[:, :inner_own], late_far[:, inner_own:]
        full_small = full_small.reshape(tp_count, -1)
        full_gain = full_small[:, :width_here].reshape(width)
        far_row = lax.dynamic_slice_in_dim(full_small, place ^ 2, 1, 0)[0, width_here:]
        far_small = unpack(far_row, small_shapes)
        full_narrow = jnp.concatenate(
            [full_wr, full_step[:, :heads_own], full_step[:, 128 : 128 + heads_own], zeros(full_wr, narrow_pad)],
            axis=1,
        )
        cot_dep = full_x
    else:
        x_mine, x_other = half_of(hidden_in, far_half), half_of(hidden_in, 1 - far_half)
        narrow_shard = jnp.concatenate(
            [proj_write_read, proj_step, swap(proj_step, 2), zeros(proj_step, narrow_pad)], axis=1
        )
        inner_far = swap(inner_shard, 2)
        x_near = swap(x_mine, 1)
        x_far = swap(after(x_other, inner_far), 2)
        gate_far = swap(after(gate_shard, x_far), 2)
        x_both = swap(x_far, 1)
        cot_dep = after(x_both, gate_far)
        out_far = swap(after(proj_out, cot_dep), 2)
        full_narrow = gathered(narrow_shard)
        full_inner = gathered(jnp.concatenate([inner_shard, inner_far], axis=1))
        full_x = ordered(x_mine, x_near, x_far, x_both, 2)
        gain = norm_gain.astype(F32)
        full_gain = ordered(gain, swap(gain, 1), swap(gain, 2), swap(gain, 3), 0)
        far_small = unpack(swap(own_small, 2), small_shapes)
    full_x = full_x.reshape(tokens, width)
    full_late = gathered(jnp.concatenate([gate_shard, gate_far, proj_out, out_far], axis=1))
    full_gate, full_out = full_late[:, :inner], full_late[:, inner:]
    cot_mine, cot_other, cot_dep = lax.optimization_barrier((cot_mine, cot_other, cot_dep))
    cot_near, cot_far, cot_both = swap(cot_mine, 1), swap(cot_other, 2), swap(cot_other, 3)
    taps = jnp.concatenate([conv_inner, far_small[0]], axis=1)
    taps_bias = jnp.concatenate([conv_inner_bias, far_small[1]])
    gain_gate = jnp.concatenate([gate_gain, far_small[2]])
    bias_step = jnp.concatenate([step_bias, far_small[3]])
    rate_log = jnp.concatenate([log_rate, far_small[4]])
    gain_skip = jnp.concatenate([skip_gain, far_small[5]])
    rate = -jnp.exp(rate_log)
    skip_lanes = jnp.repeat(gain_skip, HEADDIM)[None]

    in_float = full_x.astype(F32)
    in_scale = lax.rsqrt(jnp.mean(in_float * in_float, axis=-1, keepdims=True) + EPSILON)
    normed = (in_float * in_scale * full_gain.astype(F32)).astype(BF16)
    narrow_pre = dot(normed, full_narrow, 1, 0)
    inner_pre = dot(normed, full_inner, 1, 0).astype(BF16)
    gate_pre = dot(normed, full_gate, 1, 0).astype(BF16)
    cot_near, cot_far, cot_both, gate_pre = lax.optimization_barrier((cot_near, cot_far, cot_both, gate_pre))
    full_cot = ordered(cot_mine, cot_near, cot_far, cot_both, 2).reshape(tokens, width)

    def rim_of(pre):
        by_slot = pre.reshape(slots, seq_here, pre.shape[-1])
        return passed_along(by_slot[:, seq_here - rim_rows :].astype(BF16), "ctx", 1)

    inner_rim, narrow_rim = rim_of(inner_pre), rim_of(narrow_pre[:, : 2 * STATE])
    lane_pad = lambda x: jnp.pad(x, (0, 128 - heads))[None]
    rate_row = lane_pad(rate)
    inner_act, slope, write_read, narrow_slope, cols, cum_rows, local_state, decay_lanes = start_blocks(
        inner_pre, inner_rim, narrow_pre, narrow_rim, taps, taps_bias[None], conv_write_read,
        conv_write_read_bias[None], lane_pad(bias_step), rate_row, groups, heads,
    )
    local_state = local_state.reshape(slots, groups, STATE, inner)
    decay_lanes = decay_lanes.reshape(slots, groups, 1, inner)
    carried = local_state[:, 0]
    device_decay = decay_lanes[:, 0]
    for position in range(1, groups):
        carried = decay_lanes[:, position] * carried + local_state[:, position]
        device_decay = device_decay * decay_lanes[:, position]
    current = carried_in(device_decay, carried, None, False)
    state_list = []
    for position in range(groups):
        state_list.append(current)
        current = decay_lanes[:, position] * current + local_state[:, position]
    states = jnp.stack(state_list, axis=1)
    states_low = states.astype(BF16).reshape(blocks, STATE, inner)

    position_ids = lax.axis_index("ctx") * seq_here + jnp.arange(seq_here)
    valid_rows = (position_ids[None, :] < lengths[:, None]).astype(F32)
    valid_here = half_of(valid_rows, far_half).reshape(tokens, 1)
    masked = (full_cot.astype(F32) * valid_here).astype(BF16)
    grad_normed_out = dot(masked, full_out, 1, 0).astype(BF16)
    mixed_out, stats = mix_blocks(
        inner_act, gate_pre, grad_normed_out, write_read, cols, cum_rows, states_low, skip_lanes, gain_gate[None],
    )
    stats = stats + swap(stats, 1)
    normed_out, grad_gate_pre, grad_diag, grad_gate_gain, grad_skip_lanes, local_grad = gate_blocks(
        mixed_out, gate_pre, grad_normed_out, inner_act, stats, gain_gate[None], write_read, cols, heads
    )
    local_grad = local_grad.reshape(slots, groups, STATE, inner)

    def branch_piece(which):
        rows = lax.dynamic_slice(full_late, (which * width_here, inner), (width_here, inner))
        return dot(normed_out, rows, 1, 1)

    branch = own_features(branch_piece)
    hidden_out = (hidden_in.astype(F32) + valid_rows[..., None] * branch).astype(BF16)
    normed_out, grad_gate_pre, *_ = lax.optimization_barrier((normed_out, grad_gate_pre, ready[0], ready[1]))
    grad_proj_out = dot(masked, normed_out, 0, 0).astype(BF16)
    grad_gate_w = dot(normed, grad_gate_pre, 0, 0).astype(BF16)
    grad_by_gate = dot(grad_gate_pre, full_gate, 1, 1).astype(BF16)
    other_scale = swap(in_scale.reshape(-1, 128), 2)

    flowing = local_grad[:, groups - 1]
    for position in reversed(range(groups - 1)):
        flowing = decay_lanes[:, position] * flowing + local_grad[:, position]
    flowing = carried_in(device_decay, flowing, None, True)
    flow_list = []
    for position in reversed(range(groups)):
        flow_list.insert(0, flowing)
        flowing = decay_lanes[:, position] * flowing + local_grad[:, position]
    flows = jnp.stack(flow_list, axis=1)
    flows_low = flows.astype(BF16).reshape(blocks, STATE, inner)
    flows_low = after(flows_low, (grad_proj_out, grad_gate_w, ready[2]))

    grad_inner_pre, grad_narrow, tap_sums, narrow_sums, head_sums, halo, narrow_halo = back_blocks(
        inner_act, mixed_out, grad_diag, slope, inner_pre, inner_rim, write_read, narrow_slope, narrow_pre,
        narrow_rim, cols, cum_rows, states_low, flows_low, skip_lanes, taps, conv_write_read, rate_row, groups,
    )
    tap_sums = tap_sums.transpose(1, 0, 2).reshape(8, inner)
    grad_taps, grad_taps_bias = tap_sums[:CONV], tap_sums[CONV]
    grad_conv_write_read, grad_conv_write_read_bias = narrow_sums[:CONV], narrow_sums[CONV]
    grad_step_bias, grad_log_rate = head_sums[0, :heads], head_sums[1, :heads]

    def completed(grad, halo):
        back = passed_along(halo, "ctx", -1)
        for slot in range(slots):
            ends = (slot + 1) * seq_here
            rows = grad[ends - 8 : ends, : halo.shape[-1]].astype(F32) + back[slot]
            grad = lax.dynamic_update_slice(grad, rows.astype(BF16), (ends - 8, 0))
        return grad

    grad_inner_pre, grad_narrow = completed(grad_inner_pre, halo), completed(grad_narrow, narrow_halo)
    def reduced(x):
        return lax.psum_scatter(x, ("fsdp", "ctx"), scatter_dimension=0, tiled=True)

    early = reduced(jnp.concatenate([grad_proj_out, grad_gate_w], axis=1))
    early_away = jnp.concatenate([early[:, inner_own:inner], early[:, inner + inner_own :]], axis=1)
    grad_inner_pre, hidden_out, early_away = lax.optimization_barrier((grad_inner_pre, hidden_out, early_away))
    early_far = swap(early_away, 2)
    by_kernel = lax.axis_size("fsdp") == 4 and lax.axis_size("ctx") == 2
    late = jnp.concatenate([grad_inner_pre, grad_narrow], axis=1)
    if by_kernel:
        which = (place ^ 3) * width_here
        rows_at = lambda full: lax.dynamic_slice_in_dim(full, which, width_here, 0)
        relay_piece = (
            lax.dynamic_slice_in_dim(grad_by_gate, which, width_here, 1)
            + dot(grad_inner_pre, rows_at(full_inner), 1, 1)
            + dot(grad_narrow, rows_at(full_narrow), 1, 1)
        ).astype(BF16)
        relay = swap(relay_piece, 1)
        late = after(late, relay_piece)
    grad_late_w = dot(normed, late, 0, 0).astype(BF16)
    if by_kernel:
        by_core = grad_late_w.reshape(4, 2, -1, grad_late_w.shape[1])
        away = lax.dynamic_index_in_dim(by_core, 1 - lax.axis_index("ctx"), 1, keepdims=False)
        core = lax.ppermute(away, "ctx", [(0, 1), (1, 0)])
        grad_inner_pre, grad_narrow, *_ = lax.optimization_barrier(
            (grad_inner_pre, grad_narrow, away, early_far)
        )
    by_inner = dot(grad_inner_pre, full_inner, 1, 1)
    partial_normed = grad_by_gate + by_inner + dot(grad_narrow, full_narrow, 1, 1)
    grad_out_home = early[:, :inner_own].astype(F32) + early_far[:, :inner_own].astype(F32)
    grad_gate_home = early[:, inner : inner + inner_own].astype(F32) + early_far[:, inner_own:].astype(F32)
    by_hat = partial_normed * (full_x.astype(F32) * in_scale)
    grad_gain_full = jnp.sum(by_hat, axis=0)
    cross_part = jnp.sum(by_hat * full_gain.astype(F32), axis=1)
    partial_low = partial_normed.astype(BF16)

    grad_skip_gain = jnp.sum(grad_skip_lanes.reshape(heads, HEADDIM), axis=1)
    shared_shapes = [(CONV, 2 * STATE), (2 * STATE,), (width,)]
    head_shapes = [(CONV, inner), (inner,), (inner,), (heads,), (heads,), (heads,)]
    by_head = pack([grad_taps, grad_taps_bias, grad_gate_gain, grad_step_bias, grad_log_rate, grad_skip_gain])
    by_all = pack([grad_conv_write_read, grad_conv_write_read_bias, grad_gain_full])

    if by_kernel:
        span = max(inner, width, (CONV + 1) * 2 * STATE)
        line = lambda v: jnp.pad(v.reshape(-1, v.shape[-1]), ((0, 0), (0, span - v.shape[-1])))
        by_lines = jnp.concatenate(
            [
                line(tap_sums[: CONV + 1]),
                line(grad_gate_gain),
                line(jnp.concatenate([grad_step_bias, grad_log_rate, grad_skip_gain])),
                jnp.zeros((1, span), F32),
                line(grad_gain_full),
                line(narrow_sums[: CONV + 1].reshape(-1)),
                jnp.zeros((6, span), F32),
            ]
        )
        near, other, grad_inner_home, narrow_sum, small_own, small_far, cross_rows, cross_far = finish(
            partial_low,
            relay,
            grad_late_w,
            core,
            by_lines,
            cross_part.reshape(-1, 128),
            proj_write_read.shape[0],
        )
        kept = lax.dynamic_slice_in_dim(partial_normed, place * width_here, width_here, 1) + near.astype(F32)
        grad_normed = both_halves(
            kept.reshape(slots, seq_here, width_here), other.astype(F32).reshape(slots, seq_here, width_here)
        )
        write_read_home = narrow_sum[:, : 2 * STATE]
        step_home = (
            narrow_sum[:, 2 * STATE : 2 * STATE + heads_own]
            + narrow_sum[:, 2 * STATE + 128 + heads_own : 2 * STATE + 128 + heads]
        )
        cross_rows, cross_far = cross_rows.reshape(-1), cross_far.reshape(-1)
        homes = [
            small_own[at, :inner_own] + small_far[at, inner_own:inner] for at in (slice(0, CONV), CONV, CONV + 1)
        ] + [
            small_own[CONV + 2, k * heads : k * heads + heads_own]
            + small_far[CONV + 2, k * heads + heads_own : (k + 1) * heads]
            for k in range(3)
        ]
        shared = small_own[8:] + small_far[8:]
        grad_norm_gain = lax.dynamic_slice_in_dim(shared[0], place * width_here, width_here, 0)
        wr_sums = shared[1, : (CONV + 1) * 2 * STATE].reshape(CONV + 1, 2 * STATE)
        wr_taps, wr_bias = wr_sums[:CONV], wr_sums[CONV]
    else:

        def normed_piece(which):
            return lax.dynamic_slice_in_dim(partial_normed, which * width_here, width_here, 1)

        grad_normed = own_features(normed_piece)
        late_sum = reduced(grad_late_w)
        late_far = swap(late_sum, 2).astype(F32)
        late_sum = late_sum.astype(F32)
        grad_inner_home = late_sum[:, :inner_own] + late_far[:, inner_own:inner]
        write_read_home = late_sum[:, inner : inner + 2 * STATE] + late_far[:, inner : inner + 2 * STATE]
        write_read_home = write_read_home + swap(write_read_home, 1)
        steps_at = inner + 2 * STATE
        step_home = late_sum[:, steps_at : steps_at + heads_own] + late_far[:, steps_at + heads_own : steps_at + heads]
        cross_rows = cross_part + swap(cross_part, 1)
        cross_far = swap(cross_rows, 2)
        smalls = everywhere(pack([by_head, by_all]))
        parts = unpack(smalls[: by_head.size], head_shapes)
        away = [lax.slice_in_dim(p, p.shape[-1] // 2, p.shape[-1], axis=p.ndim - 1) for p in parts]
        far_parts = unpack(swap(pack(away), 2), small_shapes)
        shared = smalls[by_head.size :]
        shared = shared + swap(shared, 1)
        shared = shared + swap(shared, 2)
        homes = [
            lax.slice_in_dim(p, 0, p.shape[-1] // 2, axis=p.ndim - 1) + a for p, a in zip(parts, far_parts)
        ]
        wr_taps, wr_bias, gain_all = unpack(shared, shared_shapes)
        grad_norm_gain = lax.dynamic_slice_in_dim(gain_all, place * width_here, width_here, 0)

    own_gain = norm_gain.astype(F32)
    own_scale = both_halves(
        in_scale.reshape(slots, seq_here, 1), other_scale.reshape(slots, seq_here, 1)
    )
    own_hat = hidden_in.astype(F32) * own_scale
    grad_hat_in = grad_normed * own_gain
    cross_in = both_halves(
        cross_rows.reshape(slots, seq_here, 1), cross_far.reshape(slots, seq_here, 1)
    ) / width
    grad_hidden_in = own_scale * (grad_hat_in - own_hat * cross_in) + out_cotangent.astype(F32)
    return (
        hidden_out,
        grad_hidden_in,
        grad_norm_gain,
        jnp.stack([grad_gate_home, grad_inner_home], axis=1),
        write_read_home,
        step_home,
        homes[0],
        homes[1],
        wr_taps,
        wr_bias,
        homes[3],
        homes[4],
        homes[5],
        homes[2],
        grad_out_home,
    )


def solution(mesh):
    rows = ("fsdp", "ctx")
    acts = P("fsdp", "ctx", "tp")
    placed = (
        acts,
        P("fsdp"),
        P("tp"),
        P(rows, None, "tp"),
        P(rows, None),
        P(rows, "tp"),
        P(None, "tp"),
        P("tp"),
        P(),
        P(),
        P("tp"),
        P("tp"),
        P("tp"),
        P("tp"),
        P(rows, "tp"),
        acts,
    )
    return jax.shard_map(
        on_device,
        mesh=mesh,
        in_specs=placed,
        out_specs=(
            acts,
            acts,
            P("tp"),
            P(rows, None, "tp"),
            P(rows, None),
            P(rows, "tp"),
            P(None, "tp"),
            P("tp"),
            P(),
            P(),
            P("tp"),
            P("tp"),
            P("tp"),
            P("tp"),
            P(rows, "tp"),
        ),
        check_vma=False,
    )
```
